128 devices in a mesh: dp: 16 (over x, z_lo, core), tensor: 8 (over z_hi, y).
Axes of the slice: x: 4, y: 4, z: 4 (z_hi: 2, z_lo: 2; z = z_hi * 2 + z_lo), core: 2. Of those that a mesh axis runs over, the one named last changes fastest.
Arguments:
- tokens: bfloat16 [8192, 2048], P('dp'), may hold values from -6 to 6
- first_gain: float32 [2048], replicated, may hold values from 0.5 to 1.5
- first_shift: float32 [2048], replicated, may hold values from -1.75 to 1.75
- query_weight: float32 [2048, 2048], P('dp', 'tensor'), may hold values from -0.125 to 0.125
- query_bias: float32 [2048], P('tensor'), may hold values from -3 to 3
- key_weight: float32 [2048, 2048], P('dp', 'tensor'), may hold values from -0.125 to 0.125
- value_weight: float32 [2048, 2048], P('dp', 'tensor'), may hold values from -0.125 to 0.125
- value_bias: float32 [2048], P('tensor'), may hold values from -3 to 3
- out_weight: float32 [2048, 2048], P('tensor', 'dp'), may hold values from -0.5 to 0.5
- out_bias: float32 [2048], replicated, may hold values from -1.75 to 1.75
- second_gain: float32 [2048], replicated, may hold values from 0.5 to 1.5
- second_shift: float32 [2048], replicated, may hold values from -1.75 to 1.75
- up_weight: float32 [2048, 8192], P('dp', 'tensor'), may hold values from -0.125 to 0.125
- up_bias: float32 [8192], P('tensor'), may hold values from -3 to 3
- down_weight: float32 [8192, 2048], P('tensor', 'dp'), may hold values from -0.0625 to 0.0625
- down_bias: float32 [2048], replicated, may hold values from -1.75 to 1.75
- cotangent: bfloat16 [8192, 2048], P('dp'), may hold values from -6 to 6
- prefix: int32 [1], replicated, may hold values from 819 to 4096
- block_order: int32 [32], replicated, may hold values from 0 to 31, as said below
Outputs:
- layer_out: bfloat16 [8192, 2048], P('dp')
- tokens_grad: float32 [8192, 2048], P('dp')
- first_gain_grad: float32 [2048], replicated
- first_shift_grad: float32 [2048], replicated
- query_weight_grad: float32 [2048, 2048], P('dp', 'tensor')
- query_bias_grad: float32 [2048], P('tensor')
- key_weight_grad: float32 [2048, 2048], P('dp', 'tensor')
- value_weight_grad: float32 [2048, 2048], P('dp', 'tensor')
- value_bias_grad: float32 [2048], P('tensor')
- out_weight_grad: float32 [2048, 2048], P('tensor', 'dp')
- out_bias_grad: float32 [2048], replicated
- second_gain_grad: float32 [2048], replicated
- second_shift_grad: float32 [2048], replicated
- up_weight_grad: float32 [2048, 8192], P('dp', 'tensor')
- up_bias_grad: float32 [8192], P('tensor')
- down_weight_grad: float32 [8192, 2048], P('tensor', 'dp')
- down_bias_grad: float32 [2048], replicated
The draws below stay inside these ranges and needn't reach their ends.
Inputs may be any that keep to these rules, and one draw needn't show every extreme that they name: `block_order`: for each sequence s, entries s * 32 to s * 32 + 31 are a permutation of those same numbers: every stored block lies in its own sequence's rows, but its place within the sequence is shuffled.
All inputs are finite; a program needn't handle non-finite values.
Results may differ from the reference program's by a relative error of at most 0.025.
Values may be sent and summed in bfloat16 or wider, within the bound.
A program may use at most 192 MiB of HBM per device.

```python
import math
import jax
import jax.numpy as jnp
from jax import lax

D = 2048
HEADS = 16
HEAD = 128
FF = 8192
SEQ_LEN = 8192
TOKENS = 8192
SEQS = 1
BLK = 256
BPS = 32
NBLK = 32


def draw_block_order(key, part):
    seed_keys = jax.random.split(key, SEQS)
    shuffled = jax.vmap(lambda seed_key: jax.random.permutation(seed_key, BPS))(seed_keys)
    offsets = jnp.arange(SEQS, dtype=jnp.int32)[:, None] * BPS
    return (shuffled.astype(jnp.int32) + offsets).reshape(NBLK)


def strengthened(values, stream_key, source, target, blocks, factor):
    owner, partner = [(jnp.arange(values.shape[axis_at]) // (values.shape[axis_at] // blocks)).reshape([-1 if axis == axis_at else 1 for axis in range(values.ndim)]) for axis_at in (source, target)]
    chosen = jax.random.permutation(stream_key, blocks)[partner]
    strong = (owner == chosen) | (owner == (partner + blocks // 2) % blocks)
    return jnp.where(strong, factor * values, values)


def levels(key, dims, pieces, low, top_value):
    level = 1.0
    for dim, shards_of in pieces:
        draws = jax.random.uniform(jax.random.fold_in(jax.random.fold_in(key, 6), dim), (shards_of,), jnp.float32, low / len(pieces), top_value / len(pieces))
        level = level * jnp.repeat(jnp.exp(draws), dims[dim] // shards_of).reshape((-1,) + (1,) * (len(dims) - 1 - dim))
    return level


def bell_draw(own_key, extent, spread, most, pieces=(), held_as=jnp.bfloat16):
    entries = spread * jax.random.normal(own_key, extent, jnp.float32)
    if pieces:
        entries = entries * levels(own_key, extent, pieces, -0.22, 0.18)
    return jnp.clip(entries, -most, most).astype(held_as)


def noise_with(own_key, shape, width, limit, pieces, heavy, kind=jnp.bfloat16):
    entries = width * jax.random.normal(own_key, shape, jnp.float32)
    if pieces:
        entries = entries * levels(own_key, shape, pieces, -0.22, 0.18)
    return jnp.clip(strengthened(entries, jax.random.fold_in(own_key, 3), *heavy), -limit, limit).astype(kind)


def setup_inputs(seed: int = 0) -> dict:
    streams_of = jax.random.split(jax.random.key(seed), 20)
    return {
        "tokens": noise_with(streams_of[0], (TOKENS, D), 1.0, 6.0, ((0, 16),), (0, 1, 16, 2.0)),
        "first_gain": jnp.clip(1.0 + 0.1 * jax.random.normal(streams_of[1], (D,), jnp.float32), 0.5, 1.5),
        "first_shift": bell_draw(streams_of[2], (D,), 0.3, 1.75, (), jnp.float32),
        "query_weight": bell_draw(streams_of[3], (D, D), D ** -0.5, 0.125, ((0, 16), (1, 8)), jnp.float32),
        "query_bias": bell_draw(streams_of[4], (D,), 0.5, 3.0, ((0, 8),), jnp.float32),
        "key_weight": bell_draw(streams_of[5], (D, D), D ** -0.5, 0.125, ((0, 16), (1, 8)), jnp.float32),
        "value_weight": bell_draw(streams_of[6], (D, D), D ** -0.5, 0.125, ((0, 16), (1, 8)), jnp.float32),
        "value_bias": bell_draw(streams_of[7], (D,), 0.5, 3.0, ((0, 8),), jnp.float32),
        "out_weight": bell_draw(streams_of[8], (D, D), (D // 16) ** -0.5, 0.5, ((0, 8), (1, 16)), jnp.float32),
        "out_bias": bell_draw(streams_of[9], (D,), 0.3, 1.75, (), jnp.float32),
        "second_gain": jnp.clip(1.0 + 0.1 * jax.random.normal(streams_of[10], (D,), jnp.float32), 0.5, 1.5),
        "second_shift": bell_draw(streams_of[11], (D,), 0.3, 1.75, (), jnp.float32),
        "up_weight": bell_draw(streams_of[12], (D, FF), D ** -0.5, 0.125, ((0, 16), (1, 8)), jnp.float32),
        "up_bias": bell_draw(streams_of[13], (FF,), 0.5, 3.0, ((0, 8),), jnp.float32),
        "down_weight": bell_draw(streams_of[14], (FF, D), FF ** -0.5, 0.0625, ((0, 8), (1, 16)), jnp.float32),
        "down_bias": bell_draw(streams_of[15], (D,), 0.3, 1.75, (), jnp.float32),
        "cotangent": noise_with(streams_of[16], (TOKENS, D), 1.0, 6.0, ((0, 16),), (0, 1, 16, 2.0)),
        "prefix": jax.random.randint(streams_of[17], (SEQS,), SEQ_LEN // 10, SEQ_LEN // 2 + 1).astype(jnp.int32),
        "block_order": draw_block_order(jax.random.fold_in(streams_of[19], 71), 0),
    }


epsilon = 1e-05
masked_score = -1e+30
highest = lax.Precision.HIGHEST

@jax.custom_vjp
def low(v):
    return lax.optimization_barrier(v.astype(jnp.bfloat16)).astype(jnp.float32)

@jax.custom_vjp
def low_back(v):
    return v

def low_keep(v):
    return (low(v), None)

def low_pass(kept, grad):
    return (grad,)

def back_keep(v):
    return (v, None)

def back_low(kept, grad):
    return (low(grad),)
low.defvjp(low_keep, low_pass)
low_back.defvjp(back_keep, back_low)

def layer_norm(values_in, norm_gain, norm_shift):
    average = lax.optimization_barrier(jnp.mean(values_in, axis=-1, keepdims=True))
    centred = values_in - average
    variance = lax.optimization_barrier(jnp.mean(centred * centred, axis=-1, keepdims=True))
    return centred * lax.rsqrt(variance + epsilon) * norm_gain + norm_shift

def product(left_side, right_side):
    return jnp.dot(left_side, right_side, precision=highest, preferred_element_type=jnp.float32)

def token_places(block_order):
    row_ids = jnp.arange(TOKENS, dtype=jnp.int32)
    orders = block_order[row_ids // BLK]
    return orders % BPS * BLK + row_ids % BLK

def attention(queries, keys_all, values_all, places, prefix):
    score_scale = 1.0 / math.sqrt(HEAD)

    def one_sequence(members):
        seq_query, seq_keys, seq_values, seq_places, seq_prefix = members
        allowed = (seq_places[None, :] <= seq_places[:, None]) | (seq_places[None, :] < seq_prefix)

        def one_head(head_items):
            head_query, head_keys, head_values = head_items
            scores = low_back(product(head_query, head_keys.T) * score_scale)
            scores = jnp.where(allowed, scores, masked_score)
            row_max = lax.optimization_barrier(jnp.max(scores, axis=-1, keepdims=True))
            exponent = jnp.where(allowed, jnp.exp(scores - row_max), 0.0)
            probs = exponent / lax.optimization_barrier(jnp.sum(exponent, axis=-1, keepdims=True))
            return product(low(probs), head_values)
        head_parts = (seq_query.reshape(SEQ_LEN, HEADS, HEAD).transpose(1, 0, 2), seq_keys.reshape(SEQ_LEN, HEADS, HEAD).transpose(1, 0, 2), seq_values.reshape(SEQ_LEN, HEADS, HEAD).transpose(1, 0, 2))
        attended = lax.map(jax.checkpoint(one_head), head_parts)
        return attended.transpose(1, 0, 2).reshape(SEQ_LEN, D)
    members = (queries.reshape(SEQS, SEQ_LEN, D), keys_all.reshape(SEQS, SEQ_LEN, D), values_all.reshape(SEQS, SEQ_LEN, D), places.reshape(SEQS, SEQ_LEN), prefix)
    return lax.map(jax.checkpoint(one_sequence), members).reshape(TOKENS, D)

def reference(tokens, first_gain, first_shift, query_weight, query_bias, key_weight, value_weight, value_bias, out_weight, out_bias, second_gain, second_shift, up_weight, up_bias, down_weight, down_bias, cotangent, prefix, block_order):
    places = token_places(block_order)

    def forward(residual, gain_one, shift_one, weight_query, bias_query, weight_key, weight_value, bias_value, weight_out, bias_out, gain_two, shift_two, weight_up, bias_up, weight_down, bias_down):
        normed = low(layer_norm(residual, gain_one, shift_one))
        queries = low_back(low(product(normed, low(weight_query)) + bias_query))
        keys_all = low_back(low(product(normed, low(weight_key))))
        values_all = low_back(low(product(normed, low(weight_value)) + bias_value))
        attended = attention(queries, keys_all, values_all, places, prefix)
        mixed = low_back(low(attended))
        branch = low_back(product(mixed, low(weight_out)) + bias_out)
        middle = residual + branch
        normed_two = low(layer_norm(middle, gain_two, shift_two))
        pre_act = low_back(product(normed_two, low(weight_up)) + bias_up)
        hidden = low(jax.nn.gelu(pre_act, approximate=False))
        out_branch = low_back(product(hidden, low(weight_down)) + bias_down)
        return middle + out_branch
    layer_value, pullback = jax.vjp(forward, tokens.astype(jnp.float32), first_gain, first_shift, query_weight, query_bias, key_weight, value_weight, value_bias, out_weight, out_bias, second_gain, second_shift, up_weight, up_bias, down_weight, down_bias)
    gradients = pullback(cotangent.astype(jnp.float32))
    return (layer_value.astype(jnp.bfloat16), gradients[0], gradients[1], gradients[2], gradients[3], gradients[4], gradients[5], gradients[6], gradients[7], gradients[8], gradients[9], gradients[10], gradients[11], gradients[12], gradients[13], gradients[14], gradients[15])
```

```python
import functools
import math

import jax
import jax.numpy as jnp
from jax import lax
from jax.experimental import pallas as pl
from jax.experimental.pallas import tpu as pltpu
from jax.sharding import PartitionSpec as P

HEAD = 128
BLK = 256
GRP = 4
RING = 4
EPS = 1e-05
LOG2E = math.log2(math.e)
SCALE = 1.0 / math.sqrt(HEAD)
C1 = LOG2E * SCALE
NN = (((1,), (0,)), ((), ()))
NT = (((1,), (1,)), ((), ()))
TN = (((0,), (0,)), ((), ()))
MESH = pl.DeviceIdType.MESH
VM = pl.BlockSpec(memory_space=pltpu.VMEM)
SM = pl.BlockSpec(memory_space=pltpu.SMEM)
BF = jnp.bfloat16
F32 = jnp.float32
DMA = pltpu.SemaphoreType.DMA


def dg(a, b, dims):
    return lax.dot_general(a, b, dims, preferred_element_type=F32)


def struct(shape, dtype):
    return jax.ShapeDtypeStruct(shape, dtype)


class Eight:
    def __init__(self, axis):
        d, t = lax.axis_index("dp"), lax.axis_index("tensor")
        self.axis, self.d, self.t = axis, d, t
        if axis == "dp":
            self.r, self.p = d // 4, lax.rem(d // 2, 2)
        else:
            self.r, self.p = lax.rem(t, 4), t // 4

    def ring(self, i):
        return lax.rem(self.r + i, RING)

    def index(self, r, p):
        return r * 2 + p if self.axis == "dp" else p * 4 + r

    def device(self, r, p):
        if self.axis == "dp":
            return ((r * 2 + p) * 2 + lax.rem(self.d, 2), self.t)
        return (self.d, p * 4 + r)

    def others(self):
        return [self.device(self.ring(i), self.p) for i in (1, 2, 3)] + [self.device(self.r, 1 - self.p)]


def other_core():
    d = lax.axis_index("dp")
    return (d + 1 - 2 * lax.rem(d, 2), lax.axis_index("tensor"))


def greet(devices):
    barrier = pltpu.get_barrier_semaphore()
    for device in devices:
        pl.semaphore_signal(barrier, inc=1, device_id=device, device_id_type=MESH)
    pl.semaphore_wait(barrier, len(devices))


def send(src, dst, sems, k, device):
    copy = pltpu.make_async_remote_copy(
        src_ref=src, dst_ref=dst, send_sem=sems[0].at[k], recv_sem=sems[1].at[k],
        device_id=device, device_id_type=MESH)
    copy.start()
    return copy


def split_at(rows):
    return max(16, int(rows * 0.4) // 16 * 16)


class Gather:
    SEMS = 10

    def __init__(self, group, out, sems):
        self.g, self.out, self.sems = group, out, sems
        self.cut = split_at(out.shape[1])

    def start(self):
        g, out = self.g, self.out
        own = out.at[g.index(g.r, g.p)]
        self.first = [send(own, own, self.sems, 0, g.device(g.r, 1 - g.p))]
        for i in (1, 2, 3):
            self.first.append(send(own, own, self.sems, i, g.device(g.ring(i), g.p)))

    def forward(self):
        g, out, cut = self.g, self.out, self.cut
        self.second = []
        self.first[0].wait_recv()
        part = out.at[g.index(g.r, 1 - g.p), pl.ds(0, cut)]
        for i in (1, 2, 3):
            self.second.append(send(part, part, self.sems, 3 + i, g.device(g.ring(i), g.p)))
        rest = out.shape[1] - cut
        for i in (1, 2, 3):
            self.first[i].wait_recv()
            part = out.at[g.index(g.ring(4 - i), g.p), pl.ds(cut, rest)]
            self.second.append(send(part, part, self.sems, 6 + i, g.device(g.r, 1 - g.p)))

    def finish(self):
        for copy in self.second:
            copy.wait_recv()
        for copy in self.first + self.second:
            copy.wait_send()


class Scatter:
    SEMS = 14

    @staticmethod
    def scratch(rows, width):
        cut = split_at(rows)
        return [
            pltpu.VMEM((3, cut, width), BF), pltpu.VMEM((3, rows - cut, width), BF),
            pltpu.VMEM((4, rows, width), BF), pltpu.VMEM((cut, width), BF),
            pltpu.VMEM((3, rows - cut, width), BF), DMA((14,)), DMA((14,))]

    def __init__(self, group, part, scratch, step):
        self.g, self.part, self.step = group, part, step
        self.at_a, self.at_b, self.last, self.sum_a, self.sum_b = scratch[:5]
        self.sems = scratch[5:]
        self.rows = part.shape[1]
        self.cut = split_at(self.rows)
        self.low, self.high = pl.ds(0, self.cut), pl.ds(self.cut, self.rows - self.cut)

    def start(self):
        g, part, low, high = self.g, self.part, self.low, self.high
        pair = g.device(g.r, 1 - g.p)
        a, b, c = [], [], []
        for i in (1, 2, 3):
            ring = g.device(g.ring(i), g.p)
            b.append(send(part.at[g.index(g.ring(i), 1 - g.p), high], self.at_b.at[i - 1], self.sems, 2 + i, pair))
            a.append(send(part.at[g.index(g.ring(i), 1 - g.p), low], self.at_a.at[i - 1], self.sems, i - 1, ring))
        for i in (1, 2, 3):
            ring = g.device(g.ring(i), g.p)
            c.append(send(part.at[g.index(g.ring(i), g.p), low], self.last.at[i, low], self.sems, 6 + i, ring))
        c.append(send(part.at[g.index(g.r, 1 - g.p), high], self.last.at[0, high], self.sems, 6, pair))
        self.a, self.b, self.c = a, b, c

    def by_rows(self, rows, body):
        step = self.step
        count = rows // step

        @pl.loop(0, count)
        def _(n):
            body(pl.multiple_of(n * step, step), step)

        if rows % step:
            body(count * step, rows % step)

    def forward(self):
        g, part = self.g, self.part
        pair = g.device(g.r, 1 - g.p)
        for i in (1, 2, 3):
            self.b[i - 1].wait_recv()
            mine = g.index(g.ring(i), g.p)

            def add_b(at, n, i=i, mine=mine):
                rows = pl.ds(at, n)
                total = part[mine, pl.ds(self.cut + at, n), :].astype(F32) + self.at_b[i - 1, rows, :].astype(F32)
                self.sum_b[i - 1, rows, :] = total.astype(BF)

            self.by_rows(self.rows - self.cut, add_b)
            self.c.append(send(self.sum_b.at[i - 1], self.last.at[i, self.high], self.sems, 9 + i, g.device(g.ring(i), g.p)))
        for copy in self.a:
            copy.wait_recv()
        mine = g.index(g.r, 1 - g.p)

        def add_a(at, n):
            rows = pl.ds(at, n)
            total = part[mine, rows, :].astype(F32)
            for i in range(3):
                total += self.at_a[i, rows, :].astype(F32)
            self.sum_a[rows, :] = total.astype(BF)

        self.by_rows(self.cut, add_a)
        self.c.append(send(self.sum_a, self.last.at[0, self.low], self.sems, 13, pair))

    def finish(self, store):
        g = self.g
        for copy in self.c:
            copy.wait_recv()
        mine = g.index(g.r, g.p)

        def add(at, n):
            rows = pl.ds(at, n)
            total = self.part[mine, rows, :].astype(F32)
            for i in range(4):
                total += self.last[i, rows, :].astype(F32)
            store(rows, total)

        self.by_rows(self.rows, add)
        for copy in self.a + self.b + self.c:
            copy.wait_send()


def remote_call(kernel, name, cid, outs, ins, scratch, *args):
    return pl.pallas_call(
        kernel, out_shape=outs, in_specs=ins, out_specs=jax.tree.map(lambda _: VM, outs),
        scratch_shapes=scratch, name=name,
        compiler_params=pltpu.CompilerParams(collective_id=cid, has_side_effects=True, vmem_limit_bytes=56 << 20),
    )(*args)


def weights_kernel(w_ref, n_ref, w_out, n_out, ss, rs, css, crs):
    g = Eight("dp")
    c = lax.rem(g.d, 2)
    core = other_core()
    greet(g.others() + [core])
    me = g.index(g.r, g.p)
    rows = w_ref.shape[1]
    csems = (css, crs)
    swap = send(w_ref.at[1 - c], w_out.at[me, pl.ds(pl.multiple_of(c * rows, rows), rows)], csems, 0, core)
    norm = send(n_ref, n_out.at[c], csems, 1, core)
    w_out[me, pl.ds(pl.multiple_of(c * rows, rows), rows), :] = w_ref[c]
    swap.wait_recv()
    gather = Gather(g, w_out, (ss, rs))
    gather.start()
    n_out[c] = n_ref[...]
    gather.forward()
    gather.finish()
    norm.wait()
    swap.wait_send()


def gather_weights(w, n):
    rows, width = w.shape[1:]
    return remote_call(
        weights_kernel, "weights", 1,
        (struct((8, 2 * rows, width), BF), struct((2, *n.shape), BF)), [VM, VM],
        [DMA((10,)), DMA((10,)), DMA((2,)), DMA((2,))], w, n)


def keys_kernel(k_ref, out, ss, rs):
    g = Eight("dp")
    greet(g.others())
    out[g.index(g.r, g.p)] = k_ref[...]
    gather = Gather(g, out, (ss, rs))
    gather.start()
    gather.forward()
    gather.finish()


def gather_keys(kv):
    return remote_call(
        keys_kernel, "keys", 2, struct((8, *kv.shape), BF), [VM], [DMA((10,)), DMA((10,))], kv)


def invert(meta, inv, nblk):
    @pl.loop(0, nblk)
    def _(b):
        inv[meta[b]] = b


def extents(meta, a, nblk):
    place = meta[meta[nblk + 1] + a]
    prefix = meta[nblk]
    full = jnp.maximum(place, prefix // BLK)
    seen = jnp.maximum(place + 1, (prefix + BLK - 1) // BLK)
    return place, prefix, full // GRP, (seen + GRP - 1) // GRP


def attn_fwd_kernel(meta, q_ref, kv_ref, o_ref, lse_ref, inv, m_ref, acc_ref):
    rows = q_ref.shape[0]
    nblk = kv_ref.shape[0] // BLK
    invert(meta, inv, nblk)
    ones = jnp.ones((BLK, HEAD), BF)

    @pl.loop(0, rows // BLK)
    def _(a):
        place, prefix, full, seen = extents(meta, a, nblk)
        q = q_ref[pl.ds(a * BLK, BLK), :]
        m_ref[...] = jnp.full((BLK, HEAD), -1e30, F32)
        acc_ref[...] = jnp.zeros((BLK, 2 * HEAD), F32)

        def step(j, masked):
            ks, vs = [], []
            for i in range(GRP):
                kb = pl.multiple_of(inv[j * GRP + i] * BLK, BLK)
                ks.append(kv_ref[pl.ds(kb, BLK), :HEAD])
                vs.append(kv_ref[pl.ds(kb, BLK), HEAD:])
            ss = [dg(q, k, NT) for k in ks]
            if masked:
                lim = jnp.maximum(place * BLK + lax.broadcasted_iota(jnp.int32, (BLK, BLK), 0), prefix - 1)
                for i in range(GRP):
                    at = (j * GRP + i) * BLK + lax.broadcasted_iota(jnp.int32, (BLK, BLK), 1)
                    ss[i] = jnp.where(at <= lim, ss[i], -1e30)
            top = ss[0]
            for s in ss[1:]:
                top = jnp.maximum(top, s)
            old = m_ref[:, :1]
            new = jnp.maximum(old, jnp.max(top, axis=1, keepdims=True) * C1)
            alpha = jnp.exp2(old - new)
            add = None
            for s, v in zip(ss, vs):
                p = jnp.exp2(s * C1 - new).astype(BF)
                t = jnp.dot(p, jnp.concatenate([v, ones], axis=1), preferred_element_type=F32)
                add = t if add is None else add + t
            acc_ref[...] = acc_ref[...] * alpha + add
            m_ref[...] = jnp.broadcast_to(new, (BLK, HEAD))

        @pl.loop(0, full)
        def _(j):
            step(j, False)

        @pl.loop(full, seen)
        def _(j):
            step(j, True)

        total = acc_ref[:, HEAD:]
        o_ref[pl.ds(a * BLK, BLK), :] = (acc_ref[:, :HEAD] / total).astype(BF)
        lse = m_ref[...] + jnp.log2(total)
        lse_ref[pl.ds(a, 1), :] = jnp.transpose(lse)[:1, :]


def attn_fwd(meta, q, kv):
    rows = q.shape[0]
    nblk = kv.shape[0] // BLK
    return pl.pallas_call(
        attn_fwd_kernel,
        out_shape=(struct((rows, HEAD), BF), struct((rows // BLK, BLK), F32)),
        in_specs=[SM, VM, VM],
        out_specs=(VM, VM),
        scratch_shapes=[pltpu.SMEM((nblk,), jnp.int32), pltpu.VMEM((BLK, HEAD), F32), pltpu.VMEM((BLK, 2 * HEAD), F32)],
        compiler_params=pltpu.CompilerParams(vmem_limit_bytes=24 << 20),
        cost_estimate=pl.CostEstimate(flops=8 * rows * kv.shape[0] * HEAD, bytes_accessed=6 << 20, transcendentals=rows * kv.shape[0]),
        name="attn_fwd",
    )(meta, q, kv)


def attn_bwd_kernel(meta, q_ref, kv_ref, o_ref, do_ref, lse_ref, dq_ref, dkv_ref, inv, dq_acc, dk_acc, dv_acc):
    rows = q_ref.shape[0]
    nblk = kv_ref.shape[0] // BLK
    invert(meta, inv, nblk)
    dk_acc[...] = jnp.zeros_like(dk_acc)
    dv_acc[...] = jnp.zeros_like(dv_acc)

    @pl.loop(0, rows // BLK)
    def _(a):
        place, prefix, full, seen = extents(meta, a, nblk)
        mine = pl.ds(a * BLK, BLK)
        q = q_ref[mine, :]
        do = do_ref[mine, :]
        prod = do.astype(F32) * o_ref[mine, :].astype(F32)
        delta = jnp.sum(jnp.transpose(prod), axis=0, keepdims=True)
        lse = lse_ref[pl.ds(a, 1), :]
        dq_acc[...] = jnp.zeros_like(dq_acc)

        def step(j, masked):
            add = None
            for i in range(GRP):
                kb = pl.multiple_of(inv[j * GRP + i] * BLK, BLK)
                at_k = pl.ds(kb, BLK)
                k = kv_ref[at_k, :HEAD]
                v = kv_ref[at_k, HEAD:]
                p = jnp.exp2(dg(k, q, NT) * C1 - lse)
                if masked:
                    lim = jnp.maximum(place * BLK + lax.broadcasted_iota(jnp.int32, (BLK, BLK), 1), prefix - 1)
                    at = (j * GRP + i) * BLK + lax.broadcasted_iota(jnp.int32, (BLK, BLK), 0)
                    p = jnp.where(at <= lim, p, 0.0)
                ds = (p * (dg(v, do, NT) - delta)).astype(BF)
                dv_acc[at_k, :] += jnp.dot(p.astype(BF), do, preferred_element_type=F32)
                dk_acc[at_k, :] += jnp.dot(ds, q, preferred_element_type=F32)
                t = dg(ds, k, TN)
                add = t if add is None else add + t
            dq_acc[...] += add

        @pl.loop(0, full)
        def _(j):
            step(j, False)

        @pl.loop(full, seen)
        def _(j):
            step(j, True)

        dq_ref[mine, :] = (dq_acc[...] * SCALE).astype(BF)

    @pl.loop(0, nblk)
    def _(b):
        at = pl.ds(pl.multiple_of(b * BLK, BLK), BLK)
        dkv_ref[at, :HEAD] = (dk_acc[at, :] * SCALE).astype(BF)
        dkv_ref[at, HEAD:] = dv_acc[at, :].astype(BF)


def attn_bwd(meta, q, kv, o, do, lse):
    rows, keys = q.shape[0], kv.shape[0]
    nblk = keys // BLK
    return pl.pallas_call(
        attn_bwd_kernel,
        out_shape=(struct(q.shape, BF), struct(kv.shape, BF)),
        in_specs=[SM] + [VM] * 5,
        out_specs=(VM,) * 2,
        scratch_shapes=[pltpu.SMEM((nblk,), jnp.int32), pltpu.VMEM((BLK, HEAD), F32), pltpu.VMEM((keys, HEAD), F32), pltpu.VMEM((keys, HEAD), F32)],
        compiler_params=pltpu.CompilerParams(vmem_limit_bytes=32 << 20),
        cost_estimate=pl.CostEstimate(flops=20 * rows * keys * HEAD, bytes_accessed=12 << 20, transcendentals=rows * keys),
        name="attn_bwd",
    )(meta, q, kv, o, do, lse)


def chip_members():
    d, t = lax.axis_index("dp"), lax.axis_index("tensor")
    c = lax.rem(d, 2)
    out = []
    for dt in range(8):
        for dc in range(2):
            if dt or dc:
                tt = lax.rem(t + dt, 8)
                cc = lax.rem(c + dc, 2)
                out.append((tt, cc, (d - c + cc, tt)))
    return out


def norm_rows(values):
    average = jnp.mean(values, axis=-1, keepdims=True)
    centred = values - average
    variance = jnp.mean(centred * centred, axis=-1, keepdims=True)
    inverse = lax.rsqrt(variance + EPS)
    return centred * inverse, inverse


def norm_back(grad, scaled, inverse, gain):
    e = grad * gain
    first = jnp.mean(e, axis=-1, keepdims=True)
    second = jnp.mean(e * scaled, axis=-1, keepdims=True)
    return inverse * (e - first - scaled * second)


def middle_kernel(o_ref, w_ref, x_ref, bias_ref, gain_ref, shift_ref, n_out, mid_out, own_out, mixed, asems, arecv, ss, rs):
    g = Eight("tensor")
    c = lax.rem(g.d, 2)
    members = chip_members()
    greet([m[2] for m in members])
    rows = x_ref.shape[0]
    half = o_ref.shape[0] // 2
    sems = (asems, arecv)
    head = pl.ds(pl.multiple_of((2 * g.t + c) * HEAD, HEAD), HEAD)
    local = pl.ds(pl.multiple_of(c * HEAD, HEAD), HEAD)
    copies = []
    for k, (tt, cc, device) in enumerate(members):
        take = pl.ds(pl.multiple_of(cc * half + tt * rows, rows), rows)
        copies.append(send(o_ref.at[take], mixed.at[:, head], sems, k, device))
    copies.append(send(o_ref.at[pl.ds(pl.multiple_of((1 - c) * half, half), half)], own_out.at[:, local], sems, 15, other_core()))
    mixed[:, head] = o_ref[pl.ds(pl.multiple_of(c * half + g.t * rows, rows), rows), :]
    own_out[:, local] = o_ref[pl.ds(pl.multiple_of(c * half, half), half), :]
    for copy in copies:
        copy.wait_recv()
    wide = 512
    for n in range(mid_out.shape[1] // wide):
        cols = pl.ds(n * wide, wide)
        total = None
        for t in range(8):
            term = dg(mixed[:, t * 256:(t + 1) * 256], w_ref[t, cols, :], NT)
            total = term if total is None else total + term
        mid_out[:, cols] = total + (x_ref[:, cols].astype(F32) + bias_ref[:, cols])
    scaled, _ = norm_rows(mid_out[...])
    n_out[g.index(g.r, g.p)] = (scaled * gain_ref[...] + shift_ref[...]).astype(BF)
    gather = Gather(g, n_out, (ss, rs))
    gather.start()
    gather.forward()
    gather.finish()
    for copy in copies:
        copy.wait_send()


def middle_call(o, w, x, bias, gain, shift):
    rows, width = x.shape
    return remote_call(
        middle_kernel, "middle", 3,
        (struct((8, rows, width), BF), struct((rows, width), F32), struct((o.shape[0] // 2, 2 * HEAD), BF)),
        [VM] * 6,
        [pltpu.VMEM((rows, width), BF), DMA((16,)), DMA((16,)), DMA((10,)), DMA((10,))],
        o, w, x, bias, gain, shift)


def back_kernel(part_ref, opart_ref, mid_ref, g_ref, w_ref, gain_ref, bias_ref, do_out, gm_out, sums_out, gb_out, lay_out,
                total, heads, asems, arecv, gs, gr, ls, lr, *scratch):
    g = Eight("tensor")
    c = lax.rem(g.d, 2)
    members = chip_members()
    greet([m[2] for m in members])
    rows = g_ref.shape[0]
    half = do_out.shape[0] // 2
    step = 32
    first = Scatter(g, part_ref, scratch[:7], step)
    second = Scatter(g, opart_ref, scratch[7:], step)
    first.start()
    second.start()
    first.forward()

    def keep(at, value):
        total[at, :] = value

    first.finish(keep)
    scaled, inverse = norm_rows(mid_ref[...])
    grad = total[...]
    sums_out[...] = jnp.zeros_like(sums_out)
    sums_out[0:1, :] = jnp.sum(grad * scaled, axis=0, keepdims=True)
    sums_out[1:2, :] = jnp.sum(grad, axis=0, keepdims=True)
    gm = g_ref[...].astype(F32) + norm_back(grad, scaled, inverse, gain_ref[...])
    gm_out[...] = gm
    low = gm.astype(BF)
    gb_out[g.index(g.r, g.p)] = low
    sums_out[2:3, :] = jnp.sum(low.astype(F32), axis=0, keepdims=True)
    sums_out[3:4, :] = jnp.sum(g_ref[...].astype(F32), axis=0, keepdims=True)
    for t in range(8):
        heads[:, t * 256:(t + 1) * 256] = jnp.dot(low, w_ref[t], preferred_element_type=F32).astype(BF)
    sems = (asems, arecv)
    take = pl.ds(pl.multiple_of(c * half + g.t * rows, rows), rows)
    copies = []
    for k, (tt, cc, device) in enumerate(members):
        cols = pl.ds(pl.multiple_of((2 * tt + cc) * HEAD, HEAD), HEAD)
        copies.append(send(heads.at[:, cols], do_out.at[take], sems, k, device))
    do_out[take, :] = heads[:, pl.ds(pl.multiple_of((2 * g.t + c) * HEAD, HEAD), HEAD)]
    wide = Gather(g, gb_out, (gs, gr))
    wide.start()
    second.forward()
    me = g.index(g.r, g.p)

    def layer(at, value):
        lay_out[me, at, :] = (mid_ref[at, :] + (value + bias_ref[...])).astype(BF)

    second.finish(layer)
    out = Gather(g, lay_out, (ls, lr))
    out.start()
    wide.forward()
    out.forward()
    wide.finish()
    out.finish()
    for copy in copies:
        copy.wait()


def back_call(part, opart, mid, g, w, gain, bias):
    rows, width = g.shape
    chunks = struct((8, rows, width), BF)
    return remote_call(
        back_kernel, "back", 4,
        (struct((16 * rows, HEAD), BF), struct((rows, width), F32), struct((8, width), F32), chunks, chunks),
        [VM] * 7,
        [pltpu.VMEM((rows, width), F32), pltpu.VMEM((rows, width), BF), DMA((15,)), DMA((15,)),
         DMA((10,)), DMA((10,)), DMA((10,)), DMA((10,))] + Scatter.scratch(rows, width) * 2,
        part, opart, mid, g, w, gain, bias)


def key_grads_kernel(part_ref, out_ref, *scratch):
    g = Eight("dp")
    greet(g.others())
    scatter = Scatter(g, part_ref, scratch, 128)
    scatter.start()
    scatter.forward()

    def keep(at, value):
        out_ref[at, :] = value.astype(BF)

    scatter.finish(keep)


def scatter_keys(part):
    return remote_call(
        key_grads_kernel, "key_grads", 5, struct(part.shape[1:], BF), [VM], Scatter.scratch(*part.shape[1:]), part)


def tail_kernel(dw_ref, part_ref, gm_ref, x_ref, gain_ref, dw_out, tg_out, sums_out, summed, arrived, total, mine_w,
                css, crs, ss, rs, *scratch):
    dp, g = Eight("dp"), Eight("tensor")
    c = lax.rem(g.d, 2)
    core = other_core()
    greet(dp.others() + g.others() + [core])
    csems = (css, crs)
    swap = send(part_ref.at[1 - c], arrived, csems, 0, core)
    weights = Scatter(dp, dw_ref, scratch[:7], 128)
    weights.start()
    swap.wait_recv()
    rows, width = x_ref.shape
    for t in range(8):
        @pl.loop(0, rows // 32)
        def _(n):
            at = pl.ds(pl.multiple_of(n * 32, 32), 32)
            summed[t, at, :] = (part_ref[c, t, at, :].astype(F32) + arrived[t, at, :].astype(F32)).astype(BF)
    tokens = Scatter(g, summed, scratch[7:], 32)
    tokens.start()
    weights.forward()
    tokens.forward()

    def keep(at, value):
        total[at, :] = value

    tokens.finish(keep)
    scaled, inverse = norm_rows(x_ref[...].astype(F32))
    grad = total[...]
    sums_out[...] = jnp.zeros_like(sums_out)
    sums_out[0:1, :] = jnp.sum(grad * scaled, axis=0, keepdims=True)
    sums_out[1:2, :] = jnp.sum(grad, axis=0, keepdims=True)
    tg = gm_ref[...] + norm_back(grad, scaled, inverse, gain_ref[...])
    tg_out[g.index(g.r, g.p)] = tg.astype(BF)
    gather = Gather(g, tg_out, (ss, rs))
    gather.start()

    def keep_w(at, value):
        mine_w[at, :] = value.astype(BF)

    weights.finish(keep_w)
    share = dw_out.shape[1]
    there = send(mine_w.at[pl.ds(pl.multiple_of((1 - c) * share, share), share)], dw_out.at[c], csems, 1, core)
    dw_out[c] = mine_w[pl.ds(pl.multiple_of(c * share, share), share), :]
    gather.forward()
    gather.finish()
    there.wait()
    swap.wait_send()


def tail_call(dw, part, gm, x, gain):
    rows, width = x.shape
    wr, wc = dw.shape[1:]
    return remote_call(
        tail_kernel, "tail", 6,
        (struct((2, wr // 2, wc), BF), struct((8, rows, width), BF), struct((8, width), F32)),
        [VM] * 5,
        [pltpu.VMEM((8, rows, width), BF), pltpu.VMEM((8, rows, width), BF), pltpu.VMEM((rows, width), F32), pltpu.VMEM((wr, wc), BF),
         DMA((2,)), DMA((2,)), DMA((10,)), DMA((10,))] + Scatter.scratch(wr, wc) + Scatter.scratch(rows, width),
        dw, part, gm, x, gain)


def on_device(tokens, first_gain, first_shift, query_weight, query_bias, key_weight, value_weight, value_bias,
              out_weight, out_bias, second_gain, second_shift, up_weight, up_bias, down_weight, down_bias,
              cotangent, prefix, block_order):
    own, width = tokens.shape
    d, t = lax.axis_index("dp"), lax.axis_index("tensor")
    c = lax.rem(d, 2)
    nblk = block_order.shape[0]
    rows = own // 8
    meta = jnp.concatenate([block_order % nblk, prefix, (d // 2 * 4).astype(jnp.int32).reshape(1)])
    row = lambda v: v.reshape(1, -1)

    up_all = lax.all_gather(up_weight.astype(BF), "dp", axis=0, tiled=True)
    down_all = lax.all_gather(down_weight.astype(BF).T, "dp", axis=0, tiled=True)
    out_all = lax.all_gather(lax.all_gather(out_weight.astype(BF).T, "dp", axis=0, tiled=True), "tensor", axis=0)

    scaled, _ = norm_rows(tokens.astype(F32))
    normed = (scaled * first_gain + first_shift).astype(BF)
    shards = jnp.stack([
        jnp.concatenate([w[:, h * HEAD:(h + 1) * HEAD] for w in (query_weight, key_weight, value_weight)], axis=1).astype(BF)
        for h in range(2)])
    w_all, n_all = gather_weights(shards, normed)
    w_all = w_all.reshape(width, 3 * HEAD)
    n_all = n_all.reshape(2 * own, width)
    pick = lambda v: lax.dynamic_slice_in_dim(v, c * HEAD, HEAD)
    bias = jnp.concatenate([pick(query_bias), jnp.zeros((HEAD,), F32), pick(value_bias)])
    qkv = (dg(n_all, w_all, NN) + bias).astype(BF)
    q = qkv[:, :HEAD]
    kv = gather_keys(qkv[:, HEAD:]).reshape(8 * 2 * own, 2 * HEAD)
    o, lse = attn_fwd(meta, q, kv)

    here = lambda v: lax.dynamic_slice_in_dim(v, t * rows, rows)
    x_rows, g_rows = here(tokens), here(cotangent)
    n2, mid, mixed = middle_call(o, out_all, x_rows, row(out_bias), row(second_gain), row(second_shift))
    n2 = n2.reshape(own, width)
    pre = dg(n2, up_all, NN) + up_bias
    half_erf = 0.5 + 0.5 * lax.erf(pre * math.sqrt(0.5))
    hidden = (pre * half_erf).astype(BF)
    slope = half_erf + pre * jnp.exp(-0.5 * pre * pre) * (1.0 / math.sqrt(2.0 * math.pi))
    grad_pre = (dg(cotangent, down_all, NN) * slope).astype(BF)
    gn2 = dg(grad_pre, up_all, NT).astype(BF).reshape(8, rows, width)
    out_part = dg(hidden, down_all, NT).astype(BF).reshape(8, rows, width)
    do, gm, sums, gb, layer = back_call(gn2, out_part, mid, g_rows, out_all, row(second_gain), row(down_bias))
    gb = gb.reshape(own, width)
    dw_up = dg(n2, grad_pre, TN)
    dw_down = dg(cotangent, hidden, TN)
    dw_out = dg(gb, mixed, TN)
    late = lax.psum_scatter(
        jnp.concatenate([dw_up.astype(BF), dw_down.astype(BF), dw_out.astype(BF)], axis=1), "dp", scatter_dimension=0, tiled=True)

    dq, dkv = attn_bwd(meta, q, kv, o, do, lse)
    dkv = scatter_keys(dkv.reshape(8, 2 * own, 2 * HEAD))
    dqkv = jnp.concatenate([dq, dkv], axis=1)
    dw = dg(n_all, dqkv, TN).astype(BF).reshape(8, width // 8, 3 * HEAD)
    gn1 = dg(dqkv, w_all, NT).astype(BF).reshape(2, 8, rows, width)
    dw_mine, tg, sums1 = tail_call(dw, gn1, gm, x_rows, row(first_gain))

    def slot(value, count, at):
        return lax.dynamic_update_slice_in_dim(jnp.zeros((count * value.shape[0],), F32), value, at * value.shape[0], 0)

    col = jnp.sum(dqkv.astype(F32), axis=0)
    head = 2 * t + c
    up_sum = slot(jnp.sum(grad_pre.astype(F32), axis=0), 8, t)
    vec = jnp.concatenate([
        sums[0], sums[1], sums[2], sums[3], up_sum, slot(col[:HEAD], 16, head), slot(col[2 * HEAD:], 16, head), sums1[0], sums1[1]])
    vec = lax.psum(vec, ("dp", "tensor"))
    ups = up_sum.shape[0]
    at = 4 * width
    gain2, shift2, outb, downb = (vec[i * width:(i + 1) * width] for i in range(4))
    mine = lambda start, size, index: lax.dynamic_slice_in_dim(vec, start + index * size, size)
    upb = mine(at, ups // 8, t)
    qb = mine(at + ups, 2 * HEAD, t)
    vb = mine(at + ups + width, 2 * HEAD, t)
    gain1 = vec[at + ups + 2 * width:at + ups + 3 * width]
    shift1 = vec[at + ups + 3 * width:]
    hid = up_weight.shape[1]
    pieces = [
        jnp.concatenate([dw_mine[0, :, i * HEAD:(i + 1) * HEAD], dw_mine[1, :, i * HEAD:(i + 1) * HEAD]], axis=1).astype(F32)
        for i in range(3)]
    return (
        layer.reshape(own, width),
        tg.reshape(own, width).astype(F32),
        gain1, shift1,
        pieces[0], qb, pieces[1], pieces[2], vb,
        late[:, 2 * hid:].astype(F32).T, outb,
        gain2, shift2,
        late[:, :hid].astype(F32), upb,
        late[:, hid:2 * hid].astype(F32).T, downb,
    )


def solution(mesh):
    rows, cols = P("dp", "tensor"), P("tensor", "dp")
    return jax.shard_map(
        on_device,
        mesh=mesh,
        in_specs=(
            P("dp", None), P(), P(), rows, P("tensor"), rows, rows, P("tensor"), cols, P(), P(), P(), rows, P("tensor"),
            cols, P(), P("dp", None), P(), P()),
        out_specs=(
            P("dp", None), P("dp", None), P(), P(), rows, P("tensor"), rows, rows, P("tensor"), cols, P(), P(), P(), rows,
            P("tensor"), cols, P()),
        check_vma=False,
    )
```

```python
import functools
import math

import jax
import jax.numpy as jnp
from jax import lax
from jax.experimental import pallas as pl
from jax.experimental.pallas import tpu as pltpu
from jax.sharding import PartitionSpec as P

HEAD = 128
BLK = 256
GRP = 4
RING = 4
EPS = 1e-05
NEG = -(2.0 ** 100)
LOG2E = math.log2(math.e)
SCALE = 1.0 / math.sqrt(HEAD)
C1 = LOG2E * SCALE
NN = (((1,), (0,)), ((), ()))
NT = (((1,), (1,)), ((), ()))
TN = (((0,), (0,)), ((), ()))
MESH = pl.DeviceIdType.MESH
VM = pl.BlockSpec(memory_space=pltpu.VMEM)
SM = pl.BlockSpec(memory_space=pltpu.SMEM)
BF = jnp.bfloat16
F32 = jnp.float32
DMA = pltpu.SemaphoreType.DMA


def dg(a, b, dims):
    return lax.dot_general(a, b, dims, preferred_element_type=F32)


def struct(shape, dtype):
    return jax.ShapeDtypeStruct(shape, dtype)


class Eight:
    def __init__(self, axis):
        d, t = lax.axis_index("dp"), lax.axis_index("tensor")
        self.axis, self.d, self.t = axis, d, t
        if axis == "dp":
            self.r, self.p = d // 4, lax.rem(d // 2, 2)
        else:
            self.r, self.p = lax.rem(t, 4), t // 4

    def ring(self, i):
        return lax.rem(self.r + i, RING)

    def index(self, r, p):
        return r * 2 + p if self.axis == "dp" else p * 4 + r

    def device(self, r, p):
        if self.axis == "dp":
            return ((r * 2 + p) * 2 + lax.rem(self.d, 2), self.t)
        return (self.d, p * 4 + r)

    def others(self):
        return [self.device(self.ring(i), self.p) for i in (1, 2, 3)] + [self.device(self.r, 1 - self.p)]


def other_core():
    d = lax.axis_index("dp")
    return (d + 1 - 2 * lax.rem(d, 2), lax.axis_index("tensor"))


def greet(devices):
    barrier = pltpu.get_barrier_semaphore()
    for device in devices:
        pl.semaphore_signal(barrier, inc=1, device_id=device, device_id_type=MESH)
    pl.semaphore_wait(barrier, len(devices))


def send(src, dst, sems, k, device):
    copy = pltpu.make_async_remote_copy(
        src_ref=src, dst_ref=dst, send_sem=sems[0].at[k], recv_sem=sems[1].at[k],
        device_id=device, device_id_type=MESH)
    copy.start()
    return copy


def split_at(rows):
    return max(16, int(rows * 0.4) // 16 * 16)


def copy_of(src, dst, sems, k, device):
    return pltpu.make_async_remote_copy(
        src_ref=src, dst_ref=dst, send_sem=sems[0].at[k], recv_sem=sems[1].at[k],
        device_id=device, device_id_type=MESH)


def send(src, dst, sems, k, device):
    copy = copy_of(src, dst, sems, k, device)
    copy.start()
    return copy


class Gather:
    def __init__(self, group, place, rows, sems, twin=None, twin_sems=None, twin_own=True):
        self.g, self.place, self.sems = group, place, sems
        self.twin, self.twin_sems, self.twin_own = twin, twin_sems, twin_own
        cut = split_at(rows)
        self.low, self.high = pl.ds(0, cut), pl.ds(cut, rows - cut)

    @staticmethod
    def scratch(twin=False):
        return [DMA((10,)), DMA((10,))] + ([DMA((8,)), DMA((8,))] if twin else [])

    def near(self, i):
        g = self.g
        return self.place(g.index(g.ring(RING - i), g.p))

    def far(self, i):
        g = self.g
        return self.place(g.index(g.ring(RING - i), 1 - g.p))

    def first(self, i):
        g = self.g
        own = self.place(g.index(g.r, g.p))
        return copy_of(own, own, self.sems, i, g.device(g.ring(i), g.p))

    def first_pair(self):
        g = self.g
        own = self.place(g.index(g.r, g.p))
        return copy_of(own, own, self.sems, 0, g.device(g.r, 1 - g.p))

    def second_a(self, i):
        g = self.g
        part = self.place(g.index(g.r, 1 - g.p)).at[self.low]
        return copy_of(part, part, self.sems, 3 + i, g.device(g.ring(i), g.p))

    def second_b(self, i):
        g = self.g
        part = self.near(i).at[self.high]
        return copy_of(part, part, self.sems, 6 + i, g.device(g.r, 1 - g.p))

    def over(self, ref, k):
        return copy_of(ref, ref, self.twin_sems, k, self.twin)

    def start(self):
        g = self.g
        self.first_pair().start()
        for i in (1, 2, 3):
            self.first(i).start()
        if self.twin is not None and self.twin_own:
            self.over(self.place(g.index(g.r, g.p)), 0).start()

    def forward_pair(self):
        g = self.g
        self.first_pair().wait_recv()
        for i in (1, 2, 3):
            self.second_a(i).start()
        if self.twin is not None:
            self.over(self.place(g.index(g.r, 1 - g.p)), 1).start()

    def forward_near(self, i):
        self.first(i).wait_recv()
        self.second_b(i).start()
        if self.twin is not None:
            self.over(self.near(i), 1 + i).start()

    def forward(self):
        self.forward_pair()
        for i in (1, 2, 3):
            self.forward_near(i)

    def arrive_far(self, i):
        self.second_a(i).wait_recv()
        self.second_b(i).wait_recv()
        if self.twin is not None:
            self.over(self.far(i), 4 + i).start()

    def settle(self):
        g = self.g
        self.first_pair().wait_send()
        for i in (1, 2, 3):
            self.first(i).wait_send()
            self.second_a(i).wait_send()
            self.second_b(i).wait_send()
        if self.twin is not None:
            own = self.place(g.index(g.r, g.p))
            for k in range(0 if self.twin_own else 1, 8):
                self.over(own, k).wait()

    def finish(self):
        for i in (1, 2, 3):
            self.arrive_far(i)
        self.settle()


class Scatter:
    @staticmethod
    def scratch(rows, width):
        cut = split_at(rows)
        return [
            pltpu.VMEM((3, cut, width), BF), pltpu.VMEM((3, rows - cut, width), BF),
            pltpu.VMEM((4, rows, width), BF), pltpu.VMEM((cut, width), BF),
            pltpu.VMEM((3, rows - cut, width), BF), DMA((14,)), DMA((14,))]

    def __init__(self, group, part, rows, scratch, step):
        self.g, self.part, self.step = group, part, step
        self.at_a, self.at_b, self.last, self.sum_a, self.sum_b = scratch[:5]
        self.sems = scratch[5:]
        self.rows = rows
        self.cut = split_at(rows)
        self.low, self.high = pl.ds(0, self.cut), pl.ds(self.cut, rows - self.cut)

    def pair(self):
        return self.g.device(self.g.r, 1 - self.g.p)

    def ring(self, i):
        return self.g.device(self.g.ring(i), self.g.p)

    def far_part(self, i):
        return self.part(self.g.index(self.g.ring(i), 1 - self.g.p))

    def near_part(self, i):
        return self.part(self.g.index(self.g.ring(i), self.g.p))

    def pair_part(self):
        return self.part(self.g.index(self.g.r, 1 - self.g.p))

    def far_a(self, i):
        return copy_of(self.far_part(i).at[self.low], self.at_a.at[i - 1], self.sems, i - 1, self.ring(i))

    def far_b(self, i):
        return copy_of(self.far_part(i).at[self.high], self.at_b.at[i - 1], self.sems, 2 + i, self.pair())

    def near_own(self, i):
        return copy_of(self.near_part(i).at[self.low], self.last.at[i, self.low], self.sems, 6 + i, self.ring(i))

    def near_sum(self, i):
        return copy_of(self.sum_b.at[i - 1], self.last.at[i, self.high], self.sems, 9 + i, self.ring(i))

    def pair_own(self):
        return copy_of(self.pair_part().at[self.high], self.last.at[0, self.high], self.sems, 6, self.pair())

    def pair_sum(self):
        return copy_of(self.sum_a, self.last.at[0, self.low], self.sems, 13, self.pair())

    def by_rows(self, rows, body):
        step = self.step
        count = rows // step

        @pl.loop(0, count)
        def _(n):
            body(pl.multiple_of(n * step, step), step)

        if rows % step:
            body(count * step, rows % step)

    def send_far(self, i):
        self.far_b(i).start()
        self.far_a(i).start()

    def send_near(self, i):
        self.near_own(i).start()

    def add_near(self, i):
        self.far_b(i).wait_recv()
        mine = self.near_part(i)

        def add(at, n):
            rows = pl.ds(at, n)
            total = mine[pl.ds(self.cut + at, n), :].astype(F32) + self.at_b[i - 1, rows, :].astype(F32)
            self.sum_b[i - 1, rows, :] = total.astype(BF)

        self.by_rows(self.rows - self.cut, add)
        self.near_sum(i).start()

    def send_pair(self):
        self.pair_own().start()

    def add_pair(self):
        for i in (1, 2, 3):
            self.far_a(i).wait_recv()
        mine = self.pair_part()

        def add(at, n):
            rows = pl.ds(at, n)
            total = mine[rows, :].astype(F32)
            for i in range(3):
                total += self.at_a[i, rows, :].astype(F32)
            self.sum_a[rows, :] = total.astype(BF)

        self.by_rows(self.cut, add)
        self.pair_sum().start()

    def start(self):
        for i in (1, 2, 3):
            self.send_far(i)
        for i in (1, 2, 3):
            self.send_near(i)
        self.send_pair()

    def forward(self):
        for i in (1, 2, 3):
            self.add_near(i)
        self.add_pair()

    def finish(self, store):
        g = self.g
        self.pair_own().wait_recv()
        self.pair_sum().wait_recv()
        for i in (1, 2, 3):
            self.near_own(i).wait_recv()
            self.near_sum(i).wait_recv()
        mine = self.part(g.index(g.r, g.p))

        def add(at, n):
            rows = pl.ds(at, n)
            total = mine[rows, :].astype(F32)
            for i in range(4):
                total += self.last[i, rows, :].astype(F32)
            store(rows, total)

        self.by_rows(self.rows, add)
        self.pair_own().wait_send()
        self.pair_sum().wait_send()
        for i in (1, 2, 3):
            self.far_a(i).wait_send()
            self.far_b(i).wait_send()
            self.near_own(i).wait_send()
            self.near_sum(i).wait_send()


class CoreScatter:
    @staticmethod
    def scratch(rows, width):
        return [pltpu.VMEM((8, rows, width), BF), pltpu.VMEM((8, rows, width), BF), DMA((1,)), DMA((1,))] + Scatter.scratch(rows, width)

    def __init__(self, group, part, scratch, step):
        self.part, self.arrived, self.added = part, scratch[0], scratch[1]
        self.c = lax.rem(group.d, 2)
        self.sems = scratch[2:4]
        self.step = step
        self.inner = Scatter(group, lambda m: self.added.at[m], part.shape[2], scratch[4:], step)

    def swap(self):
        return copy_of(self.part.at[:, 1 - self.c], self.arrived, self.sems, 0, other_core())

    def start(self):
        self.swap().start()

    def add(self):
        self.swap().wait_recv()
        rows, step = self.part.shape[2], self.step

        @pl.loop(0, 8)
        def _(m):
            @pl.loop(0, rows // step)
            def _(n):
                at = pl.ds(pl.multiple_of(n * step, step), step)
                self.added[m, at, :] = (self.part[m, self.c, at, :].astype(F32) + self.arrived[m, at, :].astype(F32)).astype(BF)

        self.inner.start()

    def forward(self):
        self.inner.forward()

    def finish(self, store):
        self.inner.finish(store)
        self.swap().wait_send()


def remote_call(kernel, name, cid, outs, ins, scratch, *args, out_specs=None):
    return pl.pallas_call(
        kernel, out_shape=outs, in_specs=ins,
        out_specs=jax.tree.map(lambda _: VM, outs) if out_specs is None else out_specs,
        scratch_shapes=scratch, name=name,
        compiler_params=pltpu.CompilerParams(collective_id=cid, has_side_effects=True, vmem_limit_bytes=58 << 20),
    )(*args)


def weights_kernel(w_ref, n_ref, w_out, n_out, css, crs, *sems):
    g = Eight("dp")
    c = lax.rem(g.d, 2)
    core = other_core()
    greet(g.others() + [core])
    me = g.index(g.r, g.p)
    rows = w_ref.shape[1]
    csems = (css, crs)
    mine = pl.ds(pl.multiple_of(c * rows, rows), rows)
    swap = send(w_ref.at[1 - c], w_out.at[me, mine], csems, 0, core)
    norm = send(n_ref, n_out.at[c], csems, 1, core)
    w_out[me, mine, :] = w_ref[c]
    swap.wait_recv()
    gather = Gather(g, lambda m: w_out.at[m], 2 * rows, sems)
    gather.start()
    n_out[c] = n_ref[...]
    gather.forward()
    gather.finish()
    norm.wait()
    swap.wait_send()


def gather_weights(w, n):
    rows, width = w.shape[1:]
    return remote_call(
        weights_kernel, "weights", 1,
        (struct((8, 2 * rows, width), BF), struct((2, *n.shape), BF)), [VM, VM],
        [DMA((2,)), DMA((2,))] + Gather.scratch(), w, n)


def augment(meta, lanes_ref, q_ref, qa_ref, kx_ref):
    rows = q_ref.shape[0]
    nblk = kx_ref.shape[0] // BLK
    prefix = meta[nblk]
    for a in range(rows // BLK):
        at = slice(a * BLK, (a + 1) * BLK)
        hidden = jnp.where(lanes_ref[...] > meta[meta_first(meta, nblk) + a], NEG, 0.0)
        qa_ref[at, :HEAD] = q_ref[at, :]
        qa_ref[at, HEAD:] = jnp.broadcast_to(hidden, (BLK, HEAD)).astype(BF)
    lane = lax.broadcasted_iota(jnp.int32, (BLK, HEAD), 1)
    inside = lax.broadcasted_iota(jnp.int32, (BLK, HEAD), 0)

    @pl.loop(0, nblk)
    def _(b):
        late = (lane == b) & (inside >= prefix - meta[b] * BLK)
        kx_ref[pl.ds(pl.multiple_of(b * BLK, BLK), BLK), :] = jnp.where(late, 1.0, 0.0).astype(BF)


def meta_first(meta, nblk):
    return lax.axis_index("dp") // 2 * 4


def attend_kernel(meta, lanes_ref, q_ref, k_ref, out_ref, up_ref, kv_out, o_ref, lse_ref, out_all, up_all,
                  qa_ref, kx_ref, m_ref, acc_ref, lsem, *sems):
    g, gt = Eight("dp"), Eight("tensor")
    c = lax.rem(g.d, 2)
    core = other_core()
    me = g.index(g.r, g.p)
    rows = q_ref.shape[0]
    nblk = kx_ref.shape[0] // BLK
    per = rows // BLK
    shard = out_ref.shape[0]
    half = out_all.shape[1] // 2
    greet(g.others() + gt.others() + [core])
    out_place = lambda m: out_all.at[gt.t, pl.ds(pl.multiple_of((m * 2 + c) * shard, shard), shard)]
    up_place = lambda m: up_all.at[pl.ds(pl.multiple_of((m * 2 + c) * shard, shard), shard)]
    half_place = lambda m: out_all.at[m, pl.ds(pl.multiple_of(c * half, half), half)]
    keys = Gather(g, lambda m: kv_out.at[m], rows, sems[:2])
    outs = Gather(g, out_place, shard, sems[2:4], core, sems[4:6])
    ups = Gather(g, up_place, shard, sems[6:8], core, sems[8:10])
    wide = Gather(gt, half_place, half, sems[10:12], core, sems[12:14], twin_own=False)
    local = [pltpu.make_async_copy(out_ref, out_place(me), lsem.at[0]), pltpu.make_async_copy(up_ref, up_place(me), lsem.at[1])]
    for copy in local:
        copy.start()
    kv_out[me] = k_ref[...]
    keys.start()
    for copy in local:
        copy.wait()
    outs.start()
    augment(meta, lanes_ref, q_ref, qa_ref, kx_ref)
    m_ref[...] = jnp.full_like(m_ref, -1e30)
    acc_ref[...] = jnp.zeros_like(acc_ref)
    ones = jnp.ones((BLK, HEAD), BF)
    prefix = meta[nblk]

    def attend(chunk, own):
        @pl.loop(0, per)
        def _(a):
            mine = pl.ds(pl.multiple_of(a * BLK, BLK), BLK)
            q = qa_ref[mine, :]
            ss, vs = [], []
            for i in range(per):
                at = pl.ds(pl.multiple_of(chunk * rows + i * BLK, BLK), BLK)
                ss.append(dg(q, jnp.concatenate([kv_out[chunk, i * BLK:(i + 1) * BLK, :HEAD], kx_ref[at, :]], axis=1), NT))
                vs.append(jnp.concatenate([kv_out[chunk, i * BLK:(i + 1) * BLK, HEAD:], ones], axis=1))
            if own:
                edge = prefix - 1 - meta[meta_first(meta, nblk) + a] * BLK
                lim = jnp.maximum(lax.broadcasted_iota(jnp.int32, (BLK, BLK), 0), edge)
                key = lax.broadcasted_iota(jnp.int32, (BLK, BLK), 1)
                for i in range(per):
                    ss[i] = jnp.where(key <= jnp.where(a == i, lim, BLK), ss[i], NEG)
            top = ss[0]
            for s in ss[1:]:
                top = jnp.maximum(top, s)
            old = m_ref[mine, :1]
            new = jnp.maximum(old, jnp.max(top, axis=1, keepdims=True) * C1)
            alpha = jnp.exp2(old - new)
            add = None
            for s, v in zip(ss, vs):
                t = jnp.dot(jnp.exp2(s * C1 - new).astype(BF), v, preferred_element_type=F32)
                add = t if add is None else add + t
            acc_ref[mine, :] = acc_ref[mine, :] * alpha + add
            m_ref[mine, :] = jnp.broadcast_to(new, (BLK, HEAD))

    attend(me, True)
    keys.forward_pair()
    outs.forward()
    attend(g.index(g.r, 1 - g.p), False)
    outs.finish()
    wide.start()

    @pl.loop(1, RING)
    def _(i):
        keys.forward_near(i)
        attend(g.index(g.ring(RING - i), g.p), False)

    ups.start()
    wide.forward()

    @pl.loop(1, RING)
    def _(i):
        keys.arrive_far(i)
        attend(g.index(g.ring(RING - i), 1 - g.p), False)

    for a in range(per):
        at = slice(a * BLK, (a + 1) * BLK)
        total = acc_ref[at, HEAD:]
        o_ref[at, :] = (acc_ref[at, :HEAD] / total).astype(BF)
        lse_ref[a:a + 1, :] = jnp.transpose(m_ref[at, :] + jnp.log2(total))[:1, :]
    ups.forward()
    wide.finish()
    ups.finish()
    keys.settle()


def attend_call(meta, lanes, q, kv, out_w, up_w):
    rows = q.shape[0]
    shard, hid = up_w.shape
    hbm = pl.BlockSpec(memory_space=pl.ANY)
    return remote_call(
        attend_kernel, "attend", 2,
        (struct((8, *kv.shape), BF), struct((rows, HEAD), BF), struct((rows // BLK, BLK), F32),
         struct((8, 16 * shard, out_w.shape[1]), BF), struct((16 * shard, hid), BF)),
        [SM, VM, VM, VM, hbm, hbm],
        [pltpu.VMEM((rows, 2 * HEAD), BF), pltpu.VMEM((8 * rows, HEAD), BF), pltpu.VMEM((rows, HEAD), F32), pltpu.VMEM((rows, 2 * HEAD), F32),
         DMA((2,))] + Gather.scratch() + Gather.scratch(True) * 3,
        meta, lanes, q, kv, out_w, up_w, out_specs=(VM, VM, VM, hbm, hbm))


def attend_back_kernel(meta, lanes_ref, q_ref, kv_ref, o_ref, do_ref, lse_ref, opart_ref, gbr_ref, mid_ref, bias_ref, dup_ref,
                       dq_ref, dkv_out, lay_out, gb_out, dup_out,
                       qa_ref, kx_ref, part, delta_ref, dq_acc, dk_acc, dv_acc, *scratch):
    g, gt = Eight("dp"), Eight("tensor")
    core = other_core()
    me = g.index(g.r, g.p)
    rows = q_ref.shape[0]
    nblk = kx_ref.shape[0] // BLK
    per = rows // BLK
    greet(g.others() + gt.others() + [core])
    keys = Scatter(g, lambda m: part.at[m], rows, scratch[:7], 128)
    outs = Scatter(gt, lambda m: opart_ref.at[m], opart_ref.shape[1], scratch[7:14], 32)
    ups = CoreScatter(g, dup_ref, scratch[14:25], 32)
    wide = Gather(gt, lambda m: gb_out.at[m], gb_out.shape[1], scratch[25:27])
    layer = Gather(gt, lambda m: lay_out.at[m], lay_out.shape[1], scratch[27:29])
    ups.start()
    outs.start()
    mine_t = gt.index(gt.r, gt.p)
    gb_out[mine_t] = gbr_ref[...]
    wide.start()
    augment(meta, lanes_ref, q_ref, qa_ref, kx_ref)
    for a in range(per):
        at = slice(a * BLK, (a + 1) * BLK)
        prod = do_ref[at, :].astype(F32) * o_ref[at, :].astype(F32)
        delta_ref[0:1, at] = jnp.sum(jnp.transpose(prod), axis=0, keepdims=True)
        delta_ref[1:2, at] = lse_ref[a:a + 1, :]
    dq_acc[...] = jnp.zeros_like(dq_acc)
    prefix = meta[nblk]

    def attend(chunk, own):
        @pl.loop(0, per)
        def _(i):
            at_k = pl.ds(pl.multiple_of(i * BLK, BLK), BLK)
            at_x = pl.ds(pl.multiple_of(chunk * rows + i * BLK, BLK), BLK)
            k = kv_ref[chunk, at_k, :HEAD]
            v = kv_ref[chunk, at_k, HEAD:]
            kk = jnp.concatenate([k, kx_ref[at_x, :]], axis=1)
            dk = dv = None
            for a in range(per):
                at_q = slice(a * BLK, (a + 1) * BLK)
                q = q_ref[at_q, :]
                do = do_ref[at_q, :]
                p = jnp.exp2(dg(kk, qa_ref[at_q, :], NT) * C1 - delta_ref[1:2, at_q])
                if own:
                    edge = prefix - 1 - meta[meta_first(meta, nblk) + a] * BLK
                    lim = jnp.maximum(lax.broadcasted_iota(jnp.int32, (BLK, BLK), 1), edge)
                    key = lax.broadcasted_iota(jnp.int32, (BLK, BLK), 0)
                    p = jnp.where(key <= jnp.where(i == a, lim, BLK), p, 0.0)
                ds = (p * (dg(v, do, NT) - delta_ref[0:1, at_q])).astype(BF)
                tv = jnp.dot(p.astype(BF), do, preferred_element_type=F32)
                tk = jnp.dot(ds, q, preferred_element_type=F32)
                dv = tv if dv is None else dv + tv
                dk = tk if dk is None else dk + tk
                dq_acc[at_q, :] += dg(ds, k, TN)
            part[chunk, at_k, :HEAD] = (dk * SCALE).astype(BF)
            part[chunk, at_k, HEAD:] = dv.astype(BF)

    @pl.loop(1, RING)
    def _(i):
        attend(g.index(g.ring(i), 1 - g.p), False)
        keys.send_far(i)

    ups.add()
    outs.forward()
    wide.forward()

    @pl.loop(1, RING)
    def _(i):
        attend(g.index(g.ring(i), g.p), False)
        keys.send_near(i)
        keys.add_near(i)

    def lay(at, value):
        lay_out[mine_t, at, :] = (mid_ref[at, :] + (value + bias_ref[...])).astype(BF)

    outs.finish(lay)
    layer.start()
    attend(g.index(g.r, 1 - g.p), False)
    keys.send_pair()
    keys.add_pair()
    ups.forward()
    attend(me, True)
    dq_ref[...] = (dq_acc[...] * SCALE).astype(BF)
    layer.forward()
    wide.finish()

    def keep(at, value):
        dkv_out[at, :] = value.astype(BF)

    keys.finish(keep)

    def keep_up(at, value):
        dup_out[at, :] = value

    ups.finish(keep_up)
    layer.finish()


def attend_back_call(meta, lanes, q, kv, o, do, lse, opart, gb, mid, bias, dup):
    rows = q.shape[0]
    tr, width = mid.shape
    sr, sw = dup.shape[2:]
    return remote_call(
        attend_back_kernel, "attend_back", 5,
        (struct(q.shape, BF), struct((rows, 2 * HEAD), BF), struct((8, tr, width), BF), struct((8, tr, width), BF), struct((sr, sw), F32)),
        [SM] + [VM] * 11,
        [pltpu.VMEM((rows, 2 * HEAD), BF), pltpu.VMEM((8 * rows, HEAD), BF), pltpu.VMEM(kv.shape, BF), pltpu.VMEM((8, rows), F32),
         pltpu.VMEM((rows, HEAD), F32), pltpu.VMEM((8, 128), F32), pltpu.VMEM((8, 128), F32)]
        + Scatter.scratch(rows, 2 * HEAD) + Scatter.scratch(tr, width) + CoreScatter.scratch(sr, sw) + Gather.scratch() * 2,
        meta, lanes, q, kv, o, do, lse, opart, gb, mid, bias, dup)


def chip_members():
    d, t = lax.axis_index("dp"), lax.axis_index("tensor")
    c = lax.rem(d, 2)
    out = []
    for dt in range(8):
        for dc in range(2):
            if dt or dc:
                tt = lax.rem(t + dt, 8)
                cc = lax.rem(c + dc, 2)
                out.append((tt, cc, (d - c + cc, tt)))
    return out


def norm_rows(values):
    average = jnp.mean(values, axis=-1, keepdims=True)
    centred = values - average
    variance = jnp.mean(centred * centred, axis=-1, keepdims=True)
    inverse = lax.rsqrt(variance + EPS)
    return centred * inverse, inverse


def norm_back(grad, scaled, inverse, gain):
    e = grad * gain
    first = jnp.mean(e, axis=-1, keepdims=True)
    second = jnp.mean(e * scaled, axis=-1, keepdims=True)
    return inverse * (e - first - scaled * second)


def middle_kernel(o_ref, w_hbm, x_ref, bias_ref, gain_ref, shift_ref, down_ref, n_out, mid_out, own_out, down_all,
                  w_ref, mixed, lsem, asems, arecv, *sems):
    g, gd = Eight("tensor"), Eight("dp")
    c = lax.rem(g.d, 2)
    members = chip_members()
    load = pltpu.make_async_copy(w_hbm, w_ref, lsem.at[0])
    load.start()
    shard = down_ref.shape[0]
    down_place = lambda m: down_all.at[pl.ds(pl.multiple_of((m * 2 + c) * shard, shard), shard)]
    local = pltpu.make_async_copy(down_ref, down_place(gd.index(gd.r, gd.p)), lsem.at[1])
    local.start()
    greet([m[2] for m in members] + gd.others())
    rows = x_ref.shape[0]
    half = o_ref.shape[0] // 2
    asem = (asems, arecv)
    head = pl.ds(pl.multiple_of((2 * g.t + c) * HEAD, HEAD), HEAD)
    mine = pl.ds(pl.multiple_of(c * HEAD, HEAD), HEAD)
    copies = []
    for k, (tt, cc, device) in enumerate(members):
        take = pl.ds(pl.multiple_of(cc * half + tt * rows, rows), rows)
        copies.append(send(o_ref.at[take], mixed.at[:, head], asem, k, device))
    copies.append(send(o_ref.at[pl.ds(pl.multiple_of((1 - c) * half, half), half)], own_out.at[:, mine], asem, 15, other_core()))
    downs = Gather(gd, down_place, shard, sems[2:4], other_core(), sems[4:6])
    local.wait()
    downs.start()
    mixed[:, head] = o_ref[pl.ds(pl.multiple_of(c * half + g.t * rows, rows), rows), :]
    own_out[:, mine] = o_ref[pl.ds(pl.multiple_of(c * half, half), half), :]
    load.wait()
    for copy in copies:
        copy.wait_recv()
    wide = 512
    for n in range(mid_out.shape[1] // wide):
        cols = pl.ds(n * wide, wide)
        total = None
        for t in range(8):
            term = dg(mixed[:, t * 256:(t + 1) * 256], w_ref[t, cols, :], NT)
            total = term if total is None else total + term
        mid_out[:, cols] = total + (x_ref[:, cols].astype(F32) + bias_ref[:, cols])
    scaled, _ = norm_rows(mid_out[...])
    n_out[g.index(g.r, g.p)] = (scaled * gain_ref[...] + shift_ref[...]).astype(BF)
    gather = Gather(g, lambda m: n_out.at[m], rows, sems[:2])
    gather.start()
    downs.forward()
    gather.forward()
    gather.finish()
    downs.finish()
    for copy in copies:
        copy.wait_send()


def middle_call(o, w, x, bias, gain, shift, down):
    rows, width = x.shape
    hbm = pl.BlockSpec(memory_space=pl.ANY)
    return remote_call(
        middle_kernel, "middle", 3,
        (struct((8, rows, width), BF), struct((rows, width), F32), struct((o.shape[0] // 2, 2 * HEAD), BF),
         struct((16 * down.shape[0], down.shape[1]), BF)),
        [VM, hbm, VM, VM, VM, VM, hbm],
        [pltpu.VMEM(w.shape, BF), pltpu.VMEM((rows, width), BF), DMA((2,)), DMA((16,)), DMA((16,))]
        + Gather.scratch() + Gather.scratch(True),
        o, w, x, bias, gain, shift, down, out_specs=(VM, VM, VM, hbm))


def back_kernel(part_ref, mid_ref, g_ref, w_hbm, gain_ref, do_out, gm_out, sums_out, low_out,
                w_ref, total, heads, lsem, asems, arecv, *scratch):
    g = Eight("tensor")
    c = lax.rem(g.d, 2)
    members = chip_members()
    load = pltpu.make_async_copy(w_hbm, w_ref, lsem.at[0])
    load.start()
    greet([m[2] for m in members])
    rows = g_ref.shape[0]
    half = do_out.shape[0] // 2
    first = Scatter(g, lambda m: part_ref.at[m], rows, scratch, 32)
    first.start()
    first.forward()

    def keep(at, value):
        total[at, :] = value

    first.finish(keep)
    scaled, inverse = norm_rows(mid_ref[...])
    grad = total[...]
    gm = g_ref[...].astype(F32) + norm_back(grad, scaled, inverse, gain_ref[...])
    gm_out[...] = gm
    low = gm.astype(BF)
    low_out[...] = low
    load.wait()
    for t in range(8):
        heads[:, t * 256:(t + 1) * 256] = jnp.dot(low, w_ref[t], preferred_element_type=F32).astype(BF)
    sems = (asems, arecv)
    take = pl.ds(pl.multiple_of(c * half + g.t * rows, rows), rows)
    copies = []
    for k, (tt, cc, device) in enumerate(members):
        cols = pl.ds(pl.multiple_of((2 * tt + cc) * HEAD, HEAD), HEAD)
        copies.append(send(heads.at[:, cols], do_out.at[take], sems, k, device))
    do_out[take, :] = heads[:, pl.ds(pl.multiple_of((2 * g.t + c) * HEAD, HEAD), HEAD)]
    sums_out[...] = jnp.zeros_like(sums_out)
    sums_out[0:1, :] = jnp.sum(grad * scaled, axis=0, keepdims=True)
    sums_out[1:2, :] = jnp.sum(grad, axis=0, keepdims=True)
    sums_out[2:3, :] = jnp.sum(low.astype(F32), axis=0, keepdims=True)
    sums_out[3:4, :] = jnp.sum(g_ref[...].astype(F32), axis=0, keepdims=True)
    for copy in copies:
        copy.wait()


def back_call(part, mid, g, w, gain):
    rows, width = g.shape
    return remote_call(
        back_kernel, "back", 4,
        (struct((16 * rows, HEAD), BF), struct((rows, width), F32), struct((8, width), F32), struct((rows, width), BF)),
        [VM, VM, VM, pl.BlockSpec(memory_space=pl.ANY), VM],
        [pltpu.VMEM(w.shape, BF), pltpu.VMEM((rows, width), F32), pltpu.VMEM((rows, width), BF), DMA((1,)), DMA((15,)), DMA((15,))]
        + Scatter.scratch(rows, width),
        part, mid, g, w, gain)


class Sums:
    @staticmethod
    def scratch(count, rows, width):
        return [pltpu.VMEM((count, rows, width), F32), DMA((count - 1,)), DMA((count - 1,))]

    def __init__(self, axis, scratch):
        self.slots, self.sems = scratch[0], scratch[1:]
        self.count = self.slots.shape[0]
        self.axis = axis
        self.d, self.t = lax.axis_index("dp"), lax.axis_index("tensor")
        self.me = self.d if axis == "dp" else self.t

    def device(self, k):
        other = lax.rem(self.me + k, self.count)
        return (other, self.t) if self.axis == "dp" else (self.d, other)

    def copy(self, k):
        own = self.slots.at[self.me]
        return copy_of(own, own, self.sems, k - 1, self.device(k))

    def start(self):
        @pl.loop(1, self.count)
        def _(k):
            self.copy(k).start()

    def finish(self):
        @pl.loop(1, self.count)
        def _(k):
            self.copy(k).wait()
        total = self.slots[0]
        for k in range(1, self.count):
            total = total + self.slots[k]
        return total


def tail_kernel(dw_ref, part_ref, gm_ref, x_ref, gain_ref, ddown_ref, dout_ref, early_ref, lane_ref,
                dw_out, tg_out, ddown_out, dout_out, sums_out, lanes_out,
                summed, arrived, total, mine_w, css, crs, ss, rs, *scratch):
    dp, g = Eight("dp"), Eight("tensor")
    c = lax.rem(g.d, 2)
    core = other_core()
    everyone = [Sums("dp", [scratch[-3], None, None]).device(k) for k in range(1, 16)]
    everyone += [Sums("tensor", [scratch[-6], None, None]).device(k) for k in range(1, 8)]
    greet(everyone)
    csems = (css, crs)
    weights = Scatter(dp, lambda m: dw_ref.at[m], dw_ref.shape[1], scratch[:7], 128)
    tokens = Scatter(g, lambda m: summed.at[m], x_ref.shape[0], scratch[7:14], 32)
    downs = CoreScatter(dp, ddown_ref, scratch[14:25], 32)
    outs = CoreScatter(dp, dout_ref, scratch[25:36], 128)
    early_t, lanes_d, late_t, all_d = (
        Sums("tensor", scratch[36:39]), Sums("dp", scratch[39:42]), Sums("tensor", scratch[42:45]), Sums("dp", scratch[45:48]))
    swap = send(part_ref.at[1 - c], arrived, csems, 0, core)
    weights.start()
    downs.start()
    outs.start()
    early_t.slots[g.t] = early_ref[...]
    early_t.start()
    lanes_d.slots[g.d] = lane_ref[...]
    lanes_d.start()
    swap.wait_recv()
    rows, width = x_ref.shape

    @pl.loop(0, 8)
    def _(t):
        @pl.loop(0, rows // 32)
        def _(n):
            at = pl.ds(pl.multiple_of(n * 32, 32), 32)
            summed[t, at, :] = (part_ref[c, t, at, :].astype(F32) + arrived[t, at, :].astype(F32)).astype(BF)

    tokens.start()
    downs.add()
    outs.add()
    tokens.forward()
    weights.forward()

    def keep(at, value):
        total[at, :] = value

    tokens.finish(keep)
    scaled, inverse = norm_rows(x_ref[...].astype(F32))
    grad = total[...]
    tg = gm_ref[...] + norm_back(grad, scaled, inverse, gain_ref[...])
    tg_out[g.index(g.r, g.p)] = tg.astype(BF)
    gather = Gather(g, lambda m: tg_out.at[m], rows, (ss, rs))
    gather.start()
    late_t.slots[g.t] = jnp.zeros(late_t.slots.shape[1:], F32)
    late_t.slots[g.t, 0:1, :] = jnp.sum(grad * scaled, axis=0, keepdims=True)
    late_t.slots[g.t, 1:2, :] = jnp.sum(grad, axis=0, keepdims=True)
    late_t.start()
    downs.forward()
    outs.forward()
    all_d.slots[g.d, 8:16, :] = early_t.finish()
    all_d.slots[g.d, 0:8, :] = late_t.finish()
    all_d.start()

    def keep_w(at, value):
        mine_w[at, :] = value.astype(BF)

    weights.finish(keep_w)
    share = dw_out.shape[1]
    there = send(mine_w.at[pl.ds(pl.multiple_of((1 - c) * share, share), share)], dw_out.at[c], csems, 1, core)
    dw_out[c] = mine_w[pl.ds(pl.multiple_of(c * share, share), share), :]
    gather.forward()

    def keep_down(at, value):
        ddown_out[at, :] = value

    downs.finish(keep_down)

    def keep_out(at, value):
        dout_out[at, :] = value

    outs.finish(keep_out)
    lanes_out[...] = lanes_d.finish()
    sums_out[...] = all_d.finish()
    gather.finish()
    there.wait()
    swap.wait_send()


def tail_call(dw, part, gm, x, gain, ddown, dout, early, lane):
    rows, width = x.shape
    wr, wc = dw.shape[1:]
    return remote_call(
        tail_kernel, "tail", 6,
        (struct((2, wr // 2, wc), BF), struct((8, rows, width), BF), struct(ddown.shape[2:], F32), struct(dout.shape[2:], F32),
         struct((16, width), F32), struct(lane.shape, F32)),
        [VM] * 9,
        [pltpu.VMEM((8, rows, width), BF), pltpu.VMEM((8, rows, width), BF), pltpu.VMEM((rows, width), F32), pltpu.VMEM((wr, wc), BF),
         DMA((2,)), DMA((2,)), DMA((10,)), DMA((10,))] + Scatter.scratch(wr, wc) + Scatter.scratch(rows, width)
        + CoreScatter.scratch(*ddown.shape[2:]) + CoreScatter.scratch(*dout.shape[2:])
        + Sums.scratch(8, *early.shape) + Sums.scratch(16, *lane.shape) + Sums.scratch(8, 8, width) + Sums.scratch(16, 16, width),
        dw, part, gm, x, gain, ddown, dout, early, lane)


def on_device(tokens, first_gain, first_shift, query_weight, query_bias, key_weight, value_weight, value_bias,
              out_weight, out_bias, second_gain, second_shift, up_weight, up_bias, down_weight, down_bias,
              cotangent, prefix, block_order):
    own, width = tokens.shape
    d, t = lax.axis_index("dp"), lax.axis_index("tensor")
    c = lax.rem(d, 2)
    nblk = block_order.shape[0]
    rows = own // 8
    meta = jnp.concatenate([block_order % nblk, prefix])
    lanes = jnp.pad(block_order % nblk, (0, HEAD - nblk), constant_values=-1).reshape(1, HEAD)
    row = lambda v: v.reshape(1, -1)

    scaled, _ = norm_rows(tokens.astype(F32))
    normed = (scaled * first_gain + first_shift).astype(BF)
    shards = jnp.stack([
        jnp.concatenate([w[:, h * HEAD:(h + 1) * HEAD] for w in (query_weight, key_weight, value_weight)], axis=1).astype(BF)
        for h in range(2)])
    w_all, n_all = gather_weights(shards, normed)
    w_all = w_all.reshape(width, 3 * HEAD)
    n_all = n_all.reshape(2 * own, width)
    pick = lambda v: lax.dynamic_slice_in_dim(v, c * HEAD, HEAD)
    bias = jnp.concatenate([pick(query_bias), jnp.zeros((HEAD,), F32), pick(value_bias)])
    qkv = (dg(n_all, w_all, NN) + bias).astype(BF)
    q = qkv[:, :HEAD]
    kv, o, lse, out_all, up_all = attend_call(meta, lanes, q, qkv[:, HEAD:], out_weight.astype(BF).T, up_weight.astype(BF))

    here = lambda v: lax.dynamic_slice_in_dim(v, t * rows, rows)
    x_rows, g_rows = here(tokens), here(cotangent)
    n2, mid, mixed, down_all = middle_call(
        o, out_all, x_rows, row(out_bias), row(second_gain), row(second_shift), down_weight.astype(BF).T)
    n2 = n2.reshape(own, width)
    pre = dg(n2, up_all, NN) + up_bias
    half_erf = 0.5 + 0.5 * lax.erf(pre * math.sqrt(0.5))
    hidden = (pre * half_erf).astype(BF)
    slope = half_erf + pre * jnp.exp(-0.5 * pre * pre) * (1.0 / math.sqrt(2.0 * math.pi))
    grad_pre = (dg(cotangent, down_all, NN) * slope).astype(BF)
    gn2 = dg(grad_pre, up_all, NT).astype(BF).reshape(8, rows, width)
    out_part = dg(hidden, down_all, NT).astype(BF).reshape(8, rows, width)
    do, gm, sums, low = back_call(gn2, mid, g_rows, out_all, row(second_gain))
    hid = up_weight.shape[1]
    dw_up = dg(n2, grad_pre, TN).astype(BF).reshape(8, 2, width // 16, hid)
    dw_down = dg(cotangent, hidden, TN).astype(BF).reshape(8, 2, width // 16, hid)
    dq, dkv, layer, gb, up_grad = attend_back_call(meta, lanes, q, kv, o, do, lse, out_part, low, mid, row(down_bias), dw_up)
    dw_out = dg(gb.reshape(own, width), mixed, TN).astype(BF).reshape(8, 2, width // 16, 2 * HEAD)

    dqkv = jnp.concatenate([dq, dkv], axis=1)
    dw = dg(n_all, dqkv, TN).astype(BF).reshape(8, width // 8, 3 * HEAD)
    gn1 = dg(dqkv, w_all, NT).astype(BF).reshape(2, 8, rows, width)
    col = jnp.sum(dqkv.astype(F32), axis=0)
    zero = jnp.zeros((HEAD,), F32)
    two = lambda v: jnp.concatenate([jnp.where(c == 0, v, zero), jnp.where(c == 1, v, zero)])
    lane = jnp.concatenate([jnp.sum(grad_pre.astype(F32), axis=0), two(col[:HEAD]), two(col[2 * HEAD:])])
    lane = jnp.pad(lane.reshape(1, -1), ((0, 7), (0, 0)))
    dw_mine, tg, down_grad, out_grad, small, lane = tail_call(
        dw, gn1, gm, x_rows, row(first_gain), dw_down, dw_out, sums, lane)
    pieces = [
        jnp.concatenate([dw_mine[0, :, i * HEAD:(i + 1) * HEAD], dw_mine[1, :, i * HEAD:(i + 1) * HEAD]], axis=1).astype(F32)
        for i in range(3)]
    return (
        layer.reshape(own, width),
        tg.reshape(own, width).astype(F32),
        small[0], small[1],
        pieces[0], lane[0, hid:hid + 2 * HEAD], pieces[1], pieces[2], lane[0, hid + 2 * HEAD:],
        out_grad.T, small[10],
        small[8], small[9],
        up_grad, lane[0, :hid],
        down_grad.T, small[11],
    )


def solution(mesh):
    rows, cols = P("dp", "tensor"), P("tensor", "dp")
    return jax.shard_map(
        on_device,
        mesh=mesh,
        in_specs=(
            P("dp", None), P(), P(), rows, P("tensor"), rows, rows, P("tensor"), cols, P(), P(), P(), rows, P("tensor"),
            cols, P(), P("dp", None), P(), P()),
        out_specs=(
            P("dp", None), P("dp", None), P(), P(), rows, P("tensor"), rows, rows, P("tensor"), cols, P(), P(), P(), rows,
            P("tensor"), cols, P()),
        check_vma=False,
    )
```

```python
import functools
import math

import jax
import jax.numpy as jnp
from jax import lax
from jax.experimental import pallas as pl
from jax.experimental.pallas import tpu as pltpu
from jax.sharding import PartitionSpec as P

HEAD = 128
BLK = 256
GRP = 4
RING = 4
EPS = 1e-05
NEG = -(2.0 ** 100)
LOG2E = math.log2(math.e)
SCALE = 1.0 / math.sqrt(HEAD)
C1 = LOG2E * SCALE
NN = (((1,), (0,)), ((), ()))
NT = (((1,), (1,)), ((), ()))
TN = (((0,), (0,)), ((), ()))
MESH = pl.DeviceIdType.MESH
VM = pl.BlockSpec(memory_space=pltpu.VMEM)
SM = pl.BlockSpec(memory_space=pltpu.SMEM)
BF = jnp.bfloat16
F32 = jnp.float32
DMA = pltpu.SemaphoreType.DMA


def dg(a, b, dims):
    return lax.dot_general(a, b, dims, preferred_element_type=F32)


def struct(shape, dtype):
    return jax.ShapeDtypeStruct(shape, dtype)


class Eight:
    def __init__(self, axis):
        d, t = lax.axis_index("dp"), lax.axis_index("tensor")
        self.axis, self.d, self.t = axis, d, t
        if axis == "dp":
            self.r, self.p = d // 4, lax.rem(d // 2, 2)
        else:
            self.r, self.p = lax.rem(t, 4), t // 4

    def ring(self, i):
        return lax.rem(self.r + i, RING)

    def side(self, s):
        return 1 - self.p if s else self.p

    def index(self, r, p):
        return r * 2 + p if self.axis == "dp" else p * 4 + r

    def device(self, r, p):
        if self.axis == "dp":
            return ((r * 2 + p) * 2 + lax.rem(self.d, 2), self.t)
        return (self.d, p * 4 + r)

    def others(self):
        return [self.device(self.ring(i), self.p) for i in (1, 3)] + [self.device(self.r, 1 - self.p)]


def other_core():
    d = lax.axis_index("dp")
    return (d + 1 - 2 * lax.rem(d, 2), lax.axis_index("tensor"))


def greet(devices):
    barrier = pltpu.get_barrier_semaphore()
    for device in devices:
        pl.semaphore_signal(barrier, inc=1, device_id=device, device_id_type=MESH)
    pl.semaphore_wait(barrier, len(devices))


def send(src, dst, sems, k, device):
    copy = pltpu.make_async_remote_copy(
        src_ref=src, dst_ref=dst, send_sem=sems[0].at[k], recv_sem=sems[1].at[k],
        device_id=device, device_id_type=MESH)
    copy.start()
    return copy


def copy_of(src, dst, sems, k, device):
    return pltpu.make_async_remote_copy(
        src_ref=src, dst_ref=dst, send_sem=sems[0].at[k], recv_sem=sems[1].at[k],
        device_id=device, device_id_type=MESH)


def send(src, dst, sems, k, device):
    copy = copy_of(src, dst, sems, k, device)
    copy.start()
    return copy


class Gather:
    @staticmethod
    def scratch(twin=False):
        return [DMA((9,)), DMA((9,))] + ([DMA((8,)), DMA((8,))] if twin else [])

    def __init__(self, group, place, rows, sems, twin=None, twin_own=True):
        self.g, self.place, self.sems = group, place, sems[:2]
        self.twin, self.twin_sems, self.twin_own = twin, sems[2:4], twin_own
        self.halves = (pl.ds(0, rows // 2), pl.ds(rows // 2, rows // 2))

    def at(self, i, s):
        g = self.g
        return self.place(g.index(g.ring(i), g.side(s)))

    def to(self, i):
        g = self.g
        return g.device(g.ring(i), g.p)

    def pair(self):
        own = self.at(0, 0)
        return copy_of(own, own, self.sems, 0, self.g.device(self.g.r, 1 - self.g.p))

    def near(self, s, way):
        chunk = self.at(0, s)
        return copy_of(chunk, chunk, self.sems, 1 + 4 * s + way, self.to(1 + 2 * way))

    def relay(self, s, way):
        half = self.at(3 - 2 * way, s).at[self.halves[way]]
        return copy_of(half, half, self.sems, 3 + 4 * s + way, self.to(1 + 2 * way))

    def over(self, k, i, s):
        chunk = self.at(i, s)
        return copy_of(chunk, chunk, self.twin_sems, k, self.twin)

    def tell(self, i, s):
        if self.twin is not None and (i or s or self.twin_own):
            self.over(2 * i + s, i, s).start()

    def start(self):
        self.pair().start()
        for way in (0, 1):
            self.near(0, way).start()
        self.tell(0, 0)

    def forward_pair(self):
        self.pair().wait_recv()
        for way in (0, 1):
            self.near(1, way).start()
        self.tell(0, 1)

    def forward(self, s):
        for way in (0, 1):
            self.near(s, way).wait_recv()
            self.relay(s, way).start()
            self.tell(3 - 2 * way, s)

    def arrive(self, s):
        for way in (0, 1):
            self.relay(s, way).wait_recv()
        self.tell(2, s)

    def settle(self):
        self.pair().wait_send()
        for s in (0, 1):
            for way in (0, 1):
                self.near(s, way).wait_send()
                self.relay(s, way).wait_send()
        if self.twin is not None:
            for k in range(0 if self.twin_own else 1, 8):
                self.over(k, 0, 0).wait()

    def rest(self):
        self.forward_pair()
        self.forward(0)
        self.forward(1)
        self.arrive(0)
        self.arrive(1)
        self.settle()


class Scatter:
    COUNT = 9

    @staticmethod
    def scratch(rows, width):
        half = rows // 2
        return [
            pltpu.VMEM((2, 2, half, width), BF), pltpu.VMEM((2, 2, half, width), BF), pltpu.VMEM((2, 2, rows, width), BF),
            pltpu.VMEM((rows, width), BF), pltpu.VMEM((rows, width), BF), DMA((13,)), DMA((13,))]

    def __init__(self, group, part, rows, scratch, step):
        self.g, self.part, self.step, self.rows = group, part, step, rows
        self.mid, self.added, self.last, self.sum, self.end = scratch[:5]
        self.sems = scratch[5:7]
        self.half = rows // 2
        self.halves = (pl.ds(0, self.half), pl.ds(self.half, self.half))

    def at(self, i, s):
        g = self.g
        return self.part(g.index(g.ring(i), g.side(s)))

    def to(self, way):
        g = self.g
        return g.device(g.ring(1 + 2 * way), g.p)

    def far(self, s, way):
        return copy_of(self.at(2, s).at[self.halves[way]], self.mid.at[s, way], self.sems, 2 * s + way, self.to(way))

    def own(self, s, way):
        half = self.halves[1 - way]
        return copy_of(self.at(1 + 2 * way, s).at[half], self.last.at[s, way, half], self.sems, 4 + 2 * s + way, self.to(way))

    def both(self, s, way):
        return copy_of(self.added.at[s, way], self.last.at[s, way, self.halves[way]], self.sems, 8 + 2 * s + way, self.to(way))

    def pair(self):
        return copy_of(self.sum, self.end, self.sems, 12, self.g.device(self.g.r, 1 - self.g.p))

    def by_rows(self, rows, body):
        step = min(self.step, rows)

        @pl.loop(0, rows // step)
        def _(n):
            body(pl.multiple_of(n * step, step), step)

    def send_far(self, s):
        for way in (0, 1):
            self.far(s, way).start()

    def send_near(self, s):
        for way in (0, 1):
            self.own(s, way).start()

    def add_near(self, s):
        for way in (0, 1):
            self.far(s, way).wait_recv()
            mine = self.at(1 + 2 * way, s)
            base = way * self.half

            def add(at, n, way=way, mine=mine, base=base):
                rows = pl.ds(at, n)
                total = mine[pl.ds(base + at, n), :].astype(F32) + self.mid[s, way, rows, :].astype(F32)
                self.added[s, way, rows, :] = total.astype(BF)

            self.by_rows(self.half, add)
            self.both(s, way).start()

    def arrived(self, s):
        for way in (0, 1):
            self.own(s, way).wait_recv()
            self.both(s, way).wait_recv()

    def add_pair(self):
        self.arrived(1)
        mine = self.at(0, 1)

        def add(at, n):
            rows = pl.ds(at, n)
            total = mine[rows, :].astype(F32) + self.last[1, 0, rows, :].astype(F32) + self.last[1, 1, rows, :].astype(F32)
            self.sum[rows, :] = total.astype(BF)

        self.by_rows(self.rows, add)
        self.pair().start()

    def start(self):
        for s in (1, 0):
            self.send_far(s)
            self.send_near(s)

    def forward(self):
        self.add_near(1)
        self.add_near(0)
        self.add_pair()

    def finish(self, store):
        self.arrived(0)
        self.pair().wait_recv()
        mine = self.at(0, 0)

        def add(at, n):
            rows = pl.ds(at, n)
            total = mine[rows, :].astype(F32) + self.last[0, 0, rows, :].astype(F32) + self.last[0, 1, rows, :].astype(F32)
            store(rows, total + self.end[rows, :].astype(F32))

        self.by_rows(self.rows, add)
        self.pair().wait_send()
        for s in (0, 1):
            for way in (0, 1):
                self.far(s, way).wait_send()
                self.own(s, way).wait_send()
                self.both(s, way).wait_send()


class CoreScatter:
    @staticmethod
    def scratch(rows, width):
        return [pltpu.VMEM((8, rows, width), BF), pltpu.VMEM((8, rows, width), BF), DMA((1,)), DMA((1,))] + Scatter.scratch(rows, width)

    def __init__(self, group, part, scratch, step):
        self.part, self.arrived, self.added = part, scratch[0], scratch[1]
        self.c = lax.rem(group.d, 2)
        self.sems = scratch[2:4]
        self.step = step
        self.inner = Scatter(group, lambda m: self.added.at[m], part.shape[2], scratch[4:], step)

    def swap(self):
        return copy_of(self.part.at[:, 1 - self.c], self.arrived, self.sems, 0, other_core())

    def start(self):
        self.swap().start()

    def add(self):
        self.swap().wait_recv()
        rows, step = self.part.shape[2], self.step

        @pl.loop(0, 8)
        def _(m):
            @pl.loop(0, rows // step)
            def _(n):
                at = pl.ds(pl.multiple_of(n * step, step), step)
                self.added[m, at, :] = (self.part[m, self.c, at, :].astype(F32) + self.arrived[m, at, :].astype(F32)).astype(BF)

        self.inner.start()

    def forward(self):
        self.inner.forward()

    def finish(self, store):
        self.inner.finish(store)
        self.swap().wait_send()


def remote_call(kernel, name, cid, outs, ins, scratch, *args, out_specs=None):
    return pl.pallas_call(
        kernel, out_shape=outs, in_specs=ins,
        out_specs=jax.tree.map(lambda _: VM, outs) if out_specs is None else out_specs,
        scratch_shapes=scratch, name=name,
        compiler_params=pltpu.CompilerParams(collective_id=cid, has_side_effects=True, vmem_limit_bytes=58 << 20),
    )(*args)


def chip_members():
    d, t = lax.axis_index("dp"), lax.axis_index("tensor")
    c = lax.rem(d, 2)
    out = []
    for dt in range(8):
        for dc in range(2):
            if dt or dc:
                tt = lax.rem(t + dt, 8)
                cc = lax.rem(c + dc, 2)
                out.append((tt, cc, (d - c + cc, tt)))
    return out


def norm_rows(values):
    average = jnp.mean(values, axis=-1, keepdims=True)
    centred = values - average
    variance = jnp.mean(centred * centred, axis=-1, keepdims=True)
    inverse = lax.rsqrt(variance + EPS)
    return centred * inverse, inverse


def norm_back(grad, scaled, inverse, gain):
    e = grad * gain
    first = jnp.mean(e, axis=-1, keepdims=True)
    second = jnp.mean(e * scaled, axis=-1, keepdims=True)
    return inverse * (e - first - scaled * second)


def augment(meta, lanes_ref, q_ref, qa_ref, kx_ref):
    rows = q_ref.shape[0]
    nblk = kx_ref.shape[0] // BLK
    prefix = meta[nblk]
    for a in range(rows // BLK):
        at = slice(a * BLK, (a + 1) * BLK)
        hidden = jnp.where(lanes_ref[...] > meta[first_block() + a], NEG, 0.0)
        qa_ref[at, :HEAD] = q_ref[at, :]
        qa_ref[at, HEAD:] = jnp.broadcast_to(hidden, (BLK, HEAD)).astype(BF)
    lane = lax.broadcasted_iota(jnp.int32, (BLK, HEAD), 1)
    inside = lax.broadcasted_iota(jnp.int32, (BLK, HEAD), 0)

    @pl.loop(0, nblk)
    def _(b):
        late = (lane == b) & (inside >= prefix - meta[b] * BLK)
        kx_ref[pl.ds(pl.multiple_of(b * BLK, BLK), BLK), :] = jnp.where(late, 1.0, 0.0).astype(BF)


def first_block():
    return lax.axis_index("dp") // 2 * 4


def forward_kernel(meta, lanes_ref, x_ref, gain1_ref, shift1_ref, wq_ref, wk_ref, wv_ref, qb_ref, vb_ref, wo_ref, wu_ref, wd_ref,
                   bias_ref, gain2_ref, shift2_ref,
                   w_hbm, n_hbm, q_out, kv_hbm, o_ref, lse_ref, out_hbm, up_hbm, down_hbm, n2_out, mid_out, own_out,
                   w_vm, n_vm, kv_vm, out_vm, up_vm, down_vm, wsh, qa_ref, kx_ref, m_ref, acc_ref, mixed,
                   lsem, css, crs, ass, ars, *sems):
    gd, gt = Eight("dp"), Eight("tensor")
    t = gt.t
    c = lax.rem(gd.d, 2)
    core = other_core()
    members = chip_members()
    me = gd.index(gd.r, gd.p)
    own = x_ref.shape[0]
    rows = 2 * own
    nblk = kx_ref.shape[0] // BLK
    per = rows // BLK
    shard = wq_ref.shape[0]
    half = out_vm.shape[1] // 2
    small = mid_out.shape[0]
    csem, asem = (css, crs), (ass, ars)
    for h in range(2):
        cols = slice(h * HEAD, (h + 1) * HEAD)
        for i, ref in enumerate((wq_ref, wk_ref, wv_ref)):
            wsh[h, :, i * HEAD:(i + 1) * HEAD] = ref[:, cols].astype(BF)
    greet([m[2] for m in members] + gd.others())

    w_place = lambda m: w_vm.at[pl.ds(pl.multiple_of(m * 2 * shard, 2 * shard), 2 * shard)]
    row_of = lambda m: pl.ds(pl.multiple_of((m * 2 + c) * shard, shard), shard)
    mine = row_of(me)
    swap = send(wsh.at[1 - c], w_vm.at[mine], csem, 0, core)
    w_vm[mine, :] = wsh[c]
    qkv = Gather(gd, w_place, 2 * shard, sems[0:2])
    keys = Gather(gd, lambda m: kv_vm.at[m], rows, sems[2:4])
    outs = Gather(gd, lambda m: out_vm.at[t, row_of(m)], shard, sems[4:8], core)
    ups = Gather(gd, lambda m: up_vm.at[row_of(m)], shard, sems[8:12], core)
    downs = Gather(gd, lambda m: down_vm.at[row_of(m)], shard, sems[12:16], core)
    wide = Gather(gt, lambda m: out_vm.at[m, pl.ds(pl.multiple_of(c * half, half), half)], half, sems[16:20], core, twin_own=False)
    normed = Gather(gt, lambda m: n2_out.at[m], small, sems[20:22])
    swap.wait_recv()
    qkv.start()
    out_vm[t, mine, :] = jnp.transpose(wo_ref[...]).astype(BF)
    outs.start()

    def norm_part(k):
        step = 32

        @pl.loop(0, own // 2 // step)
        def _(n):
            at = pl.ds(pl.multiple_of(k * (own // 2) + n * step, step), step)
            scaled, _ = norm_rows(x_ref[at, :].astype(F32))
            n_vm[c, at, :] = (scaled * gain1_ref[...] + shift1_ref[...]).astype(BF)

        at = pl.ds(k * (own // 2), own // 2)
        return send(n_vm.at[c, at], n_vm.at[c, at], csem, 1 + k, core)

    there = [norm_part(0)]
    outs.forward_pair()
    outs.forward(0)
    qkv.forward_pair()
    qkv.forward(0)
    there.append(norm_part(1))
    outs.forward(1)
    outs.arrive(0)
    qkv.forward(1)
    up_vm[mine, :] = wu_ref[...].astype(BF)
    outs.arrive(1)
    down_vm[mine, :] = jnp.transpose(wd_ref[...]).astype(BF)
    outs.settle()
    wide.start()
    qkv.arrive(0)
    qkv.arrive(1)
    for copy in there:
        copy.wait_recv()
    local = pl.ds(pl.multiple_of(c * HEAD, HEAD), HEAD)
    bias_q, bias_v = qb_ref[:, local], vb_ref[:, local]

    @pl.loop(0, per)
    def _(b):
        at = pl.ds(pl.multiple_of(b * BLK, BLK), BLK)
        piece = dg(n_vm[b // 2, pl.ds(pl.multiple_of(lax.rem(b, 2) * BLK, BLK), BLK), :], w_vm[...], NN)
        q_out[at, :] = (piece[:, :HEAD] + bias_q).astype(BF)
        kv_vm[me, at, :HEAD] = piece[:, HEAD:2 * HEAD].astype(BF)
        kv_vm[me, at, HEAD:] = (piece[:, 2 * HEAD:] + bias_v).astype(BF)

    keys.start()
    saves = [pltpu.make_async_copy(w_vm, w_hbm, lsem.at[0]), pltpu.make_async_copy(n_vm, n_hbm, lsem.at[1])]
    for save in saves:
        save.start()
    augment(meta, lanes_ref, q_out, qa_ref, kx_ref)
    m_ref[...] = jnp.full_like(m_ref, -1e30)
    acc_ref[...] = jnp.zeros_like(acc_ref)
    ones = jnp.ones((BLK, HEAD), BF)
    prefix = meta[nblk]

    def attend(chunk, diagonal):
        @pl.loop(0, per)
        def _(a):
            take = pl.ds(pl.multiple_of(a * BLK, BLK), BLK)
            q = qa_ref[take, :]
            ss, vs = [], []
            for i in range(per):
                at = pl.ds(pl.multiple_of(chunk * rows + i * BLK, BLK), BLK)
                ss.append(dg(q, jnp.concatenate([kv_vm[chunk, i * BLK:(i + 1) * BLK, :HEAD], kx_ref[at, :]], axis=1), NT))
                vs.append(jnp.concatenate([kv_vm[chunk, i * BLK:(i + 1) * BLK, HEAD:], ones], axis=1))
            if diagonal:
                edge = prefix - 1 - meta[first_block() + a] * BLK
                lim = jnp.maximum(lax.broadcasted_iota(jnp.int32, (BLK, BLK), 0), edge)
                key = lax.broadcasted_iota(jnp.int32, (BLK, BLK), 1)
                for i in range(per):
                    ss[i] = jnp.where(key <= jnp.where(a == i, lim, BLK), ss[i], NEG)
            top = ss[0]
            for s in ss[1:]:
                top = jnp.maximum(top, s)
            old = m_ref[take, :1]
            new = jnp.maximum(old, jnp.max(top, axis=1, keepdims=True) * C1)
            alpha = jnp.exp2(old - new)
            add = None
            for s, v in zip(ss, vs):
                term = jnp.dot(jnp.exp2(s * C1 - new).astype(BF), v, preferred_element_type=F32)
                add = term if add is None else add + term
            acc_ref[take, :] = acc_ref[take, :] * alpha + add
            m_ref[take, :] = jnp.broadcast_to(new, (BLK, HEAD))

    attend(me, True)

    @pl.loop(1, 8)
    def _(k):
        kk = lax.rem(k, 4)
        i, s = kk + kk // 2 - 2 * (kk // 3), k // 4

        @pl.when(k == 1)
        def _():
            keys.forward_pair()
            keys.forward(0)

        @pl.when(k == 2)
        def _():
            wide.forward_pair()
            wide.forward(0)

        @pl.when(k == 3)
        def _():
            keys.arrive(0)

        @pl.when(k == 5)
        def _():
            keys.forward(1)
            wide.forward(1)
            ups.start()

        @pl.when(k == 7)
        def _():
            keys.arrive(1)

        attend(gd.index(gd.ring(i), gd.p + s * (1 - 2 * gd.p)), False)

    for a in range(per):
        at = slice(a * BLK, (a + 1) * BLK)
        total = acc_ref[at, HEAD:]
        o_ref[at, :] = (acc_ref[at, :HEAD] / total).astype(BF)
        lse_ref[a:a + 1, :] = jnp.transpose(m_ref[at, :] + jnp.log2(total))[:1, :]
    head = pl.ds(pl.multiple_of((2 * t + c) * HEAD, HEAD), HEAD)
    copies = []
    for k, (tt, cc, device) in enumerate(members):
        take = pl.ds(pl.multiple_of(cc * own + tt * small, small), small)
        copies.append(send(o_ref.at[take], mixed.at[:, head], asem, k, device))
    copies.append(send(o_ref.at[pl.ds(pl.multiple_of((1 - c) * own, own), own)], own_out.at[:, local], asem, 15, core))
    keys.settle()
    save = pltpu.make_async_copy(kv_vm, kv_hbm, lsem.at[2])
    save.start()
    saves.append(save)
    downs.start()
    mixed[:, head] = o_ref[pl.ds(pl.multiple_of(c * own + t * small, small), small), :]
    own_out[:, local] = o_ref[pl.ds(pl.multiple_of(c * own, own), own), :]
    ups.forward_pair()
    ups.forward(0)
    wide.arrive(0)
    wide.arrive(1)
    wide.settle()
    save = pltpu.make_async_copy(out_vm, out_hbm, lsem.at[3])
    save.start()
    saves.append(save)
    for copy in copies:
        copy.wait_recv()
    span = 512
    x_rows = pl.ds(pl.multiple_of(t * small, small), small)
    for n in range(mid_out.shape[1] // span):
        cols = pl.ds(n * span, span)
        total = None
        for k in range(8):
            term = dg(mixed[:, k * 256:(k + 1) * 256], out_vm[k, cols, :], NT)
            total = term if total is None else total + term
        mid_out[:, cols] = total + (x_ref[x_rows, cols].astype(F32) + bias_ref[:, cols])
    scaled, _ = norm_rows(mid_out[...])
    n2_out[t] = (scaled * gain2_ref[...] + shift2_ref[...]).astype(BF)
    normed.start()
    ups.forward(1)
    downs.forward_pair()
    downs.forward(0)
    normed.forward_pair()
    normed.forward(0)
    ups.arrive(0)
    ups.arrive(1)
    ups.settle()
    save = pltpu.make_async_copy(up_vm, up_hbm, lsem.at[4])
    save.start()
    saves.append(save)
    normed.forward(1)
    downs.forward(1)
    downs.arrive(0)
    downs.arrive(1)
    downs.settle()
    save = pltpu.make_async_copy(down_vm, down_hbm, lsem.at[5])
    save.start()
    saves.append(save)
    normed.arrive(0)
    normed.arrive(1)
    normed.settle()
    qkv.settle()
    swap.wait_send()
    for copy in there + copies:
        copy.wait_send()
    for save in saves:
        save.wait()


def forward_call(meta, lanes, x, gain1, shift1, wq, wk, wv, qb, vb, wo, wu, wd, bias, gain2, shift2):
    own, width = x.shape
    rows, shard, hid, small = 2 * own, wq.shape[0], wu.shape[1], own // 8
    hbm = pl.BlockSpec(memory_space=pl.ANY)
    big = [(width, 3 * HEAD), (2, own, width), (8, rows, 2 * HEAD), (8, width, 2 * HEAD), (width, hid), (width, hid)]
    w, n, kv, out, up, down = (struct(s, BF) for s in big)
    outs = (w, n, struct((rows, HEAD), BF), kv, struct((rows, HEAD), BF), struct((rows // BLK, BLK), F32), out, up, down,
            struct((8, small, width), BF), struct((small, width), F32), struct((own, 2 * HEAD), BF))
    return remote_call(
        forward_kernel, "forward", 1, outs, [SM] + [VM] * 15,
        [pltpu.VMEM(s, BF) for s in big]
        + [pltpu.VMEM((2, shard, 3 * HEAD), BF), pltpu.VMEM((rows, 2 * HEAD), BF), pltpu.VMEM((8 * rows, HEAD), BF),
           pltpu.VMEM((rows, HEAD), F32), pltpu.VMEM((rows, 2 * HEAD), F32), pltpu.VMEM((small, width), BF),
           DMA((6,)), DMA((3,)), DMA((3,)), DMA((16,)), DMA((16,))]
        + Gather.scratch() * 2 + Gather.scratch(True) * 4 + Gather.scratch(),
        meta, lanes, x, gain1, shift1, wq, wk, wv, qb, vb, wo, wu, wd, bias, gain2, shift2,
        out_specs=(hbm, hbm, VM, hbm, VM, VM, hbm, hbm, hbm, VM, VM, VM))


def attend_back_kernel(meta, lanes_ref, q_ref, kv_ref, o_ref, do_ref, lse_ref, opart_ref, gbr_ref, mid_ref, bias_ref, dup_ref,
                       dq_ref, dkv_out, lay_out, gb_out, dup_out,
                       qa_ref, kx_ref, part, delta_ref, dq_acc, *scratch):
    g, gt = Eight("dp"), Eight("tensor")
    core = other_core()
    me = g.index(g.r, g.p)
    rows = q_ref.shape[0]
    nblk = kx_ref.shape[0] // BLK
    per = rows // BLK
    greet(g.others() + gt.others() + [core])
    keys = Scatter(g, lambda m: part.at[m], rows, scratch[:7], 128)
    outs = Scatter(gt, lambda m: opart_ref.at[m], opart_ref.shape[1], scratch[7:14], 32)
    ups = CoreScatter(g, dup_ref, scratch[14:25], 32)
    wide = Gather(gt, lambda m: gb_out.at[m], gb_out.shape[1], scratch[25:27])
    layer = Gather(gt, lambda m: lay_out.at[m], lay_out.shape[1], scratch[27:29])
    ups.start()
    outs.start()
    mine_t = gt.index(gt.r, gt.p)
    gb_out[mine_t] = gbr_ref[...]
    wide.start()
    augment(meta, lanes_ref, q_ref, qa_ref, kx_ref)
    for a in range(per):
        at = slice(a * BLK, (a + 1) * BLK)
        prod = do_ref[at, :].astype(F32) * o_ref[at, :].astype(F32)
        delta_ref[0:1, at] = jnp.sum(jnp.transpose(prod), axis=0, keepdims=True)
        delta_ref[1:2, at] = lse_ref[a:a + 1, :]
    dq_acc[...] = jnp.zeros_like(dq_acc)
    prefix = meta[nblk]

    def attend(chunk, own):
        @pl.loop(0, per)
        def _(i):
            at_k = pl.ds(pl.multiple_of(i * BLK, BLK), BLK)
            at_x = pl.ds(pl.multiple_of(chunk * rows + i * BLK, BLK), BLK)
            k = kv_ref[chunk, at_k, :HEAD]
            v = kv_ref[chunk, at_k, HEAD:]
            kk = jnp.concatenate([k, kx_ref[at_x, :]], axis=1)
            dk = dv = None
            for a in range(per):
                at_q = slice(a * BLK, (a + 1) * BLK)
                q = q_ref[at_q, :]
                do = do_ref[at_q, :]
                p = jnp.exp2(dg(kk, qa_ref[at_q, :], NT) * C1 - delta_ref[1:2, at_q])
                if own:
                    edge = prefix - 1 - meta[first_block() + a] * BLK
                    lim = jnp.maximum(lax.broadcasted_iota(jnp.int32, (BLK, BLK), 1), edge)
                    key = lax.broadcasted_iota(jnp.int32, (BLK, BLK), 0)
                    p = jnp.where(key <= jnp.where(i == a, lim, BLK), p, 0.0)
                ds = (p * (dg(v, do, NT) - delta_ref[0:1, at_q])).astype(BF)
                tv = jnp.dot(p.astype(BF), do, preferred_element_type=F32)
                tk = jnp.dot(ds, q, preferred_element_type=F32)
                dv = tv if dv is None else dv + tv
                dk = tk if dk is None else dk + tk
                dq_acc[at_q, :] += dg(ds, k, TN)
            part[chunk, at_k, :HEAD] = (dk * SCALE).astype(BF)
            part[chunk, at_k, HEAD:] = dv.astype(BF)

    @pl.loop(0, 7)
    def _(k):
        kk = lax.rem(k, 3)
        i = (2 - kk + 3 * (kk // 2)) * (1 - k // 6)
        s = 1 - k // 3 + 2 * (k // 6)
        attend(g.index(g.ring(i), g.p + s * (1 - 2 * g.p)), False)

        @pl.when(k == 0)
        def _():
            keys.send_far(1)
            ups.add()

        @pl.when(k == 1)
        def _():
            wide.forward_pair()
            wide.forward(0)
            outs.add_near(1)

        @pl.when(k == 2)
        def _():
            keys.send_near(1)
            keys.add_near(1)
            outs.add_near(0)

        @pl.when(k == 3)
        def _():
            keys.send_far(0)
            outs.add_pair()
            wide.forward(1)

        @pl.when(k == 4)
        def _():
            ups.inner.add_near(1)
            ups.inner.add_near(0)

        @pl.when(k == 5)
        def _():
            keys.send_near(0)
            keys.add_near(0)

        @pl.when(k == 6)
        def _():
            keys.add_pair()

    def lay(at, value):
        lay_out[mine_t, at, :] = (mid_ref[at, :] + (value + bias_ref[...])).astype(BF)

    outs.finish(lay)
    layer.start()
    ups.inner.add_pair()
    attend(me, True)
    dq_ref[...] = (dq_acc[...] * SCALE).astype(BF)
    layer.forward_pair()
    layer.forward(0)
    wide.arrive(0)
    wide.arrive(1)
    wide.settle()

    def keep(at, value):
        dkv_out[at, :] = value.astype(BF)

    keys.finish(keep)
    layer.forward(1)

    def keep_up(at, value):
        dup_out[at, :] = value

    ups.finish(keep_up)
    layer.arrive(0)
    layer.arrive(1)
    layer.settle()


def attend_back_call(meta, lanes, q, kv, o, do, lse, opart, gb, mid, bias, dup):
    rows = q.shape[0]
    tr, width = mid.shape
    sr, sw = dup.shape[2:]
    return remote_call(
        attend_back_kernel, "attend_back", 5,
        (struct(q.shape, BF), struct((rows, 2 * HEAD), BF), struct((8, tr, width), BF), struct((8, tr, width), BF), struct((sr, sw), F32)),
        [SM] + [VM] * 11,
        [pltpu.VMEM((rows, 2 * HEAD), BF), pltpu.VMEM((8 * rows, HEAD), BF), pltpu.VMEM(kv.shape, BF), pltpu.VMEM((8, rows), F32),
         pltpu.VMEM((rows, HEAD), F32)]
        + Scatter.scratch(rows, 2 * HEAD) + Scatter.scratch(tr, width) + CoreScatter.scratch(sr, sw) + Gather.scratch() * 2,
        meta, lanes, q, kv, o, do, lse, opart, gb, mid, bias, dup)


def back_kernel(part_ref, mid_ref, g_ref, w_hbm, gain_ref, do_out, gm_out, sums_out, low_out,
                w_ref, total, heads, lsem, asems, arecv, *scratch):
    g = Eight("tensor")
    c = lax.rem(g.d, 2)
    members = chip_members()
    load = pltpu.make_async_copy(w_hbm, w_ref, lsem.at[0])
    load.start()
    greet([m[2] for m in members])
    rows = g_ref.shape[0]
    half = do_out.shape[0] // 2
    first = Scatter(g, lambda m: part_ref.at[m], rows, scratch, 32)
    first.start()
    first.forward()

    def keep(at, value):
        total[at, :] = value

    first.finish(keep)
    scaled, inverse = norm_rows(mid_ref[...])
    grad = total[...]
    gm = g_ref[...].astype(F32) + norm_back(grad, scaled, inverse, gain_ref[...])
    gm_out[...] = gm
    low = gm.astype(BF)
    low_out[...] = low
    load.wait()
    for t in range(8):
        heads[:, t * 256:(t + 1) * 256] = jnp.dot(low, w_ref[t], preferred_element_type=F32).astype(BF)
    sems = (asems, arecv)
    take = pl.ds(pl.multiple_of(c * half + g.t * rows, rows), rows)
    copies = []
    for k, (tt, cc, device) in enumerate(members):
        cols = pl.ds(pl.multiple_of((2 * tt + cc) * HEAD, HEAD), HEAD)
        copies.append(send(heads.at[:, cols], do_out.at[take], sems, k, device))
    do_out[take, :] = heads[:, pl.ds(pl.multiple_of((2 * g.t + c) * HEAD, HEAD), HEAD)]
    sums_out[...] = jnp.zeros_like(sums_out)
    sums_out[0:1, :] = jnp.sum(grad * scaled, axis=0, keepdims=True)
    sums_out[1:2, :] = jnp.sum(grad, axis=0, keepdims=True)
    sums_out[2:3, :] = jnp.sum(low.astype(F32), axis=0, keepdims=True)
    sums_out[3:4, :] = jnp.sum(g_ref[...].astype(F32), axis=0, keepdims=True)
    for copy in copies:
        copy.wait()


def back_call(part, mid, g, w, gain):
    rows, width = g.shape
    return remote_call(
        back_kernel, "back", 4,
        (struct((16 * rows, HEAD), BF), struct((rows, width), F32), struct((8, width), F32), struct((rows, width), BF)),
        [VM, VM, VM, pl.BlockSpec(memory_space=pl.ANY), VM],
        [pltpu.VMEM(w.shape, BF), pltpu.VMEM((rows, width), F32), pltpu.VMEM((rows, width), BF), DMA((1,)), DMA((15,)), DMA((15,))]
        + Scatter.scratch(rows, width),
        part, mid, g, w, gain)


class Sums:
    @staticmethod
    def scratch(count, rows, width):
        return [pltpu.VMEM((count, rows, width), F32), DMA((count - 1,)), DMA((count - 1,))]

    def __init__(self, axis, scratch):
        self.slots, self.sems = scratch[0], scratch[1:]
        self.count = self.slots.shape[0]
        self.axis = axis
        self.d, self.t = lax.axis_index("dp"), lax.axis_index("tensor")
        self.me = self.d if axis == "dp" else self.t

    def device(self, k):
        other = lax.rem(self.me + k, self.count)
        return (other, self.t) if self.axis == "dp" else (self.d, other)

    def copy(self, k):
        own = self.slots.at[self.me]
        return copy_of(own, own, self.sems, k - 1, self.device(k))

    def start(self):
        @pl.loop(1, self.count)
        def _(k):
            self.copy(k).start()

    def finish(self):
        @pl.loop(1, self.count)
        def _(k):
            self.copy(k).wait()
        total = self.slots[0]
        for k in range(1, self.count):
            total = total + self.slots[k]
        return total


def tail_kernel(dw_ref, part_ref, gm_ref, x_ref, gain_ref, ddown_ref, dout_ref, early_ref, lane_ref,
                dw_out, tg_out, ddown_out, dout_out, sums_out, lanes_out,
                summed, arrived, total, mine_w, css, crs, ss, rs, *scratch):
    dp, g = Eight("dp"), Eight("tensor")
    c = lax.rem(g.d, 2)
    core = other_core()
    everyone = [Sums("dp", [scratch[-3], None, None]).device(k) for k in range(1, 16)]
    everyone += [Sums("tensor", [scratch[-6], None, None]).device(k) for k in range(1, 8)]
    greet(everyone)
    csems = (css, crs)
    weights = Scatter(dp, lambda m: dw_ref.at[m], dw_ref.shape[1], scratch[:7], 128)
    tokens = Scatter(g, lambda m: summed.at[m], x_ref.shape[0], scratch[7:14], 32)
    downs = CoreScatter(dp, ddown_ref, scratch[14:25], 32)
    outs = CoreScatter(dp, dout_ref, scratch[25:36], 128)
    early_t, lanes_d, late_t, all_d = (
        Sums("tensor", scratch[36:39]), Sums("dp", scratch[39:42]), Sums("tensor", scratch[42:45]), Sums("dp", scratch[45:48]))
    swap = send(part_ref.at[1 - c], arrived, csems, 0, core)
    weights.start()
    downs.start()
    outs.start()
    early_t.slots[g.t] = early_ref[...]
    early_t.start()
    lanes_d.slots[g.d] = lane_ref[...]
    lanes_d.start()
    swap.wait_recv()
    rows, width = x_ref.shape

    @pl.loop(0, 8)
    def _(t):
        @pl.loop(0, rows // 32)
        def _(n):
            at = pl.ds(pl.multiple_of(n * 32, 32), 32)
            summed[t, at, :] = (part_ref[c, t, at, :].astype(F32) + arrived[t, at, :].astype(F32)).astype(BF)

    tokens.start()
    downs.add()
    outs.add()
    tokens.forward()
    weights.forward()

    def keep(at, value):
        total[at, :] = value

    tokens.finish(keep)
    scaled, inverse = norm_rows(x_ref[...].astype(F32))
    grad = total[...]
    tg = gm_ref[...] + norm_back(grad, scaled, inverse, gain_ref[...])
    tg_out[g.index(g.r, g.p)] = tg.astype(BF)
    gather = Gather(g, lambda m: tg_out.at[m], rows, (ss, rs))
    gather.start()
    late_t.slots[g.t] = jnp.zeros(late_t.slots.shape[1:], F32)
    late_t.slots[g.t, 0:1, :] = jnp.sum(grad * scaled, axis=0, keepdims=True)
    late_t.slots[g.t, 1:2, :] = jnp.sum(grad, axis=0, keepdims=True)
    late_t.start()
    downs.forward()
    outs.forward()
    all_d.slots[g.d, 8:16, :] = early_t.finish()
    all_d.slots[g.d, 0:8, :] = late_t.finish()
    all_d.start()

    def keep_w(at, value):
        mine_w[at, :] = value.astype(BF)

    weights.finish(keep_w)
    share = dw_out.shape[1]
    there = send(mine_w.at[pl.ds(pl.multiple_of((1 - c) * share, share), share)], dw_out.at[c], csems, 1, core)
    dw_out[c] = mine_w[pl.ds(pl.multiple_of(c * share, share), share), :]
    gather.forward_pair()
    gather.forward(0)

    def keep_down(at, value):
        ddown_out[at, :] = value

    downs.finish(keep_down)

    def keep_out(at, value):
        dout_out[at, :] = value

    outs.finish(keep_out)
    gather.forward(1)
    lanes_out[...] = lanes_d.finish()
    sums_out[...] = all_d.finish()
    gather.arrive(0)
    gather.arrive(1)
    gather.settle()
    there.wait()
    swap.wait_send()


def tail_call(dw, part, gm, x, gain, ddown, dout, early, lane):
    rows, width = x.shape
    wr, wc = dw.shape[1:]
    return remote_call(
        tail_kernel, "tail", 6,
        (struct((2, wr // 2, wc), BF), struct((8, rows, width), BF), struct(ddown.shape[2:], F32), struct(dout.shape[2:], F32),
         struct((16, width), F32), struct(lane.shape, F32)),
        [VM] * 9,
        [pltpu.VMEM((8, rows, width), BF), pltpu.VMEM((8, rows, width), BF), pltpu.VMEM((rows, width), F32), pltpu.VMEM((wr, wc), BF),
         DMA((2,)), DMA((2,)), DMA((9,)), DMA((9,))] + Scatter.scratch(wr, wc) + Scatter.scratch(rows, width)
        + CoreScatter.scratch(*ddown.shape[2:]) + CoreScatter.scratch(*dout.shape[2:])
        + Sums.scratch(8, *early.shape) + Sums.scratch(16, *lane.shape) + Sums.scratch(8, 8, width) + Sums.scratch(16, 16, width),
        dw, part, gm, x, gain, ddown, dout, early, lane)


def on_device(tokens, first_gain, first_shift, query_weight, query_bias, key_weight, value_weight, value_bias,
              out_weight, out_bias, second_gain, second_shift, up_weight, up_bias, down_weight, down_bias,
              cotangent, prefix, block_order):
    own, width = tokens.shape
    d, t = lax.axis_index("dp"), lax.axis_index("tensor")
    c = lax.rem(d, 2)
    nblk = block_order.shape[0]
    rows = own // 8
    meta = jnp.concatenate([block_order % nblk, prefix])
    lanes = jnp.pad(block_order % nblk, (0, HEAD - nblk), constant_values=-1).reshape(1, HEAD)
    row = lambda v: v.reshape(1, -1)

    w_all, n_all, q, kv, o, lse, out_all, up_all, down_all, n2, mid, mixed = forward_call(
        meta, lanes, tokens, row(first_gain), row(first_shift), query_weight, key_weight, value_weight, row(query_bias), row(value_bias),
        out_weight, up_weight, down_weight, row(out_bias), row(second_gain), row(second_shift))
    n_all = n_all.reshape(2 * own, width)
    here = lambda v: lax.dynamic_slice_in_dim(v, t * rows, rows)
    x_rows, g_rows = here(tokens), here(cotangent)
    n2 = n2.reshape(own, width)
    pre = dg(n2, up_all, NN) + up_bias
    half_erf = 0.5 + 0.5 * lax.erf(pre * math.sqrt(0.5))
    hidden = (pre * half_erf).astype(BF)
    slope = half_erf + pre * jnp.exp(-0.5 * pre * pre) * (1.0 / math.sqrt(2.0 * math.pi))
    grad_pre = (dg(cotangent, down_all, NN) * slope).astype(BF)
    gn2 = dg(grad_pre, up_all, NT).astype(BF).reshape(8, rows, width)
    out_part = dg(hidden, down_all, NT).astype(BF).reshape(8, rows, width)
    do, gm, sums, low = back_call(gn2, mid, g_rows, out_all, row(second_gain))
    hid = up_weight.shape[1]
    dw_up = dg(n2, grad_pre, TN).astype(BF).reshape(8, 2, width // 16, hid)
    dw_down = dg(cotangent, hidden, TN).astype(BF).reshape(8, 2, width // 16, hid)
    dq, dkv, layer, gb, up_grad = attend_back_call(meta, lanes, q, kv, o, do, lse, out_part, low, mid, row(down_bias), dw_up)
    dw_out = dg(gb.reshape(own, width), mixed, TN).astype(BF).reshape(8, 2, width // 16, 2 * HEAD)

    dqkv = jnp.concatenate([dq, dkv], axis=1)
    dw = dg(n_all, dqkv, TN).astype(BF).reshape(8, width // 8, 3 * HEAD)
    gn1 = dg(dqkv, w_all, NT).astype(BF).reshape(2, 8, rows, width)
    col = jnp.sum(dqkv.astype(F32), axis=0)
    zero = jnp.zeros((HEAD,), F32)
    two = lambda v: jnp.concatenate([jnp.where(c == 0, v, zero), jnp.where(c == 1, v, zero)])
    lane = jnp.concatenate([jnp.sum(grad_pre.astype(F32), axis=0), two(col[:HEAD]), two(col[2 * HEAD:])])
    lane = jnp.pad(lane.reshape(1, -1), ((0, 7), (0, 0)))
    dw_mine, tg, down_grad, out_grad, small, lane = tail_call(
        dw, gn1, gm, x_rows, row(first_gain), dw_down, dw_out, sums, lane)
    pieces = [
        jnp.concatenate([dw_mine[0, :, i * HEAD:(i + 1) * HEAD], dw_mine[1, :, i * HEAD:(i + 1) * HEAD]], axis=1).astype(F32)
        for i in range(3)]
    return (
        layer.reshape(own, width),
        tg.reshape(own, width).astype(F32),
        small[0], small[1],
        pieces[0], lane[0, hid:hid + 2 * HEAD], pieces[1], pieces[2], lane[0, hid + 2 * HEAD:],
        out_grad.T, small[10],
        small[8], small[9],
        up_grad, lane[0, :hid],
        down_grad.T, small[11],
    )


def solution(mesh):
    rows, cols = P("dp", "tensor"), P("tensor", "dp")
    return jax.shard_map(
        on_device,
        mesh=mesh,
        in_specs=(
            P("dp", None), P(), P(), rows, P("tensor"), rows, rows, P("tensor"), cols, P(), P(), P(), rows, P("tensor"),
            cols, P(), P("dp", None), P(), P()),
        out_specs=(
            P("dp", None), P("dp", None), P(), P(), rows, P("tensor"), rows, rows, P("tensor"), cols, P(), P(), P(), rows,
            P("tensor"), cols, P()),
        check_vma=False,
    )
```

```python
import functools
import math

import jax
import jax.numpy as jnp
from jax import lax
from jax.experimental import pallas as pl
from jax.experimental.pallas import tpu as pltpu
from jax.sharding import PartitionSpec as P

HEAD = 128
BLK = 256
GRP = 4
RING = 4
EPS = 1e-05
NEG = -(2.0 ** 100)
LOG2E = math.log2(math.e)
SCALE = 1.0 / math.sqrt(HEAD)
C1 = LOG2E * SCALE
NN = (((1,), (0,)), ((), ()))
NT = (((1,), (1,)), ((), ()))
TN = (((0,), (0,)), ((), ()))
MESH = pl.DeviceIdType.MESH
VM = pl.BlockSpec(memory_space=pltpu.VMEM)
SM = pl.BlockSpec(memory_space=pltpu.SMEM)
BF = jnp.bfloat16
F32 = jnp.float32
DMA = pltpu.SemaphoreType.DMA


def dg(a, b, dims):
    return lax.dot_general(a, b, dims, preferred_element_type=F32)


def struct(shape, dtype):
    return jax.ShapeDtypeStruct(shape, dtype)


class Eight:
    def __init__(self, axis):
        d, t = lax.axis_index("dp"), lax.axis_index("tensor")
        self.axis, self.d, self.t = axis, d, t
        if axis == "dp":
            self.r, self.p = d // 4, lax.rem(d // 2, 2)
        else:
            self.r, self.p = lax.rem(t, 4), t // 4

    def ring(self, i):
        return lax.rem(self.r + i, RING)

    def side(self, s):
        return 1 - self.p if s else self.p

    def index(self, r, p):
        return r * 2 + p if self.axis == "dp" else p * 4 + r

    def device(self, r, p):
        if self.axis == "dp":
            return ((r * 2 + p) * 2 + lax.rem(self.d, 2), self.t)
        return (self.d, p * 4 + r)

    def others(self):
        return [self.device(self.ring(i), self.p) for i in (1, 3)] + [self.device(self.r, 1 - self.p)]


def other_core():
    d = lax.axis_index("dp")
    return (d + 1 - 2 * lax.rem(d, 2), lax.axis_index("tensor"))


def greet(devices):
    barrier = pltpu.get_barrier_semaphore()
    for device in devices:
        pl.semaphore_signal(barrier, inc=1, device_id=device, device_id_type=MESH)
    pl.semaphore_wait(barrier, len(devices))


def send(src, dst, sems, k, device):
    copy = pltpu.make_async_remote_copy(
        src_ref=src, dst_ref=dst, send_sem=sems[0].at[k], recv_sem=sems[1].at[k],
        device_id=device, device_id_type=MESH)
    copy.start()
    return copy


def copy_of(src, dst, sems, k, device):
    return pltpu.make_async_remote_copy(
        src_ref=src, dst_ref=dst, send_sem=sems[0].at[k], recv_sem=sems[1].at[k],
        device_id=device, device_id_type=MESH)


def send(src, dst, sems, k, device):
    copy = copy_of(src, dst, sems, k, device)
    copy.start()
    return copy


class Gather:
    @staticmethod
    def scratch(twin=False):
        return [DMA((9,)), DMA((9,))] + ([DMA((8,)), DMA((8,))] if twin else [])

    def __init__(self, group, place, rows, sems, twin=None, twin_own=True):
        self.g, self.place, self.sems = group, place, sems[:2]
        self.twin, self.twin_sems, self.twin_own = twin, sems[2:4], twin_own
        self.halves = (pl.ds(0, rows // 2), pl.ds(rows // 2, rows // 2))

    def at(self, i, s):
        g = self.g
        return self.place(g.index(g.ring(i), g.side(s)))

    def to(self, i):
        g = self.g
        return g.device(g.ring(i), g.p)

    def pair(self):
        own = self.at(0, 0)
        return copy_of(own, own, self.sems, 0, self.g.device(self.g.r, 1 - self.g.p))

    def near(self, s, way):
        chunk = self.at(0, s)
        return copy_of(chunk, chunk, self.sems, 1 + 4 * s + way, self.to(1 + 2 * way))

    def relay(self, s, way):
        half = self.at(3 - 2 * way, s).at[self.halves[way]]
        return copy_of(half, half, self.sems, 3 + 4 * s + way, self.to(1 + 2 * way))

    def over(self, k, i, s):
        chunk = self.at(i, s)
        return copy_of(chunk, chunk, self.twin_sems, k, self.twin)

    def tell(self, i, s):
        if self.twin is not None and (i or s or self.twin_own):
            self.over(2 * i + s, i, s).start()

    def start(self):
        self.pair().start()
        for way in (0, 1):
            self.near(0, way).start()
        self.tell(0, 0)

    def forward_pair(self):
        self.pair().wait_recv()
        for way in (0, 1):
            self.near(1, way).start()
        self.tell(0, 1)

    def forward(self, s):
        for way in (0, 1):
            self.near(s, way).wait_recv()
            self.relay(s, way).start()
            self.tell(3 - 2 * way, s)

    def arrive(self, s):
        for way in (0, 1):
            self.relay(s, way).wait_recv()
        self.tell(2, s)

    def settle(self):
        self.pair().wait_send()
        for s in (0, 1):
            for way in (0, 1):
                self.near(s, way).wait_send()
                self.relay(s, way).wait_send()
        if self.twin is not None:
            for k in range(0 if self.twin_own else 1, 8):
                self.over(k, 0, 0).wait()

    def rest(self):
        self.forward_pair()
        self.forward(0)
        self.forward(1)
        self.arrive(0)
        self.arrive(1)
        self.settle()


class Scatter:
    COUNT = 6

    @staticmethod
    def scratch(rows, width):
        half = rows // 2
        return [
            pltpu.VMEM((2, 2, half, width), BF), pltpu.VMEM((2, 2, rows, width), BF),
            pltpu.VMEM((rows, width), BF), pltpu.VMEM((rows, width), BF), DMA((13,)), DMA((13,))]

    def __init__(self, group, part, rows, scratch, step):
        self.g, self.part, self.step, self.rows = group, part, step, rows
        self.mid, self.last, self.sum, self.end = scratch[:4]
        self.sems = scratch[4:6]
        self.half = rows // 2
        self.halves = (pl.ds(0, self.half), pl.ds(self.half, self.half))

    def at(self, i, s):
        g = self.g
        return self.part(g.index(g.ring(i), g.side(s)))

    def to(self, way):
        g = self.g
        return g.device(g.ring(1 + 2 * way), g.p)

    def far(self, s, way):
        return copy_of(self.at(2, s).at[self.halves[way]], self.mid.at[s, way], self.sems, 2 * s + way, self.to(way))

    def own(self, s, way):
        half = self.halves[1 - way]
        return copy_of(self.at(1 + 2 * way, s).at[half], self.last.at[s, way, half], self.sems, 4 + 2 * s + way, self.to(way))

    def both(self, s, way):
        return copy_of(self.mid.at[s, way], self.last.at[s, way, self.halves[way]], self.sems, 8 + 2 * s + way, self.to(way))

    def pair(self):
        return copy_of(self.sum, self.end, self.sems, 12, self.g.device(self.g.r, 1 - self.g.p))

    def by_rows(self, rows, body):
        step = min(self.step, rows)

        @pl.loop(0, rows // step)
        def _(n):
            body(pl.multiple_of(n * step, step), step)

    def send_far(self, s):
        for way in (0, 1):
            self.far(s, way).start()

    def send_near(self, s):
        for way in (0, 1):
            self.own(s, way).start()

    def add_near(self, s):
        for way in (0, 1):
            self.far(s, way).wait_recv()
            mine = self.at(1 + 2 * way, s)
            base = way * self.half

            def add(at, n, way=way, mine=mine, base=base):
                rows = pl.ds(at, n)
                total = mine[pl.ds(base + at, n), :].astype(F32) + self.mid[s, way, rows, :].astype(F32)
                self.mid[s, way, rows, :] = total.astype(BF)

            self.by_rows(self.half, add)
            self.both(s, way).start()

    def arrived(self, s):
        for way in (0, 1):
            self.own(s, way).wait_recv()
            self.both(s, way).wait_recv()

    def add_pair(self):
        self.arrived(1)
        mine = self.at(0, 1)

        def add(at, n):
            rows = pl.ds(at, n)
            total = mine[rows, :].astype(F32) + self.last[1, 0, rows, :].astype(F32) + self.last[1, 1, rows, :].astype(F32)
            self.sum[rows, :] = total.astype(BF)

        self.by_rows(self.rows, add)
        self.pair().start()

    def start(self):
        for s in (1, 0):
            self.send_far(s)
            self.send_near(s)

    def forward(self):
        self.add_near(1)
        self.add_near(0)
        self.add_pair()

    def finish(self, store):
        self.arrived(0)
        self.pair().wait_recv()
        mine = self.at(0, 0)

        def add(at, n):
            rows = pl.ds(at, n)
            total = mine[rows, :].astype(F32) + self.last[0, 0, rows, :].astype(F32) + self.last[0, 1, rows, :].astype(F32)
            store(rows, total + self.end[rows, :].astype(F32))

        self.by_rows(self.rows, add)
        self.pair().wait_send()
        for s in (0, 1):
            for way in (0, 1):
                self.far(s, way).wait_send()
                self.own(s, way).wait_send()
                self.both(s, way).wait_send()


class CoreScatter:
    COUNT = 9

    @staticmethod
    def scratch(rows, width):
        return [pltpu.VMEM((8, rows, width), BF), DMA((8,)), DMA((8,))] + Scatter.scratch(rows, width)

    def __init__(self, group, part, rows, scratch, step):
        self.part, self.total, self.sems = part, scratch[0], scratch[1:3]
        self.c = lax.rem(group.d, 2)
        self.rows, self.step = rows, step
        self.inner = Scatter(group, lambda m: self.total.at[m], rows, scratch[3:], step)

    def swap(self, m):
        return copy_of(self.part(m, 1 - self.c), self.total.at[m], self.sems, m, other_core())

    def start(self):
        for m in range(8):
            self.swap(m).start()

    def add(self):
        step = self.step

        @pl.loop(0, 8)
        def _(m):
            self.swap(m).wait_recv()
            mine = self.part(m, self.c)

            @pl.loop(0, self.rows // step)
            def _(n):
                at = pl.ds(pl.multiple_of(n * step, step), step)
                self.total[m, at, :] = (mine[at, :].astype(F32) + self.total[m, at, :].astype(F32)).astype(BF)

        self.inner.start()

    def finish(self, store):
        self.inner.finish(store)
        for m in range(8):
            self.swap(m).wait_send()


class RowSums:
    @staticmethod
    def scratch(width):
        cols = width // 8
        return [pltpu.VMEM((8, 8, cols), F32), pltpu.VMEM((16, 8, cols), F32)] + [DMA((7,)), DMA((7,)), DMA((15,)), DMA((15,)), DMA((7,)), DMA((7,))]

    def __init__(self, rows, out, scratch):
        self.rows, self.out = rows, out
        self.one, self.two = scratch[:2]
        self.sems = (scratch[2:4], scratch[4:6], scratch[6:8])
        self.d, self.t = lax.axis_index("dp"), lax.axis_index("tensor")
        self.cols = rows.shape[1] // 8

    def columns(self, t):
        return pl.ds(pl.multiple_of(t * self.cols, self.cols), self.cols)

    def first(self, k):
        other = lax.rem(self.t + k, 8)
        return copy_of(self.rows.at[:, self.columns(other)], self.one.at[self.t], self.sems[0], k - 1, (self.d, other))

    def second(self, k):
        own = self.two.at[self.d]
        return copy_of(own, own, self.sems[1], k - 1, (lax.rem(self.d + k, 16), self.t))

    def third(self, k):
        own = self.out.at[:, self.columns(self.t)]
        return copy_of(own, own, self.sems[2], k - 1, (self.d, lax.rem(self.t + k, 8)))

    def run(self, step, last):
        @pl.loop(1, last)
        def _(k):
            step(k)

    def start(self):
        self.run(lambda k: self.first(k).start(), 8)
        self.one[self.t] = self.rows[:, self.columns(self.t)]

    def middle(self):
        self.run(lambda k: self.first(k).wait(), 8)
        total = self.one[0]
        for k in range(1, 8):
            total = total + self.one[k]
        self.two[self.d] = total
        self.run(lambda k: self.second(k).start(), 16)

    def finish(self):
        self.run(lambda k: self.second(k).wait(), 16)
        total = self.two[0]
        for k in range(1, 16):
            total = total + self.two[k]
        self.out[:, self.columns(self.t)] = total
        self.run(lambda k: self.third(k).start(), 8)

    def settle(self):
        self.run(lambda k: self.third(k).wait(), 8)


class Sums:
    @staticmethod
    def scratch(rows, width):
        return [pltpu.VMEM((16, rows, width), F32), DMA((15,)), DMA((15,))]

    def __init__(self, scratch):
        self.slots, self.sems = scratch[0], scratch[1:3]
        self.d, self.t = lax.axis_index("dp"), lax.axis_index("tensor")

    def copy(self, k):
        own = self.slots.at[self.d]
        return copy_of(own, own, self.sems, k - 1, (lax.rem(self.d + k, 16), self.t))

    def start(self):
        @pl.loop(1, 16)
        def _(k):
            self.copy(k).start()

    def finish(self):
        @pl.loop(1, 16)
        def _(k):
            self.copy(k).wait()
        total = self.slots[0]
        for k in range(1, 16):
            total = total + self.slots[k]
        return total


def remote_call(kernel, name, cid, outs, ins, scratch, *args, out_specs=None):
    return pl.pallas_call(
        kernel, out_shape=outs, in_specs=ins,
        out_specs=jax.tree.map(lambda _: VM, outs) if out_specs is None else out_specs,
        scratch_shapes=scratch, name=name,
        compiler_params=pltpu.CompilerParams(collective_id=cid, has_side_effects=True, vmem_limit_bytes=58 << 20),
    )(*args)


def chip_members():
    d, t = lax.axis_index("dp"), lax.axis_index("tensor")
    c = lax.rem(d, 2)
    out = []
    for dt in range(8):
        for dc in range(2):
            if dt or dc:
                tt = lax.rem(t + dt, 8)
                cc = lax.rem(c + dc, 2)
                out.append((tt, cc, (d - c + cc, tt)))
    return out


def norm_rows(values):
    average = jnp.mean(values, axis=-1, keepdims=True)
    centred = values - average
    variance = jnp.mean(centred * centred, axis=-1, keepdims=True)
    inverse = lax.rsqrt(variance + EPS)
    return centred * inverse, inverse


def norm_back(grad, scaled, inverse, gain):
    e = grad * gain
    first = jnp.mean(e, axis=-1, keepdims=True)
    second = jnp.mean(e * scaled, axis=-1, keepdims=True)
    return inverse * (e - first - scaled * second)


def augment(meta, lanes_ref, q_ref, qa_ref, kx_ref):
    rows = q_ref.shape[0]
    nblk = kx_ref.shape[0] // BLK
    prefix = meta[nblk]
    for a in range(rows // BLK):
        at = slice(a * BLK, (a + 1) * BLK)
        hidden = jnp.where(lanes_ref[...] > meta[first_block() + a], NEG, 0.0)
        qa_ref[at, :HEAD] = q_ref[at, :]
        qa_ref[at, HEAD:] = jnp.broadcast_to(hidden, (BLK, HEAD)).astype(BF)
    lane = lax.broadcasted_iota(jnp.int32, (BLK, HEAD), 1)
    inside = lax.broadcasted_iota(jnp.int32, (BLK, HEAD), 0)

    @pl.loop(0, nblk)
    def _(b):
        late = (lane == b) & (inside >= prefix - meta[b] * BLK)
        kx_ref[pl.ds(pl.multiple_of(b * BLK, BLK), BLK), :] = jnp.where(late, 1.0, 0.0).astype(BF)


def first_block():
    return lax.axis_index("dp") // 2 * 4


def forward_kernel(meta, lanes_ref, x_ref, gain1_ref, shift1_ref, wq_ref, wk_ref, wv_ref, qb_ref, vb_ref, wo_ref, wu_ref, wd_ref,
                   bias_ref, gain2_ref, shift2_ref,
                   w_hbm, n_hbm, q_out, kv_hbm, o_ref, lse_ref, out_hbm, up_hbm, down_hbm, n2_out, mid_out, own_out,
                   w_vm, n_vm, kv_vm, out_vm, up_vm, down_vm, wsh, qa_ref, kx_ref, m_ref, acc_ref, mixed,
                   lsem, css, crs, ass, ars, *sems):
    gd, gt = Eight("dp"), Eight("tensor")
    t = gt.t
    c = lax.rem(gd.d, 2)
    core = other_core()
    members = chip_members()
    me = gd.index(gd.r, gd.p)
    own = x_ref.shape[0]
    rows = 2 * own
    nblk = kx_ref.shape[0] // BLK
    per = rows // BLK
    shard = wq_ref.shape[0]
    half = out_vm.shape[1] // 2
    hid = wd_ref.shape[0]
    small = mid_out.shape[0]
    csem, asem = (css, crs), (ass, ars)
    for h in range(2):
        cols = slice(h * HEAD, (h + 1) * HEAD)
        for i, ref in enumerate((wq_ref, wk_ref, wv_ref)):
            wsh[h, :, i * HEAD:(i + 1) * HEAD] = ref[:, cols].astype(BF)
    greet([m[2] for m in members] + gd.others())

    w_place = lambda m: w_vm.at[pl.ds(pl.multiple_of(m * 2 * shard, 2 * shard), 2 * shard)]
    row_of = lambda m: pl.ds(pl.multiple_of((m * 2 + c) * shard, shard), shard)
    mine = row_of(me)
    swap = send(wsh.at[1 - c], w_vm.at[mine], csem, 0, core)
    w_vm[mine, :] = wsh[c]
    qkv = Gather(gd, w_place, 2 * shard, sems[0:2])
    keys = Gather(gd, lambda m: kv_vm.at[m], rows, sems[2:4])
    outs = Gather(gd, lambda m: out_vm.at[t, :, row_of(m)], 2 * half, sems[4:8], core)
    ups = Gather(gd, lambda m: up_vm.at[row_of(m)], shard, sems[8:12], core)
    downs = Gather(gd, lambda m: down_vm.at[:, row_of(m)], hid, sems[12:16], core)
    wide = Gather(gt, lambda m: out_vm.at[m, pl.ds(pl.multiple_of(c * half, half), half)], half, sems[16:20], core, twin_own=False)
    normed = Gather(gt, lambda m: n2_out.at[m], small, sems[20:22])
    swap.wait_recv()
    qkv.start()
    out_vm[t, :, mine] = wo_ref[...].astype(BF)
    outs.start()

    def norm_part(k):
        step = 32

        @pl.loop(0, own // 2 // step)
        def _(n):
            at = pl.ds(pl.multiple_of(k * (own // 2) + n * step, step), step)
            scaled, _ = norm_rows(x_ref[at, :].astype(F32))
            n_vm[c, at, :] = (scaled * gain1_ref[...] + shift1_ref[...]).astype(BF)

        at = pl.ds(k * (own // 2), own // 2)
        return send(n_vm.at[c, at], n_vm.at[c, at], csem, 1 + k, core)

    there = [norm_part(0)]
    outs.forward_pair()
    outs.forward(0)
    qkv.forward_pair()
    qkv.forward(0)
    there.append(norm_part(1))
    outs.forward(1)
    outs.arrive(0)
    qkv.forward(1)
    up_vm[mine, :] = wu_ref[...].astype(BF)
    outs.arrive(1)
    down_vm[:, mine] = wd_ref[...].astype(BF)
    outs.settle()
    wide.start()
    qkv.arrive(0)
    qkv.arrive(1)
    for copy in there:
        copy.wait_recv()
    local = pl.ds(pl.multiple_of(c * HEAD, HEAD), HEAD)
    bias_q, bias_v = qb_ref[:, local], vb_ref[:, local]

    @pl.loop(0, per)
    def _(b):
        at = pl.ds(pl.multiple_of(b * BLK, BLK), BLK)
        piece = dg(n_vm[b // 2, pl.ds(pl.multiple_of(lax.rem(b, 2) * BLK, BLK), BLK), :], w_vm[...], NN)
        q_out[at, :] = (piece[:, :HEAD] + bias_q).astype(BF)
        kv_vm[me, at, :HEAD] = piece[:, HEAD:2 * HEAD].astype(BF)
        kv_vm[me, at, HEAD:] = (piece[:, 2 * HEAD:] + bias_v).astype(BF)

    keys.start()
    saves = [pltpu.make_async_copy(w_vm, w_hbm, lsem.at[0]), pltpu.make_async_copy(n_vm, n_hbm, lsem.at[1])]
    for save in saves:
        save.start()
    augment(meta, lanes_ref, q_out, qa_ref, kx_ref)
    m_ref[...] = jnp.full_like(m_ref, -1e30)
    acc_ref[...] = jnp.zeros_like(acc_ref)
    ones = jnp.ones((BLK, HEAD), BF)
    prefix = meta[nblk]

    def attend(chunk, diagonal):
        @pl.loop(0, per)
        def _(a):
            take = pl.ds(pl.multiple_of(a * BLK, BLK), BLK)
            q = qa_ref[take, :]
            ss, vs = [], []
            for i in range(per):
                at = pl.ds(pl.multiple_of(chunk * rows + i * BLK, BLK), BLK)
                ss.append(dg(q, jnp.concatenate([kv_vm[chunk, i * BLK:(i + 1) * BLK, :HEAD], kx_ref[at, :]], axis=1), NT))
                vs.append(jnp.concatenate([kv_vm[chunk, i * BLK:(i + 1) * BLK, HEAD:], ones], axis=1))
            if diagonal:
                edge = prefix - 1 - meta[first_block() + a] * BLK
                lim = jnp.maximum(lax.broadcasted_iota(jnp.int32, (BLK, BLK), 0), edge)
                key = lax.broadcasted_iota(jnp.int32, (BLK, BLK), 1)
                for i in range(per):
                    ss[i] = jnp.where(key <= jnp.where(a == i, lim, BLK), ss[i], NEG)
            top = ss[0]
            for s in ss[1:]:
                top = jnp.maximum(top, s)
            old = m_ref[take, :1]
            new = jnp.maximum(old, jnp.max(top, axis=1, keepdims=True) * C1)
            alpha = jnp.exp2(old - new)
            add = None
            for s, v in zip(ss, vs):
                term = jnp.dot(jnp.exp2(s * C1 - new).astype(BF), v, preferred_element_type=F32)
                add = term if add is None else add + term
            acc_ref[take, :] = acc_ref[take, :] * alpha + add
            m_ref[take, :] = jnp.broadcast_to(new, (BLK, HEAD))

    attend(me, True)

    @pl.loop(1, 8)
    def _(k):
        kk = lax.rem(k, 4)
        i, s = kk + kk // 2 - 2 * (kk // 3), k // 4

        @pl.when(k == 1)
        def _():
            keys.forward_pair()
            keys.forward(0)

        @pl.when(k == 2)
        def _():
            wide.forward_pair()
            wide.forward(0)

        @pl.when(k == 3)
        def _():
            keys.arrive(0)

        @pl.when(k == 5)
        def _():
            keys.forward(1)
            wide.forward(1)
            ups.start()

        @pl.when(k == 7)
        def _():
            keys.arrive(1)

        attend(gd.index(gd.ring(i), gd.p + s * (1 - 2 * gd.p)), False)

    for a in range(per):
        at = slice(a * BLK, (a + 1) * BLK)
        total = acc_ref[at, HEAD:]
        o_ref[at, :] = (acc_ref[at, :HEAD] / total).astype(BF)
        lse_ref[a:a + 1, :] = jnp.transpose(m_ref[at, :] + jnp.log2(total))[:1, :]
    head = pl.ds(pl.multiple_of((2 * t + c) * HEAD, HEAD), HEAD)
    copies = []
    for k, (tt, cc, device) in enumerate(members):
        take = pl.ds(pl.multiple_of(cc * own + tt * small, small), small)
        copies.append(send(o_ref.at[take], mixed.at[:, head], asem, k, device))
    copies.append(send(o_ref.at[pl.ds(pl.multiple_of((1 - c) * own, own), own)], own_out.at[:, local], asem, 15, core))
    keys.settle()
    save = pltpu.make_async_copy(kv_vm, kv_hbm, lsem.at[2])
    save.start()
    saves.append(save)
    downs.start()
    mixed[:, head] = o_ref[pl.ds(pl.multiple_of(c * own + t * small, small), small), :]
    own_out[:, local] = o_ref[pl.ds(pl.multiple_of(c * own, own), own), :]
    ups.forward_pair()
    ups.forward(0)
    wide.arrive(0)
    wide.arrive(1)
    wide.settle()
    save = pltpu.make_async_copy(out_vm, out_hbm, lsem.at[3])
    save.start()
    saves.append(save)
    for copy in copies:
        copy.wait_recv()
    span = 512
    x_rows = pl.ds(pl.multiple_of(t * small, small), small)
    for n in range(mid_out.shape[1] // span):
        cols = pl.ds(n * span, span)
        total = None
        for k in range(8):
            term = dg(mixed[:, k * 256:(k + 1) * 256], out_vm[k, :, cols], NN)
            total = term if total is None else total + term
        mid_out[:, cols] = total + (x_ref[x_rows, cols].astype(F32) + bias_ref[:, cols])
    scaled, _ = norm_rows(mid_out[...])
    n2_out[t] = (scaled * gain2_ref[...] + shift2_ref[...]).astype(BF)
    normed.start()
    ups.forward(1)
    downs.forward_pair()
    downs.forward(0)
    normed.forward_pair()
    normed.forward(0)
    ups.arrive(0)
    ups.arrive(1)
    ups.settle()
    save = pltpu.make_async_copy(up_vm, up_hbm, lsem.at[4])
    save.start()
    saves.append(save)
    normed.forward(1)
    downs.forward(1)
    downs.arrive(0)
    downs.arrive(1)
    downs.settle()
    save = pltpu.make_async_copy(down_vm, down_hbm, lsem.at[5])
    save.start()
    saves.append(save)
    normed.arrive(0)
    normed.arrive(1)
    normed.settle()
    qkv.settle()
    swap.wait_send()
    for copy in there + copies:
        copy.wait_send()
    for save in saves:
        save.wait()


def forward_call(meta, lanes, x, gain1, shift1, wq, wk, wv, qb, vb, wo, wu, wd, bias, gain2, shift2):
    own, width = x.shape
    rows, shard, hid, small = 2 * own, wq.shape[0], wu.shape[1], own // 8
    hbm = pl.BlockSpec(memory_space=pl.ANY)
    big = [(width, 3 * HEAD), (2, own, width), (8, rows, 2 * HEAD), (8, 2 * HEAD, width), (width, hid), (hid, width)]
    w, n, kv, out, up, down = (struct(s, BF) for s in big)
    outs = (w, n, struct((rows, HEAD), BF), kv, struct((rows, HEAD), BF), struct((rows // BLK, BLK), F32), out, up, down,
            struct((8, small, width), BF), struct((small, width), F32), struct((own, 2 * HEAD), BF))
    return remote_call(
        forward_kernel, "forward", 1, outs, [SM] + [VM] * 15,
        [pltpu.VMEM(s, BF) for s in big]
        + [pltpu.VMEM((2, shard, 3 * HEAD), BF), pltpu.VMEM((rows, 2 * HEAD), BF), pltpu.VMEM((8 * rows, HEAD), BF),
           pltpu.VMEM((rows, HEAD), F32), pltpu.VMEM((rows, 2 * HEAD), F32), pltpu.VMEM((small, width), BF),
           DMA((6,)), DMA((3,)), DMA((3,)), DMA((16,)), DMA((16,))]
        + Gather.scratch() * 2 + Gather.scratch(True) * 4 + Gather.scratch(),
        meta, lanes, x, gain1, shift1, wq, wk, wv, qb, vb, wo, wu, wd, bias, gain2, shift2,
        out_specs=(hbm, hbm, VM, hbm, VM, VM, hbm, hbm, hbm, VM, VM, VM))


def back_kernel(part_ref, mid_ref, g_hbm, w_hbm, gain_ref, dd_ref, do_out, gm_out, sums_out, low_out, dd_out,
                w_ref, g_ref, total, heads, lsem, asems, arecv, *scratch):
    g, gd = Eight("tensor"), Eight("dp")
    c = lax.rem(g.d, 2)
    members = chip_members()
    rows = g_ref.shape[0]
    loads = [pltpu.make_async_copy(w_hbm, w_ref, lsem.at[0]),
             pltpu.make_async_copy(g_hbm.at[pl.ds(pl.multiple_of(g.t * rows, rows), rows)], g_ref, lsem.at[1])]
    for load in loads:
        load.start()
    greet([m[2] for m in members] + gd.others())
    half = do_out.shape[0] // 2
    first = Scatter(g, lambda m: part_ref.at[m], rows, scratch, 32)
    first.start()
    share = dd_out.shape[1]
    downs = CoreScatter(
        gd, lambda m, cc: dd_ref.at[:, pl.ds(pl.multiple_of((m * 2 + cc) * share, share), share)], dd_out.shape[0], scratch[6:], 128)
    downs.start()
    first.add_near(1)
    first.add_near(0)
    first.add_pair()
    downs.add()

    def keep(at, value):
        total[at, :] = value

    first.finish(keep)
    scaled, inverse = norm_rows(mid_ref[...])
    grad = total[...]
    for load in loads:
        load.wait()
    gm = g_ref[...].astype(F32) + norm_back(grad, scaled, inverse, gain_ref[...])
    gm_out[...] = gm
    low = gm.astype(BF)
    low_out[...] = low
    for t in range(8):
        heads[:, t * 256:(t + 1) * 256] = dg(low, w_ref[t], NT).astype(BF)
    sems = (asems, arecv)
    take = pl.ds(pl.multiple_of(c * half + g.t * rows, rows), rows)
    copies = []
    for k, (tt, cc, device) in enumerate(members):
        cols = pl.ds(pl.multiple_of((2 * tt + cc) * HEAD, HEAD), HEAD)
        copies.append(send(heads.at[:, cols], do_out.at[take], sems, k, device))
    do_out[take, :] = heads[:, pl.ds(pl.multiple_of((2 * g.t + c) * HEAD, HEAD), HEAD)]
    downs.inner.add_near(1)
    downs.inner.add_near(0)
    sums_out[...] = jnp.zeros_like(sums_out)
    sums_out[0:1, :] = jnp.sum(grad * scaled, axis=0, keepdims=True)
    sums_out[1:2, :] = jnp.sum(grad, axis=0, keepdims=True)
    sums_out[2:3, :] = jnp.sum(low.astype(F32), axis=0, keepdims=True)
    sums_out[3:4, :] = jnp.sum(g_ref[...].astype(F32), axis=0, keepdims=True)
    downs.inner.add_pair()

    def keep_down(at, value):
        dd_out[at, :] = value

    downs.finish(keep_down)
    for copy in copies:
        copy.wait()


def back_call(part, mid, g, w, gain, dd):
    rows, width = mid.shape
    hbm = pl.BlockSpec(memory_space=pl.ANY)
    share = (dd.shape[0], dd.shape[1] // 16)
    return remote_call(
        back_kernel, "back", 4,
        (struct((16 * rows, HEAD), BF), struct((rows, width), F32), struct((8, width), F32), struct((rows, width), BF), struct(share, F32)),
        [VM, VM, hbm, hbm, VM, VM],
        [pltpu.VMEM(w.shape, BF), pltpu.VMEM((rows, width), BF), pltpu.VMEM((rows, width), F32), pltpu.VMEM((rows, width), BF),
         DMA((2,)), DMA((15,)), DMA((15,))] + Scatter.scratch(rows, width) + CoreScatter.scratch(*share),
        part, mid, g, w, gain, dd)


def rear_kernel(meta, lanes_ref, q_ref, kv_ref, o_ref, do_ref, lse_ref, opart_ref, gbr_ref, mid_ref, bias_ref, dup_ref,
                mixed_ref, n_hbm, w_ref, gm_ref, x_hbm, gain_ref, early_ref, lane_ref,
                lay_out, dup_out, dwo_out, dwq_out, dwk_out, dwv_out, tg_out, sums_out, lanes_out,
                qa_ref, kx_ref, part, delta_ref, dq_acc, gb, dqkv, dwo, n_buf, dw, away, arrived, summed, total, mine_w, there_w, vec, x_ref,
                lsem, css, crs, *scratch):
    g, gt = Eight("dp"), Eight("tensor")
    c = lax.rem(g.d, 2)
    core = other_core()
    me, mine_t = g.index(g.r, g.p), gt.index(gt.r, gt.p)
    rows = q_ref.shape[0]
    own = rows // 2
    nblk = kx_ref.shape[0] // BLK
    per = rows // BLK
    small, width = mid_ref.shape
    everyone = [(lax.rem(g.d + k, 16), g.t) for k in range(1, 16)] + [(g.d, lax.rem(g.t + k, 8)) for k in range(1, 8)]
    greet(everyone)
    take = list(scratch)

    def some(count):
        out = take[:count]
        del take[:count]
        return out

    share = dwo_out.shape[1]
    by_columns = lambda m, cc: dwo.at[:, pl.ds(pl.multiple_of((m * 2 + cc) * share, share), share)]
    keys = Scatter(g, lambda m: part.at[m], rows, some(6), 128)
    outs = Scatter(gt, lambda m: opart_ref.at[m], small, some(6), 32)
    ups = CoreScatter(g, lambda m, cc: dup_ref.at[m, cc], dup_out.shape[0], some(9), 32)
    dwos = CoreScatter(g, by_columns, dwo_out.shape[0], some(9), 128)
    tokens = Scatter(gt, lambda m: summed.at[m], small, some(6), 32)
    weights = Scatter(g, lambda m: dw.at[m], dw.shape[1], some(6), 128)
    wide = Gather(gt, lambda m: gb.at[pl.ds(pl.multiple_of(m * small, small), small)], small, some(2))
    layer = Gather(gt, lambda m: lay_out.at[m], small, some(2))
    final = Gather(gt, lambda m: tg_out.at[m], small, some(2))
    sums = RowSums(vec, sums_out, some(8))
    lane_sums = Sums(some(3))
    csem = (css, crs)
    x_load = pltpu.make_async_copy(x_hbm.at[pl.ds(pl.multiple_of(g.t * small, small), small)], x_ref, lsem.at[2])
    x_load.start()

    def n_load(m):
        slot = lax.rem(m, 2)
        return pltpu.make_async_copy(n_hbm.at[:, pl.ds(pl.multiple_of(m * BLK, BLK), BLK)], n_buf.at[slot], lsem.at[slot])

    ups.start()
    outs.start()
    gb[pl.ds(pl.multiple_of(mine_t * small, small), small), :] = gbr_ref[...]
    wide.start()
    augment(meta, lanes_ref, q_ref, qa_ref, kx_ref)
    for a in range(per):
        at = slice(a * BLK, (a + 1) * BLK)
        prod = do_ref[at, :].astype(F32) * o_ref[at, :].astype(F32)
        delta_ref[0:1, at] = jnp.sum(jnp.transpose(prod), axis=0, keepdims=True)
        delta_ref[1:2, at] = lse_ref[a:a + 1, :]
    dq_acc[...] = jnp.zeros_like(dq_acc)
    prefix = meta[nblk]

    def attend(chunk, diagonal):
        @pl.loop(0, per)
        def _(i):
            at_k = pl.ds(pl.multiple_of(i * BLK, BLK), BLK)
            at_x = pl.ds(pl.multiple_of(chunk * rows + i * BLK, BLK), BLK)
            k = kv_ref[chunk, at_k, :HEAD]
            v = kv_ref[chunk, at_k, HEAD:]
            kk = jnp.concatenate([k, kx_ref[at_x, :]], axis=1)
            dk = dv = None
            for a in range(per):
                at_q = slice(a * BLK, (a + 1) * BLK)
                q = q_ref[at_q, :]
                do = do_ref[at_q, :]
                p = jnp.exp2(dg(kk, qa_ref[at_q, :], NT) * C1 - delta_ref[1:2, at_q])
                if diagonal:
                    edge = prefix - 1 - meta[first_block() + a] * BLK
                    lim = jnp.maximum(lax.broadcasted_iota(jnp.int32, (BLK, BLK), 1), edge)
                    key = lax.broadcasted_iota(jnp.int32, (BLK, BLK), 0)
                    p = jnp.where(key <= jnp.where(i == a, lim, BLK), p, 0.0)
                ds = (p * (dg(v, do, NT) - delta_ref[0:1, at_q])).astype(BF)
                tv = jnp.dot(p.astype(BF), do, preferred_element_type=F32)
                tk = jnp.dot(ds, q, preferred_element_type=F32)
                dv = tv if dv is None else dv + tv
                dk = tk if dk is None else dk + tk
                dq_acc[at_q, :] += dg(ds, k, TN)
            part[chunk, at_k, :HEAD] = (dk * SCALE).astype(BF)
            part[chunk, at_k, HEAD:] = dv.astype(BF)

    @pl.loop(0, 7)
    def _(k):
        kk = lax.rem(k, 3)
        i = (2 - kk + 3 * (kk // 2)) * (1 - k // 6)
        s = 1 - k // 3 + 2 * (k // 6)
        attend(g.index(g.ring(i), g.p + s * (1 - 2 * g.p)), False)

        @pl.when(k == 0)
        def _():
            keys.send_far(1)
            ups.add()
            outs.add_near(1)
            wide.forward_pair()
            wide.forward(0)

        @pl.when(k == 1)
        def _():
            outs.add_near(0)

        @pl.when(k == 2)
        def _():
            keys.send_near(1)
            keys.add_near(1)
            outs.add_pair()
            wide.forward(1)

        @pl.when(k == 3)
        def _():
            keys.send_far(0)
            ups.inner.add_near(1)

        @pl.when(k == 4)
        def _():
            ups.inner.add_near(0)

        @pl.when(k == 5)
        def _():
            keys.send_near(0)
            keys.add_near(0)

        @pl.when(k == 6)
        def _():
            keys.add_pair()

    def lay(at, value):
        lay_out[mine_t, at, :] = (mid_ref[at, :] + (value + bias_ref[...])).astype(BF)

    outs.finish(lay)
    layer.start()
    ups.inner.add_pair()
    n_load(0).start()
    attend(me, True)
    dqkv[:, :HEAD] = (dq_acc[...] * SCALE).astype(BF)
    layer.forward_pair()
    layer.forward(0)
    wide.arrive(0)
    wide.arrive(1)
    wide.settle()
    span = 512
    for n in range(width // span):
        cols = pl.ds(n * span, span)
        dwo[:, cols] = dg(mixed_ref[...], gb[:, cols], TN).astype(BF)
    dwos.start()
    layer.forward(1)

    def keep_keys(at, value):
        dqkv[at, HEAD:] = value.astype(BF)

    keys.finish(keep_keys)

    def project(into, half):
        @pl.loop(0, own // BLK)
        def _(b):
            at = pl.ds(pl.multiple_of(half * own + b * BLK, BLK), BLK)
            for n in range(width // span):
                cols = pl.ds(n * span, span)
                piece = dg(dqkv[at, :], w_ref[cols, :], NT).astype(BF)
                for j in range(BLK // small):
                    into[b * (BLK // small) + j, :, cols] = piece[j * small:(j + 1) * small]

    project(away, 1 - c)
    swap = send(away, arrived, csem, 0, core)
    project(summed, c)
    swap.wait_recv()

    @pl.loop(0, 8)
    def _(m):
        @pl.loop(0, small // 32)
        def _(n):
            at = pl.ds(pl.multiple_of(n * 32, 32), 32)
            summed[m, at, :] = (summed[m, at, :].astype(F32) + arrived[m, at, :].astype(F32)).astype(BF)

    tokens.start()

    @pl.loop(0, 8)
    def _(m):
        @pl.when(m < 7)
        def _():
            n_load(m + 1).start()

        n_load(m).wait()
        dw[m] = dg(n_buf[lax.rem(m, 2)], dqkv[...], TN).astype(BF)

    weights.start()
    dwos.add()
    slot = lane_sums.slots
    slot[g.d] = lane_ref[...]
    local = pl.ds(pl.multiple_of(c * HEAD, HEAD), HEAD)
    slot[g.d, 4:5, local] = jnp.sum(dqkv[:, :HEAD].astype(F32), axis=0, keepdims=True)
    slot[g.d, 5:6, local] = jnp.sum(dqkv[:, 2 * HEAD:].astype(F32), axis=0, keepdims=True)
    lane_sums.start()
    tokens.add_near(1)
    tokens.add_near(0)
    tokens.add_pair()
    weights.add_near(1)
    weights.add_near(0)
    dwos.inner.add_near(1)
    dwos.inner.add_near(0)

    def keep(at, value):
        total[at, :] = value

    x_load.wait()
    tokens.finish(keep)
    scaled, inverse = norm_rows(x_ref[...].astype(F32))
    grad = total[...]
    tg = gm_ref[...] + norm_back(grad, scaled, inverse, gain_ref[...])
    tg_out[mine_t] = tg.astype(BF)
    final.start()
    vec[...] = early_ref[...]
    vec[4:5, :] = jnp.sum(grad * scaled, axis=0, keepdims=True)
    vec[5:6, :] = jnp.sum(grad, axis=0, keepdims=True)
    sums.start()
    weights.add_pair()
    dwos.inner.add_pair()

    def keep_up(at, value):
        dup_out[at, :] = value

    ups.finish(keep_up)
    sums.middle()

    def keep_w(at, value):
        mine_w[at, :] = value.astype(BF)

    weights.finish(keep_w)
    part_rows = there_w.shape[0]
    there = send(mine_w.at[pl.ds(pl.multiple_of((1 - c) * part_rows, part_rows), part_rows)], there_w, csem, 1, core)
    final.forward_pair()
    final.forward(0)
    kept = mine_w[pl.ds(pl.multiple_of(c * part_rows, part_rows), part_rows), :].astype(F32)
    sums.finish()
    far = pl.ds(pl.multiple_of((1 - c) * HEAD, HEAD), HEAD)
    there.wait()
    for i, ref in enumerate((dwq_out, dwk_out, dwv_out)):
        ref[:, local] = kept[:, i * HEAD:(i + 1) * HEAD]
        ref[:, far] = there_w[:, i * HEAD:(i + 1) * HEAD].astype(F32)
    final.forward(1)
    layer.arrive(0)
    layer.arrive(1)
    layer.settle()

    def keep_o(at, value):
        dwo_out[at, :] = value

    dwos.finish(keep_o)
    lanes_out[...] = lane_sums.finish()
    sums.settle()
    final.arrive(0)
    final.arrive(1)
    final.settle()
    swap.wait_send()


def rear_call(meta, lanes, q, kv, o, do, lse, opart, gb, mid, bias, dup, mixed, n, w, gm, x, gain, early, lane):
    rows = q.shape[0]
    small, width = mid.shape
    sr, sw = dup.shape[2:]
    hbm = pl.BlockSpec(memory_space=pl.ANY)
    chunks = (8, small, width)
    wc = 3 * HEAD
    share = width // 16
    head_grad = struct((share, 2 * HEAD), F32)
    return remote_call(
        rear_kernel, "rear", 5,
        (struct(chunks, BF), struct((sr, sw), F32), struct((2 * HEAD, share), F32), head_grad, head_grad, head_grad,
         struct(chunks, BF), struct((8, width), F32), struct(lane.shape, F32)),
        [SM] + [VM] * 12 + [hbm, VM, VM, hbm] + [VM] * 3,
        [pltpu.VMEM((rows, 2 * HEAD), BF), pltpu.VMEM((8 * rows, HEAD), BF), pltpu.VMEM(kv.shape, BF), pltpu.VMEM((8, rows), F32),
         pltpu.VMEM((rows, HEAD), F32), pltpu.VMEM((8 * small, width), BF), pltpu.VMEM((rows, wc), BF), pltpu.VMEM((2 * HEAD, width), BF),
         pltpu.VMEM((2, rows, BLK), BF), pltpu.VMEM((8, width // 8, wc), BF), pltpu.VMEM(chunks, BF), pltpu.VMEM(chunks, BF),
         pltpu.VMEM(chunks, BF), pltpu.VMEM((small, width), F32), pltpu.VMEM((width // 8, wc), BF), pltpu.VMEM((share, wc), BF),
         pltpu.VMEM((8, width), F32), pltpu.VMEM((small, width), BF), DMA((3,)), DMA((2,)), DMA((2,))]
        + Scatter.scratch(rows, 2 * HEAD) + Scatter.scratch(small, width) + CoreScatter.scratch(sr, sw)
        + CoreScatter.scratch(2 * HEAD, share) + Scatter.scratch(small, width) + Scatter.scratch(width // 8, wc)
        + Gather.scratch() * 3 + RowSums.scratch(width) + Sums.scratch(*lane.shape),
        meta, lanes, q, kv, o, do, lse, opart, gb, mid, bias, dup, mixed, n, w, gm, x, gain, early, lane)


def on_device(tokens, first_gain, first_shift, query_weight, query_bias, key_weight, value_weight, value_bias,
              out_weight, out_bias, second_gain, second_shift, up_weight, up_bias, down_weight, down_bias,
              cotangent, prefix, block_order):
    own, width = tokens.shape
    d, t = lax.axis_index("dp"), lax.axis_index("tensor")
    c = lax.rem(d, 2)
    nblk = block_order.shape[0]
    rows = own // 8
    meta = jnp.concatenate([block_order % nblk, prefix])
    lanes = jnp.pad(block_order % nblk, (0, HEAD - nblk), constant_values=-1).reshape(1, HEAD)
    row = lambda v: v.reshape(1, -1)

    w_all, n_all, q, kv, o, lse, out_all, up_all, down_all, n2, mid, mixed = forward_call(
        meta, lanes, tokens, row(first_gain), row(first_shift), query_weight, key_weight, value_weight, row(query_bias), row(value_bias),
        out_weight, up_weight, down_weight, row(out_bias), row(second_gain), row(second_shift))
    n_all = n_all.reshape(2 * own, width)
    n2 = n2.reshape(own, width)
    pre = dg(n2, up_all, NN) + up_bias
    half_erf = 0.5 + 0.5 * lax.erf(pre * math.sqrt(0.5))
    hidden = (pre * half_erf).astype(BF)
    slope = half_erf + pre * jnp.exp(-0.5 * pre * pre) * (1.0 / math.sqrt(2.0 * math.pi))
    grad_pre = (dg(cotangent, down_all, NT) * slope).astype(BF)
    gn2 = dg(grad_pre, up_all, NT).astype(BF).reshape(8, rows, width)
    out_part = dg(hidden, down_all, NN).astype(BF).reshape(8, rows, width)
    hid = up_weight.shape[1]
    dw_up = dg(n2, grad_pre, TN).astype(BF).reshape(8, 2, width // 16, hid)
    dw_down = dg(hidden, cotangent, TN).astype(BF)
    do, gm, sums, low, down_grad = back_call(gn2, mid, cotangent, out_all, row(second_gain), dw_down)
    lane = jnp.pad(jnp.sum(grad_pre.astype(F32), axis=0).reshape(hid // 256, 256), ((0, 8 - hid // 256), (0, 0)))
    layer, up_grad, out_grad, dwq, dwk, dwv, tg, small, lane = rear_call(
        meta, lanes, q, kv, o, do, lse, out_part, low, mid, row(down_bias), dw_up, mixed, n_all, w_all, gm, tokens, row(first_gain), sums, lane)
    return (
        layer.reshape(own, width),
        tg.reshape(own, width).astype(F32),
        small[4], small[5],
        dwq, lane[4], dwk, dwv, lane[5],
        out_grad, small[2],
        small[0], small[1],
        up_grad, lane[:hid // 256].reshape(hid),
        down_grad, small[3],
    )


def solution(mesh):
    rows, cols = P("dp", "tensor"), P("tensor", "dp")
    return jax.shard_map(
        on_device,
        mesh=mesh,
        in_specs=(
            P("dp", None), P(), P(), rows, P("tensor"), rows, rows, P("tensor"), cols, P(), P(), P(), rows, P("tensor"),
            cols, P(), P("dp", None), P(), P()),
        out_specs=(
            P("dp", None), P("dp", None), P(), P(), rows, P("tensor"), rows, rows, P("tensor"), cols, P(), P(), P(), rows,
            P("tensor"), cols, P()),
        check_vma=False,
    )
```

```python
import functools
import math

import jax
import jax.numpy as jnp
from jax import lax
from jax.experimental import pallas as pl
from jax.experimental.pallas import tpu as pltpu
from jax.sharding import PartitionSpec as P

HEAD = 128
BLK = 256
GRP = 4
RING = 4
EPS = 1e-05
NEG = -(2.0 ** 100)
LOG2E = math.log2(math.e)
SCALE = 1.0 / math.sqrt(HEAD)
C1 = LOG2E * SCALE
NN = (((1,), (0,)), ((), ()))
NT = (((1,), (1,)), ((), ()))
TN = (((0,), (0,)), ((), ()))
MESH = pl.DeviceIdType.MESH
VM = pl.BlockSpec(memory_space=pltpu.VMEM)
SM = pl.BlockSpec(memory_space=pltpu.SMEM)
BF = jnp.bfloat16
F32 = jnp.float32
DMA = pltpu.SemaphoreType.DMA


def dg(a, b, dims):
    return lax.dot_general(a, b, dims, preferred_element_type=F32)


def struct(shape, dtype):
    return jax.ShapeDtypeStruct(shape, dtype)


class Eight:
    def __init__(self, axis):
        d, t = lax.axis_index("dp"), lax.axis_index("tensor")
        self.axis, self.d, self.t = axis, d, t
        if axis == "dp":
            self.r, self.p = d // 4, lax.rem(d // 2, 2)
        else:
            self.r, self.p = lax.rem(t, 4), t // 4

    def ring(self, i):
        return lax.rem(self.r + i, RING)

    def side(self, s):
        return 1 - self.p if s else self.p

    def index(self, r, p):
        return r * 2 + p if self.axis == "dp" else p * 4 + r

    def device(self, r, p):
        if self.axis == "dp":
            return ((r * 2 + p) * 2 + lax.rem(self.d, 2), self.t)
        return (self.d, p * 4 + r)

    def others(self):
        return [self.device(self.ring(i), self.p) for i in (1, 3)] + [self.device(self.r, 1 - self.p)]


def other_core():
    d = lax.axis_index("dp")
    return (d + 1 - 2 * lax.rem(d, 2), lax.axis_index("tensor"))


def greet(devices):
    barrier = pltpu.get_barrier_semaphore()
    for device in devices:
        pl.semaphore_signal(barrier, inc=1, device_id=device, device_id_type=MESH)
    pl.semaphore_wait(barrier, len(devices))


def send(src, dst, sems, k, device):
    copy = pltpu.make_async_remote_copy(
        src_ref=src, dst_ref=dst, send_sem=sems[0].at[k], recv_sem=sems[1].at[k],
        device_id=device, device_id_type=MESH)
    copy.start()
    return copy


def copy_of(src, dst, sems, k, device):
    return pltpu.make_async_remote_copy(
        src_ref=src, dst_ref=dst, send_sem=sems[0].at[k], recv_sem=sems[1].at[k],
        device_id=device, device_id_type=MESH)


def send(src, dst, sems, k, device):
    copy = copy_of(src, dst, sems, k, device)
    copy.start()
    return copy


class Gather:
    @staticmethod
    def scratch(twin=False):
        return [DMA((9,)), DMA((9,))] + ([DMA((8,)), DMA((8,))] if twin else [])

    def __init__(self, group, place, rows, sems, twin=None, twin_own=True):
        self.g, self.place, self.sems = group, place, sems[:2]
        self.twin, self.twin_sems, self.twin_own = twin, sems[2:4], twin_own
        self.halves = (pl.ds(0, rows // 2), pl.ds(rows // 2, rows // 2))

    def at(self, i, s):
        g = self.g
        return self.place(g.index(g.ring(i), g.side(s)))

    def to(self, i):
        g = self.g
        return g.device(g.ring(i), g.p)

    def pair(self):
        own = self.at(0, 0)
        return copy_of(own, own, self.sems, 0, self.g.device(self.g.r, 1 - self.g.p))

    def near(self, s, way):
        chunk = self.at(0, s)
        return copy_of(chunk, chunk, self.sems, 1 + 4 * s + way, self.to(1 + 2 * way))

    def relay(self, s, way):
        half = self.at(3 - 2 * way, s).at[self.halves[way]]
        return copy_of(half, half, self.sems, 3 + 4 * s + way, self.to(1 + 2 * way))

    def over(self, k, i, s):
        chunk = self.at(i, s)
        return copy_of(chunk, chunk, self.twin_sems, k, self.twin)

    def tell(self, i, s):
        if self.twin is not None and (i or s or self.twin_own):
            self.over(2 * i + s, i, s).start()

    def start(self):
        self.pair().start()
        for way in (0, 1):
            self.near(0, way).start()
        self.tell(0, 0)

    def forward_pair(self):
        self.pair().wait_recv()
        for way in (0, 1):
            self.near(1, way).start()
        self.tell(0, 1)

    def forward(self, s):
        for way in (0, 1):
            self.near(s, way).wait_recv()
            self.relay(s, way).start()
            self.tell(3 - 2 * way, s)

    def arrive(self, s):
        for way in (0, 1):
            self.relay(s, way).wait_recv()
        self.tell(2, s)

    def settle(self):
        self.pair().wait_send()
        for s in (0, 1):
            for way in (0, 1):
                self.near(s, way).wait_send()
                self.relay(s, way).wait_send()
        if self.twin is not None:
            for k in range(0 if self.twin_own else 1, 8):
                self.over(k, 0, 0).wait()

    def rest(self):
        self.forward_pair()
        self.forward(0)
        self.forward(1)
        self.arrive(0)
        self.arrive(1)
        self.settle()


class Scatter:
    COUNT = 6

    @staticmethod
    def scratch(rows, width):
        half = rows // 2
        return [
            pltpu.VMEM((2, 2, half, width), BF), pltpu.VMEM((2, 2, rows, width), BF),
            pltpu.VMEM((rows, width), BF), pltpu.VMEM((rows, width), BF), DMA((13,)), DMA((13,))]

    def __init__(self, group, part, rows, scratch, step):
        self.g, self.part, self.step, self.rows = group, part, step, rows
        self.mid, self.last, self.sum, self.end = scratch[:4]
        self.sems = scratch[4:6]
        self.half = rows // 2
        self.halves = (pl.ds(0, self.half), pl.ds(self.half, self.half))

    def at(self, i, s):
        g = self.g
        return self.part(g.index(g.ring(i), g.side(s)))

    def to(self, way):
        g = self.g
        return g.device(g.ring(1 + 2 * way), g.p)

    def far(self, s, way):
        return copy_of(self.at(2, s).at[self.halves[way]], self.mid.at[s, way], self.sems, 2 * s + way, self.to(way))

    def own(self, s, way):
        half = self.halves[1 - way]
        return copy_of(self.at(1 + 2 * way, s).at[half], self.last.at[s, way, half], self.sems, 4 + 2 * s + way, self.to(way))

    def both(self, s, way):
        return copy_of(self.mid.at[s, way], self.last.at[s, way, self.halves[way]], self.sems, 8 + 2 * s + way, self.to(way))

    def pair(self):
        return copy_of(self.sum, self.end, self.sems, 12, self.g.device(self.g.r, 1 - self.g.p))

    def by_rows(self, rows, body):
        step = min(self.step, rows)

        @pl.loop(0, rows // step)
        def _(n):
            body(pl.multiple_of(n * step, step), step)

    def send_far(self, s):
        for way in (0, 1):
            self.far(s, way).start()

    def send_near(self, s):
        for way in (0, 1):
            self.own(s, way).start()

    def add_near(self, s):
        for way in (0, 1):
            self.far(s, way).wait_recv()
            mine = self.at(1 + 2 * way, s)
            base = way * self.half

            def add(at, n, way=way, mine=mine, base=base):
                rows = pl.ds(at, n)
                total = mine[pl.ds(base + at, n), :].astype(F32) + self.mid[s, way, rows, :].astype(F32)
                self.mid[s, way, rows, :] = total.astype(BF)

            self.by_rows(self.half, add)
            self.both(s, way).start()

    def arrived(self, s):
        for way in (0, 1):
            self.own(s, way).wait_recv()
            self.both(s, way).wait_recv()

    def add_pair(self):
        self.arrived(1)
        mine = self.at(0, 1)

        def add(at, n):
            rows = pl.ds(at, n)
            total = mine[rows, :].astype(F32) + self.last[1, 0, rows, :].astype(F32) + self.last[1, 1, rows, :].astype(F32)
            self.sum[rows, :] = total.astype(BF)

        self.by_rows(self.rows, add)
        self.pair().start()

    def start(self):
        for s in (1, 0):
            self.send_far(s)
            self.send_near(s)

    def forward(self):
        self.add_near(1)
        self.add_near(0)
        self.add_pair()

    def finish(self, store):
        self.arrived(0)
        self.pair().wait_recv()
        mine = self.at(0, 0)

        def add(at, n):
            rows = pl.ds(at, n)
            total = mine[rows, :].astype(F32) + self.last[0, 0, rows, :].astype(F32) + self.last[0, 1, rows, :].astype(F32)
            store(rows, total + self.end[rows, :].astype(F32))

        self.by_rows(self.rows, add)
        self.pair().wait_send()
        for s in (0, 1):
            for way in (0, 1):
                self.far(s, way).wait_send()
                self.own(s, way).wait_send()
                self.both(s, way).wait_send()


class CoreScatter:
    COUNT = 11

    @staticmethod
    def scratch(rows, width):
        return [pltpu.VMEM((8, rows, width), BF), DMA((8,)), DMA((8,)), pltpu.VMEM((2, rows, width), BF), DMA((2,))] + Scatter.scratch(rows, width)

    def __init__(self, group, part, rows, scratch, step):
        self.part, self.total, self.sems, self.buf, self.load_sems = part, scratch[0], scratch[1:3], scratch[3], scratch[4]
        self.c = lax.rem(group.d, 2)
        self.rows, self.step = rows, step
        self.inner = Scatter(group, lambda m: self.total.at[m], rows, scratch[5:], step)

    def swap(self, m):
        return copy_of(self.part(m, 1 - self.c), self.total.at[m], self.sems, m, other_core())

    def load(self, m):
        slot = lax.rem(m, 2)
        return pltpu.make_async_copy(self.part(m, self.c), self.buf.at[slot], self.load_sems.at[slot])

    def start(self):
        for m in range(8):
            self.swap(m).start()
        self.load(0).start()

    def add(self):
        step = self.step

        @pl.loop(0, 8)
        def _(m):
            @pl.when(m < 7)
            def _():
                self.load(m + 1).start()

            self.load(m).wait()
            self.swap(m).wait_recv()
            slot = lax.rem(m, 2)

            @pl.loop(0, self.rows // step)
            def _(n):
                at = pl.ds(pl.multiple_of(n * step, step), step)
                self.total[m, at, :] = (self.buf[slot, at, :].astype(F32) + self.total[m, at, :].astype(F32)).astype(BF)

        self.inner.start()

    def finish(self, store):
        self.inner.finish(store)
        for m in range(8):
            self.swap(m).wait_send()


class RowSums:
    @staticmethod
    def scratch(width):
        cols = width // 8
        return [pltpu.VMEM((8, 8, cols), F32), pltpu.VMEM((16, 8, cols), F32)] + [DMA((7,)), DMA((7,)), DMA((15,)), DMA((15,)), DMA((7,)), DMA((7,))]

    def __init__(self, rows, out, scratch):
        self.rows, self.out = rows, out
        self.one, self.two = scratch[:2]
        self.sems = (scratch[2:4], scratch[4:6], scratch[6:8])
        self.d, self.t = lax.axis_index("dp"), lax.axis_index("tensor")
        self.cols = rows.shape[1] // 8

    def columns(self, t):
        return pl.ds(pl.multiple_of(t * self.cols, self.cols), self.cols)

    def first(self, k):
        other = lax.rem(self.t + k, 8)
        return copy_of(self.rows.at[:, self.columns(other)], self.one.at[self.t], self.sems[0], k - 1, (self.d, other))

    def second(self, k):
        own = self.two.at[self.d]
        return copy_of(own, own, self.sems[1], k - 1, (lax.rem(self.d + k, 16), self.t))

    def third(self, k):
        own = self.out.at[:, self.columns(self.t)]
        return copy_of(own, own, self.sems[2], k - 1, (self.d, lax.rem(self.t + k, 8)))

    def run(self, step, last):
        @pl.loop(1, last)
        def _(k):
            step(k)

    def start(self):
        self.run(lambda k: self.first(k).start(), 8)
        self.one[self.t] = self.rows[:, self.columns(self.t)]

    def middle(self):
        self.run(lambda k: self.first(k).wait(), 8)
        total = self.one[0]
        for k in range(1, 8):
            total = total + self.one[k]
        self.two[self.d] = total
        self.run(lambda k: self.second(k).start(), 16)

    def finish(self):
        self.run(lambda k: self.second(k).wait(), 16)
        total = self.two[0]
        for k in range(1, 16):
            total = total + self.two[k]
        self.out[:, self.columns(self.t)] = total
        self.run(lambda k: self.third(k).start(), 8)

    def settle(self):
        self.run(lambda k: self.third(k).wait(), 8)


class Sums:
    @staticmethod
    def scratch(rows, width):
        return [pltpu.VMEM((16, rows, width), F32), DMA((15,)), DMA((15,))]

    def __init__(self, scratch):
        self.slots, self.sems = scratch[0], scratch[1:3]
        self.d, self.t = lax.axis_index("dp"), lax.axis_index("tensor")

    def copy(self, k):
        own = self.slots.at[self.d]
        return copy_of(own, own, self.sems, k - 1, (lax.rem(self.d + k, 16), self.t))

    def start(self):
        @pl.loop(1, 16)
        def _(k):
            self.copy(k).start()

    def finish(self):
        @pl.loop(1, 16)
        def _(k):
            self.copy(k).wait()
        total = self.slots[0]
        for k in range(1, 16):
            total = total + self.slots[k]
        return total


def remote_call(kernel, name, cid, outs, ins, scratch, *args, out_specs=None):
    return pl.pallas_call(
        kernel, out_shape=outs, in_specs=ins,
        out_specs=jax.tree.map(lambda _: VM, outs) if out_specs is None else out_specs,
        scratch_shapes=scratch, name=name,
        compiler_params=pltpu.CompilerParams(collective_id=cid, has_side_effects=True, vmem_limit_bytes=60 << 20),
    )(*args)


def chip_members():
    d, t = lax.axis_index("dp"), lax.axis_index("tensor")
    c = lax.rem(d, 2)
    out = []
    for dt in range(8):
        for dc in range(2):
            if dt or dc:
                tt = lax.rem(t + dt, 8)
                cc = lax.rem(c + dc, 2)
                out.append((tt, cc, (d - c + cc, tt)))
    return out


def norm_rows(values):
    average = jnp.mean(values, axis=-1, keepdims=True)
    centred = values - average
    variance = jnp.mean(centred * centred, axis=-1, keepdims=True)
    inverse = lax.rsqrt(variance + EPS)
    return centred * inverse, inverse


def norm_back(grad, scaled, inverse, gain):
    e = grad * gain
    first = jnp.mean(e, axis=-1, keepdims=True)
    second = jnp.mean(e * scaled, axis=-1, keepdims=True)
    return inverse * (e - first - scaled * second)


def augment(meta, lanes_ref, q_ref, qa_ref, kx_ref):
    rows = q_ref.shape[0]
    nblk = kx_ref.shape[0] // BLK
    prefix = meta[nblk]
    for a in range(rows // BLK):
        at = slice(a * BLK, (a + 1) * BLK)
        hidden = jnp.where(lanes_ref[...] > meta[first_block() + a], NEG, 0.0)
        qa_ref[at, :HEAD] = q_ref[at, :]
        qa_ref[at, HEAD:] = jnp.broadcast_to(hidden, (BLK, HEAD)).astype(BF)
    lane = lax.broadcasted_iota(jnp.int32, (BLK, HEAD), 1)
    inside = lax.broadcasted_iota(jnp.int32, (BLK, HEAD), 0)

    @pl.loop(0, nblk)
    def _(b):
        late = (lane == b) & (inside >= prefix - meta[b] * BLK)
        kx_ref[pl.ds(pl.multiple_of(b * BLK, BLK), BLK), :] = jnp.where(late, 1.0, 0.0).astype(BF)


def first_block():
    return lax.axis_index("dp") // 2 * 4


def front_kernel(meta, lanes_ref, x_ref, gain1_ref, shift1_ref, wq_ref, wk_ref, wv_ref, qb_ref, vb_ref, wo_ref, wu_ref, wd_ref,
                 bias_ref, gain2_ref, shift2_ref, cot_ref, ub_ref,
                 w_hbm, n_hbm, q_out, kv_hbm, o_ref, lse_ref, mid_out, own_out, do_out, gm_out, sums_out, low_out, lane_out, opart_out, du_hbm, dd_hbm,
                 w_vm, n_vm, kv_vm, out_vm, up_vm, down_vm, wsh, qa_ref, kx_ref, m_ref, acc_ref, mixed,
                 n2, gh, hidden, gp, gpart, gsum, colsum, du_buf, dd_buf,
                 lsem, css, crs, ass, ars, hss, hrs, *sems):
    gd, gt = Eight("dp"), Eight("tensor")
    t = gt.t
    c = lax.rem(gd.d, 2)
    core = other_core()
    members = chip_members()
    me = gd.index(gd.r, gd.p)
    own = x_ref.shape[0]
    rows = 2 * own
    nblk = kx_ref.shape[0] // BLK
    per = rows // BLK
    shard = wq_ref.shape[0]
    half = out_vm.shape[1] // 2
    hid = wd_ref.shape[0]
    small = mid_out.shape[0]
    csem, asem = (css, crs), (ass, ars)
    for h in range(2):
        cols = slice(h * HEAD, (h + 1) * HEAD)
        for i, ref in enumerate((wq_ref, wk_ref, wv_ref)):
            wsh[h, :, i * HEAD:(i + 1) * HEAD] = ref[:, cols].astype(BF)
    greet([m[2] for m in members] + gd.others())

    w_place = lambda m: w_vm.at[pl.ds(pl.multiple_of(m * 2 * shard, 2 * shard), 2 * shard)]
    row_of = lambda m: pl.ds(pl.multiple_of((m * 2 + c) * shard, shard), shard)
    mine = row_of(me)
    swap = send(wsh.at[1 - c], w_vm.at[mine], csem, 0, core)
    w_vm[mine, :] = wsh[c]
    qkv = Gather(gd, w_place, 2 * shard, sems[0:2])
    keys = Gather(gd, lambda m: kv_vm.at[m], rows, sems[2:4])
    outs = Gather(gd, lambda m: out_vm.at[t, :, row_of(m)], 2 * half, sems[4:8], core)
    ups = Gather(gd, lambda m: up_vm.at[row_of(m)], shard, sems[8:12], core)
    downs = Gather(gd, lambda m: down_vm.at[:, row_of(m)], hid, sems[12:16], core)
    wide = Gather(gt, lambda m: out_vm.at[m, pl.ds(pl.multiple_of(c * half, half), half)], half, sems[16:20], core, twin_own=False)
    normed = Gather(gt, lambda m: n2.at[pl.ds(pl.multiple_of(m * small, small), small)], small, sems[20:22])
    back = Scatter(gt, lambda m: gpart.at[m], small, sems[22:28], 32)
    swap.wait_recv()
    qkv.start()
    out_vm[t, :, mine] = wo_ref[...].astype(BF)
    outs.start()

    def norm_part(k):
        step = 32

        @pl.loop(0, own // 2 // step)
        def _(n):
            at = pl.ds(pl.multiple_of(k * (own // 2) + n * step, step), step)
            scaled, _ = norm_rows(x_ref[at, :].astype(F32))
            n_vm[c, at, :] = (scaled * gain1_ref[...] + shift1_ref[...]).astype(BF)

        at = pl.ds(k * (own // 2), own // 2)
        return send(n_vm.at[c, at], n_vm.at[c, at], csem, 1 + k, core)

    there = [norm_part(0)]
    outs.forward_pair()
    outs.forward(0)
    qkv.forward_pair()
    qkv.forward(0)
    there.append(norm_part(1))
    outs.forward(1)
    outs.arrive(0)
    qkv.forward(1)
    up_vm[mine, :] = wu_ref[...].astype(BF)
    outs.arrive(1)
    down_vm[:, mine] = wd_ref[...].astype(BF)
    outs.settle()
    wide.start()
    qkv.arrive(0)
    qkv.arrive(1)
    for copy in there:
        copy.wait_recv()
    local = pl.ds(pl.multiple_of(c * HEAD, HEAD), HEAD)
    bias_q, bias_v = qb_ref[:, local], vb_ref[:, local]

    @pl.loop(0, per)
    def _(b):
        at = pl.ds(pl.multiple_of(b * BLK, BLK), BLK)
        piece = dg(n_vm[b // 2, pl.ds(pl.multiple_of(lax.rem(b, 2) * BLK, BLK), BLK), :], w_vm[...], NN)
        q_out[at, :] = (piece[:, :HEAD] + bias_q).astype(BF)
        kv_vm[me, at, :HEAD] = piece[:, HEAD:2 * HEAD].astype(BF)
        kv_vm[me, at, HEAD:] = (piece[:, 2 * HEAD:] + bias_v).astype(BF)

    keys.start()
    saves = [pltpu.make_async_copy(w_vm, w_hbm, lsem.at[0]), pltpu.make_async_copy(n_vm, n_hbm, lsem.at[1])]
    for save in saves:
        save.start()
    augment(meta, lanes_ref, q_out, qa_ref, kx_ref)
    m_ref[...] = jnp.full_like(m_ref, -1e30)
    acc_ref[...] = jnp.zeros_like(acc_ref)
    ones = jnp.ones((BLK, HEAD), BF)
    prefix = meta[nblk]

    def attend(chunk, diagonal):
        ks, vs = [], []
        for i in range(per):
            at = pl.ds(pl.multiple_of(chunk * rows + i * BLK, BLK), BLK)
            ks.append(jnp.concatenate([kv_vm[chunk, i * BLK:(i + 1) * BLK, :HEAD], kx_ref[at, :]], axis=1))
            vs.append(jnp.concatenate([kv_vm[chunk, i * BLK:(i + 1) * BLK, HEAD:], ones], axis=1))
        for a in range(per):
            take = slice(a * BLK, (a + 1) * BLK)
            q = qa_ref[take, :]
            ss = [dg(q, k, NT) for k in ks]
            if diagonal:
                edge = prefix - 1 - meta[first_block() + a] * BLK
                lim = jnp.maximum(lax.broadcasted_iota(jnp.int32, (BLK, BLK), 0), edge)
                key = lax.broadcasted_iota(jnp.int32, (BLK, BLK), 1)
                ss[a] = jnp.where(key <= lim, ss[a], NEG)
            top = ss[0]
            for s in ss[1:]:
                top = jnp.maximum(top, s)
            old = m_ref[take, :1]
            new = jnp.maximum(old, jnp.max(top, axis=1, keepdims=True) * C1)
            alpha = jnp.exp2(old - new)
            add = None
            for s, v in zip(ss, vs):
                term = jnp.dot(jnp.exp2(s * C1 - new).astype(BF), v, preferred_element_type=F32)
                add = term if add is None else add + term
            acc_ref[take, :] = acc_ref[take, :] * alpha + add
            m_ref[take, :] = jnp.broadcast_to(new, (BLK, HEAD))

    attend(me, True)

    @pl.loop(1, 8)
    def _(k):
        kk = lax.rem(k, 4)
        i, s = kk + kk // 2 - 2 * (kk // 3), k // 4

        @pl.when(k == 1)
        def _():
            keys.forward_pair()
            keys.forward(0)

        @pl.when(k == 2)
        def _():
            wide.forward_pair()
            wide.forward(0)

        @pl.when(k == 3)
        def _():
            keys.arrive(0)

        @pl.when(k == 5)
        def _():
            keys.forward(1)
            wide.forward(1)
            ups.start()

        @pl.when(k == 7)
        def _():
            keys.arrive(1)

        attend(gd.index(gd.ring(i), gd.p + s * (1 - 2 * gd.p)), False)

    for a in range(per):
        at = slice(a * BLK, (a + 1) * BLK)
        total = acc_ref[at, HEAD:]
        o_ref[at, :] = (acc_ref[at, :HEAD] / total).astype(BF)
        lse_ref[a:a + 1, :] = jnp.transpose(m_ref[at, :] + jnp.log2(total))[:1, :]
    head = pl.ds(pl.multiple_of((2 * t + c) * HEAD, HEAD), HEAD)
    copies = []
    for k, (tt, cc, device) in enumerate(members):
        take = pl.ds(pl.multiple_of(cc * own + tt * small, small), small)
        copies.append(send(o_ref.at[take], mixed.at[:, head], asem, k, device))
    copies.append(send(o_ref.at[pl.ds(pl.multiple_of((1 - c) * own, own), own)], own_out.at[:, local], asem, 15, core))
    keys.settle()
    save = pltpu.make_async_copy(kv_vm, kv_hbm, lsem.at[2])
    save.start()
    saves.append(save)
    downs.start()
    mixed[:, head] = o_ref[pl.ds(pl.multiple_of(c * own + t * small, small), small), :]
    own_out[:, local] = o_ref[pl.ds(pl.multiple_of(c * own, own), own), :]
    ups.forward_pair()
    ups.forward(0)
    wide.arrive(0)
    wide.arrive(1)
    wide.settle()
    for copy in copies:
        copy.wait_recv()
    span = 512
    x_rows = pl.ds(pl.multiple_of(t * small, small), small)
    for n in range(mid_out.shape[1] // span):
        cols = pl.ds(n * span, span)
        total = None
        for k in range(8):
            term = dg(mixed[:, k * 256:(k + 1) * 256], out_vm[k, :, cols], NN)
            total = term if total is None else total + term
        mid_out[:, cols] = total + (x_ref[x_rows, cols].astype(F32) + bias_ref[:, cols])
    scaled, _ = norm_rows(mid_out[...])
    n2[pl.ds(pl.multiple_of(t * small, small), small), :] = (scaled * gain2_ref[...] + shift2_ref[...]).astype(BF)
    normed.start()
    ups.forward(1)
    normed.forward_pair()
    normed.forward(0)
    downs.forward_pair()
    downs.forward(0)
    ups.arrive(0)
    ups.arrive(1)
    ups.settle()
    normed.forward(1)
    downs.forward(1)
    downs.arrive(0)
    downs.arrive(1)
    downs.settle()
    blocks = [(slice(n * span, (n + 1) * span)) for n in range(hid // span)]

    @pl.loop(0, own // BLK)
    def _(b):
        at = pl.ds(pl.multiple_of(b * BLK, BLK), BLK)
        for cols in blocks:
            gh[at, cols] = dg(cot_ref[at, :], down_vm[cols, :], NT)

    normed.arrive(0)
    normed.arrive(1)
    normed.settle()
    colsum[...] = jnp.zeros_like(colsum)
    wide_blocks = [(slice(n * span, (n + 1) * span)) for n in range(n2.shape[1] // span)]

    @pl.loop(0, own // BLK)
    def _(b):
        at = pl.ds(pl.multiple_of(b * BLK, BLK), BLK)
        for cols in blocks:
            pre = dg(n2[at, :], up_vm[:, cols], NN) + ub_ref[:, cols]
            half_erf = 0.5 + 0.5 * lax.erf(pre * math.sqrt(0.5))
            hidden[at, cols] = (pre * half_erf).astype(BF)
            slope = half_erf + pre * jnp.exp(-0.5 * pre * pre) * (1.0 / math.sqrt(2.0 * math.pi))
            low = (gh[at, cols] * slope).astype(BF)
            gp[at, cols] = low
            colsum[0:1, cols] += jnp.sum(low.astype(F32), axis=0, keepdims=True)
        for cols in wide_blocks:
            piece = dg(gp[at, :], up_vm[cols, :], NT).astype(BF)
            for j in range(BLK // small):
                gpart[b * (BLK // small) + j, :, cols] = piece[j * small:(j + 1) * small]

    back.start()

    @pl.loop(0, own // BLK)
    def _(b):
        at = pl.ds(pl.multiple_of(b * BLK, BLK), BLK)
        for cols in wide_blocks:
            piece = dg(hidden[at, :], down_vm[:, cols], NN).astype(BF)
            for j in range(BLK // small):
                opart_out[b * (BLK // small) + j, :, cols] = piece[j * small:(j + 1) * small]

    back.add_near(1)
    back.add_near(0)

    def du_save(m):
        slot = lax.rem(m, 2)
        return pltpu.make_async_copy(du_buf.at[slot], du_hbm.at[pl.ds(pl.multiple_of(m * BLK, BLK), BLK)], lsem.at[3 + slot])

    def dd_save(m):
        slot = lax.rem(m, 2)
        return pltpu.make_async_copy(dd_buf.at[slot], dd_hbm.at[:, pl.ds(pl.multiple_of(m * BLK, BLK), BLK)], lsem.at[5 + slot])

    def weight_grads(low, high):
        @pl.loop(low, high)
        def _(m):
            slot = lax.rem(m, 2)
            cols = pl.ds(pl.multiple_of(m * BLK, BLK), BLK)

            @pl.when(m > 1)
            def _():
                du_save(m - 2).wait()
                dd_save(m - 2).wait()

            du_buf[slot] = dg(n2[:, cols], gp[...], TN).astype(BF)
            du_save(m).start()
            dd_buf[slot] = dg(hidden[...], cot_ref[:, cols], TN).astype(BF)
            dd_save(m).start()

    weight_grads(0, 4)
    back.add_pair()
    weight_grads(4, 8)

    def keep(at, value):
        gsum[at, :] = value

    back.finish(keep)
    scaled, inverse = norm_rows(mid_out[...])
    grad = gsum[...]
    g_rows = cot_ref[x_rows, :].astype(F32)
    gm = g_rows + norm_back(grad, scaled, inverse, gain2_ref[...])
    gm_out[...] = gm
    low = gm.astype(BF)
    low_out[...] = low
    for k in range(8):
        mixed[:, k * 256:(k + 1) * 256] = dg(low, out_vm[k], NT).astype(BF)
    hsem = (hss, hrs)
    take = pl.ds(pl.multiple_of(c * own + t * small, small), small)
    heads = []
    for k, (tt, cc, device) in enumerate(members):
        cols = pl.ds(pl.multiple_of((2 * tt + cc) * HEAD, HEAD), HEAD)
        heads.append(send(mixed.at[:, cols], do_out.at[take], hsem, k, device))
    do_out[take, :] = mixed[:, head]
    sums_out[...] = jnp.zeros_like(sums_out)
    sums_out[0:1, :] = jnp.sum(grad * scaled, axis=0, keepdims=True)
    sums_out[1:2, :] = jnp.sum(grad, axis=0, keepdims=True)
    sums_out[2:3, :] = jnp.sum(low.astype(F32), axis=0, keepdims=True)
    sums_out[3:4, :] = jnp.sum(g_rows, axis=0, keepdims=True)
    lane_out[...] = jnp.zeros_like(lane_out)
    for j in range(hid // 256):
        lane_out[j:j + 1, :] = colsum[0:1, j * 256:(j + 1) * 256]
    du_save(6).wait()
    dd_save(6).wait()
    du_save(7).wait()
    dd_save(7).wait()
    qkv.settle()
    swap.wait_send()
    for copy in there + copies:
        copy.wait_send()
    for save in saves:
        save.wait()
    for copy in heads:
        copy.wait()


def front_call(meta, lanes, x, gain1, shift1, wq, wk, wv, qb, vb, wo, wu, wd, bias, gain2, shift2, cot, ub):
    own, width = x.shape
    rows, shard, hid, small = 2 * own, wq.shape[0], wu.shape[1], own // 8
    hbm = pl.BlockSpec(memory_space=pl.ANY)
    big = [(width, 3 * HEAD), (2, own, width), (8, rows, 2 * HEAD), (8, 2 * HEAD, width), (width, hid), (hid, width)]
    w, n, kv, out, up, down = (struct(s, BF) for s in big)
    chunks = (8, small, width)
    outs = (w, n, struct((rows, HEAD), BF), kv, struct((rows, HEAD), BF), struct((rows // BLK, BLK), F32),
            struct((small, width), F32), struct((own, 2 * HEAD), BF), struct((rows, HEAD), BF), struct((small, width), F32),
            struct((8, width), F32), struct((small, width), BF), struct((8, 256), F32), struct(chunks, BF), up, down)
    return remote_call(
        front_kernel, "front", 1, outs, [SM] + [VM] * 17,
        [pltpu.VMEM(s, BF) for s in big]
        + [pltpu.VMEM((2, shard, 3 * HEAD), BF), pltpu.VMEM((rows, 2 * HEAD), BF), pltpu.VMEM((8 * rows, HEAD), BF),
           pltpu.VMEM((rows, HEAD), F32), pltpu.VMEM((rows, 2 * HEAD), F32), pltpu.VMEM((small, width), BF),
           pltpu.VMEM((own, width), BF), pltpu.VMEM((own, hid), F32), pltpu.VMEM((own, hid), BF), pltpu.VMEM((own, hid), BF),
           pltpu.VMEM(chunks, BF), pltpu.VMEM((small, width), F32), pltpu.VMEM((8, hid), F32),
           pltpu.VMEM((2, BLK, hid), BF), pltpu.VMEM((2, hid, BLK), BF),
           DMA((7,)), DMA((3,)), DMA((3,)), DMA((16,)), DMA((16,)), DMA((15,)), DMA((15,))]
        + Gather.scratch() * 2 + Gather.scratch(True) * 4 + Gather.scratch() + Scatter.scratch(small, width),
        meta, lanes, x, gain1, shift1, wq, wk, wv, qb, vb, wo, wu, wd, bias, gain2, shift2, cot, ub,
        out_specs=(hbm, hbm, VM, hbm) + (VM,) * 10 + (hbm, hbm))


def rear_kernel(meta, lanes_ref, q_ref, kv_ref, o_ref, do_ref, lse_ref, opart_ref, gbr_ref, mid_ref, bias_ref, dup_hbm, ddown_hbm,
                mixed_ref, n_hbm, w_ref, gm_ref, x_hbm, gain_ref, early_ref, lane_ref,
                lay_out, dup_out, ddown_out, dwo_out, dwq_out, dwk_out, dwv_out, tg_out, sums_out, lanes_out,
                qa_ref, kx_ref, part, delta_ref, dq_acc, gb, dqkv, dwo, n_buf, dw, away, arrived, summed, total, mine_w, there_w, vec, x_ref,
                lsem, css, crs, *scratch):
    g, gt = Eight("dp"), Eight("tensor")
    c = lax.rem(g.d, 2)
    core = other_core()
    me, mine_t = g.index(g.r, g.p), gt.index(gt.r, gt.p)
    rows = q_ref.shape[0]
    own = rows // 2
    nblk = kx_ref.shape[0] // BLK
    per = rows // BLK
    small, width = mid_ref.shape
    everyone = [(lax.rem(g.d + k, 16), g.t) for k in range(1, 16)] + [(g.d, lax.rem(g.t + k, 8)) for k in range(1, 8)]
    greet(everyone)
    take = list(scratch)

    def some(count):
        out = take[:count]
        del take[:count]
        return out

    share = dwo_out.shape[1]
    by_columns = lambda m, cc: dwo.at[:, pl.ds(pl.multiple_of((m * 2 + cc) * share, share), share)]
    keys = Scatter(g, lambda m: part.at[m], rows, some(6), 128)
    outs = Scatter(gt, lambda m: opart_ref.at[m], small, some(6), 32)
    ups = CoreScatter(g, lambda m, cc: dup_hbm.at[pl.ds(pl.multiple_of((m * 2 + cc) * share, share), share)], share, some(CoreScatter.COUNT), 32)
    downs = CoreScatter(
        g, lambda m, cc: ddown_hbm.at[:, pl.ds(pl.multiple_of((m * 2 + cc) * share, share), share)], ddown_out.shape[0], some(CoreScatter.COUNT), 128)
    dwos = CoreScatter(g, by_columns, dwo_out.shape[0], some(CoreScatter.COUNT), 128)
    tokens = Scatter(gt, lambda m: summed.at[m], small, some(6), 32)
    weights = Scatter(g, lambda m: dw.at[m], dw.shape[1], some(6), 128)
    wide = Gather(gt, lambda m: gb.at[pl.ds(pl.multiple_of(m * small, small), small)], small, some(2))
    layer = Gather(gt, lambda m: lay_out.at[m], small, some(2))
    final = Gather(gt, lambda m: tg_out.at[m], small, some(2))
    sums = RowSums(vec, sums_out, some(8))
    lane_sums = Sums(some(3))
    csem = (css, crs)
    x_load = pltpu.make_async_copy(x_hbm.at[pl.ds(pl.multiple_of(g.t * small, small), small)], x_ref, lsem.at[2])
    x_load.start()

    def n_load(m):
        slot = lax.rem(m, 2)
        return pltpu.make_async_copy(n_hbm.at[:, pl.ds(pl.multiple_of(m * BLK, BLK), BLK)], n_buf.at[slot], lsem.at[slot])

    ups.start()
    downs.start()
    outs.start()
    gb[pl.ds(pl.multiple_of(mine_t * small, small), small), :] = gbr_ref[...]
    wide.start()
    augment(meta, lanes_ref, q_ref, qa_ref, kx_ref)
    for a in range(per):
        at = slice(a * BLK, (a + 1) * BLK)
        prod = do_ref[at, :].astype(F32) * o_ref[at, :].astype(F32)
        delta_ref[0:1, at] = jnp.sum(jnp.transpose(prod), axis=0, keepdims=True)
        delta_ref[1:2, at] = lse_ref[a:a + 1, :]
    dq_acc[...] = jnp.zeros_like(dq_acc)
    prefix = meta[nblk]

    def attend(chunk, diagonal):
        for i in range(per):
            at_k = slice(i * BLK, (i + 1) * BLK)
            at_x = pl.ds(pl.multiple_of(chunk * rows + i * BLK, BLK), BLK)
            k = kv_ref[chunk, at_k, :HEAD]
            v = kv_ref[chunk, at_k, HEAD:]
            kk = jnp.concatenate([k, kx_ref[at_x, :]], axis=1)
            turned = jnp.transpose(k.astype(F32)).astype(BF)
            dk = dv = None
            for a in range(per):
                at_q = slice(a * BLK, (a + 1) * BLK)
                q = q_ref[at_q, :]
                do = do_ref[at_q, :]
                p = jnp.exp2(dg(kk, qa_ref[at_q, :], NT) * C1 - delta_ref[1:2, at_q])
                if diagonal and i == a:
                    edge = prefix - 1 - meta[first_block() + a] * BLK
                    lim = jnp.maximum(lax.broadcasted_iota(jnp.int32, (BLK, BLK), 1), edge)
                    p = jnp.where(lax.broadcasted_iota(jnp.int32, (BLK, BLK), 0) <= lim, p, 0.0)
                ds = (p * (dg(v, do, NT) - delta_ref[0:1, at_q])).astype(BF)
                tv = jnp.dot(p.astype(BF), do, preferred_element_type=F32)
                tk = jnp.dot(ds, q, preferred_element_type=F32)
                dv = tv if dv is None else dv + tv
                dk = tk if dk is None else dk + tk
                dq_acc[:, at_q] += jnp.dot(turned, ds, preferred_element_type=F32)
            part[chunk, at_k, :HEAD] = (dk * SCALE).astype(BF)
            part[chunk, at_k, HEAD:] = dv.astype(BF)

    @pl.loop(0, 7)
    def _(k):
        kk = lax.rem(k, 3)
        i = (2 - kk + 3 * (kk // 2)) * (1 - k // 6)
        s = 1 - k // 3 + 2 * (k // 6)
        attend(g.index(g.ring(i), g.p + s * (1 - 2 * g.p)), False)

        @pl.when(k == 0)
        def _():
            keys.send_far(1)
            ups.add()
            outs.add_near(1)
            wide.forward_pair()
            wide.forward(0)

        @pl.when(k == 1)
        def _():
            outs.add_near(0)

        @pl.when(k == 2)
        def _():
            keys.send_near(1)
            keys.add_near(1)
            outs.add_pair()
            wide.forward(1)

        @pl.when(k == 3)
        def _():
            keys.send_far(0)
            ups.inner.add_near(1)
            downs.add()

        @pl.when(k == 4)
        def _():
            ups.inner.add_near(0)

        @pl.when(k == 5)
        def _():
            keys.send_near(0)
            keys.add_near(0)

        @pl.when(k == 6)
        def _():
            keys.add_pair()
            ups.inner.add_pair()

    def lay(at, value):
        lay_out[mine_t, at, :] = (mid_ref[at, :] + (value + bias_ref[...])).astype(BF)

    outs.finish(lay)
    layer.start()
    downs.inner.add_near(1)
    n_load(0).start()
    attend(me, True)
    dqkv[:, :HEAD] = jnp.transpose(dq_acc[...] * SCALE).astype(BF)
    layer.forward_pair()
    layer.forward(0)
    wide.arrive(0)
    wide.arrive(1)
    wide.settle()
    span = 512
    for n in range(width // span):
        cols = pl.ds(n * span, span)
        dwo[:, cols] = dg(mixed_ref[...], gb[:, cols], TN).astype(BF)
    dwos.start()
    layer.forward(1)
    downs.inner.add_near(0)

    def keep_keys(at, value):
        dqkv[at, HEAD:] = value.astype(BF)

    keys.finish(keep_keys)

    def project(into, half):
        @pl.loop(0, own // BLK)
        def _(b):
            at = pl.ds(pl.multiple_of(half * own + b * BLK, BLK), BLK)
            for n in range(width // span):
                cols = pl.ds(n * span, span)
                piece = dg(dqkv[at, :], w_ref[cols, :], NT).astype(BF)
                for j in range(BLK // small):
                    into[b * (BLK // small) + j, :, cols] = piece[j * small:(j + 1) * small]

    project(away, 1 - c)
    swap = send(away, arrived, csem, 0, core)
    project(summed, c)
    swap.wait_recv()

    @pl.loop(0, 8)
    def _(m):
        @pl.loop(0, small // 32)
        def _(n):
            at = pl.ds(pl.multiple_of(n * 32, 32), 32)
            summed[m, at, :] = (summed[m, at, :].astype(F32) + arrived[m, at, :].astype(F32)).astype(BF)

    tokens.start()

    @pl.loop(0, 8)
    def _(m):
        @pl.when(m < 7)
        def _():
            n_load(m + 1).start()

        n_load(m).wait()
        dw[m] = dg(n_buf[lax.rem(m, 2)], dqkv[...], TN).astype(BF)

    weights.start()
    dwos.add()
    slot = lane_sums.slots
    slot[g.d] = lane_ref[...]
    local = pl.ds(pl.multiple_of(c * HEAD, HEAD), HEAD)
    slot[g.d, 4:5, local] = jnp.sum(dqkv[:, :HEAD].astype(F32), axis=0, keepdims=True)
    slot[g.d, 5:6, local] = jnp.sum(dqkv[:, 2 * HEAD:].astype(F32), axis=0, keepdims=True)
    lane_sums.start()
    tokens.add_near(1)
    tokens.add_near(0)
    tokens.add_pair()
    weights.add_near(1)
    weights.add_near(0)
    dwos.inner.add_near(1)
    dwos.inner.add_near(0)

    def keep(at, value):
        total[at, :] = value

    x_load.wait()
    tokens.finish(keep)
    scaled, inverse = norm_rows(x_ref[...].astype(F32))
    grad = total[...]
    tg = gm_ref[...] + norm_back(grad, scaled, inverse, gain_ref[...])
    tg_out[mine_t] = tg.astype(BF)
    final.start()
    vec[...] = early_ref[...]
    vec[4:5, :] = jnp.sum(grad * scaled, axis=0, keepdims=True)
    vec[5:6, :] = jnp.sum(grad, axis=0, keepdims=True)
    sums.start()
    weights.add_pair()
    dwos.inner.add_pair()
    downs.inner.add_pair()

    def keep_up(at, value):
        dup_out[at, :] = value

    ups.finish(keep_up)

    def keep_down(at, value):
        ddown_out[at, :] = value

    downs.finish(keep_down)
    sums.middle()

    def keep_w(at, value):
        mine_w[at, :] = value.astype(BF)

    weights.finish(keep_w)
    part_rows = there_w.shape[0]
    there = send(mine_w.at[pl.ds(pl.multiple_of((1 - c) * part_rows, part_rows), part_rows)], there_w, csem, 1, core)
    final.forward_pair()
    final.forward(0)
    kept = mine_w[pl.ds(pl.multiple_of(c * part_rows, part_rows), part_rows), :].astype(F32)
    sums.finish()
    far = pl.ds(pl.multiple_of((1 - c) * HEAD, HEAD), HEAD)
    there.wait()
    for i, ref in enumerate((dwq_out, dwk_out, dwv_out)):
        ref[:, local] = kept[:, i * HEAD:(i + 1) * HEAD]
        ref[:, far] = there_w[:, i * HEAD:(i + 1) * HEAD].astype(F32)
    final.forward(1)
    layer.arrive(0)
    layer.arrive(1)
    layer.settle()

    def keep_o(at, value):
        dwo_out[at, :] = value

    dwos.finish(keep_o)
    lanes_out[...] = lane_sums.finish()
    sums.settle()
    final.arrive(0)
    final.arrive(1)
    final.settle()
    swap.wait_send()


def rear_call(meta, lanes, q, kv, o, do, lse, opart, gb, mid, bias, dup, ddown, mixed, n, w, gm, x, gain, early, lane):
    rows = q.shape[0]
    small, width = mid.shape
    hbm = pl.BlockSpec(memory_space=pl.ANY)
    chunks = (8, small, width)
    wc = 3 * HEAD
    share = width // 16
    head_grad = struct((share, 2 * HEAD), F32)
    return remote_call(
        rear_kernel, "rear", 5,
        (struct(chunks, BF), struct((share, dup.shape[1]), F32), struct((ddown.shape[0], share), F32), struct((2 * HEAD, share), F32), head_grad, head_grad, head_grad,
         struct(chunks, BF), struct((8, width), F32), struct(lane.shape, F32)),
        [SM] + [VM] * 10 + [hbm, hbm, VM] + [hbm, VM, VM, hbm] + [VM] * 3,
        [pltpu.VMEM((rows, 2 * HEAD), BF), pltpu.VMEM((8 * rows, HEAD), BF), pltpu.VMEM(kv.shape, BF), pltpu.VMEM((8, rows), F32),
         pltpu.VMEM((HEAD, rows), F32), pltpu.VMEM((8 * small, width), BF), pltpu.VMEM((rows, wc), BF), pltpu.VMEM((2 * HEAD, width), BF),
         pltpu.VMEM((2, rows, BLK), BF), pltpu.VMEM((8, width // 8, wc), BF), pltpu.VMEM(chunks, BF), pltpu.VMEM(chunks, BF),
         pltpu.VMEM(chunks, BF), pltpu.VMEM((small, width), F32), pltpu.VMEM((width // 8, wc), BF), pltpu.VMEM((share, wc), BF),
         pltpu.VMEM((8, width), F32), pltpu.VMEM((small, width), BF), DMA((3,)), DMA((2,)), DMA((2,))]
        + Scatter.scratch(rows, 2 * HEAD) + Scatter.scratch(small, width) + CoreScatter.scratch(share, dup.shape[1])
        + CoreScatter.scratch(ddown.shape[0], share)
        + CoreScatter.scratch(2 * HEAD, share) + Scatter.scratch(small, width) + Scatter.scratch(width // 8, wc)
        + Gather.scratch() * 3 + RowSums.scratch(width) + Sums.scratch(*lane.shape),
        meta, lanes, q, kv, o, do, lse, opart, gb, mid, bias, dup, ddown, mixed, n, w, gm, x, gain, early, lane)


def on_device(tokens, first_gain, first_shift, query_weight, query_bias, key_weight, value_weight, value_bias,
              out_weight, out_bias, second_gain, second_shift, up_weight, up_bias, down_weight, down_bias,
              cotangent, prefix, block_order):
    own, width = tokens.shape
    d, t = lax.axis_index("dp"), lax.axis_index("tensor")
    c = lax.rem(d, 2)
    nblk = block_order.shape[0]
    rows = own // 8
    meta = jnp.concatenate([block_order % nblk, prefix])
    lanes = jnp.pad(block_order % nblk, (0, HEAD - nblk), constant_values=-1).reshape(1, HEAD)
    row = lambda v: v.reshape(1, -1)

    w_all, n_all, q, kv, o, lse, mid, mixed, do, gm, sums, low, lane, out_part, dw_up, dw_down = front_call(
        meta, lanes, tokens, row(first_gain), row(first_shift), query_weight, key_weight, value_weight, row(query_bias), row(value_bias),
        out_weight, up_weight, down_weight, row(out_bias), row(second_gain), row(second_shift), cotangent, row(up_bias))
    layer, up_grad, down_grad, out_grad, dwq, dwk, dwv, tg, small, lane = rear_call(
        meta, lanes, q, kv, o, do, lse, out_part, low, mid, row(down_bias), dw_up, dw_down, mixed, n_all.reshape(2 * own, width), w_all, gm,
        tokens, row(first_gain), sums, lane)
    hid = up_weight.shape[1]
    return (
        layer.reshape(own, width),
        tg.reshape(own, width).astype(F32),
        small[4], small[5],
        dwq, lane[4], dwk, dwv, lane[5],
        out_grad, small[2],
        small[0], small[1],
        up_grad, lane[:hid // 256].reshape(hid),
        down_grad, small[3],
    )


def solution(mesh):
    rows, cols = P("dp", "tensor"), P("tensor", "dp")
    return jax.shard_map(
        on_device,
        mesh=mesh,
        in_specs=(
            P("dp", None), P(), P(), rows, P("tensor"), rows, rows, P("tensor"), cols, P(), P(), P(), rows, P("tensor"),
            cols, P(), P("dp", None), P(), P()),
        out_specs=(
            P("dp", None), P("dp", None), P(), P(), rows, P("tensor"), rows, rows, P("tensor"), cols, P(), P(), P(), rows,
            P("tensor"), cols, P()),
        check_vma=False,
    )
```

```python
import functools
import math

import jax
import jax.numpy as jnp
from jax import lax
from jax.experimental import pallas as pl
from jax.experimental.pallas import tpu as pltpu
from jax.sharding import PartitionSpec as P

HEAD = 128
BLK = 256
GRP = 4
RING = 4
EPS = 1e-05
NEG = -(2.0 ** 100)
LOG2E = math.log2(math.e)
SCALE = 1.0 / math.sqrt(HEAD)
C1 = LOG2E * SCALE
NN = (((1,), (0,)), ((), ()))
NT = (((1,), (1,)), ((), ()))
TN = (((0,), (0,)), ((), ()))
MESH = pl.DeviceIdType.MESH
VM = pl.BlockSpec(memory_space=pltpu.VMEM)
SM = pl.BlockSpec(memory_space=pltpu.SMEM)
BF = jnp.bfloat16
F32 = jnp.float32
DMA = pltpu.SemaphoreType.DMA


def dg(a, b, dims):
    return lax.dot_general(a, b, dims, preferred_element_type=F32)


def struct(shape, dtype):
    return jax.ShapeDtypeStruct(shape, dtype)


class Eight:
    def __init__(self, axis):
        d, t = lax.axis_index("dp"), lax.axis_index("tensor")
        self.axis, self.d, self.t = axis, d, t
        if axis == "dp":
            self.r, self.p = d // 4, lax.rem(d // 2, 2)
        else:
            self.r, self.p = lax.rem(t, 4), t // 4

    def ring(self, i):
        return lax.rem(self.r + i, RING)

    def side(self, s):
        return 1 - self.p if s else self.p

    def index(self, r, p):
        return r * 2 + p if self.axis == "dp" else p * 4 + r

    def device(self, r, p):
        if self.axis == "dp":
            return ((r * 2 + p) * 2 + lax.rem(self.d, 2), self.t)
        return (self.d, p * 4 + r)

    def others(self):
        return [self.device(self.ring(i), self.p) for i in (1, 3)] + [self.device(self.r, 1 - self.p)]


def other_core():
    d = lax.axis_index("dp")
    return (d + 1 - 2 * lax.rem(d, 2), lax.axis_index("tensor"))


def greet(devices):
    barrier = pltpu.get_barrier_semaphore()
    for device in devices:
        pl.semaphore_signal(barrier, inc=1, device_id=device, device_id_type=MESH)
    pl.semaphore_wait(barrier, len(devices))


def send(src, dst, sems, k, device):
    copy = pltpu.make_async_remote_copy(
        src_ref=src, dst_ref=dst, send_sem=sems[0].at[k], recv_sem=sems[1].at[k],
        device_id=device, device_id_type=MESH)
    copy.start()
    return copy


def copy_of(src, dst, sems, k, device):
    return pltpu.make_async_remote_copy(
        src_ref=src, dst_ref=dst, send_sem=sems[0].at[k], recv_sem=sems[1].at[k],
        device_id=device, device_id_type=MESH)


def send(src, dst, sems, k, device):
    copy = copy_of(src, dst, sems, k, device)
    copy.start()
    return copy


class Gather:
    @staticmethod
    def scratch(twin=False):
        return [DMA((9,)), DMA((9,))] + ([DMA((8,)), DMA((8,))] if twin else [])

    def __init__(self, group, place, rows, sems, twin=None, twin_own=True):
        self.g, self.place, self.sems = group, place, sems[:2]
        self.twin, self.twin_sems, self.twin_own = twin, sems[2:4], twin_own
        self.halves = (pl.ds(0, rows // 2), pl.ds(rows // 2, rows // 2))

    def at(self, i, s):
        g = self.g
        return self.place(g.index(g.ring(i), g.side(s)))

    def to(self, i):
        g = self.g
        return g.device(g.ring(i), g.p)

    def pair(self):
        own = self.at(0, 0)
        return copy_of(own, own, self.sems, 0, self.g.device(self.g.r, 1 - self.g.p))

    def near(self, s, way):
        chunk = self.at(0, s)
        return copy_of(chunk, chunk, self.sems, 1 + 4 * s + way, self.to(1 + 2 * way))

    def relay(self, s, way):
        half = self.at(3 - 2 * way, s).at[self.halves[way]]
        return copy_of(half, half, self.sems, 3 + 4 * s + way, self.to(1 + 2 * way))

    def over(self, k, i, s):
        chunk = self.at(i, s)
        return copy_of(chunk, chunk, self.twin_sems, k, self.twin)

    def tell(self, i, s):
        if self.twin is not None and (i or s or self.twin_own):
            self.over(2 * i + s, i, s).start()

    def start(self):
        self.pair().start()
        for way in (0, 1):
            self.near(0, way).start()
        self.tell(0, 0)

    def forward_pair(self):
        self.pair().wait_recv()
        for way in (0, 1):
            self.near(1, way).start()
        self.tell(0, 1)

    def forward(self, s):
        for way in (0, 1):
            self.near(s, way).wait_recv()
            self.relay(s, way).start()
            self.tell(3 - 2 * way, s)

    def arrive(self, s):
        for way in (0, 1):
            self.relay(s, way).wait_recv()
        self.tell(2, s)

    def settle(self):
        self.pair().wait_send()
        for s in (0, 1):
            for way in (0, 1):
                self.near(s, way).wait_send()
                self.relay(s, way).wait_send()
        if self.twin is not None:
            for k in range(0 if self.twin_own else 1, 8):
                self.over(k, 0, 0).wait()

    def rest(self):
        self.forward_pair()
        self.forward(0)
        self.forward(1)
        self.arrive(0)
        self.arrive(1)
        self.settle()


class Scatter:
    COUNT = 6

    @staticmethod
    def scratch(rows, width):
        half = rows // 2
        return [
            pltpu.VMEM((2, 2, half, width), BF), pltpu.VMEM((2, 2, rows, width), BF),
            pltpu.VMEM((rows, width), BF), pltpu.VMEM((rows, width), BF), DMA((13,)), DMA((13,))]

    def __init__(self, group, part, rows, scratch, step):
        self.g, self.part, self.step, self.rows = group, part, step, rows
        self.mid, self.last, self.sum, self.end = scratch[:4]
        self.sems = scratch[4:6]
        self.half = rows // 2
        self.halves = (pl.ds(0, self.half), pl.ds(self.half, self.half))

    def at(self, i, s):
        g = self.g
        return self.part(g.index(g.ring(i), g.side(s)))

    def to(self, way):
        g = self.g
        return g.device(g.ring(1 + 2 * way), g.p)

    def far(self, s, way):
        return copy_of(self.at(2, s).at[self.halves[way]], self.mid.at[s, way], self.sems, 2 * s + way, self.to(way))

    def own(self, s, way):
        half = self.halves[1 - way]
        return copy_of(self.at(1 + 2 * way, s).at[half], self.last.at[s, way, half], self.sems, 4 + 2 * s + way, self.to(way))

    def both(self, s, way):
        return copy_of(self.mid.at[s, way], self.last.at[s, way, self.halves[way]], self.sems, 8 + 2 * s + way, self.to(way))

    def pair(self):
        return copy_of(self.sum, self.end, self.sems, 12, self.g.device(self.g.r, 1 - self.g.p))

    def by_rows(self, rows, body):
        step = min(self.step, rows)

        @pl.loop(0, rows // step)
        def _(n):
            body(pl.multiple_of(n * step, step), step)

    def send_far(self, s):
        for way in (0, 1):
            self.far(s, way).start()

    def send_near(self, s):
        for way in (0, 1):
            self.own(s, way).start()

    def add_near(self, s):
        for way in (0, 1):
            self.far(s, way).wait_recv()
            mine = self.at(1 + 2 * way, s)
            base = way * self.half

            def add(at, n, way=way, mine=mine, base=base):
                rows = pl.ds(at, n)
                total = mine[pl.ds(base + at, n), :].astype(F32) + self.mid[s, way, rows, :].astype(F32)
                self.mid[s, way, rows, :] = total.astype(BF)

            self.by_rows(self.half, add)
            self.both(s, way).start()

    def arrived(self, s):
        for way in (0, 1):
            self.own(s, way).wait_recv()
            self.both(s, way).wait_recv()

    def add_pair(self):
        self.arrived(1)
        mine = self.at(0, 1)

        def add(at, n):
            rows = pl.ds(at, n)
            total = mine[rows, :].astype(F32) + self.last[1, 0, rows, :].astype(F32) + self.last[1, 1, rows, :].astype(F32)
            self.sum[rows, :] = total.astype(BF)

        self.by_rows(self.rows, add)
        self.pair().start()

    def start(self):
        for s in (1, 0):
            self.send_far(s)
            self.send_near(s)

    def forward(self):
        self.add_near(1)
        self.add_near(0)
        self.add_pair()

    def finish(self, store):
        self.arrived(0)
        self.pair().wait_recv()
        mine = self.at(0, 0)

        def add(at, n):
            rows = pl.ds(at, n)
            total = mine[rows, :].astype(F32) + self.last[0, 0, rows, :].astype(F32) + self.last[0, 1, rows, :].astype(F32)
            store(rows, total + self.end[rows, :].astype(F32))

        self.by_rows(self.rows, add)
        self.pair().wait_send()
        for s in (0, 1):
            for way in (0, 1):
                self.far(s, way).wait_send()
                self.own(s, way).wait_send()
                self.both(s, way).wait_send()


class CoreScatter:
    COUNT = 11

    @staticmethod
    def scratch(rows, width):
        return [pltpu.VMEM((8, rows, width), BF), DMA((8,)), DMA((8,)), pltpu.VMEM((2, rows, width), BF), DMA((2,))] + Scatter.scratch(rows, width)

    def __init__(self, group, part, rows, scratch, step):
        self.part, self.total, self.sems, self.buf, self.load_sems = part, scratch[0], scratch[1:3], scratch[3], scratch[4]
        self.c = lax.rem(group.d, 2)
        self.rows, self.step = rows, step
        self.inner = Scatter(group, lambda m: self.total.at[m], rows, scratch[5:], step)

    def swap(self, m):
        return copy_of(self.part(m, 1 - self.c), self.total.at[m], self.sems, m, other_core())

    def load(self, m):
        slot = lax.rem(m, 2)
        return pltpu.make_async_copy(self.part(m, self.c), self.buf.at[slot], self.load_sems.at[slot])

    def start(self):
        for m in range(8):
            self.swap(m).start()
        self.load(0).start()

    def add(self):
        step = self.step

        @pl.loop(0, 8)
        def _(m):
            @pl.when(m < 7)
            def _():
                self.load(m + 1).start()

            self.load(m).wait()
            self.swap(m).wait_recv()
            slot = lax.rem(m, 2)

            @pl.loop(0, self.rows // step)
            def _(n):
                at = pl.ds(pl.multiple_of(n * step, step), step)
                self.total[m, at, :] = (self.buf[slot, at, :].astype(F32) + self.total[m, at, :].astype(F32)).astype(BF)

        self.inner.start()

    def finish(self, store):
        self.inner.finish(store)
        for m in range(8):
            self.swap(m).wait_send()


class RowSums:
    @staticmethod
    def scratch(width):
        cols = width // 8
        return [pltpu.VMEM((8, 8, cols), F32), pltpu.VMEM((16, 8, cols), F32)] + [DMA((7,)), DMA((7,)), DMA((15,)), DMA((15,)), DMA((7,)), DMA((7,))]

    def __init__(self, rows, out, scratch):
        self.rows, self.out = rows, out
        self.one, self.two = scratch[:2]
        self.sems = (scratch[2:4], scratch[4:6], scratch[6:8])
        self.d, self.t = lax.axis_index("dp"), lax.axis_index("tensor")
        self.cols = rows.shape[1] // 8

    def columns(self, t):
        return pl.ds(pl.multiple_of(t * self.cols, self.cols), self.cols)

    def first(self, k):
        other = lax.rem(self.t + k, 8)
        return copy_of(self.rows.at[:, self.columns(other)], self.one.at[self.t], self.sems[0], k - 1, (self.d, other))

    def second(self, k):
        own = self.two.at[self.d]
        return copy_of(own, own, self.sems[1], k - 1, (lax.rem(self.d + k, 16), self.t))

    def third(self, k):
        own = self.out.at[:, self.columns(self.t)]
        return copy_of(own, own, self.sems[2], k - 1, (self.d, lax.rem(self.t + k, 8)))

    def run(self, step, last):
        @pl.loop(1, last)
        def _(k):
            step(k)

    def start(self):
        self.run(lambda k: self.first(k).start(), 8)
        self.one[self.t] = self.rows[:, self.columns(self.t)]

    def middle(self):
        self.run(lambda k: self.first(k).wait(), 8)
        total = self.one[0]
        for k in range(1, 8):
            total = total + self.one[k]
        self.two[self.d] = total
        self.run(lambda k: self.second(k).start(), 16)

    def finish(self):
        self.run(lambda k: self.second(k).wait(), 16)
        total = self.two[0]
        for k in range(1, 16):
            total = total + self.two[k]
        self.out[:, self.columns(self.t)] = total
        self.run(lambda k: self.third(k).start(), 8)

    def settle(self):
        self.run(lambda k: self.third(k).wait(), 8)


class Sums:
    @staticmethod
    def scratch(rows, width):
        return [pltpu.VMEM((16, rows, width), F32), DMA((15,)), DMA((15,))]

    def __init__(self, scratch):
        self.slots, self.sems = scratch[0], scratch[1:3]
        self.d, self.t = lax.axis_index("dp"), lax.axis_index("tensor")

    def copy(self, k):
        own = self.slots.at[self.d]
        return copy_of(own, own, self.sems, k - 1, (lax.rem(self.d + k, 16), self.t))

    def start(self):
        @pl.loop(1, 16)
        def _(k):
            self.copy(k).start()

    def finish(self):
        @pl.loop(1, 16)
        def _(k):
            self.copy(k).wait()
        total = self.slots[0]
        for k in range(1, 16):
            total = total + self.slots[k]
        return total


def remote_call(kernel, name, cid, outs, ins, scratch, *args, out_specs=None):
    return pl.pallas_call(
        kernel, out_shape=outs, in_specs=ins,
        out_specs=jax.tree.map(lambda _: VM, outs) if out_specs is None else out_specs,
        scratch_shapes=scratch, name=name,
        compiler_params=pltpu.CompilerParams(collective_id=cid, has_side_effects=True, vmem_limit_bytes=60 << 20),
    )(*args)


def chip_members():
    d, t = lax.axis_index("dp"), lax.axis_index("tensor")
    c = lax.rem(d, 2)
    out = []
    for dt in range(8):
        for dc in range(2):
            if dt or dc:
                tt = lax.rem(t + dt, 8)
                cc = lax.rem(c + dc, 2)
                out.append((tt, cc, (d - c + cc, tt)))
    return out


def norm_rows(values):
    average = jnp.mean(values, axis=-1, keepdims=True)
    centred = values - average
    variance = jnp.mean(centred * centred, axis=-1, keepdims=True)
    inverse = lax.rsqrt(variance + EPS)
    return centred * inverse, inverse


def norm_back(grad, scaled, inverse, gain):
    e = grad * gain
    first = jnp.mean(e, axis=-1, keepdims=True)
    second = jnp.mean(e * scaled, axis=-1, keepdims=True)
    return inverse * (e - first - scaled * second)


def augment(meta, lanes_ref, q_ref, qa_ref, kx_ref):
    rows = q_ref.shape[0]
    nblk = kx_ref.shape[0] // BLK
    prefix = meta[nblk]
    for a in range(rows // BLK):
        at = slice(a * BLK, (a + 1) * BLK)
        hidden = jnp.where(lanes_ref[...] > meta[first_block() + a], NEG, 0.0)
        qa_ref[at, :HEAD] = q_ref[at, :]
        qa_ref[at, HEAD:] = jnp.broadcast_to(hidden, (BLK, HEAD)).astype(BF)
    lane = lax.broadcasted_iota(jnp.int32, (BLK, HEAD), 1)
    inside = lax.broadcasted_iota(jnp.int32, (BLK, HEAD), 0)

    @pl.loop(0, nblk)
    def _(b):
        late = (lane == b) & (inside >= prefix - meta[b] * BLK)
        kx_ref[pl.ds(pl.multiple_of(b * BLK, BLK), BLK), :] = jnp.where(late, 1.0, 0.0).astype(BF)


def first_block():
    return lax.axis_index("dp") // 2 * 4


def front_kernel(meta, lanes_ref, x_ref, gain1_ref, shift1_ref, wq_ref, wk_ref, wv_ref, qb_ref, vb_ref, wo_ref, wu_ref, wd_ref,
                 bias_ref, gain2_ref, shift2_ref, cot_ref, ub_ref, db_ref,
                 w_hbm, n_hbm, q_out, kv_hbm, o_ref, lse_ref, mid_out, own_out, do_out, gm_out, sums_out, low_out, lane_out, lay_out, du_hbm, dd_hbm, dup_out,
                 w_vm, n_vm, kv_vm, out_vm, up_vm, down_vm, wsh, mixed, n2, gsum, colsum,
                 lsem, css, crs, ass, ars, hss, hrs, *sems):
    gd, gt = Eight("dp"), Eight("tensor")
    t = gt.t
    c = lax.rem(gd.d, 2)
    core = other_core()
    members = chip_members()
    me = gd.index(gd.r, gd.p)
    own = x_ref.shape[0]
    rows = 2 * own
    nblk = 8 * rows // BLK
    per = rows // BLK
    shard = wq_ref.shape[0]
    half = out_vm.shape[1] // 2
    hid = wd_ref.shape[0]
    small = mid_out.shape[0]
    csem, asem = (css, crs), (ass, ars)
    for h in range(2):
        cols = slice(h * HEAD, (h + 1) * HEAD)
        for i, ref in enumerate((wq_ref, wk_ref, wv_ref)):
            wsh[h, :, i * HEAD:(i + 1) * HEAD] = ref[:, cols].astype(BF)
    greet([m[2] for m in members] + gd.others())

    w_place = lambda m: w_vm.at[pl.ds(pl.multiple_of(m * 2 * shard, 2 * shard), 2 * shard)]
    row_of = lambda m: pl.ds(pl.multiple_of((m * 2 + c) * shard, shard), shard)
    mine = row_of(me)
    swap = send(wsh.at[1 - c], w_vm.at[mine], csem, 0, core)
    w_vm[mine, :] = wsh[c]
    qkv = Gather(gd, w_place, 2 * shard, sems[0:2])
    keys = Gather(gd, lambda m: kv_vm.at[m], rows, sems[2:4])
    outs = Gather(gd, lambda m: out_vm.at[t, :, row_of(m)], 2 * half, sems[4:8], core)
    ups = Gather(gd, lambda m: up_vm.at[row_of(m)], shard, sems[8:12], core)
    downs = Gather(gd, lambda m: down_vm.at[:, row_of(m)], hid, sems[12:16], core)
    wide = Gather(gt, lambda m: out_vm.at[m, pl.ds(pl.multiple_of(c * half, half), half)], half, sems[16:20], core, twin_own=False)
    normed = Gather(gt, lambda m: n2.at[pl.ds(pl.multiple_of(m * small, small), small)], small, sems[20:22])
    spare = lambda k: (lambda m: n_vm.at[k, pl.ds(pl.multiple_of(m * small, small), small)])
    back = Scatter(gt, spare(0), small, sems[22:28], 32)
    result = Scatter(gt, spare(1), small, sems[28:34], 32)
    grads = CoreScatter(gd, lambda m, cc: du_hbm.at[pl.ds(pl.multiple_of((m * 2 + cc) * shard, shard), shard)], shard, sems[34:45], 32)
    swap.wait_recv()
    qkv.start()

    def norm_part(k):
        step = 32

        @pl.loop(0, own // 2 // step)
        def _(n):
            at = pl.ds(pl.multiple_of(k * (own // 2) + n * step, step), step)
            scaled, _ = norm_rows(x_ref[at, :].astype(F32))
            n_vm[c, at, :] = (scaled * gain1_ref[...] + shift1_ref[...]).astype(BF)

        at = pl.ds(k * (own // 2), own // 2)
        return send(n_vm.at[c, at], n_vm.at[c, at], csem, 1 + k, core)

    there = [norm_part(0)]
    qkv.forward_pair()
    qkv.forward(0)
    out_vm[t, :, mine] = wo_ref[...].astype(BF)
    outs.start()
    there.append(norm_part(1))
    qkv.forward(1)
    up_vm[mine, :] = wu_ref[...].astype(BF)
    down_vm[:, mine] = wd_ref[...].astype(BF)
    outs.forward_pair()
    outs.forward(0)
    qkv.arrive(0)
    for copy in there:
        copy.wait_recv()
    qkv.arrive(1)
    local = pl.ds(pl.multiple_of(c * HEAD, HEAD), HEAD)
    bias_q, bias_v = qb_ref[:, local], vb_ref[:, local]

    @pl.loop(0, per)
    def _(b):
        at = pl.ds(pl.multiple_of(b * BLK, BLK), BLK)
        piece = dg(n_vm[b // 2, pl.ds(pl.multiple_of(lax.rem(b, 2) * BLK, BLK), BLK), :], w_vm[...], NN)
        q_out[at, :] = (piece[:, :HEAD] + bias_q).astype(BF)
        kv_vm[me, at, :HEAD] = piece[:, HEAD:2 * HEAD].astype(BF)
        kv_vm[me, at, HEAD:] = (piece[:, 2 * HEAD:] + bias_v).astype(BF)

    keys.start()
    outs.forward(1)
    saves = [pltpu.make_async_copy(w_vm, w_hbm, lsem.at[0]), pltpu.make_async_copy(n_vm, n_hbm, lsem.at[1])]
    for save in saves:
        save.start()
    def attention(qa_ref, kx_ref, m_ref, acc_ref):
        augment(meta, lanes_ref, q_out, qa_ref, kx_ref)
        outs.arrive(0)
        outs.arrive(1)
        outs.settle()
        wide.start()
        m_ref[...] = jnp.full_like(m_ref, -1e30)
        acc_ref[...] = jnp.zeros_like(acc_ref)
        ones = jnp.ones((BLK, HEAD), BF)
        prefix = meta[nblk]

        def attend(chunk, diagonal):
            ks, vs = [], []
            for i in range(per):
                at = pl.ds(pl.multiple_of(chunk * rows + i * BLK, BLK), BLK)
                ks.append(jnp.concatenate([kv_vm[chunk, i * BLK:(i + 1) * BLK, :HEAD], kx_ref[at, :]], axis=1))
                vs.append(jnp.concatenate([kv_vm[chunk, i * BLK:(i + 1) * BLK, HEAD:], ones], axis=1))
            for a in range(per):
                take = slice(a * BLK, (a + 1) * BLK)
                q = qa_ref[take, :]
                ss = [dg(q, k, NT) for k in ks]
                if diagonal:
                    edge = prefix - 1 - meta[first_block() + a] * BLK
                    lim = jnp.maximum(lax.broadcasted_iota(jnp.int32, (BLK, BLK), 0), edge)
                    key = lax.broadcasted_iota(jnp.int32, (BLK, BLK), 1)
                    ss[a] = jnp.where(key <= lim, ss[a], NEG)
                top = ss[0]
                for s in ss[1:]:
                    top = jnp.maximum(top, s)
                old = m_ref[take, :1]
                new = jnp.maximum(old, jnp.max(top, axis=1, keepdims=True) * C1)
                alpha = jnp.exp2(old - new)
                add = None
                for s, v in zip(ss, vs):
                    term = jnp.dot(jnp.exp2(s * C1 - new).astype(BF), v, preferred_element_type=F32)
                    add = term if add is None else add + term
                acc_ref[take, :] = acc_ref[take, :] * alpha + add
                m_ref[take, :] = jnp.broadcast_to(new, (BLK, HEAD))

        attend(me, True)

        @pl.loop(1, 8)
        def _(k):
            kk = lax.rem(k, 4)
            i, s = kk + kk // 2 - 2 * (kk // 3), k // 4

            @pl.when(k == 1)
            def _():
                keys.forward_pair()
                keys.forward(0)

            @pl.when(k == 2)
            def _():
                wide.forward_pair()
                wide.forward(0)

            @pl.when(k == 3)
            def _():
                keys.arrive(0)

            @pl.when(k == 5)
            def _():
                keys.forward(1)
                wide.forward(1)
                ups.start()

            @pl.when(k == 7)
            def _():
                keys.arrive(1)

            attend(gd.index(gd.ring(i), gd.p + s * (1 - 2 * gd.p)), False)

        for a in range(per):
            at = slice(a * BLK, (a + 1) * BLK)
            total = acc_ref[at, HEAD:]
            o_ref[at, :] = (acc_ref[at, :HEAD] / total).astype(BF)
            lse_ref[a:a + 1, :] = jnp.transpose(m_ref[at, :] + jnp.log2(total))[:1, :]

    pl.run_scoped(
        attention, pltpu.VMEM((rows, 2 * HEAD), BF), pltpu.VMEM((8 * rows, HEAD), BF), pltpu.VMEM((rows, HEAD), F32), pltpu.VMEM((rows, 2 * HEAD), F32))
    head = pl.ds(pl.multiple_of((2 * t + c) * HEAD, HEAD), HEAD)
    copies = []
    for k, (tt, cc, device) in enumerate(members):
        take = pl.ds(pl.multiple_of(cc * own + tt * small, small), small)
        copies.append(send(o_ref.at[take], mixed.at[:, head], asem, k, device))
    copies.append(send(o_ref.at[pl.ds(pl.multiple_of((1 - c) * own, own), own)], own_out.at[:, local], asem, 15, core))
    keys.settle()
    save = pltpu.make_async_copy(kv_vm, kv_hbm, lsem.at[2])
    save.start()
    saves.append(save)
    downs.start()
    mixed[:, head] = o_ref[pl.ds(pl.multiple_of(c * own + t * small, small), small), :]
    own_out[:, local] = o_ref[pl.ds(pl.multiple_of(c * own, own), own), :]
    ups.forward_pair()
    ups.forward(0)
    wide.arrive(0)
    wide.arrive(1)
    wide.settle()
    for copy in copies:
        copy.wait_recv()
    span = 512
    x_rows = pl.ds(pl.multiple_of(t * small, small), small)
    for n in range(mid_out.shape[1] // span):
        cols = pl.ds(n * span, span)
        total = None
        for k in range(8):
            term = dg(mixed[:, k * 256:(k + 1) * 256], out_vm[k, :, cols], NN)
            total = term if total is None else total + term
        mid_out[:, cols] = total + (x_ref[x_rows, cols].astype(F32) + bias_ref[:, cols])
    scaled, _ = norm_rows(mid_out[...])
    n2[pl.ds(pl.multiple_of(t * small, small), small), :] = (scaled * gain2_ref[...] + shift2_ref[...]).astype(BF)
    normed.start()
    ups.forward(1)
    normed.forward_pair()
    normed.forward(0)
    downs.forward_pair()
    downs.forward(0)
    ups.arrive(0)
    ups.arrive(1)
    ups.settle()
    normed.forward(1)
    downs.forward(1)
    downs.arrive(0)
    downs.arrive(1)
    downs.settle()
    saves.pop(1).wait()
    for copy in there:
        copy.wait_send()
    blocks = [(slice(n * span, (n + 1) * span)) for n in range(hid // span)]
    wide_blocks = [(slice(n * span, (n + 1) * span)) for n in range(n2.shape[1] // span)]

    def feed_forward(gh, hidden, gp, du_buf, dd_buf):
        @pl.loop(0, own // BLK)
        def _(b):
            at = pl.ds(pl.multiple_of(b * BLK, BLK), BLK)
            for cols in blocks:
                gh[at, cols] = dg(cot_ref[at, :], down_vm[cols, :], NT)

        normed.arrive(0)
        normed.arrive(1)
        normed.settle()
        colsum[...] = jnp.zeros_like(colsum)

        @pl.loop(0, own // BLK)
        def _(b):
            at = pl.ds(pl.multiple_of(b * BLK, BLK), BLK)
            for cols in blocks:
                pre = dg(n2[at, :], up_vm[:, cols], NN) + ub_ref[:, cols]
                half_erf = 0.5 + 0.5 * lax.erf(pre * math.sqrt(0.5))
                hidden[at, cols] = (pre * half_erf).astype(BF)
                slope = half_erf + pre * jnp.exp(-0.5 * pre * pre) * (1.0 / math.sqrt(2.0 * math.pi))
                low = (gh[at, cols] * slope).astype(BF)
                gp[at, cols] = low
                colsum[0:1, cols] += jnp.sum(low.astype(F32), axis=0, keepdims=True)
            for cols in wide_blocks:
                n_vm[0, at, cols] = dg(gp[at, :], up_vm[cols, :], NT).astype(BF)

        back.start()

        def du_save(m):
            slot = lax.rem(m, 2)
            return pltpu.make_async_copy(du_buf.at[slot], du_hbm.at[pl.ds(pl.multiple_of(m * BLK, BLK), BLK)], lsem.at[3 + slot])

        def dd_save(m):
            slot = lax.rem(m, 2)
            return pltpu.make_async_copy(dd_buf.at[slot], dd_hbm.at[:, pl.ds(pl.multiple_of(m * BLK, BLK), BLK)], lsem.at[5 + slot])

        def blocks_of(save, buf, value):
            @pl.loop(0, 8)
            def _(m):
                @pl.when(m > 1)
                def _():
                    save(m - 2).wait()

                buf[lax.rem(m, 2)] = value(pl.ds(pl.multiple_of(m * BLK, BLK), BLK)).astype(BF)
                save(m).start()

        blocks_of(du_save, du_buf, lambda cols: dg(n2[:, cols], gp[...], TN))
        back.add_near(1)
        back.add_near(0)
        du_save(6).wait()
        du_save(7).wait()
        grads.start()

        @pl.loop(0, own // BLK)
        def _(b):
            at = pl.ds(pl.multiple_of(b * BLK, BLK), BLK)
            for cols in wide_blocks:
                n_vm[1, at, cols] = dg(hidden[at, :], down_vm[:, cols], NN).astype(BF)

        back.add_pair()
        result.start()
        grads.add()
        blocks_of(dd_save, dd_buf, lambda cols: dg(hidden[...], cot_ref[:, cols], TN))
        dd_save(6).wait()
        dd_save(7).wait()

    pl.run_scoped(
        feed_forward, pltpu.VMEM((own, hid), F32), pltpu.VMEM((own, hid), BF), pltpu.VMEM((own, hid), BF), pltpu.VMEM((2, BLK, hid), BF),
        pltpu.VMEM((2, hid, BLK), BF))

    def keep(at, value):
        gsum[at, :] = value

    back.finish(keep)
    scaled, inverse = norm_rows(mid_out[...])
    grad = gsum[...]
    g_rows = cot_ref[x_rows, :].astype(F32)
    gm = g_rows + norm_back(grad, scaled, inverse, gain2_ref[...])
    gm_out[...] = gm
    low = gm.astype(BF)
    low_out[...] = low
    for k in range(8):
        mixed[:, k * 256:(k + 1) * 256] = dg(low, out_vm[k], NT).astype(BF)
    hsem = (hss, hrs)
    take = pl.ds(pl.multiple_of(c * own + t * small, small), small)
    heads = []
    for k, (tt, cc, device) in enumerate(members):
        cols = pl.ds(pl.multiple_of((2 * tt + cc) * HEAD, HEAD), HEAD)
        heads.append(send(mixed.at[:, cols], do_out.at[take], hsem, k, device))
    do_out[take, :] = mixed[:, head]
    result.add_near(1)
    result.add_near(0)
    grads.inner.add_near(1)
    grads.inner.add_near(0)
    result.add_pair()
    sums_out[...] = jnp.zeros_like(sums_out)
    sums_out[0:1, :] = jnp.sum(grad * scaled, axis=0, keepdims=True)
    sums_out[1:2, :] = jnp.sum(grad, axis=0, keepdims=True)
    sums_out[2:3, :] = jnp.sum(low.astype(F32), axis=0, keepdims=True)
    sums_out[3:4, :] = jnp.sum(g_rows, axis=0, keepdims=True)
    lane_out[...] = jnp.zeros_like(lane_out)
    for j in range(hid // 256):
        lane_out[j:j + 1, :] = colsum[0:1, j * 256:(j + 1) * 256]
    grads.inner.add_pair()

    def lay(at, value):
        lay_out[at, :] = (mid_out[at, :] + (value + db_ref[...])).astype(BF)

    result.finish(lay)

    def keep_up(at, value):
        dup_out[at, :] = value

    grads.finish(keep_up)
    qkv.settle()
    swap.wait_send()
    for copy in copies:
        copy.wait_send()
    for save in saves:
        save.wait()
    for copy in heads:
        copy.wait()


def front_call(meta, lanes, x, gain1, shift1, wq, wk, wv, qb, vb, wo, wu, wd, bias, gain2, shift2, cot, ub, db):
    own, width = x.shape
    rows, shard, hid, small = 2 * own, wq.shape[0], wu.shape[1], own // 8
    hbm = pl.BlockSpec(memory_space=pl.ANY)
    big = [(width, 3 * HEAD), (2, own, width), (8, rows, 2 * HEAD), (8, 2 * HEAD, width), (width, hid), (hid, width)]
    w, n, kv, out, up, down = (struct(s, BF) for s in big)
    outs = (w, n, struct((rows, HEAD), BF), kv, struct((rows, HEAD), BF), struct((rows // BLK, BLK), F32),
            struct((small, width), F32), struct((own, 2 * HEAD), BF), struct((rows, HEAD), BF), struct((small, width), F32),
            struct((8, width), F32), struct((small, width), BF), struct((8, 256), F32), struct((small, width), BF), up, down, struct((shard, hid), F32))
    return remote_call(
        front_kernel, "front", 1, outs, [SM] + [VM] * 18,
        [pltpu.VMEM(s, BF) for s in big]
        + [pltpu.VMEM((2, shard, 3 * HEAD), BF), pltpu.VMEM((small, width), BF), pltpu.VMEM((own, width), BF),
           pltpu.VMEM((small, width), F32), pltpu.VMEM((8, hid), F32),
           DMA((7,)), DMA((3,)), DMA((3,)), DMA((16,)), DMA((16,)), DMA((15,)), DMA((15,))]
        + Gather.scratch() * 2 + Gather.scratch(True) * 4 + Gather.scratch() + Scatter.scratch(small, width) * 2 + CoreScatter.scratch(shard, hid),
        meta, lanes, x, gain1, shift1, wq, wk, wv, qb, vb, wo, wu, wd, bias, gain2, shift2, cot, ub, db,
        out_specs=(hbm, hbm, VM, hbm) + (VM,) * 10 + (hbm, hbm, VM))


def rear_kernel(meta, lanes_ref, q_ref, kv_hbm, o_ref, do_ref, lse_ref, gbr_ref, layr_ref, ddown_hbm,
                mixed_ref, n_hbm, w_ref, gm_ref, x_hbm, gain_ref, early_ref, lane_ref,
                lay_out, ddown_out, dwo_out, dwq_out, dwk_out, dwv_out, tg_out, sums_out, lanes_out,
                kv_ref, qa_ref, kx_ref, part, delta_ref, dq_acc, gb, dqkv, dwo, n_buf, dw, away, arrived, summed, total, mine_w, there_w, vec, x_ref,
                lsem, css, crs, *scratch):
    g, gt = Eight("dp"), Eight("tensor")
    c = lax.rem(g.d, 2)
    core = other_core()
    me, mine_t = g.index(g.r, g.p), gt.index(gt.r, gt.p)
    rows = q_ref.shape[0]
    own = rows // 2
    nblk = kx_ref.shape[0] // BLK
    per = rows // BLK
    small, width = gm_ref.shape
    order = [(2, 1), (1, 1), (3, 1), (2, 0), (1, 0), (3, 0), (0, 1), (0, 0)]

    def kv_load(n):
        i, s = order[n]
        m = g.index(g.ring(i), g.side(s))
        return pltpu.make_async_copy(kv_hbm.at[m], kv_ref.at[m], lsem.at[3 + n])

    for n in range(8):
        kv_load(n).start()
    everyone = [(lax.rem(g.d + k, 16), g.t) for k in range(1, 16)] + [(g.d, lax.rem(g.t + k, 8)) for k in range(1, 8)]
    greet(everyone)
    take = list(scratch)

    def some(count):
        out = take[:count]
        del take[:count]
        return out

    share = dwo_out.shape[1]
    by_columns = lambda m, cc: dwo.at[:, pl.ds(pl.multiple_of((m * 2 + cc) * share, share), share)]
    keys = Scatter(g, lambda m: part.at[m], rows, some(6), 128)
    downs = CoreScatter(
        g, lambda m, cc: ddown_hbm.at[:, pl.ds(pl.multiple_of((m * 2 + cc) * share, share), share)], ddown_out.shape[0], some(CoreScatter.COUNT), 128)
    dwos = CoreScatter(g, by_columns, dwo_out.shape[0], some(CoreScatter.COUNT), 128)
    tokens = Scatter(gt, lambda m: summed.at[m], small, some(6), 32)
    weights = Scatter(g, lambda m: dw.at[m], dw.shape[1], some(6), 128)
    wide = Gather(gt, lambda m: gb.at[pl.ds(pl.multiple_of(m * small, small), small)], small, some(2))
    layer = Gather(gt, lambda m: lay_out.at[m], small, some(2))
    final = Gather(gt, lambda m: tg_out.at[m], small, some(2))
    sums = RowSums(vec, sums_out, some(8))
    lane_sums = Sums(some(3))
    csem = (css, crs)
    x_load = pltpu.make_async_copy(x_hbm.at[pl.ds(pl.multiple_of(g.t * small, small), small)], x_ref, lsem.at[2])
    x_load.start()

    def n_load(m):
        slot = lax.rem(m, 2)
        return pltpu.make_async_copy(n_hbm.at[:, pl.ds(pl.multiple_of(m * BLK, BLK), BLK)], n_buf.at[slot], lsem.at[slot])

    downs.start()
    lay_out[mine_t] = layr_ref[...]
    gb[pl.ds(pl.multiple_of(mine_t * small, small), small), :] = gbr_ref[...]
    wide.start()
    layer.start()
    augment(meta, lanes_ref, q_ref, qa_ref, kx_ref)
    for a in range(per):
        at = slice(a * BLK, (a + 1) * BLK)
        prod = do_ref[at, :].astype(F32) * o_ref[at, :].astype(F32)
        delta_ref[0:1, at] = jnp.sum(jnp.transpose(prod), axis=0, keepdims=True)
        delta_ref[1:2, at] = lse_ref[a:a + 1, :]
    dq_acc[...] = jnp.zeros_like(dq_acc)
    prefix = meta[nblk]

    def attend(chunk, diagonal):
        for i in range(per):
            at_k = slice(i * BLK, (i + 1) * BLK)
            at_x = pl.ds(pl.multiple_of(chunk * rows + i * BLK, BLK), BLK)
            k = kv_ref[chunk, at_k, :HEAD]
            v = kv_ref[chunk, at_k, HEAD:]
            kk = jnp.concatenate([k, kx_ref[at_x, :]], axis=1)
            turned = jnp.transpose(k.astype(F32)).astype(BF)
            dk = dv = None
            for a in range(per):
                at_q = slice(a * BLK, (a + 1) * BLK)
                q = q_ref[at_q, :]
                do = do_ref[at_q, :]
                p = jnp.exp2(dg(kk, qa_ref[at_q, :], NT) * C1 - delta_ref[1:2, at_q])
                if diagonal and i == a:
                    edge = prefix - 1 - meta[first_block() + a] * BLK
                    lim = jnp.maximum(lax.broadcasted_iota(jnp.int32, (BLK, BLK), 1), edge)
                    p = jnp.where(lax.broadcasted_iota(jnp.int32, (BLK, BLK), 0) <= lim, p, 0.0)
                ds = (p * (dg(v, do, NT) - delta_ref[0:1, at_q])).astype(BF)
                tv = jnp.dot(p.astype(BF), do, preferred_element_type=F32)
                tk = jnp.dot(ds, q, preferred_element_type=F32)
                dv = tv if dv is None else dv + tv
                dk = tk if dk is None else dk + tk
                dq_acc[:, at_q] += jnp.dot(turned, ds, preferred_element_type=F32)
            part[chunk, at_k, :HEAD] = (dk * SCALE).astype(BF)
            part[chunk, at_k, HEAD:] = dv.astype(BF)

    for n in range(8):
        kv_load(n).wait()

    @pl.loop(0, 7)
    def _(k):
        kk = lax.rem(k, 3)
        i = (2 - kk + 3 * (kk // 2)) * (1 - k // 6)
        s = 1 - k // 3 + 2 * (k // 6)
        attend(g.index(g.ring(i), g.p + s * (1 - 2 * g.p)), False)

        @pl.when(k == 0)
        def _():
            keys.send_far(1)
            wide.forward_pair()
            wide.forward(0)

        @pl.when(k == 1)
        def _():
            layer.forward_pair()
            layer.forward(0)

        @pl.when(k == 2)
        def _():
            keys.send_near(1)
            keys.add_near(1)
            wide.forward(1)

        @pl.when(k == 3)
        def _():
            keys.send_far(0)

        @pl.when(k == 4)
        def _():
            layer.forward(1)

        @pl.when(k == 5)
        def _():
            keys.send_near(0)
            keys.add_near(0)

        @pl.when(k == 6)
        def _():
            keys.add_pair()

    n_load(0).start()
    attend(me, True)
    dqkv[:, :HEAD] = jnp.transpose(dq_acc[...] * SCALE).astype(BF)
    wide.arrive(0)
    wide.arrive(1)
    wide.settle()
    span = 512
    for n in range(width // span):
        cols = pl.ds(n * span, span)
        dwo[:, cols] = dg(mixed_ref[...], gb[:, cols], TN).astype(BF)
    dwos.start()

    def keep_keys(at, value):
        dqkv[at, HEAD:] = value.astype(BF)

    keys.finish(keep_keys)

    def project(into, half):
        @pl.loop(0, own // BLK)
        def _(b):
            at = pl.ds(pl.multiple_of(half * own + b * BLK, BLK), BLK)
            for n in range(width // span):
                cols = pl.ds(n * span, span)
                piece = dg(dqkv[at, :], w_ref[cols, :], NT).astype(BF)
                for j in range(BLK // small):
                    into[b * (BLK // small) + j, :, cols] = piece[j * small:(j + 1) * small]

    project(away, 1 - c)
    swap = send(away, arrived, csem, 0, core)
    project(summed, c)
    downs.add()
    swap.wait_recv()

    @pl.loop(0, 8)
    def _(m):
        @pl.loop(0, small // 32)
        def _(n):
            at = pl.ds(pl.multiple_of(n * 32, 32), 32)
            summed[m, at, :] = (summed[m, at, :].astype(F32) + arrived[m, at, :].astype(F32)).astype(BF)

    tokens.start()

    @pl.loop(0, 8)
    def _(m):
        @pl.when(m < 7)
        def _():
            n_load(m + 1).start()

        n_load(m).wait()
        dw[m] = dg(n_buf[lax.rem(m, 2)], dqkv[...], TN).astype(BF)

    weights.start()
    tokens.add_near(1)
    tokens.add_near(0)
    tokens.add_pair()
    dwos.add()
    slot = lane_sums.slots
    slot[g.d] = lane_ref[...]
    local = pl.ds(pl.multiple_of(c * HEAD, HEAD), HEAD)
    slot[g.d, 4:5, local] = jnp.sum(dqkv[:, :HEAD].astype(F32), axis=0, keepdims=True)
    slot[g.d, 5:6, local] = jnp.sum(dqkv[:, 2 * HEAD:].astype(F32), axis=0, keepdims=True)
    lane_sums.start()
    downs.inner.add_near(1)
    downs.inner.add_near(0)

    def keep(at, value):
        total[at, :] = value

    x_load.wait()
    tokens.finish(keep)
    scaled, inverse = norm_rows(x_ref[...].astype(F32))
    grad = total[...]
    tg = gm_ref[...] + norm_back(grad, scaled, inverse, gain_ref[...])
    tg_out[mine_t] = tg.astype(BF)
    final.start()
    vec[...] = early_ref[...]
    vec[4:5, :] = jnp.sum(grad * scaled, axis=0, keepdims=True)
    vec[5:6, :] = jnp.sum(grad, axis=0, keepdims=True)
    sums.start()
    weights.add_near(1)
    weights.add_near(0)
    final.forward_pair()
    final.forward(0)
    dwos.inner.add_near(1)
    dwos.inner.add_near(0)
    downs.inner.add_pair()
    sums.middle()
    weights.add_pair()
    final.forward(1)
    dwos.inner.add_pair()

    def keep_w(at, value):
        mine_w[at, :] = value.astype(BF)

    weights.finish(keep_w)
    part_rows = there_w.shape[0]
    there = send(mine_w.at[pl.ds(pl.multiple_of((1 - c) * part_rows, part_rows), part_rows)], there_w, csem, 1, core)

    def keep_down(at, value):
        ddown_out[at, :] = value

    downs.finish(keep_down)
    sums.finish()

    def keep_o(at, value):
        dwo_out[at, :] = value

    dwos.finish(keep_o)
    kept = mine_w[pl.ds(pl.multiple_of(c * part_rows, part_rows), part_rows), :].astype(F32)
    far = pl.ds(pl.multiple_of((1 - c) * HEAD, HEAD), HEAD)
    there.wait()
    for i, ref in enumerate((dwq_out, dwk_out, dwv_out)):
        ref[:, local] = kept[:, i * HEAD:(i + 1) * HEAD]
        ref[:, far] = there_w[:, i * HEAD:(i + 1) * HEAD].astype(F32)
    lanes_out[...] = lane_sums.finish()
    layer.arrive(0)
    layer.arrive(1)
    layer.settle()
    final.arrive(0)
    final.arrive(1)
    sums.settle()
    final.settle()
    swap.wait_send()


def rear_call(meta, lanes, q, kv, o, do, lse, gb, lay, ddown, mixed, n, w, gm, x, gain, early, lane):
    rows = q.shape[0]
    small, width = gm.shape
    hbm = pl.BlockSpec(memory_space=pl.ANY)
    chunks = (8, small, width)
    wc = 3 * HEAD
    share = width // 16
    head_grad = struct((share, 2 * HEAD), F32)
    return remote_call(
        rear_kernel, "rear", 5,
        (struct(chunks, BF), struct((ddown.shape[0], share), F32), struct((2 * HEAD, share), F32), head_grad, head_grad, head_grad,
         struct(chunks, BF), struct((8, width), F32), struct(lane.shape, F32)),
        [SM, VM, VM, hbm] + [VM] * 5 + [hbm, VM] + [hbm, VM, VM, hbm] + [VM] * 3,
        [pltpu.VMEM(kv.shape, BF), pltpu.VMEM((rows, 2 * HEAD), BF), pltpu.VMEM((8 * rows, HEAD), BF), pltpu.VMEM(kv.shape, BF), pltpu.VMEM((8, rows), F32),
         pltpu.VMEM((HEAD, rows), F32), pltpu.VMEM((8 * small, width), BF), pltpu.VMEM((rows, wc), BF), pltpu.VMEM((2 * HEAD, width), BF),
         pltpu.VMEM((2, rows, BLK), BF), pltpu.VMEM((8, width // 8, wc), BF), pltpu.VMEM(chunks, BF), pltpu.VMEM(chunks, BF),
         pltpu.VMEM(chunks, BF), pltpu.VMEM((small, width), F32), pltpu.VMEM((width // 8, wc), BF), pltpu.VMEM((share, wc), BF),
         pltpu.VMEM((8, width), F32), pltpu.VMEM((small, width), BF), DMA((11,)), DMA((2,)), DMA((2,))]
        + Scatter.scratch(rows, 2 * HEAD) + CoreScatter.scratch(ddown.shape[0], share)
        + CoreScatter.scratch(2 * HEAD, share) + Scatter.scratch(small, width) + Scatter.scratch(width // 8, wc)
        + Gather.scratch() * 3 + RowSums.scratch(width) + Sums.scratch(*lane.shape),
        meta, lanes, q, kv, o, do, lse, gb, lay, ddown, mixed, n, w, gm, x, gain, early, lane)


def finish_kernel(layer, tg, small_ref, lane_ref, up, down, out, wq, wk, wv,
                  layer_out, tg_out, gain1, shift1, qb, vb, ob, gain2, shift2, ub, db, up_out, down_out, out_out, wq_out, wk_out, wv_out,
                  low, high, *scratch):
    ways = ((layer, layer_out), (up, up_out), (down, down_out), (out, out_out), (wq, wq_out), (wk, wk_out), (wv, wv_out))
    buffers, (insem, outsem, tin, tout) = scratch[:7], scratch[7:]
    parts = tg.shape[0]
    loads = [pltpu.make_async_copy(tg.at[k], low.at[k], tin.at[k]) for k in range(parts)]
    saves = [pltpu.make_async_copy(high.at[k], tg_out.at[k], tout.at[k]) for k in range(parts)]
    there = [pltpu.make_async_copy(way[0], buffer, insem.at[k]) for k, (way, buffer) in enumerate(zip(ways, buffers))]
    back = [pltpu.make_async_copy(buffer, way[1], outsem.at[k]) for k, (way, buffer) in enumerate(zip(ways, buffers))]
    for copy in loads + there:
        copy.start()
    for k, ref in ((4, gain1), (5, shift1), (2, ob), (0, gain2), (1, shift2), (3, db)):
        ref[...] = small_ref[k:k + 1, :]
    for j in range(ub.shape[1] // 256):
        ub[:, j * 256:(j + 1) * 256] = lane_ref[j:j + 1, :]
    qb[...] = lane_ref[4:5, :]
    vb[...] = lane_ref[5:6, :]
    for k in range(parts):
        loads[k].wait()
        high[k] = low[k].astype(F32)
        saves[k].start()
    for one, two in zip(there, back):
        one.wait()
        two.start()
    for copy in saves + back:
        copy.wait()


def finish_call(layer, tg, small, lane, hid, rest):
    hbm = pl.BlockSpec(memory_space=pl.ANY)
    width = small.shape[1]
    line = lambda n: struct((1, n), F32)
    return pl.pallas_call(
        finish_kernel,
        out_shape=(struct(layer.shape, BF), struct(tg.shape, F32), line(width), line(width), line(256), line(256), line(width), line(width),
                   line(width), line(hid), line(width)) + tuple(struct(r.shape, F32) for r in rest),
        in_specs=[hbm, hbm, VM, VM] + [hbm] * 6,
        out_specs=(hbm, hbm) + (VM,) * 9 + (hbm,) * 6,
        scratch_shapes=[pltpu.VMEM(tg.shape, BF), pltpu.VMEM(tg.shape, F32), pltpu.VMEM(layer.shape, BF)] + [pltpu.VMEM(r.shape, F32) for r in rest]
        + [DMA((7,)), DMA((7,)), DMA((tg.shape[0],)), DMA((tg.shape[0],))],
        compiler_params=pltpu.CompilerParams(vmem_limit_bytes=60 << 20),
        name="finish",
    )(layer, tg, small, lane, *rest)


def on_device(tokens, first_gain, first_shift, query_weight, query_bias, key_weight, value_weight, value_bias,
              out_weight, out_bias, second_gain, second_shift, up_weight, up_bias, down_weight, down_bias,
              cotangent, prefix, block_order):
    own, width = tokens.shape
    d, t = lax.axis_index("dp"), lax.axis_index("tensor")
    c = lax.rem(d, 2)
    nblk = block_order.shape[0]
    rows = own // 8
    meta = jnp.concatenate([block_order, prefix])
    lanes = jnp.pad(block_order, (0, HEAD - nblk), constant_values=-1).reshape(1, HEAD)
    row = lambda v: v.reshape(1, -1)

    w_all, n_all, q, kv, o, lse, mid, mixed, do, gm, sums, low, lane, layer, dw_up, dw_down, up_grad = front_call(
        meta, lanes, tokens, row(first_gain), row(first_shift), query_weight, key_weight, value_weight, row(query_bias), row(value_bias),
        out_weight, up_weight, down_weight, row(out_bias), row(second_gain), row(second_shift), cotangent, row(up_bias), row(down_bias))
    layer, down_grad, out_grad, dwq, dwk, dwv, tg, small, lane = rear_call(
        meta, lanes, q, kv, o, do, lse, low, layer, dw_down, mixed, n_all.reshape(2 * own, width), w_all, gm,
        tokens, row(first_gain), sums, lane)
    hid = up_weight.shape[1]
    layer, tg, gain1, shift1, qb, vb, ob, gain2, shift2, ub, db, up_grad, down_grad, out_grad, dwq, dwk, dwv = finish_call(
        layer, tg, small, lane, hid, (up_grad, down_grad, out_grad, dwq, dwk, dwv))
    flat = lambda v: v.reshape(-1)
    return (
        layer.reshape(own, width), tg.reshape(own, width), flat(gain1), flat(shift1), dwq, flat(qb), dwk, dwv, flat(vb), out_grad, flat(ob),
        flat(gain2), flat(shift2), up_grad, flat(ub), down_grad, flat(db))


def solution(mesh):
    rows, cols = P("dp", "tensor"), P("tensor", "dp")
    return jax.shard_map(
        on_device,
        mesh=mesh,
        in_specs=(
            P("dp", None), P(), P(), rows, P("tensor"), rows, rows, P("tensor"), cols, P(), P(), P(), rows, P("tensor"),
            cols, P(), P("dp", None), P(), P()),
        out_specs=(
            P("dp", None), P("dp", None), P(), P(), rows, P("tensor"), rows, rows, P("tensor"), cols, P(), P(), P(), rows,
            P("tensor"), cols, P()),
        check_vma=False,
    )
```

```python
import functools
import math

import jax
import jax.numpy as jnp
from jax import lax
from jax.experimental import pallas as pl
from jax.experimental.pallas import tpu as pltpu
from jax.sharding import PartitionSpec as P

HEAD = 128
BLK = 256
GRP = 4
RING = 4
EPS = 1e-05
NEG = -(2.0 ** 100)
LOG2E = math.log2(math.e)
SCALE = 1.0 / math.sqrt(HEAD)
C1 = LOG2E * SCALE
NN = (((1,), (0,)), ((), ()))
NT = (((1,), (1,)), ((), ()))
TN = (((0,), (0,)), ((), ()))
MESH = pl.DeviceIdType.MESH
VM = pl.BlockSpec(memory_space=pltpu.VMEM)
SM = pl.BlockSpec(memory_space=pltpu.SMEM)
BF = jnp.bfloat16
F32 = jnp.float32
DMA = pltpu.SemaphoreType.DMA


def dg(a, b, dims):
    return lax.dot_general(a, b, dims, preferred_element_type=F32)


def struct(shape, dtype):
    return jax.ShapeDtypeStruct(shape, dtype)


class Eight:
    def __init__(self, axis):
        d, t = lax.axis_index("dp"), lax.axis_index("tensor")
        self.axis, self.d, self.t = axis, d, t
        if axis == "dp":
            self.r, self.p = d // 4, lax.rem(d // 2, 2)
        else:
            self.r, self.p = lax.rem(t, 4), t // 4

    def ring(self, i):
        return lax.rem(self.r + i, RING)

    def side(self, s):
        return 1 - self.p if s else self.p

    def index(self, r, p):
        return r * 2 + p if self.axis == "dp" else p * 4 + r

    def device(self, r, p):
        if self.axis == "dp":
            return ((r * 2 + p) * 2 + lax.rem(self.d, 2), self.t)
        return (self.d, p * 4 + r)

    def others(self):
        return [self.device(self.ring(i), self.p) for i in (1, 3)] + [self.device(self.r, 1 - self.p)]


def other_core():
    d = lax.axis_index("dp")
    return (d + 1 - 2 * lax.rem(d, 2), lax.axis_index("tensor"))


def greet(devices):
    barrier = pltpu.get_barrier_semaphore()
    for device in devices:
        pl.semaphore_signal(barrier, inc=1, device_id=device, device_id_type=MESH)
    pl.semaphore_wait(barrier, len(devices))


def send(src, dst, sems, k, device):
    copy = pltpu.make_async_remote_copy(
        src_ref=src, dst_ref=dst, send_sem=sems[0].at[k], recv_sem=sems[1].at[k],
        device_id=device, device_id_type=MESH)
    copy.start()
    return copy


def copy_of(src, dst, sems, k, device):
    return pltpu.make_async_remote_copy(
        src_ref=src, dst_ref=dst, send_sem=sems[0].at[k], recv_sem=sems[1].at[k],
        device_id=device, device_id_type=MESH)


def send(src, dst, sems, k, device):
    copy = copy_of(src, dst, sems, k, device)
    copy.start()
    return copy


class Gather:
    @staticmethod
    def scratch(twin=False):
        return [DMA((9,)), DMA((9,))] + ([DMA((8,)), DMA((8,))] if twin else [])

    def __init__(self, group, place, rows, sems, twin=None, twin_own=True):
        self.g, self.place, self.sems = group, place, sems[:2]
        self.twin, self.twin_sems, self.twin_own = twin, sems[2:4], twin_own
        self.halves = (pl.ds(0, rows // 2), pl.ds(rows // 2, rows // 2))

    def at(self, i, s):
        g = self.g
        return self.place(g.index(g.ring(i), g.side(s)))

    def to(self, i):
        g = self.g
        return g.device(g.ring(i), g.p)

    def pair(self):
        own = self.at(0, 0)
        return copy_of(own, own, self.sems, 0, self.g.device(self.g.r, 1 - self.g.p))

    def near(self, s, way):
        chunk = self.at(0, s)
        return copy_of(chunk, chunk, self.sems, 1 + 4 * s + way, self.to(1 + 2 * way))

    def relay(self, s, way):
        half = self.at(3 - 2 * way, s).at[self.halves[way]]
        return copy_of(half, half, self.sems, 3 + 4 * s + way, self.to(1 + 2 * way))

    def over(self, k, i, s):
        chunk = self.at(i, s)
        return copy_of(chunk, chunk, self.twin_sems, k, self.twin)

    def tell(self, i, s):
        if self.twin is not None and (i or s or self.twin_own):
            self.over(2 * i + s, i, s).start()

    def start(self):
        self.pair().start()
        for way in (0, 1):
            self.near(0, way).start()
        self.tell(0, 0)

    def forward_pair(self):
        self.pair().wait_recv()
        for way in (0, 1):
            self.near(1, way).start()
        self.tell(0, 1)

    def forward(self, s):
        for way in (0, 1):
            self.near(s, way).wait_recv()
            self.relay(s, way).start()
            self.tell(3 - 2 * way, s)

    def arrive(self, s):
        for way in (0, 1):
            self.relay(s, way).wait_recv()
        self.tell(2, s)

    def settle(self):
        self.pair().wait_send()
        for s in (0, 1):
            for way in (0, 1):
                self.near(s, way).wait_send()
                self.relay(s, way).wait_send()
        if self.twin is not None:
            for k in range(0 if self.twin_own else 1, 8):
                self.over(k, 0, 0).wait()

    def rest(self):
        self.forward_pair()
        self.forward(0)
        self.forward(1)
        self.arrive(0)
        self.arrive(1)
        self.settle()


class Scatter:
    COUNT = 6

    @staticmethod
    def scratch(rows, width):
        half = rows // 2
        return [
            pltpu.VMEM((2, 2, half, width), BF), pltpu.VMEM((2, 2, rows, width), BF),
            pltpu.VMEM((rows, width), BF), pltpu.VMEM((rows, width), BF), DMA((13,)), DMA((13,))]

    def __init__(self, group, part, rows, scratch, step):
        self.g, self.part, self.step, self.rows = group, part, step, rows
        self.mid, self.last, self.sum, self.end = scratch[:4]
        self.sems = scratch[4:6]
        self.half = rows // 2
        self.halves = (pl.ds(0, self.half), pl.ds(self.half, self.half))

    def at(self, i, s):
        g = self.g
        return self.part(g.index(g.ring(i), g.side(s)))

    def to(self, way):
        g = self.g
        return g.device(g.ring(1 + 2 * way), g.p)

    def far(self, s, way):
        return copy_of(self.at(2, s).at[self.halves[way]], self.mid.at[s, way], self.sems, 2 * s + way, self.to(way))

    def own(self, s, way):
        half = self.halves[1 - way]
        return copy_of(self.at(1 + 2 * way, s).at[half], self.last.at[s, way, half], self.sems, 4 + 2 * s + way, self.to(way))

    def both(self, s, way):
        return copy_of(self.mid.at[s, way], self.last.at[s, way, self.halves[way]], self.sems, 8 + 2 * s + way, self.to(way))

    def pair(self):
        return copy_of(self.sum, self.end, self.sems, 12, self.g.device(self.g.r, 1 - self.g.p))

    def by_rows(self, rows, body):
        step = min(self.step, rows)

        @pl.loop(0, rows // step)
        def _(n):
            body(pl.multiple_of(n * step, step), step)

    def send_far(self, s):
        for way in (0, 1):
            self.far(s, way).start()

    def send_near(self, s):
        for way in (0, 1):
            self.own(s, way).start()

    def add_near(self, s):
        for way in (0, 1):
            self.far(s, way).wait_recv()
            mine = self.at(1 + 2 * way, s)
            base = way * self.half

            def add(at, n, way=way, mine=mine, base=base):
                rows = pl.ds(at, n)
                total = mine[pl.ds(base + at, n), :].astype(F32) + self.mid[s, way, rows, :].astype(F32)
                self.mid[s, way, rows, :] = total.astype(BF)

            self.by_rows(self.half, add)
            self.both(s, way).start()

    def arrived(self, s):
        for way in (0, 1):
            self.own(s, way).wait_recv()
            self.both(s, way).wait_recv()

    def add_pair(self):
        self.arrived(1)
        mine = self.at(0, 1)

        def add(at, n):
            rows = pl.ds(at, n)
            total = mine[rows, :].astype(F32) + self.last[1, 0, rows, :].astype(F32) + self.last[1, 1, rows, :].astype(F32)
            self.sum[rows, :] = total.astype(BF)

        self.by_rows(self.rows, add)
        self.pair().start()

    def start(self):
        for s in (1, 0):
            self.send_far(s)
            self.send_near(s)

    def forward(self):
        self.add_near(1)
        self.add_near(0)
        self.add_pair()

    def finish(self, store):
        self.arrived(0)
        self.pair().wait_recv()
        mine = self.at(0, 0)

        def add(at, n):
            rows = pl.ds(at, n)
            total = mine[rows, :].astype(F32) + self.last[0, 0, rows, :].astype(F32) + self.last[0, 1, rows, :].astype(F32)
            store(rows, total + self.end[rows, :].astype(F32))

        self.by_rows(self.rows, add)
        self.pair().wait_send()
        for s in (0, 1):
            for way in (0, 1):
                self.far(s, way).wait_send()
                self.own(s, way).wait_send()
                self.both(s, way).wait_send()


class CoreScatter:
    COUNT = 11

    @staticmethod
    def scratch(rows, width):
        return [pltpu.VMEM((8, rows, width), BF), DMA((8,)), DMA((8,)), pltpu.VMEM((2, rows, width), BF), DMA((2,))] + Scatter.scratch(rows, width)

    def __init__(self, group, part, rows, scratch, step):
        self.part, self.total, self.sems, self.buf, self.load_sems = part, scratch[0], scratch[1:3], scratch[3], scratch[4]
        self.c = lax.rem(group.d, 2)
        self.rows, self.step = rows, step
        self.inner = Scatter(group, lambda m: self.total.at[m], rows, scratch[5:], step)

    def swap(self, m):
        return copy_of(self.part(m, 1 - self.c), self.total.at[m], self.sems, m, other_core())

    def load(self, m):
        slot = lax.rem(m, 2)
        return pltpu.make_async_copy(self.part(m, self.c), self.buf.at[slot], self.load_sems.at[slot])

    def start(self):
        for m in range(8):
            self.swap(m).start()
        self.load(0).start()

    def add(self):
        step = self.step

        @pl.loop(0, 8)
        def _(m):
            @pl.when(m < 7)
            def _():
                self.load(m + 1).start()

            self.load(m).wait()
            self.swap(m).wait_recv()
            slot = lax.rem(m, 2)

            @pl.loop(0, self.rows // step)
            def _(n):
                at = pl.ds(pl.multiple_of(n * step, step), step)
                self.total[m, at, :] = (self.buf[slot, at, :].astype(F32) + self.total[m, at, :].astype(F32)).astype(BF)

        self.inner.start()

    def finish(self, store):
        self.inner.finish(store)
        for m in range(8):
            self.swap(m).wait_send()


class RowSums:
    @staticmethod
    def scratch(width):
        cols = width // 8
        return [pltpu.VMEM((8, 8, cols), F32), pltpu.VMEM((16, 8, cols), F32)] + [DMA((7,)), DMA((7,)), DMA((15,)), DMA((15,)), DMA((7,)), DMA((7,))]

    def __init__(self, rows, out, scratch):
        self.rows, self.out = rows, out
        self.one, self.two = scratch[:2]
        self.sems = (scratch[2:4], scratch[4:6], scratch[6:8])
        self.d, self.t = lax.axis_index("dp"), lax.axis_index("tensor")
        self.cols = rows.shape[1] // 8

    def columns(self, t):
        return pl.ds(pl.multiple_of(t * self.cols, self.cols), self.cols)

    def first(self, k):
        other = lax.rem(self.t + k, 8)
        return copy_of(self.rows.at[:, self.columns(other)], self.one.at[self.t], self.sems[0], k - 1, (self.d, other))

    def second(self, k):
        own = self.two.at[self.d]
        return copy_of(own, own, self.sems[1], k - 1, (lax.rem(self.d + k, 16), self.t))

    def third(self, k):
        own = self.out.at[:, self.columns(self.t)]
        return copy_of(own, own, self.sems[2], k - 1, (self.d, lax.rem(self.t + k, 8)))

    def run(self, step, last):
        @pl.loop(1, last)
        def _(k):
            step(k)

    def start(self):
        self.run(lambda k: self.first(k).start(), 8)
        self.one[self.t] = self.rows[:, self.columns(self.t)]

    def middle(self):
        self.run(lambda k: self.first(k).wait(), 8)
        total = self.one[0]
        for k in range(1, 8):
            total = total + self.one[k]
        self.two[self.d] = total
        self.run(lambda k: self.second(k).start(), 16)

    def finish(self):
        self.run(lambda k: self.second(k).wait(), 16)
        total = self.two[0]
        for k in range(1, 16):
            total = total + self.two[k]
        self.out[:, self.columns(self.t)] = total
        self.run(lambda k: self.third(k).start(), 8)

    def settle(self):
        self.run(lambda k: self.third(k).wait(), 8)


class Sums:
    @staticmethod
    def scratch(rows, width):
        return [pltpu.VMEM((16, rows, width), F32), DMA((15,)), DMA((15,))]

    def __init__(self, scratch):
        self.slots, self.sems = scratch[0], scratch[1:3]
        self.d, self.t = lax.axis_index("dp"), lax.axis_index("tensor")

    def copy(self, k):
        own = self.slots.at[self.d]
        return copy_of(own, own, self.sems, k - 1, (lax.rem(self.d + k, 16), self.t))

    def start(self):
        @pl.loop(1, 16)
        def _(k):
            self.copy(k).start()

    def finish(self):
        @pl.loop(1, 16)
        def _(k):
            self.copy(k).wait()
        total = self.slots[0]
        for k in range(1, 16):
            total = total + self.slots[k]
        return total


def remote_call(kernel, name, cid, outs, ins, scratch, *args, out_specs=None):
    return pl.pallas_call(
        kernel, out_shape=outs, in_specs=ins,
        out_specs=jax.tree.map(lambda _: VM, outs) if out_specs is None else out_specs,
        scratch_shapes=scratch, name=name,
        compiler_params=pltpu.CompilerParams(collective_id=cid, has_side_effects=True, vmem_limit_bytes=60 << 20),
    )(*args)


def chip_members():
    d, t = lax.axis_index("dp"), lax.axis_index("tensor")
    c = lax.rem(d, 2)
    out = []
    for dt in range(8):
        for dc in range(2):
            if dt or dc:
                tt = lax.rem(t + dt, 8)
                cc = lax.rem(c + dc, 2)
                out.append((tt, cc, (d - c + cc, tt)))
    return out


def norm_rows(values):
    average = jnp.mean(values, axis=-1, keepdims=True)
    centred = values - average
    variance = jnp.mean(centred * centred, axis=-1, keepdims=True)
    inverse = lax.rsqrt(variance + EPS)
    return centred * inverse, inverse


def norm_back(grad, scaled, inverse, gain):
    e = grad * gain
    first = jnp.mean(e, axis=-1, keepdims=True)
    second = jnp.mean(e * scaled, axis=-1, keepdims=True)
    return inverse * (e - first - scaled * second)


def augment(meta, edge_ref, lanes_ref, q_ref, qa_ref, kx_ref):
    rows = q_ref.shape[0]
    nblk = kx_ref.shape[0] // BLK
    prefix = edge_ref[0]
    for a in range(rows // BLK):
        at = slice(a * BLK, (a + 1) * BLK)
        hidden = jnp.where(lanes_ref[...] > meta[first_block() + a], NEG, 0.0)
        qa_ref[at, :HEAD] = q_ref[at, :]
        qa_ref[at, HEAD:] = jnp.zeros((BLK, HEAD), BF)
        qa_ref[at, HEAD:HEAD + nblk] = jnp.broadcast_to(hidden, (BLK, nblk)).astype(BF)
    lane = lax.broadcasted_iota(jnp.int32, (BLK, HEAD), 1)
    inside = lax.broadcasted_iota(jnp.int32, (BLK, HEAD), 0)

    @pl.loop(0, nblk)
    def _(b):
        late = (lane == b) & (inside >= prefix - meta[b] * BLK)
        kx_ref[pl.ds(pl.multiple_of(b * BLK, BLK), BLK), :] = jnp.where(late, 1.0, 0.0).astype(BF)


def first_block():
    return lax.axis_index("dp") // 2 * 4


def front_kernel(meta, edge_ref, lanes_ref, x_ref, gain1_ref, shift1_ref, wq_ref, wk_ref, wv_ref, qb_ref, vb_ref, wo_ref, wu_ref, wd_ref,
                 bias_ref, gain2_ref, shift2_ref, cot_ref, ub_ref, db_ref,
                 w_hbm, n_hbm, q_out, kv_hbm, o_ref, lse_ref, mid_out, own_out, do_out, gm_out, sums_out, low_out, lane_out, lay_out, du_hbm, dd_hbm, dup_out,
                 w_vm, n_vm, kv_vm, out_vm, up_vm, down_vm, wsh, mixed, n2, gsum, colsum,
                 lsem, css, crs, ass, ars, hss, hrs, *sems):
    gd, gt = Eight("dp"), Eight("tensor")
    t = gt.t
    c = lax.rem(gd.d, 2)
    core = other_core()
    members = chip_members()
    me = gd.index(gd.r, gd.p)
    own = x_ref.shape[0]
    rows = 2 * own
    nblk = 8 * rows // BLK
    per = rows // BLK
    shard = wq_ref.shape[0]
    half = out_vm.shape[1] // 2
    hid = wd_ref.shape[0]
    small = mid_out.shape[0]
    csem, asem = (css, crs), (ass, ars)
    for h in range(2):
        cols = slice(h * HEAD, (h + 1) * HEAD)
        for i, ref in enumerate((wq_ref, wk_ref, wv_ref)):
            wsh[h, :, i * HEAD:(i + 1) * HEAD] = ref[:, cols].astype(BF)
    greet([m[2] for m in members] + gd.others())

    w_place = lambda m: w_vm.at[pl.ds(pl.multiple_of(m * 2 * shard, 2 * shard), 2 * shard)]
    row_of = lambda m: pl.ds(pl.multiple_of((m * 2 + c) * shard, shard), shard)
    mine = row_of(me)
    swap = send(wsh.at[1 - c], w_vm.at[mine], csem, 0, core)
    w_vm[mine, :] = wsh[c]
    qkv = Gather(gd, w_place, 2 * shard, sems[0:2])
    keys = Gather(gd, lambda m: kv_vm.at[m], rows, sems[2:4])
    outs = Gather(gd, lambda m: out_vm.at[t, :, row_of(m)], 2 * half, sems[4:8], core)
    ups = Gather(gd, lambda m: up_vm.at[row_of(m)], shard, sems[8:12], core)
    downs = Gather(gd, lambda m: down_vm.at[:, row_of(m)], hid, sems[12:16], core)
    wide = Gather(gt, lambda m: out_vm.at[m, pl.ds(pl.multiple_of(c * half, half), half)], half, sems[16:20], core, twin_own=False)
    normed = Gather(gt, lambda m: n2.at[pl.ds(pl.multiple_of(m * small, small), small)], small, sems[20:22])
    spare = lambda k: (lambda m: n_vm.at[k, pl.ds(pl.multiple_of(m * small, small), small)])
    back = Scatter(gt, spare(0), small, sems[22:28], 32)
    result = Scatter(gt, spare(1), small, sems[28:34], 32)
    grads = CoreScatter(gd, lambda m, cc: du_hbm.at[pl.ds(pl.multiple_of((m * 2 + cc) * shard, shard), shard)], shard, sems[34:45], 32)
    swap.wait_recv()
    qkv.start()

    def norm_part(k):
        step = 32

        @pl.loop(0, own // 2 // step)
        def _(n):
            at = pl.ds(pl.multiple_of(k * (own // 2) + n * step, step), step)
            scaled, _ = norm_rows(x_ref[at, :].astype(F32))
            n_vm[c, at, :] = (scaled * gain1_ref[...] + shift1_ref[...]).astype(BF)

        at = pl.ds(k * (own // 2), own // 2)
        return send(n_vm.at[c, at], n_vm.at[c, at], csem, 1 + k, core)

    there = [norm_part(0)]
    qkv.forward_pair()
    qkv.forward(0)
    out_vm[t, :, mine] = wo_ref[...].astype(BF)
    outs.start()
    there.append(norm_part(1))
    qkv.forward(1)
    up_vm[mine, :] = wu_ref[...].astype(BF)
    down_vm[:, mine] = wd_ref[...].astype(BF)
    for copy in there:
        copy.wait_recv()
    local = pl.ds(pl.multiple_of(c * HEAD, HEAD), HEAD)
    bias_q, bias_v = qb_ref[:, local], vb_ref[:, local]

    def project(sums):
        def term(i, s, first=False):
            m = gd.index(gd.ring(i), gd.side(s))
            cols = pl.ds(pl.multiple_of(m * 2 * shard, 2 * shard), 2 * shard)
            for h in range(2):
                piece = dg(n_vm[h, :, cols], w_vm[cols, :], NN)
                at = slice(h * own, (h + 1) * own)
                sums[at, :] = piece if first else sums[at, :] + piece

        term(0, 0, True)
        for i, s in ((1, 0), (3, 0), (0, 1)):
            term(i, s)
        outs.forward_pair()
        outs.forward(0)
        for i in (1, 3):
            term(i, 1)
        qkv.arrive(0)
        term(2, 0)
        qkv.arrive(1)
        term(2, 1)
        q_out[...] = (sums[:, :HEAD] + bias_q).astype(BF)
        kv_vm[me, :, :HEAD] = sums[:, HEAD:2 * HEAD].astype(BF)
        kv_vm[me, :, HEAD:] = (sums[:, 2 * HEAD:] + bias_v).astype(BF)

    pl.run_scoped(project, pltpu.VMEM((rows, 3 * HEAD), F32))
    keys.start()
    outs.forward(1)
    saves = [pltpu.make_async_copy(w_vm, w_hbm, lsem.at[0]), pltpu.make_async_copy(n_vm, n_hbm, lsem.at[1])]
    for save in saves:
        save.start()
    def attention(qa_ref, kx_ref, m_ref, acc_ref):
        augment(meta, edge_ref, lanes_ref, q_out, qa_ref, kx_ref)
        outs.arrive(0)
        outs.arrive(1)
        outs.settle()
        wide.start()
        m_ref[...] = jnp.full_like(m_ref, -1e30)
        acc_ref[...] = jnp.zeros_like(acc_ref)
        ones = jnp.ones((BLK, HEAD), BF)
        prefix = edge_ref[0]

        def attend(chunk, diagonal):
            ks, vs = [], []
            for i in range(per):
                at = pl.ds(pl.multiple_of(chunk * rows + i * BLK, BLK), BLK)
                ks.append(jnp.concatenate([kv_vm[chunk, i * BLK:(i + 1) * BLK, :HEAD], kx_ref[at, :]], axis=1))
                vs.append(jnp.concatenate([kv_vm[chunk, i * BLK:(i + 1) * BLK, HEAD:], ones], axis=1))
            for a in range(per):
                take = slice(a * BLK, (a + 1) * BLK)
                q = qa_ref[take, :]
                ss = [dg(q, k, NT) for k in ks]
                if diagonal:
                    edge = prefix - 1 - meta[first_block() + a] * BLK
                    lim = jnp.maximum(lax.broadcasted_iota(jnp.int32, (BLK, BLK), 0), edge)
                    key = lax.broadcasted_iota(jnp.int32, (BLK, BLK), 1)
                    ss[a] = jnp.where(key <= lim, ss[a], NEG)
                top = ss[0]
                for s in ss[1:]:
                    top = jnp.maximum(top, s)
                old = m_ref[take, :1]
                new = jnp.maximum(old, jnp.max(top, axis=1, keepdims=True) * C1)
                alpha = jnp.exp2(old - new)
                add = None
                for s, v in zip(ss, vs):
                    term = jnp.dot(jnp.exp2(s * C1 - new).astype(BF), v, preferred_element_type=F32)
                    add = term if add is None else add + term
                acc_ref[take, :] = acc_ref[take, :] * alpha + add
                m_ref[take, :] = jnp.broadcast_to(new, (BLK, HEAD))

        attend(me, True)

        @pl.loop(1, 8)
        def _(k):
            kk = lax.rem(k, 4)
            i, s = kk + kk // 2 - 2 * (kk // 3), k // 4

            @pl.when(k == 1)
            def _():
                keys.forward_pair()
                keys.forward(0)

            @pl.when(k == 2)
            def _():
                wide.forward_pair()
                wide.forward(0)

            @pl.when(k == 3)
            def _():
                keys.arrive(0)

            @pl.when(k == 5)
            def _():
                keys.forward(1)
                wide.forward(1)
                ups.start()

            @pl.when(k == 7)
            def _():
                keys.arrive(1)

            attend(gd.index(gd.ring(i), gd.p + s * (1 - 2 * gd.p)), False)

        for a in range(per):
            at = slice(a * BLK, (a + 1) * BLK)
            total = acc_ref[at, HEAD:]
            o_ref[at, :] = (acc_ref[at, :HEAD] / total).astype(BF)
            lse_ref[a:a + 1, :] = jnp.transpose(m_ref[at, :] + jnp.log2(total))[:1, :]

    pl.run_scoped(
        attention, pltpu.VMEM((rows, 2 * HEAD), BF), pltpu.VMEM((8 * rows, HEAD), BF), pltpu.VMEM((rows, HEAD), F32), pltpu.VMEM((rows, 2 * HEAD), F32))
    head = pl.ds(pl.multiple_of((2 * t + c) * HEAD, HEAD), HEAD)
    copies = []
    for k, (tt, cc, device) in enumerate(members):
        take = pl.ds(pl.multiple_of(cc * own + tt * small, small), small)
        copies.append(send(o_ref.at[take], mixed.at[:, head], asem, k, device))
    copies.append(send(o_ref.at[pl.ds(pl.multiple_of((1 - c) * own, own), own)], own_out.at[:, local], asem, 15, core))
    keys.settle()
    save = pltpu.make_async_copy(kv_vm, kv_hbm, lsem.at[2])
    save.start()
    saves.append(save)
    downs.start()
    mixed[:, head] = o_ref[pl.ds(pl.multiple_of(c * own + t * small, small), small), :]
    own_out[:, local] = o_ref[pl.ds(pl.multiple_of(c * own, own), own), :]
    ups.forward_pair()
    ups.forward(0)
    wide.arrive(0)
    wide.arrive(1)
    wide.settle()
    ups.forward(1)
    downs.forward_pair()
    for copy in copies:
        copy.wait_recv()
    span = 512
    x_rows = pl.ds(pl.multiple_of(t * small, small), small)
    for n in range(mid_out.shape[1] // span):
        cols = pl.ds(n * span, span)
        total = None
        for k in range(8):
            term = dg(mixed[:, k * 256:(k + 1) * 256], out_vm[k, :, cols], NN)
            total = term if total is None else total + term
        mid_out[:, cols] = total + (x_ref[x_rows, cols].astype(F32) + bias_ref[:, cols])
    scaled, _ = norm_rows(mid_out[...])
    n2[pl.ds(pl.multiple_of(t * small, small), small), :] = (scaled * gain2_ref[...] + shift2_ref[...]).astype(BF)
    normed.start()
    downs.forward(0)
    ups.arrive(0)
    ups.arrive(1)
    normed.forward_pair()
    normed.forward(0)
    downs.forward(1)
    normed.forward(1)
    ups.settle()
    downs.arrive(0)
    downs.arrive(1)
    downs.settle()
    saves.pop(1).wait()
    for copy in there:
        copy.wait_send()
    blocks = [(slice(n * span, (n + 1) * span)) for n in range(hid // span)]
    wide_blocks = [(slice(n * span, (n + 1) * span)) for n in range(n2.shape[1] // span)]

    def feed_forward(gh, hidden, gp, du_buf, dd_buf):
        @pl.loop(0, own // BLK)
        def _(b):
            at = pl.ds(pl.multiple_of(b * BLK, BLK), BLK)
            for cols in blocks:
                gh[at, cols] = dg(cot_ref[at, :], down_vm[cols, :], NT)

        normed.arrive(0)
        normed.arrive(1)
        normed.settle()
        colsum[...] = jnp.zeros_like(colsum)

        @pl.loop(0, own // BLK)
        def _(b):
            at = pl.ds(pl.multiple_of(b * BLK, BLK), BLK)
            for cols in blocks:
                pre = dg(n2[at, :], up_vm[:, cols], NN) + ub_ref[:, cols]
                half_erf = 0.5 + 0.5 * lax.erf(pre * math.sqrt(0.5))
                hidden[at, cols] = (pre * half_erf).astype(BF)
                slope = half_erf + pre * jnp.exp(-0.5 * pre * pre) * (1.0 / math.sqrt(2.0 * math.pi))
                low = (gh[at, cols] * slope).astype(BF)
                gp[at, cols] = low
                colsum[0:1, cols] += jnp.sum(low.astype(F32), axis=0, keepdims=True)
            for cols in wide_blocks:
                n_vm[0, at, cols] = dg(gp[at, :], up_vm[cols, :], NT).astype(BF)

        back.start()

        def du_save(m):
            slot = lax.rem(m, 2)
            return pltpu.make_async_copy(du_buf.at[slot], du_hbm.at[pl.ds(pl.multiple_of(m * BLK, BLK), BLK)], lsem.at[3 + slot])

        def dd_save(m):
            slot = lax.rem(m, 2)
            return pltpu.make_async_copy(dd_buf.at[slot], dd_hbm.at[:, pl.ds(pl.multiple_of(m * BLK, BLK), BLK)], lsem.at[5 + slot])

        def blocks_of(save, buf, value):
            @pl.loop(0, 8)
            def _(m):
                @pl.when(m > 1)
                def _():
                    save(m - 2).wait()

                buf[lax.rem(m, 2)] = value(pl.ds(pl.multiple_of(m * BLK, BLK), BLK)).astype(BF)
                save(m).start()

        blocks_of(du_save, du_buf, lambda cols: dg(n2[:, cols], gp[...], TN))
        back.add_near(1)
        back.add_near(0)
        du_save(6).wait()
        du_save(7).wait()
        grads.start()

        @pl.loop(0, own // BLK)
        def _(b):
            at = pl.ds(pl.multiple_of(b * BLK, BLK), BLK)
            for cols in wide_blocks:
                n_vm[1, at, cols] = dg(hidden[at, :], down_vm[:, cols], NN).astype(BF)

        back.add_pair()
        result.start()
        grads.add()
        blocks_of(dd_save, dd_buf, lambda cols: dg(hidden[...], cot_ref[:, cols], TN))
        dd_save(6).wait()
        dd_save(7).wait()

    pl.run_scoped(
        feed_forward, pltpu.VMEM((own, hid), F32), pltpu.VMEM((own, hid), BF), pltpu.VMEM((own, hid), BF), pltpu.VMEM((2, BLK, hid), BF),
        pltpu.VMEM((2, hid, BLK), BF))

    def keep(at, value):
        gsum[at, :] = value

    back.finish(keep)
    scaled, inverse = norm_rows(mid_out[...])
    grad = gsum[...]
    g_rows = cot_ref[x_rows, :].astype(F32)
    gm = g_rows + norm_back(grad, scaled, inverse, gain2_ref[...])
    gm_out[...] = gm
    low = gm.astype(BF)
    low_out[...] = low
    for k in range(8):
        mixed[:, k * 256:(k + 1) * 256] = dg(low, out_vm[k], NT).astype(BF)
    hsem = (hss, hrs)
    take = pl.ds(pl.multiple_of(c * own + t * small, small), small)
    heads = []
    for k, (tt, cc, device) in enumerate(members):
        cols = pl.ds(pl.multiple_of((2 * tt + cc) * HEAD, HEAD), HEAD)
        heads.append(send(mixed.at[:, cols], do_out.at[take], hsem, k, device))
    do_out[take, :] = mixed[:, head]
    result.add_near(1)
    result.add_near(0)
    grads.inner.add_near(1)
    grads.inner.add_near(0)
    result.add_pair()
    sums_out[...] = jnp.zeros_like(sums_out)
    sums_out[0:1, :] = jnp.sum(grad * scaled, axis=0, keepdims=True)
    sums_out[1:2, :] = jnp.sum(grad, axis=0, keepdims=True)
    sums_out[2:3, :] = jnp.sum(low.astype(F32), axis=0, keepdims=True)
    sums_out[3:4, :] = jnp.sum(g_rows, axis=0, keepdims=True)
    lane_out[...] = jnp.zeros_like(lane_out)
    for j in range(hid // 256):
        lane_out[j:j + 1, :] = colsum[0:1, j * 256:(j + 1) * 256]
    grads.inner.add_pair()

    def lay(at, value):
        lay_out[at, :] = (mid_out[at, :] + (value + db_ref[...])).astype(BF)

    result.finish(lay)

    def keep_up(at, value):
        dup_out[at, :] = value

    grads.finish(keep_up)
    qkv.settle()
    swap.wait_send()
    for copy in copies:
        copy.wait_send()
    for save in saves:
        save.wait()
    for copy in heads:
        copy.wait()


def front_call(meta, edge, lanes, x, gain1, shift1, wq, wk, wv, qb, vb, wo, wu, wd, bias, gain2, shift2, cot, ub, db):
    own, width = x.shape
    rows, shard, hid, small = 2 * own, wq.shape[0], wu.shape[1], own // 8
    hbm = pl.BlockSpec(memory_space=pl.ANY)
    big = [(width, 3 * HEAD), (2, own, width), (8, rows, 2 * HEAD), (8, 2 * HEAD, width), (width, hid), (hid, width)]
    w, n, kv, out, up, down = (struct(s, BF) for s in big)
    outs = (w, n, struct((rows, HEAD), BF), kv, struct((rows, HEAD), BF), struct((rows // BLK, BLK), F32),
            struct((small, width), F32), struct((own, 2 * HEAD), BF), struct((rows, HEAD), BF), struct((small, width), F32),
            struct((8, width), F32), struct((small, width), BF), struct((8, 256), F32), struct((small, width), BF), up, down, struct((shard, hid), F32))
    return remote_call(
        front_kernel, "front", 1, outs, [SM, SM] + [VM] * 18,
        [pltpu.VMEM(s, BF) for s in big]
        + [pltpu.VMEM((2, shard, 3 * HEAD), BF), pltpu.VMEM((small, width), BF), pltpu.VMEM((own, width), BF),
           pltpu.VMEM((small, width), F32), pltpu.VMEM((8, hid), F32),
           DMA((7,)), DMA((3,)), DMA((3,)), DMA((16,)), DMA((16,)), DMA((15,)), DMA((15,))]
        + Gather.scratch() * 2 + Gather.scratch(True) * 4 + Gather.scratch() + Scatter.scratch(small, width) * 2 + CoreScatter.scratch(shard, hid),
        meta, edge, lanes, x, gain1, shift1, wq, wk, wv, qb, vb, wo, wu, wd, bias, gain2, shift2, cot, ub, db,
        out_specs=(hbm, hbm, VM, hbm) + (VM,) * 10 + (hbm, hbm, VM))


def rear_kernel(meta, edge_ref, lanes_ref, q_ref, kv_hbm, o_ref, do_ref, lse_ref, gbr_ref, layr_ref, ddown_hbm,
                mixed_ref, n_hbm, w_ref, gm_ref, x_hbm, gain_ref, early_ref, lane_ref,
                lay_out, ddown_out, dwo_out, dwq_out, dwk_out, dwv_out, tg_out, sums_out, lanes_out,
                kv_ref, qa_ref, kx_ref, part, delta_ref, dq_acc, gb, dqkv, dwo, n_buf, dw, away, arrived, summed, total, mine_w, there_w, vec, x_ref,
                lsem, css, crs, *scratch):
    g, gt = Eight("dp"), Eight("tensor")
    c = lax.rem(g.d, 2)
    core = other_core()
    me, mine_t = g.index(g.r, g.p), gt.index(gt.r, gt.p)
    rows = q_ref.shape[0]
    own = rows // 2
    nblk = kx_ref.shape[0] // BLK
    per = rows // BLK
    small, width = gm_ref.shape
    order = [(2, 1), (1, 1), (3, 1), (2, 0), (1, 0), (3, 0), (0, 1), (0, 0)]

    def kv_load(n):
        i, s = order[n]
        m = g.index(g.ring(i), g.side(s))
        return pltpu.make_async_copy(kv_hbm.at[m], kv_ref.at[m], lsem.at[3 + n])

    for n in range(8):
        kv_load(n).start()
    everyone = [(lax.rem(g.d + k, 16), g.t) for k in range(1, 16)] + [(g.d, lax.rem(g.t + k, 8)) for k in range(1, 8)]
    greet(everyone)
    take = list(scratch)

    def some(count):
        out = take[:count]
        del take[:count]
        return out

    share = dwo_out.shape[1]
    by_columns = lambda m, cc: dwo.at[:, pl.ds(pl.multiple_of((m * 2 + cc) * share, share), share)]
    keys = Scatter(g, lambda m: part.at[m], rows, some(6), 128)
    downs = CoreScatter(
        g, lambda m, cc: ddown_hbm.at[:, pl.ds(pl.multiple_of((m * 2 + cc) * share, share), share)], ddown_out.shape[0], some(CoreScatter.COUNT), 128)
    dwos = CoreScatter(g, by_columns, dwo_out.shape[0], some(CoreScatter.COUNT), 128)
    tokens = Scatter(gt, lambda m: summed.at[m], small, some(6), 32)
    weights = Scatter(g, lambda m: dw.at[m], dw.shape[1], some(6), 128)
    wide = Gather(gt, lambda m: gb.at[pl.ds(pl.multiple_of(m * small, small), small)], small, some(2))
    layer = Gather(gt, lambda m: lay_out.at[m], small, some(2))
    final = Gather(gt, lambda m: tg_out.at[m], small, some(2))
    sums = RowSums(vec, sums_out, some(8))
    lane_sums = Sums(some(3))
    csem = (css, crs)
    x_load = pltpu.make_async_copy(x_hbm.at[pl.ds(pl.multiple_of(g.t * small, small), small)], x_ref, lsem.at[2])
    x_load.start()

    def n_load(m):
        slot = lax.rem(m, 2)
        return pltpu.make_async_copy(n_hbm.at[:, pl.ds(pl.multiple_of(m * BLK, BLK), BLK)], n_buf.at[slot], lsem.at[slot])

    downs.start()
    lay_out[mine_t] = layr_ref[...]
    gb[pl.ds(pl.multiple_of(mine_t * small, small), small), :] = gbr_ref[...]
    wide.start()
    layer.start()
    augment(meta, edge_ref, lanes_ref, q_ref, qa_ref, kx_ref)
    for a in range(per):
        at = slice(a * BLK, (a + 1) * BLK)
        prod = do_ref[at, :].astype(F32) * o_ref[at, :].astype(F32)
        delta_ref[0:1, at] = jnp.sum(jnp.transpose(prod), axis=0, keepdims=True)
        delta_ref[1:2, at] = lse_ref[a:a + 1, :]
    dq_acc[...] = jnp.zeros_like(dq_acc)
    prefix = edge_ref[0]

    def attend(chunk, diagonal):
        k = kv_ref[chunk, :, :HEAD]
        v = kv_ref[chunk, :, HEAD:]
        kk = jnp.concatenate([k, kx_ref[pl.ds(pl.multiple_of(chunk * rows, rows), rows), :]], axis=1)
        turned = jnp.transpose(k.astype(F32)).astype(BF)
        dk = dv = None
        for a in range(per):
            at_q = slice(a * BLK, (a + 1) * BLK)
            q = q_ref[at_q, :]
            do = do_ref[at_q, :]
            p = jnp.exp2(dg(kk, qa_ref[at_q, :], NT) * C1 - delta_ref[1:2, at_q])
            if diagonal:
                edge = prefix - 1 - meta[first_block() + a] * BLK
                lim = jnp.maximum(lax.broadcasted_iota(jnp.int32, (BLK, BLK), 1), edge)
                mid = jnp.where(lax.broadcasted_iota(jnp.int32, (BLK, BLK), 0) <= lim, p[a * BLK:(a + 1) * BLK], 0.0)
                p = jnp.concatenate([p[b * BLK:(b + 1) * BLK] if b != a else mid for b in range(per)], axis=0)
            ds = (p * (dg(v, do, NT) - delta_ref[0:1, at_q])).astype(BF)
            tv = jnp.dot(p.astype(BF), do, preferred_element_type=F32)
            tk = jnp.dot(ds, q, preferred_element_type=F32)
            dv = tv if dv is None else dv + tv
            dk = tk if dk is None else dk + tk
            dq_acc[:, at_q] += jnp.dot(turned, ds, preferred_element_type=F32)
        part[chunk, :, :HEAD] = (dk * SCALE).astype(BF)
        part[chunk, :, HEAD:] = dv.astype(BF)

    for n in range(8):
        kv_load(n).wait()

    @pl.loop(0, 7)
    def _(k):
        kk = lax.rem(k, 3)
        i = (2 - kk + 3 * (kk // 2)) * (1 - k // 6)
        s = 1 - k // 3 + 2 * (k // 6)
        attend(g.index(g.ring(i), g.p + s * (1 - 2 * g.p)), False)

        @pl.when(k == 0)
        def _():
            keys.send_far(1)
            wide.forward_pair()
            wide.forward(0)

        @pl.when(k == 1)
        def _():
            layer.forward_pair()
            layer.forward(0)

        @pl.when(k == 2)
        def _():
            keys.send_near(1)
            keys.add_near(1)
            wide.forward(1)

        @pl.when(k == 3)
        def _():
            keys.send_far(0)

        @pl.when(k == 4)
        def _():
            layer.forward(1)

        @pl.when(k == 5)
        def _():
            keys.send_near(0)
            keys.add_near(0)

        @pl.when(k == 6)
        def _():
            keys.add_pair()

    n_load(0).start()
    attend(me, True)
    dqkv[:, :HEAD] = jnp.transpose(dq_acc[...] * SCALE).astype(BF)
    wide.arrive(0)
    wide.arrive(1)
    wide.settle()
    span = 512
    for n in range(width // span):
        cols = pl.ds(n * span, span)
        dwo[:, cols] = dg(mixed_ref[...], gb[:, cols], TN).astype(BF)
    dwos.start()

    def keep_keys(at, value):
        dqkv[at, HEAD:] = value.astype(BF)

    keys.finish(keep_keys)

    def project(into, half):
        @pl.loop(0, own // BLK)
        def _(b):
            at = pl.ds(pl.multiple_of(half * own + b * BLK, BLK), BLK)
            for n in range(width // span):
                cols = pl.ds(n * span, span)
                piece = dg(dqkv[at, :], w_ref[cols, :], NT).astype(BF)
                for j in range(BLK // small):
                    into[b * (BLK // small) + j, :, cols] = piece[j * small:(j + 1) * small]

    project(away, 1 - c)
    swap = send(away, arrived, csem, 0, core)
    project(summed, c)
    downs.add()
    swap.wait_recv()

    @pl.loop(0, 8)
    def _(m):
        @pl.loop(0, small // 32)
        def _(n):
            at = pl.ds(pl.multiple_of(n * 32, 32), 32)
            summed[m, at, :] = (summed[m, at, :].astype(F32) + arrived[m, at, :].astype(F32)).astype(BF)

    tokens.start()

    @pl.loop(0, 8)
    def _(m):
        @pl.when(m < 7)
        def _():
            n_load(m + 1).start()

        n_load(m).wait()
        dw[m] = dg(n_buf[lax.rem(m, 2)], dqkv[...], TN).astype(BF)

    weights.start()
    tokens.add_near(1)
    tokens.add_near(0)
    tokens.add_pair()
    dwos.add()
    slot = lane_sums.slots
    slot[g.d] = lane_ref[...]
    local = pl.ds(pl.multiple_of(c * HEAD, HEAD), HEAD)
    slot[g.d, 4:5, local] = jnp.sum(dqkv[:, :HEAD].astype(F32), axis=0, keepdims=True)
    slot[g.d, 5:6, local] = jnp.sum(dqkv[:, 2 * HEAD:].astype(F32), axis=0, keepdims=True)
    lane_sums.start()
    downs.inner.add_near(1)
    downs.inner.add_near(0)

    def keep(at, value):
        total[at, :] = value

    x_load.wait()
    tokens.finish(keep)
    scaled, inverse = norm_rows(x_ref[...].astype(F32))
    grad = total[...]
    tg = gm_ref[...] + norm_back(grad, scaled, inverse, gain_ref[...])
    tg_out[mine_t] = tg.astype(BF)
    final.start()
    vec[...] = early_ref[...]
    vec[4:5, :] = jnp.sum(grad * scaled, axis=0, keepdims=True)
    vec[5:6, :] = jnp.sum(grad, axis=0, keepdims=True)
    sums.start()
    weights.add_near(1)
    weights.add_near(0)
    final.forward_pair()
    final.forward(0)
    dwos.inner.add_near(1)
    dwos.inner.add_near(0)
    downs.inner.add_pair()
    sums.middle()
    weights.add_pair()
    final.forward(1)
    dwos.inner.add_pair()

    def keep_w(at, value):
        mine_w[at, :] = value.astype(BF)

    weights.finish(keep_w)
    part_rows = there_w.shape[0]
    there = send(mine_w.at[pl.ds(pl.multiple_of((1 - c) * part_rows, part_rows), part_rows)], there_w, csem, 1, core)

    def keep_down(at, value):
        ddown_out[at, :] = value

    downs.finish(keep_down)
    sums.finish()

    def keep_o(at, value):
        dwo_out[at, :] = value

    dwos.finish(keep_o)
    kept = mine_w[pl.ds(pl.multiple_of(c * part_rows, part_rows), part_rows), :].astype(F32)
    far = pl.ds(pl.multiple_of((1 - c) * HEAD, HEAD), HEAD)
    there.wait()
    for i, ref in enumerate((dwq_out, dwk_out, dwv_out)):
        ref[:, local] = kept[:, i * HEAD:(i + 1) * HEAD]
        ref[:, far] = there_w[:, i * HEAD:(i + 1) * HEAD].astype(F32)
    lanes_out[...] = lane_sums.finish()
    layer.arrive(0)
    layer.arrive(1)
    layer.settle()
    final.arrive(0)
    final.arrive(1)
    sums.settle()
    final.settle()
    swap.wait_send()


def rear_call(meta, edge, lanes, q, kv, o, do, lse, gb, lay, ddown, mixed, n, w, gm, x, gain, early, lane):
    rows = q.shape[0]
    small, width = gm.shape
    hbm = pl.BlockSpec(memory_space=pl.ANY)
    chunks = (8, small, width)
    wc = 3 * HEAD
    share = width // 16
    head_grad = struct((share, 2 * HEAD), F32)
    return remote_call(
        rear_kernel, "rear", 5,
        (struct(chunks, BF), struct((ddown.shape[0], share), F32), struct((2 * HEAD, share), F32), head_grad, head_grad, head_grad,
         struct(chunks, BF), struct((8, width), F32), struct(lane.shape, F32)),
        [SM, SM, VM, VM, hbm] + [VM] * 5 + [hbm, VM] + [hbm, VM, VM, hbm] + [VM] * 3,
        [pltpu.VMEM(kv.shape, BF), pltpu.VMEM((rows, 2 * HEAD), BF), pltpu.VMEM((8 * rows, HEAD), BF), pltpu.VMEM(kv.shape, BF), pltpu.VMEM((8, rows), F32),
         pltpu.VMEM((HEAD, rows), F32), pltpu.VMEM((8 * small, width), BF), pltpu.VMEM((rows, wc), BF), pltpu.VMEM((2 * HEAD, width), BF),
         pltpu.VMEM((2, rows, BLK), BF), pltpu.VMEM((8, width // 8, wc), BF), pltpu.VMEM(chunks, BF), pltpu.VMEM(chunks, BF),
         pltpu.VMEM(chunks, BF), pltpu.VMEM((small, width), F32), pltpu.VMEM((width // 8, wc), BF), pltpu.VMEM((share, wc), BF),
         pltpu.VMEM((8, width), F32), pltpu.VMEM((small, width), BF), DMA((11,)), DMA((2,)), DMA((2,))]
        + Scatter.scratch(rows, 2 * HEAD) + CoreScatter.scratch(ddown.shape[0], share)
        + CoreScatter.scratch(2 * HEAD, share) + Scatter.scratch(small, width) + Scatter.scratch(width // 8, wc)
        + Gather.scratch() * 3 + RowSums.scratch(width) + Sums.scratch(*lane.shape),
        meta, edge, lanes, q, kv, o, do, lse, gb, lay, ddown, mixed, n, w, gm, x, gain, early, lane)


def finish_kernel(layer, tg, small_ref, lane_ref, up, down, out, wq, wk, wv,
                  layer_out, tg_out, gain1, shift1, qb, vb, ob, gain2, shift2, ub, db, up_out, down_out, out_out, wq_out, wk_out, wv_out,
                  low, high, *scratch):
    ways = ((layer, layer_out), (up, up_out), (down, down_out), (out, out_out), (wq, wq_out), (wk, wk_out), (wv, wv_out))
    buffers, (insem, outsem, tin, tout) = scratch[:7], scratch[7:]
    parts = tg.shape[0]
    loads = [pltpu.make_async_copy(tg.at[k], low.at[k], tin.at[k]) for k in range(parts)]
    saves = [pltpu.make_async_copy(high.at[k], tg_out.at[k], tout.at[k]) for k in range(parts)]
    there = [pltpu.make_async_copy(way[0], buffer, insem.at[k]) for k, (way, buffer) in enumerate(zip(ways, buffers))]
    back = [pltpu.make_async_copy(buffer, way[1], outsem.at[k]) for k, (way, buffer) in enumerate(zip(ways, buffers))]
    for copy in loads + there:
        copy.start()
    for k, ref in ((4, gain1), (5, shift1), (2, ob), (0, gain2), (1, shift2), (3, db)):
        ref[...] = small_ref[k:k + 1, :]
    for j in range(ub.shape[1] // 256):
        ub[:, j * 256:(j + 1) * 256] = lane_ref[j:j + 1, :]
    qb[...] = lane_ref[4:5, :]
    vb[...] = lane_ref[5:6, :]
    for k in range(parts):
        loads[k].wait()
        high[k] = low[k].astype(F32)
        saves[k].start()
    for one, two in zip(there, back):
        one.wait()
        two.start()
    for copy in saves + back:
        copy.wait()


def finish_call(layer, tg, small, lane, hid, rest):
    hbm = pl.BlockSpec(memory_space=pl.ANY)
    width = small.shape[1]
    line = lambda n: struct((1, n), F32)
    return pl.pallas_call(
        finish_kernel,
        out_shape=(struct(layer.shape, BF), struct(tg.shape, F32), line(width), line(width), line(256), line(256), line(width), line(width),
                   line(width), line(hid), line(width)) + tuple(struct(r.shape, F32) for r in rest),
        in_specs=[hbm, hbm, VM, VM] + [hbm] * 6,
        out_specs=(hbm, hbm) + (VM,) * 9 + (hbm,) * 6,
        scratch_shapes=[pltpu.VMEM(tg.shape, BF), pltpu.VMEM(tg.shape, F32), pltpu.VMEM(layer.shape, BF)] + [pltpu.VMEM(r.shape, F32) for r in rest]
        + [DMA((7,)), DMA((7,)), DMA((tg.shape[0],)), DMA((tg.shape[0],))],
        compiler_params=pltpu.CompilerParams(vmem_limit_bytes=60 << 20),
        name="finish",
    )(layer, tg, small, lane, *rest)


def on_device(tokens, first_gain, first_shift, query_weight, query_bias, key_weight, value_weight, value_bias,
              out_weight, out_bias, second_gain, second_shift, up_weight, up_bias, down_weight, down_bias,
              cotangent, prefix, block_order):
    own, width = tokens.shape
    d, t = lax.axis_index("dp"), lax.axis_index("tensor")
    c = lax.rem(d, 2)
    nblk = block_order.shape[0]
    rows = own // 8
    meta, edge, lanes = block_order, prefix, block_order.reshape(1, nblk)
    row = lambda v: v.reshape(1, -1)

    w_all, n_all, q, kv, o, lse, mid, mixed, do, gm, sums, low, lane, layer, dw_up, dw_down, up_grad = front_call(
        meta, edge, lanes, tokens, row(first_gain), row(first_shift), query_weight, key_weight, value_weight, row(query_bias), row(value_bias),
        out_weight, up_weight, down_weight, row(out_bias), row(second_gain), row(second_shift), cotangent, row(up_bias), row(down_bias))
    layer, down_grad, out_grad, dwq, dwk, dwv, tg, small, lane = rear_call(
        meta, edge, lanes, q, kv, o, do, lse, low, layer, dw_down, mixed, n_all.reshape(2 * own, width), w_all, gm,
        tokens, row(first_gain), sums, lane)
    hid = up_weight.shape[1]
    layer, tg, gain1, shift1, qb, vb, ob, gain2, shift2, ub, db, up_grad, down_grad, out_grad, dwq, dwk, dwv = finish_call(
        layer, tg, small, lane, hid, (up_grad, down_grad, out_grad, dwq, dwk, dwv))
    flat = lambda v: v.reshape(-1)
    return (
        layer.reshape(own, width), tg.reshape(own, width), flat(gain1), flat(shift1), dwq, flat(qb), dwk, dwv, flat(vb), out_grad, flat(ob),
        flat(gain2), flat(shift2), up_grad, flat(ub), down_grad, flat(db))


def solution(mesh):
    rows, cols = P("dp", "tensor"), P("tensor", "dp")
    return jax.shard_map(
        on_device,
        mesh=mesh,
        in_specs=(
            P("dp", None), P(), P(), rows, P("tensor"), rows, rows, P("tensor"), cols, P(), P(), P(), rows, P("tensor"),
            cols, P(), P("dp", None), P(), P()),
        out_specs=(
            P("dp", None), P("dp", None), P(), P(), rows, P("tensor"), rows, rows, P("tensor"), cols, P(), P(), P(), rows,
            P("tensor"), cols, P()),
        check_vma=False,
    )
```

```python
import functools
import math

import jax
import jax.numpy as jnp
from jax import lax
from jax.experimental import pallas as pl
from jax.experimental.pallas import tpu as pltpu
from jax.sharding import PartitionSpec as P

HEAD = 128
BLK = 256
GRP = 4
RING = 4
EPS = 1e-05
NEG = -(2.0 ** 100)
LOG2E = math.log2(math.e)
SCALE = 1.0 / math.sqrt(HEAD)
C1 = LOG2E * SCALE
NN = (((1,), (0,)), ((), ()))
NT = (((1,), (1,)), ((), ()))
TN = (((0,), (0,)), ((), ()))
MESH = pl.DeviceIdType.MESH
VM = pl.BlockSpec(memory_space=pltpu.VMEM)
SM = pl.BlockSpec(memory_space=pltpu.SMEM)
BF = jnp.bfloat16
F32 = jnp.float32
DMA = pltpu.SemaphoreType.DMA


def dg(a, b, dims):
    return lax.dot_general(a, b, dims, preferred_element_type=F32)


def struct(shape, dtype):
    return jax.ShapeDtypeStruct(shape, dtype)


class Eight:
    def __init__(self, axis):
        d, t = lax.axis_index("dp"), lax.axis_index("tensor")
        self.axis, self.d, self.t = axis, d, t
        if axis == "dp":
            self.r, self.p = d // 4, lax.rem(d // 2, 2)
        else:
            self.r, self.p = lax.rem(t, 4), t // 4

    def ring(self, i):
        return lax.rem(self.r + i, RING)

    def side(self, s):
        return 1 - self.p if s else self.p

    def index(self, r, p):
        return r * 2 + p if self.axis == "dp" else p * 4 + r

    def device(self, r, p):
        if self.axis == "dp":
            return ((r * 2 + p) * 2 + lax.rem(self.d, 2), self.t)
        return (self.d, p * 4 + r)

    def others(self):
        return [self.device(self.ring(i), self.p) for i in (1, 3)] + [self.device(self.r, 1 - self.p)]


def other_core():
    d = lax.axis_index("dp")
    return (d + 1 - 2 * lax.rem(d, 2), lax.axis_index("tensor"))


def greet(devices):
    barrier = pltpu.get_barrier_semaphore()
    for device in devices:
        pl.semaphore_signal(barrier, inc=1, device_id=device, device_id_type=MESH)
    pl.semaphore_wait(barrier, len(devices))


def send(src, dst, sems, k, device):
    copy = pltpu.make_async_remote_copy(
        src_ref=src, dst_ref=dst, send_sem=sems[0].at[k], recv_sem=sems[1].at[k],
        device_id=device, device_id_type=MESH)
    copy.start()
    return copy


def copy_of(src, dst, sems, k, device):
    return pltpu.make_async_remote_copy(
        src_ref=src, dst_ref=dst, send_sem=sems[0].at[k], recv_sem=sems[1].at[k],
        device_id=device, device_id_type=MESH)


def send(src, dst, sems, k, device):
    copy = copy_of(src, dst, sems, k, device)
    copy.start()
    return copy


class Gather:
    @staticmethod
    def scratch(twin=False):
        return [DMA((9,)), DMA((9,))] + ([DMA((8,)), DMA((8,))] if twin else [])

    def __init__(self, group, place, rows, sems, twin=None, twin_own=True):
        self.g, self.place, self.sems = group, place, sems[:2]
        self.twin, self.twin_sems, self.twin_own = twin, sems[2:4], twin_own
        self.halves = (pl.ds(0, rows // 2), pl.ds(rows // 2, rows // 2))

    def at(self, i, s):
        g = self.g
        return self.place(g.index(g.ring(i), g.side(s)))

    def to(self, i):
        g = self.g
        return g.device(g.ring(i), g.p)

    def pair(self):
        own = self.at(0, 0)
        return copy_of(own, own, self.sems, 0, self.g.device(self.g.r, 1 - self.g.p))

    def near(self, s, way):
        chunk = self.at(0, s)
        return copy_of(chunk, chunk, self.sems, 1 + 4 * s + way, self.to(1 + 2 * way))

    def relay(self, s, way):
        half = self.at(3 - 2 * way, s).at[self.halves[way]]
        return copy_of(half, half, self.sems, 3 + 4 * s + way, self.to(1 + 2 * way))

    def over(self, k, i, s):
        chunk = self.at(i, s)
        return copy_of(chunk, chunk, self.twin_sems, k, self.twin)

    def tell(self, i, s):
        if self.twin is not None and (i or s or self.twin_own):
            self.over(2 * i + s, i, s).start()

    def start(self):
        self.pair().start()
        for way in (0, 1):
            self.near(0, way).start()
        self.tell(0, 0)

    def forward_pair(self):
        self.pair().wait_recv()
        for way in (0, 1):
            self.near(1, way).start()
        self.tell(0, 1)

    def forward(self, s):
        for way in (0, 1):
            self.near(s, way).wait_recv()
            self.relay(s, way).start()
            self.tell(3 - 2 * way, s)

    def arrive(self, s):
        for way in (0, 1):
            self.relay(s, way).wait_recv()
        self.tell(2, s)

    def settle(self):
        self.pair().wait_send()
        for s in (0, 1):
            for way in (0, 1):
                self.near(s, way).wait_send()
                self.relay(s, way).wait_send()
        if self.twin is not None:
            for k in range(0 if self.twin_own else 1, 8):
                self.over(k, 0, 0).wait()

    def rest(self):
        self.forward_pair()
        self.forward(0)
        self.forward(1)
        self.arrive(0)
        self.arrive(1)
        self.settle()


class Scatter:
    COUNT = 6

    @staticmethod
    def scratch(rows, width):
        half = rows // 2
        return [
            pltpu.VMEM((2, 2, half, width), BF), pltpu.VMEM((2, 2, rows, width), BF),
            pltpu.VMEM((rows, width), BF), pltpu.VMEM((rows, width), BF), DMA((13,)), DMA((13,))]

    def __init__(self, group, part, rows, scratch, step):
        self.g, self.part, self.step, self.rows = group, part, step, rows
        self.mid, self.last, self.sum, self.end = scratch[:4]
        self.sems = scratch[4:6]
        self.half = rows // 2
        self.halves = (pl.ds(0, self.half), pl.ds(self.half, self.half))

    def at(self, i, s):
        g = self.g
        return self.part(g.index(g.ring(i), g.side(s)))

    def to(self, way):
        g = self.g
        return g.device(g.ring(1 + 2 * way), g.p)

    def far(self, s, way):
        return copy_of(self.at(2, s).at[self.halves[way]], self.mid.at[s, way], self.sems, 2 * s + way, self.to(way))

    def own(self, s, way):
        half = self.halves[1 - way]
        return copy_of(self.at(1 + 2 * way, s).at[half], self.last.at[s, way, half], self.sems, 4 + 2 * s + way, self.to(way))

    def both(self, s, way):
        return copy_of(self.mid.at[s, way], self.last.at[s, way, self.halves[way]], self.sems, 8 + 2 * s + way, self.to(way))

    def pair(self):
        return copy_of(self.sum, self.end, self.sems, 12, self.g.device(self.g.r, 1 - self.g.p))

    def by_rows(self, rows, body):
        step = min(self.step, rows)

        @pl.loop(0, rows // step)
        def _(n):
            body(pl.multiple_of(n * step, step), step)

    def send_far(self, s):
        for way in (0, 1):
            self.far(s, way).start()

    def send_near(self, s):
        for way in (0, 1):
            self.own(s, way).start()

    def add_near(self, s):
        for way in (0, 1):
            self.far(s, way).wait_recv()
            mine = self.at(1 + 2 * way, s)
            base = way * self.half

            def add(at, n, way=way, mine=mine, base=base):
                rows = pl.ds(at, n)
                total = mine[pl.ds(base + at, n), :].astype(F32) + self.mid[s, way, rows, :].astype(F32)
                self.mid[s, way, rows, :] = total.astype(BF)

            self.by_rows(self.half, add)
            self.both(s, way).start()

    def arrived(self, s):
        for way in (0, 1):
            self.own(s, way).wait_recv()
            self.both(s, way).wait_recv()

    def add_pair(self):
        self.arrived(1)
        mine = self.at(0, 1)

        def add(at, n):
            rows = pl.ds(at, n)
            total = mine[rows, :].astype(F32) + self.last[1, 0, rows, :].astype(F32) + self.last[1, 1, rows, :].astype(F32)
            self.sum[rows, :] = total.astype(BF)

        self.by_rows(self.rows, add)
        self.pair().start()

    def start(self):
        for s in (1, 0):
            self.send_far(s)
            self.send_near(s)

    def forward(self):
        self.add_near(1)
        self.add_near(0)
        self.add_pair()

    def finish(self, store):
        self.arrived(0)
        self.pair().wait_recv()
        mine = self.at(0, 0)

        def add(at, n):
            rows = pl.ds(at, n)
            total = mine[rows, :].astype(F32) + self.last[0, 0, rows, :].astype(F32) + self.last[0, 1, rows, :].astype(F32)
            store(rows, total + self.end[rows, :].astype(F32))

        self.by_rows(self.rows, add)
        self.pair().wait_send()
        for s in (0, 1):
            for way in (0, 1):
                self.far(s, way).wait_send()
                self.own(s, way).wait_send()
                self.both(s, way).wait_send()


class CoreScatter:
    COUNT = 11

    @staticmethod
    def scratch(rows, width):
        return [pltpu.VMEM((8, rows, width), BF), DMA((8,)), DMA((8,)), pltpu.VMEM((2, rows, width), BF), DMA((2,))] + Scatter.scratch(rows, width)

    def __init__(self, group, part, rows, scratch, step):
        self.part, self.total, self.sems, self.buf, self.load_sems = part, scratch[0], scratch[1:3], scratch[3], scratch[4]
        self.c = lax.rem(group.d, 2)
        self.rows, self.step = rows, step
        self.inner = Scatter(group, lambda m: self.total.at[m], rows, scratch[5:], step)

    def swap(self, m):
        return copy_of(self.part(m, 1 - self.c), self.total.at[m], self.sems, m, other_core())

    def load(self, m):
        slot = lax.rem(m, 2)
        return pltpu.make_async_copy(self.part(m, self.c), self.buf.at[slot], self.load_sems.at[slot])

    def start(self):
        for m in range(8):
            self.swap(m).start()
        self.load(0).start()

    def add(self):
        step = self.step

        @pl.loop(0, 8)
        def _(m):
            @pl.when(m < 7)
            def _():
                self.load(m + 1).start()

            self.load(m).wait()
            self.swap(m).wait_recv()
            slot = lax.rem(m, 2)

            @pl.loop(0, self.rows // step)
            def _(n):
                at = pl.ds(pl.multiple_of(n * step, step), step)
                self.total[m, at, :] = (self.buf[slot, at, :].astype(F32) + self.total[m, at, :].astype(F32)).astype(BF)

        self.inner.start()

    def finish(self, store):
        self.inner.finish(store)
        for m in range(8):
            self.swap(m).wait_send()


class RowSums:
    @staticmethod
    def scratch(width):
        cols = width // 8
        return [pltpu.VMEM((8, 8, cols), F32), pltpu.VMEM((16, 8, cols), F32)] + [DMA((7,)), DMA((7,)), DMA((15,)), DMA((15,)), DMA((7,)), DMA((7,))]

    def __init__(self, rows, out, scratch):
        self.rows, self.out = rows, out
        self.one, self.two = scratch[:2]
        self.sems = (scratch[2:4], scratch[4:6], scratch[6:8])
        self.d, self.t = lax.axis_index("dp"), lax.axis_index("tensor")
        self.cols = rows.shape[1] // 8

    def columns(self, t):
        return pl.ds(pl.multiple_of(t * self.cols, self.cols), self.cols)

    def first(self, k):
        other = lax.rem(self.t + k, 8)
        return copy_of(self.rows.at[:, self.columns(other)], self.one.at[self.t], self.sems[0], k - 1, (self.d, other))

    def second(self, k):
        own = self.two.at[self.d]
        return copy_of(own, own, self.sems[1], k - 1, (lax.rem(self.d + k, 16), self.t))

    def third(self, k):
        own = self.out.at[:, self.columns(self.t)]
        return copy_of(own, own, self.sems[2], k - 1, (self.d, lax.rem(self.t + k, 8)))

    def run(self, step, last):
        @pl.loop(1, last)
        def _(k):
            step(k)

    def start(self):
        self.run(lambda k: self.first(k).start(), 8)
        self.one[self.t] = self.rows[:, self.columns(self.t)]

    def middle(self):
        self.run(lambda k: self.first(k).wait(), 8)
        total = self.one[0]
        for k in range(1, 8):
            total = total + self.one[k]
        self.two[self.d] = total
        self.run(lambda k: self.second(k).start(), 16)

    def finish(self):
        self.run(lambda k: self.second(k).wait(), 16)
        total = self.two[0]
        for k in range(1, 16):
            total = total + self.two[k]
        self.out[:, self.columns(self.t)] = total
        self.run(lambda k: self.third(k).start(), 8)

    def settle(self):
        self.run(lambda k: self.third(k).wait(), 8)


class Sums:
    @staticmethod
    def scratch(rows, width):
        return [pltpu.VMEM((16, rows, width), F32), DMA((15,)), DMA((15,))]

    def __init__(self, scratch):
        self.slots, self.sems = scratch[0], scratch[1:3]
        self.d, self.t = lax.axis_index("dp"), lax.axis_index("tensor")

    def copy(self, k):
        own = self.slots.at[self.d]
        return copy_of(own, own, self.sems, k - 1, (lax.rem(self.d + k, 16), self.t))

    def start(self):
        @pl.loop(1, 16)
        def _(k):
            self.copy(k).start()

    def finish(self):
        @pl.loop(1, 16)
        def _(k):
            self.copy(k).wait()
        total = self.slots[0]
        for k in range(1, 16):
            total = total + self.slots[k]
        return total


def remote_call(kernel, name, cid, outs, ins, scratch, *args, out_specs=None):
    return pl.pallas_call(
        kernel, out_shape=outs, in_specs=ins,
        out_specs=jax.tree.map(lambda _: VM, outs) if out_specs is None else out_specs,
        scratch_shapes=scratch, name=name,
        compiler_params=pltpu.CompilerParams(collective_id=cid, has_side_effects=True, vmem_limit_bytes=60 << 20),
    )(*args)


def chip_members():
    d, t = lax.axis_index("dp"), lax.axis_index("tensor")
    c = lax.rem(d, 2)
    out = []
    for dt in range(8):
        for dc in range(2):
            if dt or dc:
                tt = lax.rem(t + dt, 8)
                cc = lax.rem(c + dc, 2)
                out.append((tt, cc, (d - c + cc, tt)))
    return out


def norm_rows(values):
    average = jnp.mean(values, axis=-1, keepdims=True)
    centred = values - average
    variance = jnp.mean(centred * centred, axis=-1, keepdims=True)
    inverse = lax.rsqrt(variance + EPS)
    return centred * inverse, inverse


def norm_back(grad, scaled, inverse, gain):
    e = grad * gain
    first = jnp.mean(e, axis=-1, keepdims=True)
    second = jnp.mean(e * scaled, axis=-1, keepdims=True)
    return inverse * (e - first - scaled * second)


def augment(meta, edge_ref, lanes_ref, q_ref, qa_ref, kx_ref):
    rows = q_ref.shape[0]
    nblk = kx_ref.shape[0] // BLK
    prefix = edge_ref[0]
    for a in range(rows // BLK):
        at = slice(a * BLK, (a + 1) * BLK)
        hidden = jnp.where(lanes_ref[...] > meta[first_block() + a], NEG, 0.0)
        qa_ref[at, :HEAD] = q_ref[at, :]
        qa_ref[at, HEAD:] = jnp.zeros((BLK, HEAD), BF)
        qa_ref[at, HEAD:HEAD + nblk] = jnp.broadcast_to(hidden, (BLK, nblk)).astype(BF)
    lane = lax.broadcasted_iota(jnp.int32, (BLK, HEAD), 1)
    inside = lax.broadcasted_iota(jnp.int32, (BLK, HEAD), 0)

    @pl.loop(0, nblk)
    def _(b):
        late = (lane == b) & (inside >= prefix - meta[b] * BLK)
        kx_ref[pl.ds(pl.multiple_of(b * BLK, BLK), BLK), :] = jnp.where(late, 1.0, 0.0).astype(BF)


def first_block():
    return lax.axis_index("dp") // 2 * 4


def front_kernel(meta, edge_ref, lanes_ref, x_hbm, gain1_ref, shift1_ref, wq_ref, wk_ref, wv_ref, qb_ref, vb_ref, wo_hbm, wu_hbm, wd_hbm,
                 bias_ref, gain2_ref, shift2_ref, cot_hbm, ub_ref, db_ref,
                 w_hbm, n_hbm, q_out, kv_hbm, o_ref, lse_ref, own_out, do_out, gm_out, sums_out, low_out, lane_out, lay_out, du_hbm, dd_hbm, dup_out,
                 w_vm, n_vm, kv_vm, out_vm, up_vm, down_vm, wsh, mixed, n2, gsum, colsum,
                 mid_out, x_ref, wo_ref, wu_ref, wd_ref, cot_ref,
                 lsem, css, crs, ass, ars, hss, hrs, *sems):
    gd, gt = Eight("dp"), Eight("tensor")
    t = gt.t
    c = lax.rem(gd.d, 2)
    core = other_core()
    members = chip_members()
    me = gd.index(gd.r, gd.p)
    own = x_ref.shape[0]
    rows = 2 * own
    nblk = 8 * rows // BLK
    per = rows // BLK
    shard = wq_ref.shape[0]
    half = out_vm.shape[1] // 2
    hid = wd_ref.shape[0]
    small = mid_out.shape[0]
    csem, asem = (css, crs), (ass, ars)
    x_load, wo_load, wu_load, wd_load, cot_load = (
        pltpu.make_async_copy(one, two, lsem.at[7 + k]) for k, (one, two) in enumerate(
            ((x_hbm, x_ref), (wo_hbm, wo_ref), (wu_hbm, wu_ref), (wd_hbm, wd_ref), (cot_hbm, cot_ref))))
    for load in (x_load, wo_load, wu_load, wd_load, cot_load):
        load.start()
    for h in range(2):
        cols = slice(h * HEAD, (h + 1) * HEAD)
        for i, ref in enumerate((wq_ref, wk_ref, wv_ref)):
            wsh[h, :, i * HEAD:(i + 1) * HEAD] = ref[:, cols].astype(BF)
    greet([m[2] for m in members] + gd.others())

    w_place = lambda m: w_vm.at[pl.ds(pl.multiple_of(m * 2 * shard, 2 * shard), 2 * shard)]
    row_of = lambda m: pl.ds(pl.multiple_of((m * 2 + c) * shard, shard), shard)
    mine = row_of(me)
    swap = send(wsh.at[1 - c], w_vm.at[mine], csem, 0, core)
    w_vm[mine, :] = wsh[c]
    qkv = Gather(gd, w_place, 2 * shard, sems[0:2])
    keys = Gather(gd, lambda m: kv_vm.at[m], rows, sems[2:4])
    outs = Gather(gd, lambda m: out_vm.at[t, :, row_of(m)], 2 * half, sems[4:8], core)
    ups = Gather(gd, lambda m: up_vm.at[row_of(m)], shard, sems[8:12], core)
    downs = Gather(gd, lambda m: down_vm.at[:, row_of(m)], hid, sems[12:16], core)
    wide = Gather(gt, lambda m: out_vm.at[m, pl.ds(pl.multiple_of(c * half, half), half)], half, sems[16:20], core, twin_own=False)
    normed = Gather(gt, lambda m: n2.at[pl.ds(pl.multiple_of(m * small, small), small)], small, sems[20:22])
    spare = lambda k: (lambda m: n_vm.at[k, pl.ds(pl.multiple_of(m * small, small), small)])
    back = Scatter(gt, spare(0), small, sems[22:28], 32)
    result = Scatter(gt, spare(1), small, sems[28:34], 32)
    grads = CoreScatter(gd, lambda m, cc: du_hbm.at[pl.ds(pl.multiple_of((m * 2 + cc) * shard, shard), shard)], shard, sems[34:45], 32)
    swap.wait_recv()
    qkv.start()

    def norm_part(k):
        step = 32

        @pl.loop(0, own // 2 // step)
        def _(n):
            at = pl.ds(pl.multiple_of(k * (own // 2) + n * step, step), step)
            scaled, _ = norm_rows(x_ref[at, :].astype(F32))
            n_vm[c, at, :] = (scaled * gain1_ref[...] + shift1_ref[...]).astype(BF)

        at = pl.ds(k * (own // 2), own // 2)
        return send(n_vm.at[c, at], n_vm.at[c, at], csem, 1 + k, core)

    x_load.wait()
    there = [norm_part(0)]
    qkv.forward_pair()
    qkv.forward(0)
    wo_load.wait()
    out_vm[t, :, mine] = wo_ref[...].astype(BF)
    outs.start()
    there.append(norm_part(1))
    qkv.forward(1)
    wu_load.wait()
    wd_load.wait()
    up_vm[mine, :] = wu_ref[...].astype(BF)
    down_vm[:, mine] = wd_ref[...].astype(BF)
    for copy in there:
        copy.wait_recv()
    local = pl.ds(pl.multiple_of(c * HEAD, HEAD), HEAD)
    bias_q, bias_v = qb_ref[:, local], vb_ref[:, local]

    def project(sums):
        def term(i, s, first=False):
            m = gd.index(gd.ring(i), gd.side(s))
            cols = pl.ds(pl.multiple_of(m * 2 * shard, 2 * shard), 2 * shard)
            for h in range(2):
                piece = dg(n_vm[h, :, cols], w_vm[cols, :], NN)
                at = slice(h * own, (h + 1) * own)
                sums[at, :] = piece if first else sums[at, :] + piece

        term(0, 0, True)
        for i, s in ((1, 0), (3, 0), (0, 1)):
            term(i, s)
        outs.forward_pair()
        outs.forward(0)
        for i in (1, 3):
            term(i, 1)
        qkv.arrive(0)
        term(2, 0)
        qkv.arrive(1)
        term(2, 1)
        q_out[...] = (sums[:, :HEAD] + bias_q).astype(BF)
        kv_vm[me, :, :HEAD] = sums[:, HEAD:2 * HEAD].astype(BF)
        kv_vm[me, :, HEAD:] = (sums[:, 2 * HEAD:] + bias_v).astype(BF)

    pl.run_scoped(project, pltpu.VMEM((rows, 3 * HEAD), F32))
    keys.start()
    outs.forward(1)
    saves = [pltpu.make_async_copy(w_vm, w_hbm, lsem.at[0]), pltpu.make_async_copy(n_vm, n_hbm, lsem.at[1])]
    for save in saves:
        save.start()
    def attention(qa_ref, kx_ref, m_ref, acc_ref):
        augment(meta, edge_ref, lanes_ref, q_out, qa_ref, kx_ref)
        outs.arrive(0)
        outs.arrive(1)
        outs.settle()
        wide.start()
        m_ref[...] = jnp.full_like(m_ref, -1e30)
        acc_ref[...] = jnp.zeros_like(acc_ref)
        ones = jnp.ones((BLK, HEAD), BF)
        prefix = edge_ref[0]

        def attend(chunk, diagonal):
            ks, vs = [], []
            for i in range(per):
                at = pl.ds(pl.multiple_of(chunk * rows + i * BLK, BLK), BLK)
                ks.append(jnp.concatenate([kv_vm[chunk, i * BLK:(i + 1) * BLK, :HEAD], kx_ref[at, :]], axis=1))
                vs.append(jnp.concatenate([kv_vm[chunk, i * BLK:(i + 1) * BLK, HEAD:], ones], axis=1))
            for a in range(per):
                take = slice(a * BLK, (a + 1) * BLK)
                q = qa_ref[take, :]
                ss = [dg(q, k, NT) for k in ks]
                if diagonal:
                    edge = prefix - 1 - meta[first_block() + a] * BLK
                    lim = jnp.maximum(lax.broadcasted_iota(jnp.int32, (BLK, BLK), 0), edge)
                    key = lax.broadcasted_iota(jnp.int32, (BLK, BLK), 1)
                    ss[a] = jnp.where(key <= lim, ss[a], NEG)
                top = ss[0]
                for s in ss[1:]:
                    top = jnp.maximum(top, s)
                old = m_ref[take, :1]
                new = jnp.maximum(old, jnp.max(top, axis=1, keepdims=True) * C1)
                alpha = jnp.exp2(old - new)
                add = None
                for s, v in zip(ss, vs):
                    term = jnp.dot(jnp.exp2(s * C1 - new).astype(BF), v, preferred_element_type=F32)
                    add = term if add is None else add + term
                acc_ref[take, :] = acc_ref[take, :] * alpha + add
                m_ref[take, :] = jnp.broadcast_to(new, (BLK, HEAD))

        attend(me, True)

        @pl.loop(1, 8)
        def _(k):
            kk = lax.rem(k, 4)
            i, s = kk + kk // 2 - 2 * (kk // 3), k // 4

            @pl.when(k == 1)
            def _():
                keys.forward_pair()
                keys.forward(0)

            @pl.when(k == 2)
            def _():
                wide.forward_pair()
                wide.forward(0)

            @pl.when(k == 3)
            def _():
                keys.arrive(0)

            @pl.when(k == 5)
            def _():
                keys.forward(1)
                wide.forward(1)
                ups.start()

            @pl.when(k == 7)
            def _():
                keys.arrive(1)

            attend(gd.index(gd.ring(i), gd.p + s * (1 - 2 * gd.p)), False)

        for a in range(per):
            at = slice(a * BLK, (a + 1) * BLK)
            total = acc_ref[at, HEAD:]
            o_ref[at, :] = (acc_ref[at, :HEAD] / total).astype(BF)
            lse_ref[a:a + 1, :] = jnp.transpose(m_ref[at, :] + jnp.log2(total))[:1, :]

    pl.run_scoped(
        attention, pltpu.VMEM((rows, 2 * HEAD), BF), pltpu.VMEM((8 * rows, HEAD), BF), pltpu.VMEM((rows, HEAD), F32), pltpu.VMEM((rows, 2 * HEAD), F32))
    head = pl.ds(pl.multiple_of((2 * t + c) * HEAD, HEAD), HEAD)
    copies = []
    for k, (tt, cc, device) in enumerate(members):
        take = pl.ds(pl.multiple_of(cc * own + tt * small, small), small)
        copies.append(send(o_ref.at[take], mixed.at[:, head], asem, k, device))
    copies.append(send(o_ref.at[pl.ds(pl.multiple_of((1 - c) * own, own), own)], own_out.at[:, local], asem, 15, core))
    keys.settle()
    save = pltpu.make_async_copy(kv_vm, kv_hbm, lsem.at[2])
    save.start()
    saves.append(save)
    downs.start()
    mixed[:, head] = o_ref[pl.ds(pl.multiple_of(c * own + t * small, small), small), :]
    own_out[:, local] = o_ref[pl.ds(pl.multiple_of(c * own, own), own), :]
    ups.forward_pair()
    ups.forward(0)
    wide.arrive(0)
    wide.arrive(1)
    wide.settle()
    ups.forward(1)
    downs.forward_pair()
    for copy in copies:
        copy.wait_recv()
    span = 512
    x_rows = pl.ds(pl.multiple_of(t * small, small), small)
    for n in range(mid_out.shape[1] // span):
        cols = pl.ds(n * span, span)
        total = None
        for k in range(8):
            term = dg(mixed[:, k * 256:(k + 1) * 256], out_vm[k, :, cols], NN)
            total = term if total is None else total + term
        mid_out[:, cols] = total + (x_ref[x_rows, cols].astype(F32) + bias_ref[:, cols])
    scaled, _ = norm_rows(mid_out[...])
    n2[pl.ds(pl.multiple_of(t * small, small), small), :] = (scaled * gain2_ref[...] + shift2_ref[...]).astype(BF)
    normed.start()
    downs.forward(0)
    ups.arrive(0)
    ups.arrive(1)
    normed.forward_pair()
    normed.forward(0)
    downs.forward(1)
    normed.forward(1)
    ups.settle()
    downs.arrive(0)
    downs.arrive(1)
    downs.settle()
    cot_load.wait()
    saves.pop(1).wait()
    for copy in there:
        copy.wait_send()
    blocks = [(slice(n * span, (n + 1) * span)) for n in range(hid // span)]
    wide_blocks = [(slice(n * span, (n + 1) * span)) for n in range(n2.shape[1] // span)]

    def feed_forward(gh, hidden, gp, du_buf, dd_buf):
        @pl.loop(0, own // BLK)
        def _(b):
            at = pl.ds(pl.multiple_of(b * BLK, BLK), BLK)
            for cols in blocks:
                gh[at, cols] = dg(cot_ref[at, :], down_vm[cols, :], NT)

        normed.arrive(0)
        normed.arrive(1)
        normed.settle()
        colsum[...] = jnp.zeros_like(colsum)

        @pl.loop(0, own // BLK)
        def _(b):
            at = pl.ds(pl.multiple_of(b * BLK, BLK), BLK)
            for cols in blocks:
                pre = dg(n2[at, :], up_vm[:, cols], NN) + ub_ref[:, cols]
                half_erf = 0.5 + 0.5 * lax.erf(pre * math.sqrt(0.5))
                hidden[at, cols] = (pre * half_erf).astype(BF)
                slope = half_erf + pre * jnp.exp(-0.5 * pre * pre) * (1.0 / math.sqrt(2.0 * math.pi))
                low = (gh[at, cols] * slope).astype(BF)
                gp[at, cols] = low
                colsum[0:1, cols] += jnp.sum(low.astype(F32), axis=0, keepdims=True)
            for cols in wide_blocks:
                n_vm[0, at, cols] = dg(gp[at, :], up_vm[cols, :], NT).astype(BF)

        back.start()

        def du_save(m):
            slot = lax.rem(m, 2)
            return pltpu.make_async_copy(du_buf.at[slot], du_hbm.at[pl.ds(pl.multiple_of(m * BLK, BLK), BLK)], lsem.at[3 + slot])

        def dd_save(m):
            slot = lax.rem(m, 2)
            return pltpu.make_async_copy(dd_buf.at[slot], dd_hbm.at[:, pl.ds(pl.multiple_of(m * BLK, BLK), BLK)], lsem.at[5 + slot])

        def blocks_of(save, buf, value):
            @pl.loop(0, 8)
            def _(m):
                @pl.when(m > 1)
                def _():
                    save(m - 2).wait()

                buf[lax.rem(m, 2)] = value(pl.ds(pl.multiple_of(m * BLK, BLK), BLK)).astype(BF)
                save(m).start()

        blocks_of(du_save, du_buf, lambda cols: dg(n2[:, cols], gp[...], TN))
        back.add_near(1)
        back.add_near(0)
        du_save(6).wait()
        du_save(7).wait()
        grads.start()

        @pl.loop(0, own // BLK)
        def _(b):
            at = pl.ds(pl.multiple_of(b * BLK, BLK), BLK)
            for cols in wide_blocks:
                n_vm[1, at, cols] = dg(hidden[at, :], down_vm[:, cols], NN).astype(BF)

        back.add_pair()
        result.start()
        grads.add()
        blocks_of(dd_save, dd_buf, lambda cols: dg(hidden[...], cot_ref[:, cols], TN))
        dd_save(6).wait()
        dd_save(7).wait()

    pl.run_scoped(
        feed_forward, pltpu.VMEM((own, hid), F32), pltpu.VMEM((own, hid), BF), pltpu.VMEM((own, hid), BF), pltpu.VMEM((2, BLK, hid), BF),
        pltpu.VMEM((2, hid, BLK), BF))

    def keep(at, value):
        gsum[at, :] = value

    back.finish(keep)
    scaled, inverse = norm_rows(mid_out[...])
    grad = gsum[...]
    g_rows = cot_ref[x_rows, :].astype(F32)
    gm = g_rows + norm_back(grad, scaled, inverse, gain2_ref[...])
    gm_out[...] = gm
    low = gm.astype(BF)
    low_out[...] = low
    for k in range(8):
        mixed[:, k * 256:(k + 1) * 256] = dg(low, out_vm[k], NT).astype(BF)
    hsem = (hss, hrs)
    take = pl.ds(pl.multiple_of(c * own + t * small, small), small)
    heads = []
    for k, (tt, cc, device) in enumerate(members):
        cols = pl.ds(pl.multiple_of((2 * tt + cc) * HEAD, HEAD), HEAD)
        heads.append(send(mixed.at[:, cols], do_out.at[take], hsem, k, device))
    do_out[take, :] = mixed[:, head]
    result.add_near(1)
    result.add_near(0)
    grads.inner.add_near(1)
    grads.inner.add_near(0)
    result.add_pair()
    sums_out[...] = jnp.zeros_like(sums_out)
    sums_out[0:1, :] = jnp.sum(grad * scaled, axis=0, keepdims=True)
    sums_out[1:2, :] = jnp.sum(grad, axis=0, keepdims=True)
    sums_out[2:3, :] = jnp.sum(low.astype(F32), axis=0, keepdims=True)
    sums_out[3:4, :] = jnp.sum(g_rows, axis=0, keepdims=True)
    lane_out[...] = jnp.zeros_like(lane_out)
    for j in range(hid // 256):
        lane_out[j:j + 1, :] = colsum[0:1, j * 256:(j + 1) * 256]
    grads.inner.add_pair()

    def lay(at, value):
        lay_out[at, :] = (mid_out[at, :] + (value + db_ref[...])).astype(BF)

    result.finish(lay)

    def keep_up(at, value):
        dup_out[at, :] = value

    grads.finish(keep_up)
    qkv.settle()
    swap.wait_send()
    for copy in copies:
        copy.wait_send()
    for save in saves:
        save.wait()
    for copy in heads:
        copy.wait()


def front_call(meta, edge, lanes, x, gain1, shift1, wq, wk, wv, qb, vb, wo, wu, wd, bias, gain2, shift2, cot, ub, db):
    own, width = x.shape
    rows, shard, hid, small = 2 * own, wq.shape[0], wu.shape[1], own // 8
    hbm = pl.BlockSpec(memory_space=pl.ANY)
    big = [(width, 3 * HEAD), (2, own, width), (8, rows, 2 * HEAD), (8, 2 * HEAD, width), (width, hid), (hid, width)]
    w, n, kv, out, up, down = (struct(s, BF) for s in big)
    outs = (w, n, struct((rows, HEAD), BF), kv, struct((rows, HEAD), BF), struct((rows // BLK, BLK), F32),
            struct((own, 2 * HEAD), BF), struct((rows, HEAD), BF), struct((small, width), F32),
            struct((8, width), F32), struct((small, width), BF), struct((8, 256), F32), struct((small, width), BF), up, down, struct((shard, hid), F32))
    return remote_call(
        front_kernel, "front", 1, outs, [SM, SM, VM, hbm] + [VM] * 7 + [hbm] * 3 + [VM] * 3 + [hbm, VM, VM],
        [pltpu.VMEM(s, BF) for s in big]
        + [pltpu.VMEM((2, shard, 3 * HEAD), BF), pltpu.VMEM((small, width), BF), pltpu.VMEM((own, width), BF),
           pltpu.VMEM((small, width), F32), pltpu.VMEM((8, hid), F32),
           pltpu.VMEM((small, width), F32), pltpu.VMEM(x.shape, BF), pltpu.VMEM(wo.shape, F32), pltpu.VMEM(wu.shape, F32), pltpu.VMEM(wd.shape, F32),
           pltpu.VMEM(cot.shape, BF),
           DMA((12,)), DMA((3,)), DMA((3,)), DMA((16,)), DMA((16,)), DMA((15,)), DMA((15,))]
        + Gather.scratch() * 2 + Gather.scratch(True) * 4 + Gather.scratch() + Scatter.scratch(small, width) * 2 + CoreScatter.scratch(shard, hid),
        meta, edge, lanes, x, gain1, shift1, wq, wk, wv, qb, vb, wo, wu, wd, bias, gain2, shift2, cot, ub, db,
        out_specs=(hbm, hbm, VM, hbm) + (VM,) * 9 + (hbm, hbm, VM))


def rear_kernel(meta, edge_ref, lanes_ref, q_ref, kv_hbm, o_ref, do_ref, lse_ref, gbr_ref, layr_ref, ddown_hbm,
                mixed_hbm, n_hbm, w_hbm, gm_hbm, x_hbm, gain_ref, early_ref, lane_ref,
                lay_out, ddown_out, dwo_out, dwq_out, dwk_out, dwv_out, tg_out, sums_out, lanes_out,
                kv_ref, qa_ref, kx_ref, part, delta_ref, dq_acc, gb, dqkv, dwo, n_buf, dw, away, arrived, summed, total, mine_w, there_w, vec, x_ref, mixed_ref, w_ref, gm_ref,
                lsem, css, crs, *scratch):
    g, gt = Eight("dp"), Eight("tensor")
    c = lax.rem(g.d, 2)
    core = other_core()
    me, mine_t = g.index(g.r, g.p), gt.index(gt.r, gt.p)
    rows = q_ref.shape[0]
    own = rows // 2
    nblk = kx_ref.shape[0] // BLK
    per = rows // BLK
    small, width = gm_ref.shape
    order = [(2, 1), (1, 1), (3, 1), (2, 0), (1, 0), (3, 0), (0, 1), (0, 0)]

    def kv_load(n):
        i, s = order[n]
        m = g.index(g.ring(i), g.side(s))
        return pltpu.make_async_copy(kv_hbm.at[m], kv_ref.at[m], lsem.at[3 + n])

    for n in range(8):
        kv_load(n).start()
    mixed_load, w_load, gm_load = (
        pltpu.make_async_copy(one, two, lsem.at[11 + k]) for k, (one, two) in enumerate(
            ((mixed_hbm, mixed_ref), (w_hbm, w_ref), (gm_hbm, gm_ref))))
    for load in (mixed_load, w_load, gm_load):
        load.start()
    everyone = [(lax.rem(g.d + k, 16), g.t) for k in range(1, 16)] + [(g.d, lax.rem(g.t + k, 8)) for k in range(1, 8)]
    greet(everyone)
    take = list(scratch)

    def some(count):
        out = take[:count]
        del take[:count]
        return out

    share = dwo_out.shape[1]
    by_columns = lambda m, cc: dwo.at[:, pl.ds(pl.multiple_of((m * 2 + cc) * share, share), share)]
    keys = Scatter(g, lambda m: part.at[m], rows, some(6), 128)
    downs = CoreScatter(
        g, lambda m, cc: ddown_hbm.at[:, pl.ds(pl.multiple_of((m * 2 + cc) * share, share), share)], ddown_out.shape[0], some(CoreScatter.COUNT), 128)
    dwos = CoreScatter(g, by_columns, dwo_out.shape[0], some(CoreScatter.COUNT), 128)
    tokens = Scatter(gt, lambda m: summed.at[m], small, some(6), 32)
    weights = Scatter(g, lambda m: dw.at[m], dw.shape[1], some(6), 128)
    wide = Gather(gt, lambda m: gb.at[pl.ds(pl.multiple_of(m * small, small), small)], small, some(2))
    layer = Gather(gt, lambda m: lay_out.at[m], small, some(2))
    final = Gather(gt, lambda m: tg_out.at[m], small, some(2))
    sums = RowSums(vec, sums_out, some(8))
    lane_sums = Sums(some(3))
    csem = (css, crs)
    x_load = pltpu.make_async_copy(x_hbm.at[pl.ds(pl.multiple_of(g.t * small, small), small)], x_ref, lsem.at[2])
    x_load.start()

    def n_load(m):
        slot = lax.rem(m, 2)
        return pltpu.make_async_copy(n_hbm.at[:, pl.ds(pl.multiple_of(m * BLK, BLK), BLK)], n_buf.at[slot], lsem.at[slot])

    downs.start()
    lay_out[mine_t] = layr_ref[...]
    gb[pl.ds(pl.multiple_of(mine_t * small, small), small), :] = gbr_ref[...]
    wide.start()
    layer.start()
    augment(meta, edge_ref, lanes_ref, q_ref, qa_ref, kx_ref)
    for a in range(per):
        at = slice(a * BLK, (a + 1) * BLK)
        prod = do_ref[at, :].astype(F32) * o_ref[at, :].astype(F32)
        delta_ref[0:1, at] = jnp.sum(jnp.transpose(prod), axis=0, keepdims=True)
        delta_ref[1:2, at] = lse_ref[a:a + 1, :]
    dq_acc[...] = jnp.zeros_like(dq_acc)
    prefix = edge_ref[0]

    def attend(chunk, diagonal):
        k = kv_ref[chunk, :, :HEAD]
        v = kv_ref[chunk, :, HEAD:]
        kk = jnp.concatenate([k, kx_ref[pl.ds(pl.multiple_of(chunk * rows, rows), rows), :]], axis=1)
        turned = jnp.transpose(k.astype(F32)).astype(BF)
        dk = dv = None
        for a in range(per):
            at_q = slice(a * BLK, (a + 1) * BLK)
            q = q_ref[at_q, :]
            do = do_ref[at_q, :]
            p = jnp.exp2(dg(kk, qa_ref[at_q, :], NT) * C1 - delta_ref[1:2, at_q])
            if diagonal:
                edge = prefix - 1 - meta[first_block() + a] * BLK
                lim = jnp.maximum(lax.broadcasted_iota(jnp.int32, (BLK, BLK), 1), edge)
                mid = jnp.where(lax.broadcasted_iota(jnp.int32, (BLK, BLK), 0) <= lim, p[a * BLK:(a + 1) * BLK], 0.0)
                p = jnp.concatenate([p[b * BLK:(b + 1) * BLK] if b != a else mid for b in range(per)], axis=0)
            ds = (p * (dg(v, do, NT) - delta_ref[0:1, at_q])).astype(BF)
            tv = jnp.dot(p.astype(BF), do, preferred_element_type=F32)
            tk = jnp.dot(ds, q, preferred_element_type=F32)
            dv = tv if dv is None else dv + tv
            dk = tk if dk is None else dk + tk
            dq_acc[:, at_q] += jnp.dot(turned, ds, preferred_element_type=F32)
        part[chunk, :, :HEAD] = (dk * SCALE).astype(BF)
        part[chunk, :, HEAD:] = dv.astype(BF)

    for n in range(8):
        kv_load(n).wait()

    @pl.loop(0, 7)
    def _(k):
        kk = lax.rem(k, 3)
        i = (2 - kk + 3 * (kk // 2)) * (1 - k // 6)
        s = 1 - k // 3 + 2 * (k // 6)
        attend(g.index(g.ring(i), g.p + s * (1 - 2 * g.p)), False)

        @pl.when(k == 0)
        def _():
            keys.send_far(1)
            wide.forward_pair()
            wide.forward(0)

        @pl.when(k == 1)
        def _():
            layer.forward_pair()
            layer.forward(0)

        @pl.when(k == 2)
        def _():
            keys.send_near(1)
            keys.add_near(1)
            wide.forward(1)

        @pl.when(k == 3)
        def _():
            keys.send_far(0)

        @pl.when(k == 4)
        def _():
            layer.forward(1)

        @pl.when(k == 5)
        def _():
            keys.send_near(0)
            keys.add_near(0)

        @pl.when(k == 6)
        def _():
            keys.add_pair()

    n_load(0).start()
    attend(me, True)
    dqkv[:, :HEAD] = jnp.transpose(dq_acc[...] * SCALE).astype(BF)
    wide.arrive(0)
    wide.arrive(1)
    wide.settle()
    span = 512
    mixed_load.wait()
    for n in range(width // span):
        cols = pl.ds(n * span, span)
        dwo[:, cols] = dg(mixed_ref[...], gb[:, cols], TN).astype(BF)
    dwos.start()

    def keep_keys(at, value):
        dqkv[at, HEAD:] = value.astype(BF)

    keys.finish(keep_keys)

    def project(into, half):
        @pl.loop(0, own // BLK)
        def _(b):
            at = pl.ds(pl.multiple_of(half * own + b * BLK, BLK), BLK)
            for n in range(width // span):
                cols = pl.ds(n * span, span)
                piece = dg(dqkv[at, :], w_ref[cols, :], NT).astype(BF)
                for j in range(BLK // small):
                    into[b * (BLK // small) + j, :, cols] = piece[j * small:(j + 1) * small]

    w_load.wait()
    project(away, 1 - c)
    swap = send(away, arrived, csem, 0, core)
    project(summed, c)
    downs.add()
    swap.wait_recv()

    @pl.loop(0, 8)
    def _(m):
        @pl.loop(0, small // 32)
        def _(n):
            at = pl.ds(pl.multiple_of(n * 32, 32), 32)
            summed[m, at, :] = (summed[m, at, :].astype(F32) + arrived[m, at, :].astype(F32)).astype(BF)

    tokens.start()

    @pl.loop(0, 8)
    def _(m):
        @pl.when(m < 7)
        def _():
            n_load(m + 1).start()

        n_load(m).wait()
        dw[m] = dg(n_buf[lax.rem(m, 2)], dqkv[...], TN).astype(BF)

    weights.start()
    tokens.add_near(1)
    tokens.add_near(0)
    tokens.add_pair()
    dwos.add()
    slot = lane_sums.slots
    slot[g.d] = lane_ref[...]
    local = pl.ds(pl.multiple_of(c * HEAD, HEAD), HEAD)
    slot[g.d, 4:5, local] = jnp.sum(dqkv[:, :HEAD].astype(F32), axis=0, keepdims=True)
    slot[g.d, 5:6, local] = jnp.sum(dqkv[:, 2 * HEAD:].astype(F32), axis=0, keepdims=True)
    lane_sums.start()
    downs.inner.add_near(1)
    downs.inner.add_near(0)

    def keep(at, value):
        total[at, :] = value

    x_load.wait()
    gm_load.wait()
    tokens.finish(keep)
    scaled, inverse = norm_rows(x_ref[...].astype(F32))
    grad = total[...]
    tg = gm_ref[...] + norm_back(grad, scaled, inverse, gain_ref[...])
    tg_out[mine_t] = tg.astype(BF)
    final.start()
    vec[...] = early_ref[...]
    vec[4:5, :] = jnp.sum(grad * scaled, axis=0, keepdims=True)
    vec[5:6, :] = jnp.sum(grad, axis=0, keepdims=True)
    sums.start()
    weights.add_near(1)
    weights.add_near(0)
    final.forward_pair()
    final.forward(0)
    dwos.inner.add_near(1)
    dwos.inner.add_near(0)
    downs.inner.add_pair()
    sums.middle()
    weights.add_pair()
    final.forward(1)
    dwos.inner.add_pair()

    def keep_w(at, value):
        mine_w[at, :] = value.astype(BF)

    weights.finish(keep_w)
    part_rows = there_w.shape[0]
    there = send(mine_w.at[pl.ds(pl.multiple_of((1 - c) * part_rows, part_rows), part_rows)], there_w, csem, 1, core)

    def keep_down(at, value):
        ddown_out[at, :] = value

    downs.finish(keep_down)
    sums.finish()

    def keep_o(at, value):
        dwo_out[at, :] = value

    dwos.finish(keep_o)
    kept = mine_w[pl.ds(pl.multiple_of(c * part_rows, part_rows), part_rows), :].astype(F32)
    far = pl.ds(pl.multiple_of((1 - c) * HEAD, HEAD), HEAD)
    there.wait()
    for i, ref in enumerate((dwq_out, dwk_out, dwv_out)):
        ref[:, local] = kept[:, i * HEAD:(i + 1) * HEAD]
        ref[:, far] = there_w[:, i * HEAD:(i + 1) * HEAD].astype(F32)
    lanes_out[...] = lane_sums.finish()
    layer.arrive(0)
    layer.arrive(1)
    layer.settle()
    final.arrive(0)
    final.arrive(1)
    sums.settle()
    final.settle()
    swap.wait_send()


def rear_call(meta, edge, lanes, q, kv, o, do, lse, gb, lay, ddown, mixed, n, w, gm, x, gain, early, lane):
    rows = q.shape[0]
    small, width = gm.shape
    hbm = pl.BlockSpec(memory_space=pl.ANY)
    chunks = (8, small, width)
    wc = 3 * HEAD
    share = width // 16
    head_grad = struct((share, 2 * HEAD), F32)
    return remote_call(
        rear_kernel, "rear", 5,
        (struct(chunks, BF), struct((ddown.shape[0], share), F32), struct((2 * HEAD, share), F32), head_grad, head_grad, head_grad,
         struct(chunks, BF), struct((8, width), F32), struct(lane.shape, F32)),
        [SM, SM, VM, VM, hbm] + [VM] * 5 + [hbm] * 6 + [VM] * 3,
        [pltpu.VMEM(kv.shape, BF), pltpu.VMEM((rows, 2 * HEAD), BF), pltpu.VMEM((8 * rows, HEAD), BF), pltpu.VMEM(kv.shape, BF), pltpu.VMEM((8, rows), F32),
         pltpu.VMEM((HEAD, rows), F32), pltpu.VMEM((8 * small, width), BF), pltpu.VMEM((rows, wc), BF), pltpu.VMEM((2 * HEAD, width), BF),
         pltpu.VMEM((2, rows, BLK), BF), pltpu.VMEM((8, width // 8, wc), BF), pltpu.VMEM(chunks, BF), pltpu.VMEM(chunks, BF),
         pltpu.VMEM(chunks, BF), pltpu.VMEM((small, width), F32), pltpu.VMEM((width // 8, wc), BF), pltpu.VMEM((share, wc), BF),
         pltpu.VMEM((8, width), F32), pltpu.VMEM((small, width), BF), pltpu.VMEM(mixed.shape, BF),
         pltpu.VMEM(w.shape, BF), pltpu.VMEM(gm.shape, F32), DMA((14,)), DMA((2,)), DMA((2,))]
        + Scatter.scratch(rows, 2 * HEAD) + CoreScatter.scratch(ddown.shape[0], share)
        + CoreScatter.scratch(2 * HEAD, share) + Scatter.scratch(small, width) + Scatter.scratch(width // 8, wc)
        + Gather.scratch() * 3 + RowSums.scratch(width) + Sums.scratch(*lane.shape),
        meta, edge, lanes, q, kv, o, do, lse, gb, lay, ddown, mixed, n, w, gm, x, gain, early, lane)


def finish_kernel(layer, tg, small_ref, lane_ref, up, down, out, wq, wk, wv,
                  layer_out, tg_out, gain1, shift1, qb, vb, ob, gain2, shift2, ub, db, up_out, down_out, out_out, wq_out, wk_out, wv_out,
                  low, high, *scratch):
    ways = ((layer, layer_out), (up, up_out), (down, down_out), (out, out_out), (wq, wq_out), (wk, wk_out), (wv, wv_out))
    buffers, (insem, outsem, tin, tout) = scratch[:7], scratch[7:]
    parts = tg.shape[0]
    loads = [pltpu.make_async_copy(tg.at[k], low.at[k], tin.at[k]) for k in range(parts)]
    saves = [pltpu.make_async_copy(high.at[k], tg_out.at[k], tout.at[k]) for k in range(parts)]
    there = [pltpu.make_async_copy(way[0], buffer, insem.at[k]) for k, (way, buffer) in enumerate(zip(ways, buffers))]
    back = [pltpu.make_async_copy(buffer, way[1], outsem.at[k]) for k, (way, buffer) in enumerate(zip(ways, buffers))]
    for copy in there + loads:
        copy.start()
    for k, ref in ((4, gain1), (5, shift1), (2, ob), (0, gain2), (1, shift2), (3, db)):
        ref[...] = small_ref[k:k + 1, :]
    for j in range(ub.shape[1] // 256):
        ub[:, j * 256:(j + 1) * 256] = lane_ref[j:j + 1, :]
    qb[...] = lane_ref[4:5, :]
    vb[...] = lane_ref[5:6, :]
    for one, two in zip(there, back):
        one.wait()
        two.start()
    for k in range(parts):
        loads[k].wait()
        high[k] = low[k].astype(F32)
        saves[k].start()
    for copy in saves + back:
        copy.wait()


def finish_call(layer, tg, small, lane, hid, rest):
    hbm = pl.BlockSpec(memory_space=pl.ANY)
    width = small.shape[1]
    line = lambda n: struct((1, n), F32)
    return pl.pallas_call(
        finish_kernel,
        out_shape=(struct(layer.shape, BF), struct(tg.shape, F32), line(width), line(width), line(256), line(256), line(width), line(width),
                   line(width), line(hid), line(width)) + tuple(struct(r.shape, F32) for r in rest),
        in_specs=[hbm, hbm, VM, VM] + [hbm] * 6,
        out_specs=(hbm, hbm) + (VM,) * 9 + (hbm,) * 6,
        scratch_shapes=[pltpu.VMEM(tg.shape, BF), pltpu.VMEM(tg.shape, F32), pltpu.VMEM(layer.shape, BF)] + [pltpu.VMEM(r.shape, F32) for r in rest]
        + [DMA((7,)), DMA((7,)), DMA((tg.shape[0],)), DMA((tg.shape[0],))],
        compiler_params=pltpu.CompilerParams(vmem_limit_bytes=60 << 20),
        name="finish",
    )(layer, tg, small, lane, *rest)


def on_device(tokens, first_gain, first_shift, query_weight, query_bias, key_weight, value_weight, value_bias,
              out_weight, out_bias, second_gain, second_shift, up_weight, up_bias, down_weight, down_bias,
              cotangent, prefix, block_order):
    own, width = tokens.shape
    d, t = lax.axis_index("dp"), lax.axis_index("tensor")
    c = lax.rem(d, 2)
    nblk = block_order.shape[0]
    rows = own // 8
    meta, edge, lanes = block_order, prefix, block_order.reshape(1, nblk)
    row = lambda v: v.reshape(1, -1)

    w_all, n_all, q, kv, o, lse, mixed, do, gm, sums, low, lane, layer, dw_up, dw_down, up_grad = front_call(
        meta, edge, lanes, tokens, row(first_gain), row(first_shift), query_weight, key_weight, value_weight, row(query_bias), row(value_bias),
        out_weight, up_weight, down_weight, row(out_bias), row(second_gain), row(second_shift), cotangent, row(up_bias), row(down_bias))
    layer, down_grad, out_grad, dwq, dwk, dwv, tg, small, lane = rear_call(
        meta, edge, lanes, q, kv, o, do, lse, low, layer, dw_down, mixed, n_all.reshape(2 * own, width), w_all, gm,
        tokens, row(first_gain), sums, lane)
    hid = up_weight.shape[1]
    layer, tg, gain1, shift1, qb, vb, ob, gain2, shift2, ub, db, up_grad, down_grad, out_grad, dwq, dwk, dwv = finish_call(
        layer, tg, small, lane, hid, (up_grad, down_grad, out_grad, dwq, dwk, dwv))
    flat = lambda v: v.reshape(-1)
    return (
        layer.reshape(own, width), tg.reshape(own, width), flat(gain1), flat(shift1), dwq, flat(qb), dwk, dwv, flat(vb), out_grad, flat(ob),
        flat(gain2), flat(shift2), up_grad, flat(ub), down_grad, flat(db))


def solution(mesh):
    rows, cols = P("dp", "tensor"), P("tensor", "dp")
    return jax.shard_map(
        on_device,
        mesh=mesh,
        in_specs=(
            P("dp", None), P(), P(), rows, P("tensor"), rows, rows, P("tensor"), cols, P(), P(), P(), rows, P("tensor"),
            cols, P(), P("dp", None), P(), P()),
        out_specs=(
            P("dp", None), P("dp", None), P(), P(), rows, P("tensor"), rows, rows, P("tensor"), cols, P(), P(), P(), rows,
            P("tensor"), cols, P()),
        check_vma=False,
    )
```

```python
import functools
import math

import jax
import jax.numpy as jnp
from jax import lax
from jax.experimental import pallas as pl
from jax.experimental.pallas import tpu as pltpu
from jax.sharding import PartitionSpec as P

HEAD = 128
BLK = 256
GRP = 4
RING = 4
EPS = 1e-05
NEG = -(2.0 ** 100)
LOG2E = math.log2(math.e)
SCALE = 1.0 / math.sqrt(HEAD)
C1 = LOG2E * SCALE
NN = (((1,), (0,)), ((), ()))
NT = (((1,), (1,)), ((), ()))
TN = (((0,), (0,)), ((), ()))
MESH = pl.DeviceIdType.MESH
VM = pl.BlockSpec(memory_space=pltpu.VMEM)
SM = pl.BlockSpec(memory_space=pltpu.SMEM)
BF = jnp.bfloat16
F32 = jnp.float32
DMA = pltpu.SemaphoreType.DMA


def dg(a, b, dims):
    return lax.dot_general(a, b, dims, preferred_element_type=F32)


def struct(shape, dtype):
    return jax.ShapeDtypeStruct(shape, dtype)


class Eight:
    def __init__(self, axis):
        d, t = lax.axis_index("dp"), lax.axis_index("tensor")
        self.axis, self.d, self.t = axis, d, t
        if axis == "dp":
            self.r, self.p = d // 4, lax.rem(d // 2, 2)
        else:
            self.r, self.p = lax.rem(t, 4), t // 4

    def ring(self, i):
        return lax.rem(self.r + i, RING)

    def side(self, s):
        return 1 - self.p if s else self.p

    def index(self, r, p):
        return r * 2 + p if self.axis == "dp" else p * 4 + r

    def device(self, r, p):
        if self.axis == "dp":
            return ((r * 2 + p) * 2 + lax.rem(self.d, 2), self.t)
        return (self.d, p * 4 + r)

    def others(self):
        return [self.device(self.ring(i), self.p) for i in (1, 3)] + [self.device(self.r, 1 - self.p)]


def other_core():
    d = lax.axis_index("dp")
    return (d + 1 - 2 * lax.rem(d, 2), lax.axis_index("tensor"))


def greet(devices):
    barrier = pltpu.get_barrier_semaphore()
    for device in devices:
        pl.semaphore_signal(barrier, inc=1, device_id=device, device_id_type=MESH)
    pl.semaphore_wait(barrier, len(devices))


def send(src, dst, sems, k, device):
    copy = pltpu.make_async_remote_copy(
        src_ref=src, dst_ref=dst, send_sem=sems[0].at[k], recv_sem=sems[1].at[k],
        device_id=device, device_id_type=MESH)
    copy.start()
    return copy


def copy_of(src, dst, sems, k, device):
    return pltpu.make_async_remote_copy(
        src_ref=src, dst_ref=dst, send_sem=sems[0].at[k], recv_sem=sems[1].at[k],
        device_id=device, device_id_type=MESH)


def send(src, dst, sems, k, device):
    copy = copy_of(src, dst, sems, k, device)
    copy.start()
    return copy


class Gather:
    @staticmethod
    def scratch(twin=False):
        return [DMA((9,)), DMA((9,))] + ([DMA((8,)), DMA((8,))] if twin else [])

    def __init__(self, group, place, rows, sems, twin=None, twin_own=True):
        self.g, self.place, self.sems = group, place, sems[:2]
        self.twin, self.twin_sems, self.twin_own = twin, sems[2:4], twin_own
        self.halves = (pl.ds(0, rows // 2), pl.ds(rows // 2, rows // 2))

    def at(self, i, s):
        g = self.g
        return self.place(g.index(g.ring(i), g.side(s)))

    def to(self, i):
        g = self.g
        return g.device(g.ring(i), g.p)

    def pair(self):
        own = self.at(0, 0)
        return copy_of(own, own, self.sems, 0, self.g.device(self.g.r, 1 - self.g.p))

    def near(self, s, way):
        chunk = self.at(0, s)
        return copy_of(chunk, chunk, self.sems, 1 + 4 * s + way, self.to(1 + 2 * way))

    def relay(self, s, way):
        half = self.at(3 - 2 * way, s).at[self.halves[way]]
        return copy_of(half, half, self.sems, 3 + 4 * s + way, self.to(1 + 2 * way))

    def over(self, k, i, s):
        chunk = self.at(i, s)
        return copy_of(chunk, chunk, self.twin_sems, k, self.twin)

    def tell(self, i, s):
        if self.twin is not None and (i or s or self.twin_own):
            self.over(2 * i + s, i, s).start()

    def start(self):
        self.pair().start()
        for way in (0, 1):
            self.near(0, way).start()
        self.tell(0, 0)

    def forward_pair(self):
        self.pair().wait_recv()
        for way in (0, 1):
            self.near(1, way).start()
        self.tell(0, 1)

    def forward(self, s):
        for way in (0, 1):
            self.near(s, way).wait_recv()
            self.relay(s, way).start()
            self.tell(3 - 2 * way, s)

    def arrive(self, s):
        for way in (0, 1):
            self.relay(s, way).wait_recv()
        self.tell(2, s)

    def settle(self):
        self.pair().wait_send()
        for s in (0, 1):
            for way in (0, 1):
                self.near(s, way).wait_send()
                self.relay(s, way).wait_send()
        if self.twin is not None:
            for k in range(0 if self.twin_own else 1, 8):
                self.over(k, 0, 0).wait()

    def rest(self):
        self.forward_pair()
        self.forward(0)
        self.forward(1)
        self.arrive(0)
        self.arrive(1)
        self.settle()


class Scatter:
    COUNT = 6

    @staticmethod
    def scratch(rows, width):
        half = rows // 2
        return [
            pltpu.VMEM((2, 2, half, width), BF), pltpu.VMEM((2, 2, rows, width), BF),
            pltpu.VMEM((rows, width), BF), pltpu.VMEM((rows, width), BF), DMA((13,)), DMA((13,))]

    def __init__(self, group, part, rows, scratch, step):
        self.g, self.part, self.step, self.rows = group, part, step, rows
        self.mid, self.last, self.sum, self.end = scratch[:4]
        self.sems = scratch[4:6]
        self.half = rows // 2
        self.halves = (pl.ds(0, self.half), pl.ds(self.half, self.half))

    def at(self, i, s):
        g = self.g
        return self.part(g.index(g.ring(i), g.side(s)))

    def to(self, way):
        g = self.g
        return g.device(g.ring(1 + 2 * way), g.p)

    def far(self, s, way):
        return copy_of(self.at(2, s).at[self.halves[way]], self.mid.at[s, way], self.sems, 2 * s + way, self.to(way))

    def own(self, s, way):
        half = self.halves[1 - way]
        return copy_of(self.at(1 + 2 * way, s).at[half], self.last.at[s, way, half], self.sems, 4 + 2 * s + way, self.to(way))

    def both(self, s, way):
        return copy_of(self.mid.at[s, way], self.last.at[s, way, self.halves[way]], self.sems, 8 + 2 * s + way, self.to(way))

    def pair(self):
        return copy_of(self.sum, self.end, self.sems, 12, self.g.device(self.g.r, 1 - self.g.p))

    def by_rows(self, rows, body):
        step = min(self.step, rows)

        @pl.loop(0, rows // step)
        def _(n):
            body(pl.multiple_of(n * step, step), step)

    def send_far(self, s):
        for way in (0, 1):
            self.far(s, way).start()

    def send_near(self, s):
        for way in (0, 1):
            self.own(s, way).start()

    def add_near(self, s):
        for way in (0, 1):
            self.far(s, way).wait_recv()
            mine = self.at(1 + 2 * way, s)
            base = way * self.half

            def add(at, n, way=way, mine=mine, base=base):
                rows = pl.ds(at, n)
                total = mine[pl.ds(base + at, n), :].astype(F32) + self.mid[s, way, rows, :].astype(F32)
                self.mid[s, way, rows, :] = total.astype(BF)

            self.by_rows(self.half, add)
            self.both(s, way).start()

    def arrived(self, s):
        for way in (0, 1):
            self.own(s, way).wait_recv()
            self.both(s, way).wait_recv()

    def add_pair(self):
        self.arrived(1)
        mine = self.at(0, 1)

        def add(at, n):
            rows = pl.ds(at, n)
            total = mine[rows, :].astype(F32) + self.last[1, 0, rows, :].astype(F32) + self.last[1, 1, rows, :].astype(F32)
            self.sum[rows, :] = total.astype(BF)

        self.by_rows(self.rows, add)
        self.pair().start()

    def start(self):
        for s in (1, 0):
            self.send_far(s)
            self.send_near(s)

    def forward(self):
        self.add_near(1)
        self.add_near(0)
        self.add_pair()

    def finish(self, store):
        self.arrived(0)
        self.pair().wait_recv()
        mine = self.at(0, 0)

        def add(at, n):
            rows = pl.ds(at, n)
            total = mine[rows, :].astype(F32) + self.last[0, 0, rows, :].astype(F32) + self.last[0, 1, rows, :].astype(F32)
            store(rows, total + self.end[rows, :].astype(F32))

        self.by_rows(self.rows, add)
        self.pair().wait_send()
        for s in (0, 1):
            for way in (0, 1):
                self.far(s, way).wait_send()
                self.own(s, way).wait_send()
                self.both(s, way).wait_send()


class CoreScatter:
    COUNT = 11

    @staticmethod
    def scratch(rows, width):
        return [pltpu.VMEM((8, rows, width), BF), DMA((8,)), DMA((8,)), pltpu.VMEM((2, rows, width), BF), DMA((2,))] + Scatter.scratch(rows, width)

    def __init__(self, group, part, rows, scratch, step):
        self.part, self.total, self.sems, self.buf, self.load_sems = part, scratch[0], scratch[1:3], scratch[3], scratch[4]
        self.c = lax.rem(group.d, 2)
        self.rows, self.step = rows, step
        self.inner = Scatter(group, lambda m: self.total.at[m], rows, scratch[5:], step)

    def swap(self, m):
        return copy_of(self.part(m, 1 - self.c), self.total.at[m], self.sems, m, other_core())

    def load(self, m):
        slot = lax.rem(m, 2)
        return pltpu.make_async_copy(self.part(m, self.c), self.buf.at[slot], self.load_sems.at[slot])

    def start(self):
        for m in range(8):
            self.swap(m).start()
        self.load(0).start()

    def add(self):
        step = self.step

        @pl.loop(0, 8)
        def _(m):
            @pl.when(m < 7)
            def _():
                self.load(m + 1).start()

            self.load(m).wait()
            self.swap(m).wait_recv()
            slot = lax.rem(m, 2)

            @pl.loop(0, self.rows // step)
            def _(n):
                at = pl.ds(pl.multiple_of(n * step, step), step)
                self.total[m, at, :] = (self.buf[slot, at, :].astype(F32) + self.total[m, at, :].astype(F32)).astype(BF)

        self.inner.start()

    def finish(self, store):
        self.inner.finish(store)
        for m in range(8):
            self.swap(m).wait_send()


class RowSums:
    @staticmethod
    def scratch(width):
        cols = width // 8
        return [pltpu.VMEM((8, 8, cols), F32), pltpu.VMEM((16, 8, cols), F32)] + [DMA((7,)), DMA((7,)), DMA((15,)), DMA((15,)), DMA((7,)), DMA((7,))]

    def __init__(self, rows, out, scratch):
        self.rows, self.out = rows, out
        self.one, self.two = scratch[:2]
        self.sems = (scratch[2:4], scratch[4:6], scratch[6:8])
        self.d, self.t = lax.axis_index("dp"), lax.axis_index("tensor")
        self.cols = rows.shape[1] // 8

    def columns(self, t):
        return pl.ds(pl.multiple_of(t * self.cols, self.cols), self.cols)

    def first(self, k):
        other = lax.rem(self.t + k, 8)
        return copy_of(self.rows.at[:, self.columns(other)], self.one.at[self.t], self.sems[0], k - 1, (self.d, other))

    def second(self, k):
        own = self.two.at[self.d]
        return copy_of(own, own, self.sems[1], k - 1, (lax.rem(self.d + k, 16), self.t))

    def third(self, k):
        own = self.out.at[:, self.columns(self.t)]
        return copy_of(own, own, self.sems[2], k - 1, (self.d, lax.rem(self.t + k, 8)))

    def run(self, step, last):
        @pl.loop(1, last)
        def _(k):
            step(k)

    def start(self):
        self.run(lambda k: self.first(k).start(), 8)
        self.one[self.t] = self.rows[:, self.columns(self.t)]

    def middle(self):
        self.run(lambda k: self.first(k).wait(), 8)
        total = self.one[0]
        for k in range(1, 8):
            total = total + self.one[k]
        self.two[self.d] = total
        self.run(lambda k: self.second(k).start(), 16)

    def finish(self):
        self.run(lambda k: self.second(k).wait(), 16)
        total = self.two[0]
        for k in range(1, 16):
            total = total + self.two[k]
        self.out[:, self.columns(self.t)] = total
        self.run(lambda k: self.third(k).start(), 8)

    def settle(self):
        self.run(lambda k: self.third(k).wait(), 8)


class Sums:
    @staticmethod
    def scratch(rows, width):
        return [pltpu.VMEM((16, rows, width), F32), DMA((15,)), DMA((15,))]

    def __init__(self, scratch):
        self.slots, self.sems = scratch[0], scratch[1:3]
        self.d, self.t = lax.axis_index("dp"), lax.axis_index("tensor")

    def copy(self, k):
        own = self.slots.at[self.d]
        return copy_of(own, own, self.sems, k - 1, (lax.rem(self.d + k, 16), self.t))

    def start(self):
        @pl.loop(1, 16)
        def _(k):
            self.copy(k).start()

    def finish(self):
        @pl.loop(1, 16)
        def _(k):
            self.copy(k).wait()
        total = self.slots[0]
        for k in range(1, 16):
            total = total + self.slots[k]
        return total


def remote_call(kernel, name, cid, outs, ins, scratch, *args, out_specs=None):
    return pl.pallas_call(
        kernel, out_shape=outs, in_specs=ins,
        out_specs=jax.tree.map(lambda _: VM, outs) if out_specs is None else out_specs,
        scratch_shapes=scratch, name=name,
        compiler_params=pltpu.CompilerParams(collective_id=cid, has_side_effects=True, vmem_limit_bytes=60 << 20),
    )(*args)


def chip_members():
    d, t = lax.axis_index("dp"), lax.axis_index("tensor")
    c = lax.rem(d, 2)
    out = []
    for dt in range(8):
        for dc in range(2):
            if dt or dc:
                tt = lax.rem(t + dt, 8)
                cc = lax.rem(c + dc, 2)
                out.append((tt, cc, (d - c + cc, tt)))
    return out


def norm_rows(values):
    average = jnp.mean(values, axis=-1, keepdims=True)
    centred = values - average
    variance = jnp.mean(centred * centred, axis=-1, keepdims=True)
    inverse = lax.rsqrt(variance + EPS)
    return centred * inverse, inverse


def norm_back(grad, scaled, inverse, gain):
    e = grad * gain
    first = jnp.mean(e, axis=-1, keepdims=True)
    second = jnp.mean(e * scaled, axis=-1, keepdims=True)
    return inverse * (e - first - scaled * second)


def augment(meta, edge_ref, lanes_ref, q_ref, qa_ref, kx_ref):
    rows = q_ref.shape[0]
    nblk = kx_ref.shape[0] // BLK
    prefix = edge_ref[0]
    for a in range(rows // BLK):
        at = slice(a * BLK, (a + 1) * BLK)
        hidden = jnp.where(lanes_ref[...] > meta[first_block() + a], NEG, 0.0)
        qa_ref[at, :HEAD] = q_ref[at, :]
        qa_ref[at, HEAD:] = jnp.zeros((BLK, HEAD), BF)
        qa_ref[at, HEAD:HEAD + nblk] = jnp.broadcast_to(hidden, (BLK, nblk)).astype(BF)
    lane = lax.broadcasted_iota(jnp.int32, (BLK, HEAD), 1)
    inside = lax.broadcasted_iota(jnp.int32, (BLK, HEAD), 0)

    @pl.loop(0, nblk)
    def _(b):
        late = (lane == b) & (inside >= prefix - meta[b] * BLK)
        kx_ref[pl.ds(pl.multiple_of(b * BLK, BLK), BLK), :] = jnp.where(late, 1.0, 0.0).astype(BF)


def first_block():
    return lax.axis_index("dp") // 2 * 4


def front_kernel(meta, edge_ref, lanes_ref, x_hbm, gain1_ref, shift1_ref, wq_ref, wk_ref, wv_ref, qb_ref, vb_ref, wo_hbm, wu_hbm, wd_hbm,
                 bias_ref, gain2_ref, shift2_ref, cot_hbm, ub_ref, db_ref,
                 w_hbm, n_hbm, q_out, kv_hbm, o_ref, lse_ref, own_out, do_out, gm_out, sums_out, low_out, lane_out, lay_out, du_hbm, dd_hbm, dup_out,
                 w_vm, n_vm, kv_vm, out_vm, up_vm, down_vm, wsh, mixed, n2, gsum, colsum,
                 mid_out, x_ref, wo_ref, wu_ref, wd_ref, cot_ref,
                 lsem, css, crs, ass, ars, hss, hrs, *sems):
    gd, gt = Eight("dp"), Eight("tensor")
    t = gt.t
    c = lax.rem(gd.d, 2)
    core = other_core()
    members = chip_members()
    me = gd.index(gd.r, gd.p)
    own = x_ref.shape[0]
    rows = 2 * own
    nblk = 8 * rows // BLK
    per = rows // BLK
    shard = wq_ref.shape[0]
    half = out_vm.shape[1] // 2
    hid = wd_ref.shape[0]
    small = mid_out.shape[0]
    csem, asem = (css, crs), (ass, ars)
    x_load, wo_load, wu_load, wd_load, cot_load = (
        pltpu.make_async_copy(one, two, lsem.at[7 + k]) for k, (one, two) in enumerate(
            ((x_hbm, x_ref), (wo_hbm, wo_ref), (wu_hbm, wu_ref), (wd_hbm, wd_ref), (cot_hbm, cot_ref))))
    for load in (x_load, wo_load, wu_load, wd_load, cot_load):
        load.start()
    for h in range(2):
        cols = slice(h * HEAD, (h + 1) * HEAD)
        for i, ref in enumerate((wq_ref, wk_ref, wv_ref)):
            wsh[h, :, i * HEAD:(i + 1) * HEAD] = ref[:, cols].astype(BF)
    greet([m[2] for m in members] + gd.others())

    w_place = lambda m: w_vm.at[pl.ds(pl.multiple_of(m * 2 * shard, 2 * shard), 2 * shard)]
    row_of = lambda m: pl.ds(pl.multiple_of((m * 2 + c) * shard, shard), shard)
    mine = row_of(me)
    swap = send(wsh.at[1 - c], w_vm.at[mine], csem, 0, core)
    w_vm[mine, :] = wsh[c]
    qkv = Gather(gd, w_place, 2 * shard, sems[0:2])
    keys = Gather(gd, lambda m: kv_vm.at[m], rows, sems[2:4])
    outs = Gather(gd, lambda m: out_vm.at[t, :, row_of(m)], 2 * half, sems[4:8], core)
    ups = Gather(gd, lambda m: up_vm.at[row_of(m)], shard, sems[8:12], core)
    downs = Gather(gd, lambda m: down_vm.at[:, row_of(m)], hid, sems[12:16], core)
    wide = Gather(gt, lambda m: out_vm.at[m, pl.ds(pl.multiple_of(c * half, half), half)], half, sems[16:20], core, twin_own=False)
    normed = Gather(gt, lambda m: n2.at[pl.ds(pl.multiple_of(m * small, small), small)], small, sems[20:22])
    spare = lambda k: (lambda m: n_vm.at[k, pl.ds(pl.multiple_of(m * small, small), small)])
    back = Scatter(gt, spare(0), small, sems[22:28], 32)
    result = Scatter(gt, spare(1), small, sems[28:34], 32)
    grads = CoreScatter(gd, lambda m, cc: du_hbm.at[pl.ds(pl.multiple_of((m * 2 + cc) * shard, shard), shard)], shard, sems[34:45], 32)
    swap.wait_recv()
    qkv.start()

    def norm_part(k):
        step = 32

        @pl.loop(0, own // 2 // step)
        def _(n):
            at = pl.ds(pl.multiple_of(k * (own // 2) + n * step, step), step)
            scaled, _ = norm_rows(x_ref[at, :].astype(F32))
            n_vm[c, at, :] = (scaled * gain1_ref[...] + shift1_ref[...]).astype(BF)

        at = pl.ds(k * (own // 2), own // 2)
        return send(n_vm.at[c, at], n_vm.at[c, at], csem, 1 + k, core)

    x_load.wait()
    there = [norm_part(0)]
    qkv.forward_pair()
    qkv.forward(0)
    wo_load.wait()
    out_vm[t, :, mine] = wo_ref[...].astype(BF)
    outs.start()
    there.append(norm_part(1))
    qkv.forward(1)
    wu_load.wait()
    wd_load.wait()
    up_vm[mine, :] = wu_ref[...].astype(BF)
    down_vm[:, mine] = wd_ref[...].astype(BF)
    for copy in there:
        copy.wait_recv()
    local = pl.ds(pl.multiple_of(c * HEAD, HEAD), HEAD)
    bias_q, bias_v = qb_ref[:, local], vb_ref[:, local]

    def project(sums):
        def term(i, s, first=False):
            m = gd.index(gd.ring(i), gd.side(s))
            cols = pl.ds(pl.multiple_of(m * 2 * shard, 2 * shard), 2 * shard)
            for h in range(2):
                piece = dg(n_vm[h, :, cols], w_vm[cols, :], NN)
                at = slice(h * own, (h + 1) * own)
                sums[at, :] = piece if first else sums[at, :] + piece

        term(0, 0, True)
        for i, s in ((1, 0), (3, 0), (0, 1)):
            term(i, s)
        outs.forward_pair()
        outs.forward(0)
        for i in (1, 3):
            term(i, 1)
        qkv.arrive(0)
        term(2, 0)
        qkv.arrive(1)
        term(2, 1)
        q_out[...] = (sums[:, :HEAD] + bias_q).astype(BF)
        kv_vm[me, :, :HEAD] = sums[:, HEAD:2 * HEAD].astype(BF)
        kv_vm[me, :, HEAD:] = (sums[:, 2 * HEAD:] + bias_v).astype(BF)

    pl.run_scoped(project, pltpu.VMEM((rows, 3 * HEAD), F32))
    keys.start()
    outs.forward(1)
    saves = [pltpu.make_async_copy(w_vm, w_hbm, lsem.at[0]), pltpu.make_async_copy(n_vm, n_hbm, lsem.at[1])]
    for save in saves:
        save.start()
    def attention(qa_ref, kx_ref, m_ref, acc_ref):
        augment(meta, edge_ref, lanes_ref, q_out, qa_ref, kx_ref)
        outs.arrive(0)
        outs.arrive(1)
        outs.settle()
        wide.start()
        m_ref[...] = jnp.full_like(m_ref, -1e30)
        acc_ref[...] = jnp.zeros_like(acc_ref)
        ones = jnp.ones((BLK, HEAD), BF)
        prefix = edge_ref[0]

        def attend(chunk, diagonal):
            ks, vs = [], []
            for i in range(per):
                at = pl.ds(pl.multiple_of(chunk * rows + i * BLK, BLK), BLK)
                ks.append(jnp.concatenate([kv_vm[chunk, i * BLK:(i + 1) * BLK, :HEAD], kx_ref[at, :]], axis=1))
                vs.append(jnp.concatenate([kv_vm[chunk, i * BLK:(i + 1) * BLK, HEAD:], ones], axis=1))
            for a in range(per):
                take = slice(a * BLK, (a + 1) * BLK)
                q = qa_ref[take, :]
                ss = [dg(q, k, NT) for k in ks]
                if diagonal:
                    edge = prefix - 1 - meta[first_block() + a] * BLK
                    lim = jnp.maximum(lax.broadcasted_iota(jnp.int32, (BLK, BLK), 0), edge)
                    key = lax.broadcasted_iota(jnp.int32, (BLK, BLK), 1)
                    ss[a] = jnp.where(key <= lim, ss[a], NEG)
                top = ss[0]
                for s in ss[1:]:
                    top = jnp.maximum(top, s)
                old = m_ref[take, :1]
                new = jnp.maximum(old, jnp.max(top, axis=1, keepdims=True) * C1)
                alpha = jnp.exp2(old - new)
                add = None
                for s, v in zip(ss, vs):
                    term = jnp.dot(jnp.exp2(s * C1 - new).astype(BF), v, preferred_element_type=F32)
                    add = term if add is None else add + term
                acc_ref[take, :] = acc_ref[take, :] * alpha + add
                m_ref[take, :] = jnp.broadcast_to(new, (BLK, HEAD))

        attend(me, True)

        @pl.loop(1, 8)
        def _(k):
            kk = lax.rem(k, 4)
            i, s = kk + kk // 2 - 2 * (kk // 3), k // 4

            @pl.when(k == 1)
            def _():
                keys.forward_pair()
                keys.forward(0)

            @pl.when(k == 2)
            def _():
                wide.forward_pair()
                wide.forward(0)

            @pl.when(k == 3)
            def _():
                keys.arrive(0)

            @pl.when(k == 5)
            def _():
                keys.forward(1)
                wide.forward(1)
                ups.start()

            @pl.when(k == 7)
            def _():
                keys.arrive(1)

            attend(gd.index(gd.ring(i), gd.p + s * (1 - 2 * gd.p)), False)

        for a in range(per):
            at = slice(a * BLK, (a + 1) * BLK)
            total = acc_ref[at, HEAD:]
            o_ref[at, :] = (acc_ref[at, :HEAD] / total).astype(BF)
            lse_ref[a:a + 1, :] = jnp.transpose(m_ref[at, :] + jnp.log2(total))[:1, :]

    pl.run_scoped(
        attention, pltpu.VMEM((rows, 2 * HEAD), BF), pltpu.VMEM((8 * rows, HEAD), BF), pltpu.VMEM((rows, HEAD), F32), pltpu.VMEM((rows, 2 * HEAD), F32))
    head = pl.ds(pl.multiple_of((2 * t + c) * HEAD, HEAD), HEAD)
    copies = []
    for k, (tt, cc, device) in enumerate(members):
        take = pl.ds(pl.multiple_of(cc * own + tt * small, small), small)
        copies.append(send(o_ref.at[take], mixed.at[:, head], asem, k, device))
    copies.append(send(o_ref.at[pl.ds(pl.multiple_of((1 - c) * own, own), own)], own_out.at[:, local], asem, 15, core))
    keys.settle()
    save = pltpu.make_async_copy(kv_vm, kv_hbm, lsem.at[2])
    save.start()
    saves.append(save)
    downs.start()
    mixed[:, head] = o_ref[pl.ds(pl.multiple_of(c * own + t * small, small), small), :]
    own_out[:, local] = o_ref[pl.ds(pl.multiple_of(c * own, own), own), :]
    ups.forward_pair()
    ups.forward(0)
    wide.arrive(0)
    wide.arrive(1)
    wide.settle()
    ups.forward(1)
    downs.forward_pair()
    for copy in copies:
        copy.wait_recv()
    span = 512
    x_rows = pl.ds(pl.multiple_of(t * small, small), small)
    for n in range(mid_out.shape[1] // span):
        cols = pl.ds(n * span, span)
        total = None
        for k in range(8):
            term = dg(mixed[:, k * 256:(k + 1) * 256], out_vm[k, :, cols], NN)
            total = term if total is None else total + term
        mid_out[:, cols] = total + (x_ref[x_rows, cols].astype(F32) + bias_ref[:, cols])
    scaled, _ = norm_rows(mid_out[...])
    n2[pl.ds(pl.multiple_of(t * small, small), small), :] = (scaled * gain2_ref[...] + shift2_ref[...]).astype(BF)
    normed.start()
    downs.forward(0)
    ups.arrive(0)
    ups.arrive(1)
    normed.forward_pair()
    normed.forward(0)
    downs.forward(1)
    normed.forward(1)
    ups.settle()
    downs.arrive(0)
    downs.arrive(1)
    downs.settle()
    cot_load.wait()
    saves.pop(1).wait()
    for copy in there:
        copy.wait_send()
    blocks = [(slice(n * span, (n + 1) * span)) for n in range(hid // span)]
    wide_blocks = [(slice(n * span, (n + 1) * span)) for n in range(n2.shape[1] // span)]

    def feed_forward(gh, hidden, gp, du_buf, dd_buf):
        @pl.loop(0, own // BLK)
        def _(b):
            at = pl.ds(pl.multiple_of(b * BLK, BLK), BLK)
            for cols in blocks:
                gh[at, cols] = dg(cot_ref[at, :], down_vm[cols, :], NT)

        normed.arrive(0)
        normed.arrive(1)
        normed.settle()
        colsum[...] = jnp.zeros_like(colsum)

        @pl.loop(0, own // BLK)
        def _(b):
            at = pl.ds(pl.multiple_of(b * BLK, BLK), BLK)
            for cols in blocks:
                pre = dg(n2[at, :], up_vm[:, cols], NN) + ub_ref[:, cols]
                half_erf = 0.5 + 0.5 * lax.erf(pre * math.sqrt(0.5))
                hidden[at, cols] = (pre * half_erf).astype(BF)
                slope = half_erf + pre * jnp.exp(-0.5 * pre * pre) * (1.0 / math.sqrt(2.0 * math.pi))
                low = (gh[at, cols] * slope).astype(BF)
                gp[at, cols] = low
                colsum[0:1, cols] += jnp.sum(low.astype(F32), axis=0, keepdims=True)
            for cols in wide_blocks:
                n_vm[0, at, cols] = dg(gp[at, :], up_vm[cols, :], NT).astype(BF)

        back.start()

        def du_save(m):
            slot = lax.rem(m, 2)
            return pltpu.make_async_copy(du_buf.at[slot], du_hbm.at[pl.ds(pl.multiple_of(m * BLK, BLK), BLK)], lsem.at[3 + slot])

        def dd_save(m):
            slot = lax.rem(m, 2)
            return pltpu.make_async_copy(dd_buf.at[slot], dd_hbm.at[:, pl.ds(pl.multiple_of(m * BLK, BLK), BLK)], lsem.at[5 + slot])

        def blocks_of(save, buf, value):
            @pl.loop(0, 8)
            def _(m):
                @pl.when(m > 1)
                def _():
                    save(m - 2).wait()

                buf[lax.rem(m, 2)] = value(pl.ds(pl.multiple_of(m * BLK, BLK), BLK)).astype(BF)
                save(m).start()

        blocks_of(du_save, du_buf, lambda cols: dg(n2[:, cols], gp[...], TN))
        back.add_near(1)
        back.add_near(0)
        du_save(6).wait()
        du_save(7).wait()
        grads.start()

        @pl.loop(0, own // BLK)
        def _(b):
            at = pl.ds(pl.multiple_of(b * BLK, BLK), BLK)
            for cols in wide_blocks:
                n_vm[1, at, cols] = dg(hidden[at, :], down_vm[:, cols], NN).astype(BF)

        back.add_pair()
        result.start()
        grads.add()
        blocks_of(dd_save, dd_buf, lambda cols: dg(hidden[...], cot_ref[:, cols], TN))
        dd_save(6).wait()
        dd_save(7).wait()

    pl.run_scoped(
        feed_forward, pltpu.VMEM((own, hid), F32), pltpu.VMEM((own, hid), BF), pltpu.VMEM((own, hid), BF), pltpu.VMEM((2, BLK, hid), BF),
        pltpu.VMEM((2, hid, BLK), BF))

    def keep(at, value):
        gsum[at, :] = value

    back.finish(keep)
    scaled, inverse = norm_rows(mid_out[...])
    grad = gsum[...]
    g_rows = cot_ref[x_rows, :].astype(F32)
    gm = g_rows + norm_back(grad, scaled, inverse, gain2_ref[...])
    gm_out[...] = gm
    low = gm.astype(BF)
    low_out[...] = low
    for k in range(8):
        mixed[:, k * 256:(k + 1) * 256] = dg(low, out_vm[k], NT).astype(BF)
    hsem = (hss, hrs)
    take = pl.ds(pl.multiple_of(c * own + t * small, small), small)
    heads = []
    for k, (tt, cc, device) in enumerate(members):
        cols = pl.ds(pl.multiple_of((2 * tt + cc) * HEAD, HEAD), HEAD)
        heads.append(send(mixed.at[:, cols], do_out.at[take], hsem, k, device))
    do_out[take, :] = mixed[:, head]
    result.add_near(1)
    result.add_near(0)
    grads.inner.add_near(1)
    grads.inner.add_near(0)
    result.add_pair()
    sums_out[...] = jnp.zeros_like(sums_out)
    sums_out[0:1, :] = jnp.sum(grad * scaled, axis=0, keepdims=True)
    sums_out[1:2, :] = jnp.sum(grad, axis=0, keepdims=True)
    sums_out[2:3, :] = jnp.sum(low.astype(F32), axis=0, keepdims=True)
    sums_out[3:4, :] = jnp.sum(g_rows, axis=0, keepdims=True)
    lane_out[...] = jnp.zeros_like(lane_out)
    for j in range(hid // 256):
        lane_out[j:j + 1, :] = colsum[0:1, j * 256:(j + 1) * 256]
    grads.inner.add_pair()

    def lay(at, value):
        lay_out[at, :] = (mid_out[at, :] + (value + db_ref[...])).astype(BF)

    result.finish(lay)

    def keep_up(at, value):
        dup_out[at, :] = value

    grads.finish(keep_up)
    qkv.settle()
    swap.wait_send()
    for copy in copies:
        copy.wait_send()
    for save in saves:
        save.wait()
    for copy in heads:
        copy.wait()


def front_call(meta, edge, lanes, x, gain1, shift1, wq, wk, wv, qb, vb, wo, wu, wd, bias, gain2, shift2, cot, ub, db):
    own, width = x.shape
    rows, shard, hid, small = 2 * own, wq.shape[0], wu.shape[1], own // 8
    hbm = pl.BlockSpec(memory_space=pl.ANY)
    big = [(width, 3 * HEAD), (2, own, width), (8, rows, 2 * HEAD), (8, 2 * HEAD, width), (width, hid), (hid, width)]
    w, n, kv, out, up, down = (struct(s, BF) for s in big)
    outs = (w, n, struct((rows, HEAD), BF), kv, struct((rows, HEAD), BF), struct((rows // BLK, BLK), F32),
            struct((own, 2 * HEAD), BF), struct((rows, HEAD), BF), struct((small, width), F32),
            struct((8, width), F32), struct((small, width), BF), struct((8, 256), F32), struct((small, width), BF), up, down, struct((shard, hid), F32))
    return remote_call(
        front_kernel, "front", 1, outs, [SM, SM, VM, hbm] + [VM] * 7 + [hbm] * 3 + [VM] * 3 + [hbm, VM, VM],
        [pltpu.VMEM(s, BF) for s in big]
        + [pltpu.VMEM((2, shard, 3 * HEAD), BF), pltpu.VMEM((small, width), BF), pltpu.VMEM((own, width), BF),
           pltpu.VMEM((small, width), F32), pltpu.VMEM((8, hid), F32),
           pltpu.VMEM((small, width), F32), pltpu.VMEM(x.shape, BF), pltpu.VMEM(wo.shape, F32), pltpu.VMEM(wu.shape, F32), pltpu.VMEM(wd.shape, F32),
           pltpu.VMEM(cot.shape, BF),
           DMA((12,)), DMA((3,)), DMA((3,)), DMA((16,)), DMA((16,)), DMA((15,)), DMA((15,))]
        + Gather.scratch() * 2 + Gather.scratch(True) * 4 + Gather.scratch() + Scatter.scratch(small, width) * 2 + CoreScatter.scratch(shard, hid),
        meta, edge, lanes, x, gain1, shift1, wq, wk, wv, qb, vb, wo, wu, wd, bias, gain2, shift2, cot, ub, db,
        out_specs=(hbm, hbm, VM, hbm) + (VM,) * 9 + (hbm, hbm, VM))


def rear_kernel(meta, edge_ref, lanes_ref, q_ref, kv_hbm, o_ref, do_ref, lse_ref, gbr_ref, layr_ref, ddown_hbm,
                mixed_hbm, n_hbm, w_hbm, gm_hbm, x_hbm, gain_ref, early_ref, lane_ref,
                lay_out, ddown_out, dwo_out, dwq_out, dwk_out, dwv_out, tg_out, sums_out, lanes_out,
                kv_ref, qa_ref, kx_ref, part, delta_ref, dq_acc, gb, dqkv, dwo, n_buf, dw, away, arrived, summed, total, mine_w, there_w, vec, x_ref, mixed_ref, w_ref, gm_ref,
                lsem, css, crs, *scratch):
    g, gt = Eight("dp"), Eight("tensor")
    c = lax.rem(g.d, 2)
    core = other_core()
    me, mine_t = g.index(g.r, g.p), gt.index(gt.r, gt.p)
    rows = q_ref.shape[0]
    own = rows // 2
    nblk = kx_ref.shape[0] // BLK
    per = rows // BLK
    small, width = gm_ref.shape
    order = [(2, 1), (1, 1), (3, 1), (2, 0), (1, 0), (3, 0), (0, 1), (0, 0)]

    def kv_load(n):
        i, s = order[n]
        m = g.index(g.ring(i), g.side(s))
        return pltpu.make_async_copy(kv_hbm.at[m], kv_ref.at[m], lsem.at[3 + n])

    for n in range(8):
        kv_load(n).start()
    mixed_load, w_load, gm_load = (
        pltpu.make_async_copy(one, two, lsem.at[11 + k]) for k, (one, two) in enumerate(
            ((mixed_hbm, mixed_ref), (w_hbm, w_ref), (gm_hbm, gm_ref))))
    for load in (mixed_load, w_load, gm_load):
        load.start()
    everyone = [(lax.rem(g.d + k, 16), g.t) for k in range(1, 16)] + [(g.d, lax.rem(g.t + k, 8)) for k in range(1, 8)]
    greet(everyone)
    take = list(scratch)

    def some(count):
        out = take[:count]
        del take[:count]
        return out

    share = dwo_out.shape[1]
    by_columns = lambda m, cc: dwo.at[:, pl.ds(pl.multiple_of((m * 2 + cc) * share, share), share)]
    keys = Scatter(g, lambda m: part.at[m], rows, some(6), 128)
    downs = CoreScatter(
        g, lambda m, cc: ddown_hbm.at[:, pl.ds(pl.multiple_of((m * 2 + cc) * share, share), share)], ddown_out.shape[0], some(CoreScatter.COUNT), 128)
    dwos = CoreScatter(g, by_columns, dwo_out.shape[0], some(CoreScatter.COUNT), 128)
    tokens = Scatter(gt, lambda m: summed.at[m], small, some(6), 32)
    weights = Scatter(g, lambda m: dw.at[m], dw.shape[1], some(6), 128)
    wide = Gather(gt, lambda m: gb.at[pl.ds(pl.multiple_of(m * small, small), small)], small, some(2))
    layer = Gather(gt, lambda m: lay_out.at[m], small, some(2))
    final = Gather(gt, lambda m: tg_out.at[m], small, some(2))
    sums = RowSums(vec, sums_out, some(8))
    lane_sums = Sums(some(3))
    csem = (css, crs)
    x_load = pltpu.make_async_copy(x_hbm.at[pl.ds(pl.multiple_of(g.t * small, small), small)], x_ref, lsem.at[2])
    x_load.start()

    def n_load(m):
        slot = lax.rem(m, 2)
        return pltpu.make_async_copy(n_hbm.at[:, pl.ds(pl.multiple_of(m * BLK, BLK), BLK)], n_buf.at[slot], lsem.at[slot])

    downs.start()
    lay_out[mine_t] = layr_ref[...]
    gb[pl.ds(pl.multiple_of(mine_t * small, small), small), :] = gbr_ref[...]
    wide.start()
    layer.start()
    augment(meta, edge_ref, lanes_ref, q_ref, qa_ref, kx_ref)
    for a in range(per):
        at = slice(a * BLK, (a + 1) * BLK)
        prod = do_ref[at, :].astype(F32) * o_ref[at, :].astype(F32)
        delta_ref[0:1, at] = jnp.sum(jnp.transpose(prod), axis=0, keepdims=True)
        delta_ref[1:2, at] = lse_ref[a:a + 1, :]
    dq_acc[...] = jnp.zeros_like(dq_acc)
    prefix = edge_ref[0]

    def attend(chunk, diagonal):
        k = kv_ref[chunk, :, :HEAD]
        v = kv_ref[chunk, :, HEAD:]
        kk = jnp.concatenate([k, kx_ref[pl.ds(pl.multiple_of(chunk * rows, rows), rows), :]], axis=1)
        turned = jnp.transpose(k.astype(F32)).astype(BF)
        dk = dv = None
        for a in range(per):
            at_q = slice(a * BLK, (a + 1) * BLK)
            q = q_ref[at_q, :]
            do = do_ref[at_q, :]
            p = jnp.exp2(dg(kk, qa_ref[at_q, :], NT) * C1 - delta_ref[1:2, at_q])
            if diagonal:
                edge = prefix - 1 - meta[first_block() + a] * BLK
                lim = jnp.maximum(lax.broadcasted_iota(jnp.int32, (BLK, BLK), 1), edge)
                mid = jnp.where(lax.broadcasted_iota(jnp.int32, (BLK, BLK), 0) <= lim, p[a * BLK:(a + 1) * BLK], 0.0)
                p = jnp.concatenate([p[b * BLK:(b + 1) * BLK] if b != a else mid for b in range(per)], axis=0)
            ds = (p * (dg(v, do, NT) - delta_ref[0:1, at_q])).astype(BF)
            tv = jnp.dot(p.astype(BF), do, preferred_element_type=F32)
            tk = jnp.dot(ds, q, preferred_element_type=F32)
            dv = tv if dv is None else dv + tv
            dk = tk if dk is None else dk + tk
            dq_acc[:, at_q] += jnp.dot(turned, ds, preferred_element_type=F32)
        part[chunk, :, :HEAD] = (dk * SCALE).astype(BF)
        part[chunk, :, HEAD:] = dv.astype(BF)

    for n in range(8):
        kv_load(n).wait()

    @pl.loop(0, 7)
    def _(k):
        kk = lax.rem(k, 3)
        i = (2 - kk + 3 * (kk // 2)) * (1 - k // 6)
        s = 1 - k // 3 + 2 * (k // 6)
        attend(g.index(g.ring(i), g.p + s * (1 - 2 * g.p)), False)

        @pl.when(k == 0)
        def _():
            keys.send_far(1)
            wide.forward_pair()
            wide.forward(0)

        @pl.when(k == 1)
        def _():
            layer.forward_pair()
            layer.forward(0)

        @pl.when(k == 2)
        def _():
            keys.send_near(1)
            keys.add_near(1)
            wide.forward(1)

        @pl.when(k == 3)
        def _():
            keys.send_far(0)

        @pl.when(k == 4)
        def _():
            layer.forward(1)

        @pl.when(k == 5)
        def _():
            keys.send_near(0)
            keys.add_near(0)

        @pl.when(k == 6)
        def _():
            keys.add_pair()

    n_load(0).start()
    attend(me, True)
    dqkv[:, :HEAD] = jnp.transpose(dq_acc[...] * SCALE).astype(BF)
    wide.arrive(0)
    wide.arrive(1)
    wide.settle()
    span = 512
    mixed_load.wait()
    for n in range(width // span):
        cols = pl.ds(n * span, span)
        dwo[:, cols] = dg(mixed_ref[...], gb[:, cols], TN).astype(BF)
    dwos.start()
    downs.add()

    def keep_keys(at, value):
        dqkv[at, HEAD:] = value.astype(BF)

    keys.finish(keep_keys)

    def project(into, half):
        @pl.loop(0, own // BLK)
        def _(b):
            at = pl.ds(pl.multiple_of(half * own + b * BLK, BLK), BLK)
            for n in range(width // span):
                cols = pl.ds(n * span, span)
                piece = dg(dqkv[at, :], w_ref[cols, :], NT).astype(BF)
                for j in range(BLK // small):
                    into[b * (BLK // small) + j, :, cols] = piece[j * small:(j + 1) * small]

    w_load.wait()
    project(away, 1 - c)
    swap = send(away, arrived, csem, 0, core)
    project(summed, c)
    swap.wait_recv()

    @pl.loop(0, 8)
    def _(m):
        @pl.loop(0, small // 32)
        def _(n):
            at = pl.ds(pl.multiple_of(n * 32, 32), 32)
            summed[m, at, :] = (summed[m, at, :].astype(F32) + arrived[m, at, :].astype(F32)).astype(BF)

    tokens.start()

    @pl.loop(0, 8)
    def _(m):
        @pl.when(m < 7)
        def _():
            n_load(m + 1).start()

        n_load(m).wait()
        dw[m] = dg(n_buf[lax.rem(m, 2)], dqkv[...], TN).astype(BF)

    weights.start()
    tokens.add_near(1)
    tokens.add_near(0)
    tokens.add_pair()
    dwos.add()
    slot = lane_sums.slots
    slot[g.d] = lane_ref[...]
    local = pl.ds(pl.multiple_of(c * HEAD, HEAD), HEAD)
    slot[g.d, 4:5, local] = jnp.sum(dqkv[:, :HEAD].astype(F32), axis=0, keepdims=True)
    slot[g.d, 5:6, local] = jnp.sum(dqkv[:, 2 * HEAD:].astype(F32), axis=0, keepdims=True)
    lane_sums.start()
    downs.inner.add_near(1)
    downs.inner.add_near(0)

    def keep(at, value):
        total[at, :] = value

    x_load.wait()
    gm_load.wait()
    tokens.finish(keep)
    scaled, inverse = norm_rows(x_ref[...].astype(F32))
    grad = total[...]
    tg = gm_ref[...] + norm_back(grad, scaled, inverse, gain_ref[...])
    tg_out[mine_t] = tg.astype(BF)
    final.start()
    vec[...] = early_ref[...]
    vec[4:5, :] = jnp.sum(grad * scaled, axis=0, keepdims=True)
    vec[5:6, :] = jnp.sum(grad, axis=0, keepdims=True)
    sums.start()
    weights.add_near(1)
    weights.add_near(0)
    final.forward_pair()
    final.forward(0)
    dwos.inner.add_near(1)
    dwos.inner.add_near(0)
    downs.inner.add_pair()
    sums.middle()
    weights.add_pair()
    final.forward(1)
    dwos.inner.add_pair()

    def keep_w(at, value):
        mine_w[at, :] = value.astype(BF)

    weights.finish(keep_w)
    part_rows = there_w.shape[0]
    there = send(mine_w.at[pl.ds(pl.multiple_of((1 - c) * part_rows, part_rows), part_rows)], there_w, csem, 1, core)

    def keep_down(at, value):
        ddown_out[at, :] = value

    downs.finish(keep_down)
    sums.finish()

    def keep_o(at, value):
        dwo_out[at, :] = value

    dwos.finish(keep_o)
    kept = mine_w[pl.ds(pl.multiple_of(c * part_rows, part_rows), part_rows), :].astype(F32)
    far = pl.ds(pl.multiple_of((1 - c) * HEAD, HEAD), HEAD)
    there.wait()
    for i, ref in enumerate((dwq_out, dwk_out, dwv_out)):
        ref[:, local] = kept[:, i * HEAD:(i + 1) * HEAD]
        ref[:, far] = there_w[:, i * HEAD:(i + 1) * HEAD].astype(F32)
    lanes_out[...] = lane_sums.finish()
    layer.arrive(0)
    layer.arrive(1)
    layer.settle()
    final.arrive(0)
    final.arrive(1)
    sums.settle()
    final.settle()
    swap.wait_send()


def rear_call(meta, edge, lanes, q, kv, o, do, lse, gb, lay, ddown, mixed, n, w, gm, x, gain, early, lane):
    rows = q.shape[0]
    small, width = gm.shape
    hbm = pl.BlockSpec(memory_space=pl.ANY)
    chunks = (8, small, width)
    wc = 3 * HEAD
    share = width // 16
    head_grad = struct((share, 2 * HEAD), F32)
    return remote_call(
        rear_kernel, "rear", 5,
        (struct(chunks, BF), struct((ddown.shape[0], share), F32), struct((2 * HEAD, share), F32), head_grad, head_grad, head_grad,
         struct(chunks, BF), struct((8, width), F32), struct(lane.shape, F32)),
        [SM, SM, VM, VM, hbm] + [VM] * 5 + [hbm] * 6 + [VM] * 3,
        [pltpu.VMEM(kv.shape, BF), pltpu.VMEM((rows, 2 * HEAD), BF), pltpu.VMEM((8 * rows, HEAD), BF), pltpu.VMEM(kv.shape, BF), pltpu.VMEM((8, rows), F32),
         pltpu.VMEM((HEAD, rows), F32), pltpu.VMEM((8 * small, width), BF), pltpu.VMEM((rows, wc), BF), pltpu.VMEM((2 * HEAD, width), BF),
         pltpu.VMEM((2, rows, BLK), BF), pltpu.VMEM((8, width // 8, wc), BF), pltpu.VMEM(chunks, BF), pltpu.VMEM(chunks, BF),
         pltpu.VMEM(chunks, BF), pltpu.VMEM((small, width), F32), pltpu.VMEM((width // 8, wc), BF), pltpu.VMEM((share, wc), BF),
         pltpu.VMEM((8, width), F32), pltpu.VMEM((small, width), BF), pltpu.VMEM(mixed.shape, BF),
         pltpu.VMEM(w.shape, BF), pltpu.VMEM(gm.shape, F32), DMA((14,)), DMA((2,)), DMA((2,))]
        + Scatter.scratch(rows, 2 * HEAD) + CoreScatter.scratch(ddown.shape[0], share)
        + CoreScatter.scratch(2 * HEAD, share) + Scatter.scratch(small, width) + Scatter.scratch(width // 8, wc)
        + Gather.scratch() * 3 + RowSums.scratch(width) + Sums.scratch(*lane.shape),
        meta, edge, lanes, q, kv, o, do, lse, gb, lay, ddown, mixed, n, w, gm, x, gain, early, lane)


def finish_kernel(layer, tg, small_ref, lane_ref, up, down, out, wq, wk, wv,
                  layer_out, tg_out, gain1, shift1, qb, vb, ob, gain2, shift2, ub, db, up_out, down_out, out_out, wq_out, wk_out, wv_out,
                  low, high, *scratch):
    ways = ((layer, layer_out), (up, up_out), (down, down_out), (out, out_out), (wq, wq_out), (wk, wk_out), (wv, wv_out))
    buffers, (insem, outsem, tin, tout) = scratch[:7], scratch[7:]
    parts = tg.shape[0]
    loads = [pltpu.make_async_copy(tg.at[k], low.at[k], tin.at[k]) for k in range(parts)]
    saves = [pltpu.make_async_copy(high.at[k], tg_out.at[k], tout.at[k]) for k in range(parts)]
    there = [pltpu.make_async_copy(way[0], buffer, insem.at[k]) for k, (way, buffer) in enumerate(zip(ways, buffers))]
    back = [pltpu.make_async_copy(buffer, way[1], outsem.at[k]) for k, (way, buffer) in enumerate(zip(ways, buffers))]
    for copy in there + loads:
        copy.start()
    for k, ref in ((4, gain1), (5, shift1), (2, ob), (0, gain2), (1, shift2), (3, db)):
        ref[...] = small_ref[k:k + 1, :]
    for j in range(ub.shape[1] // 256):
        ub[:, j * 256:(j + 1) * 256] = lane_ref[j:j + 1, :]
    qb[...] = lane_ref[4:5, :]
    vb[...] = lane_ref[5:6, :]
    for one, two in zip(there, back):
        one.wait()
        two.start()
    for k in range(parts):
        loads[k].wait()
        high[k] = low[k].astype(F32)
        saves[k].start()
    for copy in saves + back:
        copy.wait()


def finish_call(layer, tg, small, lane, hid, rest):
    hbm = pl.BlockSpec(memory_space=pl.ANY)
    width = small.shape[1]
    line = lambda n: struct((1, n), F32)
    return pl.pallas_call(
        finish_kernel,
        out_shape=(struct(layer.shape, BF), struct(tg.shape, F32), line(width), line(width), line(256), line(256), line(width), line(width),
                   line(width), line(hid), line(width)) + tuple(struct(r.shape, F32) for r in rest),
        in_specs=[hbm, hbm, VM, VM] + [hbm] * 6,
        out_specs=(hbm, hbm) + (VM,) * 9 + (hbm,) * 6,
        scratch_shapes=[pltpu.VMEM(tg.shape, BF), pltpu.VMEM(tg.shape, F32), pltpu.VMEM(layer.shape, BF)] + [pltpu.VMEM(r.shape, F32) for r in rest]
        + [DMA((7,)), DMA((7,)), DMA((tg.shape[0],)), DMA((tg.shape[0],))],
        compiler_params=pltpu.CompilerParams(vmem_limit_bytes=60 << 20),
        name="finish",
    )(layer, tg, small, lane, *rest)


def on_device(tokens, first_gain, first_shift, query_weight, query_bias, key_weight, value_weight, value_bias,
              out_weight, out_bias, second_gain, second_shift, up_weight, up_bias, down_weight, down_bias,
              cotangent, prefix, block_order):
    own, width = tokens.shape
    d, t = lax.axis_index("dp"), lax.axis_index("tensor")
    c = lax.rem(d, 2)
    nblk = block_order.shape[0]
    rows = own // 8
    meta, edge, lanes = block_order, prefix, block_order.reshape(1, nblk)
    row = lambda v: v.reshape(1, -1)

    w_all, n_all, q, kv, o, lse, mixed, do, gm, sums, low, lane, layer, dw_up, dw_down, up_grad = front_call(
        meta, edge, lanes, tokens, row(first_gain), row(first_shift), query_weight, key_weight, value_weight, row(query_bias), row(value_bias),
        out_weight, up_weight, down_weight, row(out_bias), row(second_gain), row(second_shift), cotangent, row(up_bias), row(down_bias))
    layer, down_grad, out_grad, dwq, dwk, dwv, tg, small, lane = rear_call(
        meta, edge, lanes, q, kv, o, do, lse, low, layer, dw_down, mixed, n_all.reshape(2 * own, width), w_all, gm,
        tokens, row(first_gain), sums, lane)
    hid = up_weight.shape[1]
    layer, tg, gain1, shift1, qb, vb, ob, gain2, shift2, ub, db, up_grad, down_grad, out_grad, dwq, dwk, dwv = finish_call(
        layer, tg, small, lane, hid, (up_grad, down_grad, out_grad, dwq, dwk, dwv))
    flat = lambda v: v.reshape(-1)
    return (
        layer.reshape(own, width), tg.reshape(own, width), flat(gain1), flat(shift1), dwq, flat(qb), dwk, dwv, flat(vb), out_grad, flat(ob),
        flat(gain2), flat(shift2), up_grad, flat(ub), down_grad, flat(db))


def solution(mesh):
    rows, cols = P("dp", "tensor"), P("tensor", "dp")
    return jax.shard_map(
        on_device,
        mesh=mesh,
        in_specs=(
            P("dp", None), P(), P(), rows, P("tensor"), rows, rows, P("tensor"), cols, P(), P(), P(), rows, P("tensor"),
            cols, P(), P("dp", None), P(), P()),
        out_specs=(
            P("dp", None), P("dp", None), P(), P(), rows, P("tensor"), rows, rows, P("tensor"), cols, P(), P(), P(), rows,
            P("tensor"), cols, P()),
        check_vma=False,
    )
```
